32 devices in a mesh: exp: 16 (over z, y, x), head: 2 (over core).
Axes of the slice: x: 2, y: 2, z: 4, core: 2. Of those that a mesh axis runs over, the one named last changes fastest.
Arguments:
- tokens: bfloat16 [4096, 1024], P('exp'), may hold values from -6 to 6
- norm_one: float32 [1024], replicated, may hold values from 0.5 to 1.5
- w_query: bfloat16 [1024, 1024], P(None, 'head'), may hold values from -0.625 to 0.625
- key_weight: bfloat16 [1024, 512], P(None, 'head'), may hold values from -0.625 to 0.625
- value_weight: bfloat16 [1024, 512], P(None, 'head'), may hold values from -0.1875 to 0.1875
- w_output: bfloat16 [1024, 1024], P('head'), may hold values from -9 to 9
- norm_two: float32 [1024], replicated, may hold values from 0.5 to 1.5
- w_router: bfloat16 [1024, 32], replicated, may hold values from -0.08984375 to 0.08984375
- w_gate: bfloat16 [1024, 16384], P(None, 'exp'), may hold values from -0.1875 to 0.1875
- w_up: bfloat16 [1024, 16384], P(None, 'exp'), may hold values from -0.1875 to 0.1875
- w_down: bfloat16 [16384, 1024], P('exp'), may hold values from -6 to 6
- routes: int32 [4096, 8], P('exp'), may hold values from 0 to 31, all different within a row
- priority: int32 [32, 128], P(('exp', 'head')), may hold values from 0 to 127, each once within a row
- cotangent: bfloat16 [4096, 1024], P(('exp', 'head')), may hold values from -6 to 6
Outputs:
- layer_out: bfloat16 [4096, 1024], P(('exp', 'head'))
- grad_tokens: float32 [4096, 1024], P(('exp', 'head'))
- grad_norm_one: float32 [1024], replicated
- grad_query: float32 [1024, 1024], P(None, 'head')
- grad_key: float32 [1024, 512], P(None, 'head')
- grad_value: float32 [1024, 512], P(None, 'head')
- grad_output: float32 [1024, 1024], P('head')
- grad_norm_two: float32 [1024], replicated
- grad_router: float32 [1024, 32], replicated
- grad_gate: float32 [1024, 16384], P(None, 'exp')
- grad_up: float32 [1024, 16384], P(None, 'exp')
- grad_down: float32 [16384, 1024], P('exp')
The draws below stay inside these ranges and needn't reach their ends.
Inputs may be any that keep to these rules, and one draw needn't show every extreme that they name: `routes`: each row names 8 different experts; every expert is named by some row. `priority`: each row is an ordering of the 128 tokens of one row block: a smaller number takes a slot first.
All inputs are finite; a program needn't handle non-finite values.
Results may differ from the reference program's by a relative error of at most 0.018.
The reference program's roundings to bfloat16 on the way count: a program that leaves them out, or rounds other values in their place, can miss the bound.
Values may be sent and summed in bfloat16 or wider, within the bound.
A program may use at most 192 MiB of HBM per device.

```python
import jax
import jax.numpy as jnp
from jax import lax

MODEL_DIMENSION = 1024
QUERY_HEADS = 16
KEY_VALUE_HEADS = 8
HEAD_DIMENSION = 64
FF = 512
TOPK = 8
EXPERTS = 32
TOKENS_PER_GROUP = 256
PROMPT_LEN = 128
CONT_LEN = 64
PROMPT_GROUPS = 16
TOKEN_TOTAL = 4096
HALF = 128
CAP = 40
SPLIT = 1
N_EXP = 16
N_HEAD = 2


def shard_levels(rng, dims, cuts, least, largest):
    loudness, own = 1.0, jax.random.fold_in(rng, 6)
    for axis_at, shards_of in cuts:
        steps = jnp.exp(jax.random.uniform(jax.random.fold_in(own, axis_at), (shards_of,), jnp.float32, least / len(cuts), largest / len(cuts)))
        loudness = loudness * jnp.repeat(steps, dims[axis_at] // shards_of).reshape([-1 if axis == axis_at else 1 for axis in range(len(dims))])
    return loudness


def distinct(rng, rows, number_of, top, lift):
    ranking = jax.random.permutation(jax.random.fold_in(rng, 1), number_of)
    pull = ranking
    for power in range(3):
        pull = pull * pull // number_of
    pull = pull * lift // number_of
    chance = jax.random.randint(jax.random.fold_in(rng, 2), (rows, number_of), 0, 4096) + pull
    sure = jax.random.permutation(jax.random.fold_in(rng, 3), rows)[jnp.arange(number_of) % rows]
    chance = jnp.where(jnp.arange(rows)[:, None] == sure[None, :], 1 << 14, chance)
    score = chance * number_of + jnp.arange(number_of)
    return lax.top_k(score.astype(jnp.int32), top)[1].astype(jnp.int32)


def scatter_about(stream_key, dims, scale, limit, shards=(), kind=jnp.bfloat16):
    array = jax.random.normal(stream_key, dims, jnp.float32) * scale
    if len(shards) > 0:
        array = shard_levels(stream_key, dims, shards, -0.22, 0.18) * array
    return jnp.clip(array, min=-limit, max=limit).astype(kind)


def setup_inputs(seed: int = 0) -> dict:
    keys = jax.random.split(jax.random.key(seed), 15)
    return {
        "tokens": scatter_about(keys[0], (TOKEN_TOTAL, MODEL_DIMENSION), 1.0, 6.0, ((0, 16),)),
        "norm_one": jnp.clip(1.0 + 0.1 * jax.random.normal(keys[1], (MODEL_DIMENSION,), jnp.float32), 0.5, 1.5),
        "w_query": scatter_about(keys[2], (MODEL_DIMENSION, QUERY_HEADS * HEAD_DIMENSION), (MODEL_DIMENSION // 12) ** -0.5, 0.625, ((1, 2),)),
        "key_weight": scatter_about(keys[3], (MODEL_DIMENSION, KEY_VALUE_HEADS * HEAD_DIMENSION), (MODEL_DIMENSION // 12) ** -0.5, 0.625, ((1, 2),)),
        "value_weight": scatter_about(keys[4], (MODEL_DIMENSION, KEY_VALUE_HEADS * HEAD_DIMENSION), MODEL_DIMENSION ** -0.5, 0.1875, ((1, 2),)),
        "w_output": scatter_about(keys[5], (QUERY_HEADS * HEAD_DIMENSION, MODEL_DIMENSION), 1.5, 9.0, ((0, 2),)),
        "norm_two": jnp.clip(1.0 + 0.1 * jax.random.normal(keys[6], (MODEL_DIMENSION,), jnp.float32), 0.5, 1.5),
        "w_router": scatter_about(keys[7], (MODEL_DIMENSION, EXPERTS), 0.015625, 0.08984375),
        "w_gate": scatter_about(keys[8], (MODEL_DIMENSION, EXPERTS * FF), MODEL_DIMENSION ** -0.5, 0.1875, ((1, 16),)),
        "w_up": scatter_about(keys[9], (MODEL_DIMENSION, EXPERTS * FF), MODEL_DIMENSION ** -0.5, 0.1875, ((1, 16),)),
        "w_down": scatter_about(keys[10], (EXPERTS * FF, MODEL_DIMENSION), 1.0, 6.0, ((0, 16),)),
        "routes": distinct(keys[11], TOKEN_TOTAL, EXPERTS, TOPK, 4096),
        "priority": jax.vmap(lambda own: jax.random.permutation(own, HALF))(jax.random.split(keys[12], (N_EXP * N_HEAD))).reshape((N_EXP * N_HEAD, HALF)).astype(jnp.int32),
        "cotangent": scatter_about(keys[13], (TOKEN_TOTAL, MODEL_DIMENSION), 1.0, 6.0, ((0, 32),)),
    }


RESIDUAL_SCALE = 0.22
ATTENTION_SCALE = 0.015625
ROPE_BASE = 10000.0
NORM_EPS = 1e-06
MASKED_SCORE = -1e+30

@jax.custom_vjp
def lowered_rows(v):
    return lax.optimization_barrier(v.astype(jnp.bfloat16)).astype(jnp.float32)

@jax.custom_vjp
def lowered_gradient(v):
    return v

def low_keep(v):
    return (lowered_rows(v), None)

def low_pass(kept, grad):
    return (grad,)

def back_keep(v):
    return (v, None)

def back_low(kept, grad):
    return (lowered_rows(grad),)
lowered_rows.defvjp(low_keep, low_pass)
lowered_gradient.defvjp(back_keep, back_low)

def matrix_product(left, right):
    return jnp.dot(left, right, precision=lax.Precision.HIGHEST, preferred_element_type=jnp.float32)

def rms_scale(values, scale_row):
    return values * lax.rsqrt(lax.optimization_barrier(jnp.mean(values * values, axis=-1, keepdims=True)) + NORM_EPS) * scale_row

def softmax_rows(scores):
    row_max = lax.optimization_barrier(jnp.max(scores, axis=-1, keepdims=True))
    weights = jnp.exp(scores - row_max)
    return weights / lax.optimization_barrier(jnp.sum(weights, axis=-1, keepdims=True))

def apply_rotary(values, cosine_values, sine_values):
    half_width = values.shape[-1] // 2
    lower_part = values[..., :half_width]
    upper_part = values[..., half_width:]
    return jnp.concatenate([lower_part * cosine_values - upper_part * sine_values, upper_part * cosine_values + lower_part * sine_values], axis=-1)

def angle_tables(row_count):
    token_index = jnp.arange(row_count, dtype=jnp.int32) % TOKENS_PER_GROUP
    position = jnp.where(token_index < PROMPT_LEN, token_index, PROMPT_LEN + (token_index - PROMPT_LEN) % CONT_LEN)
    frequency = ROPE_BASE ** (-(2.0 * jnp.arange(HEAD_DIMENSION // 2, dtype=jnp.float32)) / HEAD_DIMENSION)
    angle_table = position.astype(jnp.float32)[:, None] * frequency[None, :]
    return (jnp.cos(angle_table)[:, None, :], jnp.sin(angle_table)[:, None, :])

def attend_block(query_block, key_group, value_group, block_start):
    query_index = block_start + jnp.arange(query_block.shape[0], dtype=jnp.int32)
    key_index = jnp.arange(key_group.shape[0], dtype=jnp.int32)
    query_col = query_index[:, None]
    key_row = key_index[None, :]
    from_prompt = (key_row < PROMPT_LEN) & ((query_col >= PROMPT_LEN) | (key_row <= query_col))
    same_cont = (key_row >= PROMPT_LEN) & (query_col >= PROMPT_LEN) & (key_row <= query_col) & ((key_row - PROMPT_LEN) // CONT_LEN == (query_col - PROMPT_LEN) // CONT_LEN)
    visible = from_prompt | same_cont
    raw_scores = jnp.einsum('qhgd,khd->hgqk', query_block, key_group, precision=lax.Precision.HIGHEST) * ATTENTION_SCALE
    scores = jnp.where(visible[None, None], lowered_gradient(raw_scores), MASKED_SCORE)
    probs = softmax_rows(scores)
    return jnp.einsum('hgqk,khd->qhgd', lowered_rows(probs), value_group, precision=lax.Precision.HIGHEST)

def group_attention(group_parts):
    grouped_queries, key_group, value_group = group_parts
    rows_per_block = min(512, TOKENS_PER_GROUP)
    count_of_blocks = TOKENS_PER_GROUP // rows_per_block
    block_list = grouped_queries.reshape(count_of_blocks, rows_per_block, KEY_VALUE_HEADS, QUERY_HEADS // KEY_VALUE_HEADS, HEAD_DIMENSION)
    block_starts = jnp.arange(count_of_blocks, dtype=jnp.int32) * rows_per_block
    block_step = jax.checkpoint(lambda parts: attend_block(parts[0], key_group, value_group, parts[1]))
    return lax.map(block_step, (block_list, block_starts)).reshape(TOKENS_PER_GROUP, QUERY_HEADS * HEAD_DIMENSION)

def dispatch_tables(routes, priority):
    halves = priority.shape[0]
    half_rows = priority.shape[1]
    grouped = routes.reshape(halves, half_rows, TOPK)
    route_hot = grouped[..., None] == jnp.arange(EXPERTS, dtype=jnp.int32)
    member = jnp.any(route_hot, axis=2).astype(jnp.int32)
    earlier = (priority[:, None, :] < priority[:, :, None]).astype(jnp.int32)
    before = jnp.einsum('brs,bse->bre', earlier, member)
    slot_rank = jnp.take_along_axis(before, grouped, axis=2)
    is_kept = slot_rank < CAP
    half_id = jnp.arange(halves, dtype=jnp.int32)[:, None, None]
    spare_slot = EXPERTS * halves * CAP
    target = jnp.where(is_kept, grouped * (halves * CAP) + half_id * CAP + slot_rank, spare_slot).reshape(TOKEN_TOTAL, TOPK).astype(jnp.int32)
    token_id = jnp.broadcast_to(jnp.arange(TOKEN_TOTAL, dtype=jnp.int32)[:, None], (TOKEN_TOTAL, TOPK))
    assign_id = jnp.arange(TOKEN_TOTAL * TOPK, dtype=jnp.int32).reshape(TOKEN_TOTAL, TOPK)
    source_row = jnp.zeros(spare_slot + 1, jnp.int32).at[target.ravel()].set(token_id.ravel())[:spare_slot]
    source_pick = jnp.zeros(spare_slot + 1, jnp.int32).at[target.ravel()].set(assign_id.ravel())[:spare_slot]
    filled = jnp.zeros(spare_slot + 1, jnp.int32).at[target.ravel()].set(1)[:spare_slot] > 0
    return (target, source_row, source_pick, filled)

def reference(tokens, norm_one, w_query, key_weight, value_weight, w_output, norm_two, w_router, w_gate, w_up, w_down, routes, priority, cotangent):
    target, source_row, source_pick, filled = dispatch_tables(routes, priority)
    cosine_values, sine_values = angle_tables(TOKEN_TOTAL)
    block_width = FF // SPLIT

    def layer_forward(tokens_in, gain_one, query_w, key_matrix, value_matrix, output_w, gain_two, router_w, gate_w, up_w, down_w):
        normed_input_first = lowered_rows(rms_scale(tokens_in, gain_one))
        rotated_queries = lowered_rows(apply_rotary(lowered_gradient(matrix_product(normed_input_first, query_w)).reshape(TOKEN_TOTAL, QUERY_HEADS, HEAD_DIMENSION), cosine_values, sine_values))
        rotated_keys = lowered_rows(apply_rotary(lowered_gradient(matrix_product(normed_input_first, key_matrix)).reshape(TOKEN_TOTAL, KEY_VALUE_HEADS, HEAD_DIMENSION), cosine_values, sine_values))
        value_row_list = lowered_rows(lowered_gradient(matrix_product(normed_input_first, value_matrix))).reshape(TOKEN_TOTAL, KEY_VALUE_HEADS, HEAD_DIMENSION)
        head_outputs = lax.map(jax.checkpoint(group_attention), (rotated_queries.reshape(PROMPT_GROUPS, TOKENS_PER_GROUP, KEY_VALUE_HEADS, QUERY_HEADS // KEY_VALUE_HEADS, HEAD_DIMENSION), rotated_keys.reshape(PROMPT_GROUPS, TOKENS_PER_GROUP, KEY_VALUE_HEADS, HEAD_DIMENSION), value_row_list.reshape(PROMPT_GROUPS, TOKENS_PER_GROUP, KEY_VALUE_HEADS, HEAD_DIMENSION)))
        head_outputs = lowered_rows(lowered_gradient(head_outputs.reshape(TOKEN_TOTAL, QUERY_HEADS * HEAD_DIMENSION)))
        branch = lowered_gradient(matrix_product(head_outputs, output_w))
        middle = tokens_in + RESIDUAL_SCALE * branch
        xn_two = lowered_rows(rms_scale(middle, gain_two))
        logits = lowered_gradient(matrix_product(xn_two, router_w))
        chosen = jnp.take_along_axis(logits, routes, axis=1)
        gate_probs = softmax_rows(chosen)
        gate_low = lowered_rows(lowered_gradient(gate_probs))
        slot_gates = jnp.where(filled, gate_low.reshape(-1)[source_pick], 0.0)
        gate_blocks = gate_w.reshape(MODEL_DIMENSION, EXPERTS, SPLIT, block_width).transpose(1, 2, 0, 3)
        up_blocks = up_w.reshape(MODEL_DIMENSION, EXPERTS, SPLIT, block_width).transpose(1, 2, 0, 3)
        down_blocks = down_w.reshape(EXPERTS, SPLIT, block_width, MODEL_DIMENSION)

        def expert_rows(parts):
            rows_index, rows_filled, rows_gate, gate_e, up_e, down_e = parts
            slot_rows = jnp.where(rows_filled[:, None], xn_two[rows_index], 0.0)
            split_rows = lowered_gradient(jnp.broadcast_to(slot_rows[None], (SPLIT,) + slot_rows.shape))
            gate_pre = lowered_gradient(jnp.einsum('brd,bdf->brf', split_rows, gate_e, precision=lax.Precision.HIGHEST))
            up_pre = lowered_gradient(jnp.einsum('brd,bdf->brf', split_rows, up_e, precision=lax.Precision.HIGHEST))
            hidden = lowered_rows(gate_pre * jax.nn.sigmoid(gate_pre) * up_pre)
            result = lowered_gradient(jnp.einsum('brf,bfd->brd', hidden, down_e, precision=lax.Precision.HIGHEST))
            split_gate = lowered_gradient(jnp.broadcast_to(rows_gate[None], (SPLIT,) + rows_gate.shape))
            return lax.optimization_barrier(jnp.sum(lowered_rows(lowered_gradient(split_gate[:, :, None] * result)), axis=0))
        weighted = lax.map(jax.checkpoint(expert_rows), (source_row.reshape(EXPERTS, -1), filled.reshape(EXPERTS, -1), slot_gates.reshape(EXPERTS, -1), gate_blocks, up_blocks, down_blocks))
        returned = jnp.concatenate([weighted.reshape(-1, MODEL_DIMENSION), jnp.zeros((1, MODEL_DIMENSION), jnp.float32)], axis=0)
        expert_sum = returned[target[:, 0]]
        for pick_index in range(1, TOPK):
            expert_sum = expert_sum + returned[target[:, pick_index]]
        return middle + RESIDUAL_SCALE * expert_sum
    primal = tuple((array_in.astype(jnp.float32) for array_in in (tokens, norm_one, w_query, key_weight, value_weight, w_output, norm_two, w_router, w_gate, w_up, w_down)))
    layer_out, pullback = jax.vjp(layer_forward, *primal)
    gradients = pullback(cotangent.astype(jnp.float32))
    return (layer_out.astype(jnp.bfloat16), gradients[0], gradients[1], gradients[2], gradients[3], gradients[4], gradients[5], gradients[6], gradients[7], gradients[8], gradients[9], gradients[10])
```

```python
import jax
import jax.numpy as jnp
from jax import lax
from jax.experimental import pallas as pl
from jax.experimental.pallas import tpu as pltpu
from jax.sharding import PartitionSpec as P

HEAD_DIMENSION = 64
FF = 512
TOPK = 8


RESIDUAL_SCALE = 0.22
ATTENTION_SCALE = 0.015625
ROPE_BASE = 10000.0
NORM_EPS = 1e-06
MASKED_SCORE = -1e30


def rms_scale(values, scale_row):
    return (
        values * lax.rsqrt(jnp.mean(values * values, axis=-1, keepdims=True) + NORM_EPS) * scale_row
    )


def apply_rotary(values, cosine_values, sine_values):
    half_width = values.shape[-1] // 2
    lower_part = values[..., :half_width]
    upper_part = values[..., half_width:]
    return jnp.concatenate(
        [
            lower_part * cosine_values - upper_part * sine_values,
            upper_part * cosine_values + lower_part * sine_values,
        ],
        axis=-1,
    )


def rotate_back(values, cosine_values, sine_values):
    half_width = values.shape[-1] // 2
    lower_part = values[..., :half_width]
    upper_part = values[..., half_width:]
    return jnp.concatenate(
        [
            lower_part * cosine_values + upper_part * sine_values,
            upper_part * cosine_values - lower_part * sine_values,
        ],
        axis=-1,
    )


def shards(
    tokens,
    norm_one,
    w_query,
    key_weight,
    value_weight,
    w_output,
    norm_two,
    w_router,
    w_gate,
    w_up,
    w_down,
    routes,
    priority,
    cotangent,
):
    tok_rows, model_width = tokens.shape
    heads_count = lax.axis_size("head")
    head_rank = lax.axis_index("head")
    exp_count = lax.axis_size("exp")
    half_rows = tok_rows // heads_count
    prompt_rows = tok_rows // 2
    cont_rows = tok_rows // 4
    kv_heads = key_weight.shape[1] // HEAD_DIMENSION
    query_groups = w_query.shape[1] // key_weight.shape[1]
    experts = w_router.shape[1]
    held_cols = w_gate.shape[1]
    held = max(1, held_cols // FF)
    split = max(1, FF // held_cols)
    block_width = held_cols // held
    capacity = max(2, (5 * half_rows * TOPK + 4 * experts - 1) // (4 * experts))
    rows_per_block = min(512, tok_rows)
    count_of_blocks = tok_rows // rows_per_block
    local_index = jnp.arange(tok_rows, dtype=jnp.int32)
    position = jnp.where(
        local_index < prompt_rows,
        local_index,
        prompt_rows + (local_index - prompt_rows) % cont_rows,
    )
    frequency = ROPE_BASE ** (
        -(2.0 * jnp.arange(HEAD_DIMENSION // 2, dtype=jnp.float32)) / HEAD_DIMENSION
    )
    angle_table = position.astype(jnp.float32)[:, None] * frequency[None, :]
    cosine_values = jnp.cos(angle_table)[:, None, :]
    sine_values = jnp.sin(angle_table)[:, None, :]
    x_full = tokens.astype(jnp.float32)
    normed_input_first = rms_scale(x_full, norm_one).astype(jnp.bfloat16)
    rotated_queries = apply_rotary(
        jnp.dot(normed_input_first, w_query, preferred_element_type=jnp.float32).reshape(
            tok_rows, -1, HEAD_DIMENSION
        ),
        cosine_values,
        sine_values,
    ).astype(jnp.bfloat16)
    keys_all = apply_rotary(
        jnp.dot(normed_input_first, key_weight, preferred_element_type=jnp.float32).reshape(
            tok_rows, -1, HEAD_DIMENSION
        ),
        cosine_values,
        sine_values,
    ).astype(jnp.bfloat16)
    values_all = (
        jnp.dot(normed_input_first, value_weight, preferred_element_type=jnp.float32)
        .astype(jnp.bfloat16)
        .reshape(tok_rows, kv_heads, HEAD_DIMENSION)
    )

    def visible_pairs(block_start):
        query_col = (block_start + jnp.arange(rows_per_block, dtype=jnp.int32))[:, None]
        key_row = jnp.arange(tok_rows, dtype=jnp.int32)[None, :]
        from_prompt = (key_row < prompt_rows) & (
            (query_col >= prompt_rows) | (key_row <= query_col)
        )
        same_cont = (
            (key_row >= prompt_rows)
            & (query_col >= prompt_rows)
            & (key_row <= query_col)
            & ((key_row - prompt_rows) // cont_rows == (query_col - prompt_rows) // cont_rows)
        )
        return from_prompt | same_cont

    def scores_of(query_block, block_start):
        raw_scores = (
            jnp.einsum("qhgd,khd->hgqk", query_block, keys_all, preferred_element_type=jnp.float32)
            * ATTENTION_SCALE
        )
        return jnp.where(visible_pairs(block_start)[None, None], raw_scores, MASKED_SCORE)

    def forward_block(parts):
        query_block, block_start = parts
        scores = scores_of(query_block, block_start)
        row_max = jnp.max(scores, axis=-1, keepdims=True)
        weights = jnp.exp(scores - row_max)
        row_total = jnp.sum(weights, axis=-1, keepdims=True)
        probs_low = (weights / row_total).astype(jnp.bfloat16)
        mixed = jnp.einsum(
            "hgqk,khd->qhgd", probs_low, values_all, preferred_element_type=jnp.float32
        )
        return (mixed.astype(jnp.bfloat16), row_max + jnp.log(row_total))

    query_blocks = rotated_queries.reshape(
        count_of_blocks, rows_per_block, kv_heads, query_groups, HEAD_DIMENSION
    )
    block_starts = jnp.arange(count_of_blocks, dtype=jnp.int32) * rows_per_block
    heads_blocks, log_total = lax.map(forward_block, (query_blocks, block_starts))
    head_outputs = heads_blocks.reshape(tok_rows, -1)
    head_terms = jnp.dot(head_outputs, w_output, preferred_element_type=jnp.float32)
    branch_half = lax.dynamic_slice_in_dim(
        lax.psum(head_terms, "head"), head_rank * half_rows, half_rows, 0
    )
    x_half = lax.dynamic_slice_in_dim(x_full, head_rank * half_rows, half_rows, 0)
    middle = x_half + RESIDUAL_SCALE * branch_half
    xn_two = rms_scale(middle, norm_two).astype(jnp.bfloat16)
    logits = jnp.dot(xn_two, w_router, preferred_element_type=jnp.float32)
    my_routes = lax.dynamic_slice_in_dim(routes, head_rank * half_rows, half_rows, 0)
    route_hot = my_routes[:, :, None] == jnp.arange(experts, dtype=jnp.int32)[None, None, :]
    chosen = jnp.sum(jnp.where(route_hot, logits[:, None, :], 0.0), axis=-1)
    chosen_max = jnp.max(chosen, axis=-1, keepdims=True)
    chosen_exp = jnp.exp(chosen - chosen_max)
    gate_probs = chosen_exp / jnp.sum(chosen_exp, axis=-1, keepdims=True)
    gate_low = gate_probs.astype(jnp.bfloat16)
    member = jnp.any(route_hot, axis=1).astype(jnp.bfloat16)
    order_rank = priority[0]
    earlier = (order_rank[None, :] < order_rank[:, None]).astype(jnp.bfloat16)
    before = jnp.dot(earlier, member, preferred_element_type=jnp.float32)
    slot_rank = jnp.sum(jnp.where(route_hot, before[:, None, :], 0.0), axis=-1).astype(jnp.int32)
    is_kept = slot_rank < capacity
    spare_slot = experts * capacity
    target = jnp.where(is_kept, my_routes * capacity + slot_rank, spare_slot)
    row_ids = jnp.broadcast_to(jnp.arange(half_rows, dtype=jnp.int32)[:, None], target.shape)
    assign_ids = jnp.arange(half_rows * TOPK, dtype=jnp.int32).reshape(target.shape)
    source_row = (
        jnp.zeros(spare_slot + 1, jnp.int32).at[target.ravel()].set(row_ids.ravel())[:spare_slot]
    )
    source_pick = (
        jnp.zeros(spare_slot + 1, jnp.int32).at[target.ravel()].set(assign_ids.ravel())[:spare_slot]
    )
    filled = jnp.zeros(spare_slot + 1, jnp.int32).at[target.ravel()].set(1)[:spare_slot] > 0
    slot_inputs = jnp.where(filled[:, None], xn_two[source_row], 0).reshape(
        experts, capacity, model_width
    )
    slot_gates = jnp.where(filled, gate_low.ravel()[source_pick], 0).reshape(experts, capacity)

    def to_owners(per_expert):
        shape_in = per_expert.shape
        spread = jnp.broadcast_to(per_expert[:, None], (shape_in[0], split) + shape_in[1:])
        return spread.reshape((exp_count, held) + shape_in[1:])

    def from_owners(per_owner):
        shape_in = per_owner.shape
        return jnp.sum(
            per_owner.reshape((experts, split) + shape_in[2:]).astype(jnp.float32), axis=1
        )

    gate_cols = w_gate.reshape(model_width, held, block_width)
    up_cols = w_up.reshape(model_width, held, block_width)
    down_rows = w_down.reshape(held, block_width, model_width)
    send_rows = to_owners(slot_inputs)
    send_gates = to_owners(slot_gates)
    slot_rows = lax.all_to_all(send_rows, "exp", split_axis=0, concat_axis=0, tiled=True)
    slot_gate = lax.all_to_all(send_gates, "exp", split_axis=0, concat_axis=0, tiled=True)
    gate_pre = jnp.einsum(
        "sjcd,djf->sjcf", slot_rows, gate_cols, preferred_element_type=jnp.float32
    )
    up_pre = jnp.einsum("sjcd,djf->sjcf", slot_rows, up_cols, preferred_element_type=jnp.float32)
    hidden = (gate_pre * jax.nn.sigmoid(gate_pre) * up_pre).astype(jnp.bfloat16)
    result = jnp.einsum("sjcf,jfd->sjcd", hidden, down_rows, preferred_element_type=jnp.float32)
    weighted = (slot_gate[..., None].astype(jnp.float32) * result).astype(jnp.bfloat16)
    returned = lax.all_to_all(weighted, "exp", split_axis=0, concat_axis=0, tiled=True)
    returned, held_rows, held_gates = (returned, slot_rows, slot_gate)
    back_flat = jnp.concatenate(
        [
            from_owners(returned).reshape(spare_slot, model_width),
            jnp.zeros((1, model_width), jnp.float32),
        ],
        axis=0,
    )
    expert_sum = jnp.sum(back_flat[target], axis=1)
    layer_out = (middle + RESIDUAL_SCALE * expert_sum).astype(jnp.bfloat16)
    out_grad = cotangent.astype(jnp.float32)
    weighted_rows = (RESIDUAL_SCALE * out_grad).astype(jnp.bfloat16)
    grad_slots = to_owners(
        jnp.where(filled[:, None], weighted_rows[source_row], 0).reshape(
            experts, capacity, model_width
        )
    )
    back_grads, back_rows, back_gates = (
        lax.all_to_all(grad_slots, "exp", split_axis=0, concat_axis=0, tiled=True),
        lax.all_to_all(send_rows, "exp", split_axis=0, concat_axis=0, tiled=True),
        lax.all_to_all(send_gates, "exp", split_axis=0, concat_axis=0, tiled=True),
    )
    owner_gates = back_gates[..., None].astype(jnp.float32)
    gate_pre = jnp.einsum(
        "sjcd,djf->sjcf", back_rows, gate_cols, preferred_element_type=jnp.float32
    )
    up_pre = jnp.einsum("sjcd,djf->sjcf", back_rows, up_cols, preferred_element_type=jnp.float32)
    gate_sigmoid = jax.nn.sigmoid(gate_pre)
    gate_act = gate_pre * gate_sigmoid
    hidden = (gate_act * up_pre).astype(jnp.bfloat16)
    result = jnp.einsum("sjcf,jfd->sjcd", hidden, down_rows, preferred_element_type=jnp.float32)
    gate_part = jnp.sum(back_grads.astype(jnp.float32) * result, axis=-1)
    result_grad = (owner_gates * back_grads).astype(jnp.bfloat16)
    grad_down_w = jnp.einsum(
        "sjcf,sjcd->jfd", hidden, result_grad, preferred_element_type=jnp.float32
    ).reshape(held_cols, model_width)
    hidden_grad = jnp.einsum(
        "sjcd,jfd->sjcf", result_grad, down_rows, preferred_element_type=jnp.float32
    )
    gate_pre_grad = (
        hidden_grad * up_pre * gate_sigmoid * (1.0 + gate_pre * (1.0 - gate_sigmoid))
    ).astype(jnp.bfloat16)
    up_pre_grad = (hidden_grad * gate_act).astype(jnp.bfloat16)
    grad_gate_w = jnp.einsum(
        "sjcd,sjcf->djf", back_rows, gate_pre_grad, preferred_element_type=jnp.float32
    ).reshape(model_width, held_cols)
    grad_up_w = jnp.einsum(
        "sjcd,sjcf->djf", back_rows, up_pre_grad, preferred_element_type=jnp.float32
    ).reshape(model_width, held_cols)
    rows_grad = (
        jnp.einsum("sjcf,djf->sjcd", gate_pre_grad, gate_cols, preferred_element_type=jnp.float32)
        + jnp.einsum("sjcf,djf->sjcd", up_pre_grad, up_cols, preferred_element_type=jnp.float32)
    ).astype(jnp.bfloat16)
    rows_back, gates_back = (
        lax.all_to_all(rows_grad, "exp", split_axis=0, concat_axis=0, tiled=True),
        lax.all_to_all(
            gate_part.astype(jnp.bfloat16), "exp", split_axis=0, concat_axis=0, tiled=True
        ),
    )
    rows_flat = jnp.concatenate(
        [
            from_owners(rows_back).reshape(spare_slot, model_width),
            jnp.zeros((1, model_width), jnp.float32),
        ],
        axis=0,
    )
    xn_two_grad = jnp.sum(rows_flat[target], axis=1)
    gate_total = from_owners(gates_back).astype(jnp.bfloat16).reshape(spare_slot)
    gates_flat = jnp.concatenate([gate_total, jnp.zeros((1,), jnp.bfloat16)], axis=0)
    gate_grad_tok = gates_flat[target].astype(jnp.float32)
    chosen_grad = gate_probs * (
        gate_grad_tok - jnp.sum(gate_probs * gate_grad_tok, axis=-1, keepdims=True)
    )
    logit_grad = jnp.sum(jnp.where(route_hot, chosen_grad[:, :, None], 0.0), axis=1).astype(
        jnp.bfloat16
    )
    grad_router = jnp.einsum("rd,re->de", xn_two, logit_grad, preferred_element_type=jnp.float32)
    xn_two_grad = xn_two_grad + jnp.einsum(
        "re,de->rd", logit_grad, w_router, preferred_element_type=jnp.float32
    )
    middle_norm_pull = jax.vjp(rms_scale, middle, norm_two)[1]
    middle_norm_grad, grad_norm_two = middle_norm_pull(xn_two_grad)
    middle_grad = out_grad + middle_norm_grad
    branch_rows = (RESIDUAL_SCALE * middle_grad).astype(jnp.bfloat16)
    branch_grad = lax.all_gather(branch_rows, "head", axis=0, tiled=True)
    heads_grad = jnp.einsum(
        "td,hd->th", branch_grad, w_output, preferred_element_type=jnp.float32
    ).astype(jnp.bfloat16)
    grad_output_w = jnp.einsum(
        "th,td->hd", head_outputs, branch_grad, preferred_element_type=jnp.float32
    )

    def backward_block(running, parts):
        key_grad, value_grad = running
        query_block, heads_block, block_total, block_start = parts
        scores = scores_of(query_block, block_start)
        probs = jnp.exp(scores - block_total)
        probs_low = probs.astype(jnp.bfloat16)
        prob_grad = jnp.einsum(
            "qhgd,khd->hgqk", heads_block, values_all, preferred_element_type=jnp.float32
        )
        row_inner = jnp.sum(probs * prob_grad, axis=-1, keepdims=True)
        score_grad = (probs * (prob_grad - row_inner)).astype(jnp.bfloat16)
        query_grad = (
            jnp.einsum("hgqk,khd->qhgd", score_grad, keys_all, preferred_element_type=jnp.float32)
            * ATTENTION_SCALE
        )
        key_grad = (
            key_grad
            + jnp.einsum(
                "hgqk,qhgd->khd", score_grad, query_block, preferred_element_type=jnp.float32
            )
            * ATTENTION_SCALE
        )
        value_grad = value_grad + jnp.einsum(
            "hgqk,qhgd->khd", probs_low, heads_block, preferred_element_type=jnp.float32
        )
        return ((key_grad, value_grad), query_grad)

    heads_grad_blocks = heads_grad.reshape(
        count_of_blocks, rows_per_block, kv_heads, query_groups, HEAD_DIMENSION
    )
    zero_keys = jnp.zeros((tok_rows, kv_heads, HEAD_DIMENSION), jnp.float32)
    (own_key, own_value), query_grad = lax.scan(
        backward_block,
        (zero_keys, zero_keys),
        (query_blocks, heads_grad_blocks, log_total, block_starts),
    )
    query_pre_grad = (
        rotate_back(query_grad.reshape(tok_rows, -1, HEAD_DIMENSION), cosine_values, sine_values)
        .reshape(tok_rows, -1)
        .astype(jnp.bfloat16)
    )
    key_pre_grad = (
        rotate_back(own_key, cosine_values, sine_values).reshape(tok_rows, -1).astype(jnp.bfloat16)
    )
    value_low_grad = own_value.reshape(tok_rows, -1).astype(jnp.bfloat16)
    grad_query_w = jnp.einsum(
        "td,th->dh", normed_input_first, query_pre_grad, preferred_element_type=jnp.float32
    )
    grad_key_w = jnp.einsum(
        "td,th->dh", normed_input_first, key_pre_grad, preferred_element_type=jnp.float32
    )
    grad_value_w = jnp.einsum(
        "td,th->dh", normed_input_first, value_low_grad, preferred_element_type=jnp.float32
    )
    xn_one_terms = (
        jnp.einsum("th,dh->td", query_pre_grad, w_query, preferred_element_type=jnp.float32)
        + jnp.einsum("th,dh->td", key_pre_grad, key_weight, preferred_element_type=jnp.float32)
        + jnp.einsum("th,dh->td", value_low_grad, value_weight, preferred_element_type=jnp.float32)
    )
    xn_one_grad = lax.psum_scatter(
        xn_one_terms.astype(jnp.bfloat16), "head", scatter_dimension=0, tiled=True
    ).astype(jnp.float32)
    input_norm_pull = jax.vjp(rms_scale, x_half, norm_one)[1]
    input_norm_grad, grad_norm_one = input_norm_pull(xn_one_grad)
    grad_tokens = middle_grad + input_norm_grad
    grad_gate_w, grad_up_w, grad_down_w, grad_router, grad_norm_one, grad_norm_two = (
        lax.psum(grad_gate_w.astype(jnp.bfloat16), "head").astype(jnp.float32),
        lax.psum(grad_up_w.astype(jnp.bfloat16), "head").astype(jnp.float32),
        lax.psum(grad_down_w.astype(jnp.bfloat16), "head").astype(jnp.float32),
        lax.psum(grad_router.astype(jnp.bfloat16), "head").astype(jnp.float32),
        lax.psum(grad_norm_one.astype(jnp.bfloat16), "head").astype(jnp.float32),
        lax.psum(grad_norm_two.astype(jnp.bfloat16), "head").astype(jnp.float32),
    )
    (
        grad_query_w,
        grad_key_w,
        grad_value_w,
        grad_output_w,
        grad_router,
        grad_norm_one,
        grad_norm_two,
    ) = lax.psum(
        (
            grad_query_w,
            grad_key_w,
            grad_value_w,
            grad_output_w,
            grad_router,
            grad_norm_one,
            grad_norm_two,
        ),
        "exp",
    )
    return (
        layer_out,
        grad_tokens,
        grad_norm_one,
        grad_query_w,
        grad_key_w,
        grad_value_w,
        grad_output_w,
        grad_norm_two,
        grad_router,
        grad_gate_w,
        grad_up_w,
        grad_down_w,
    )


MESH = pl.DeviceIdType.MESH
FLAT = 128
SLOTS = 40
UNKEPT = -1000.0


def remote(source, target, send_sem, recv_sem, device):
    return pltpu.make_async_remote_copy(
        src_ref=source,
        dst_ref=target,
        send_sem=send_sem,
        recv_sem=recv_sem,
        device_id=device,
        device_id_type=MESH,
    )


def places():
    e = lax.axis_index("exp")
    h = lax.axis_index("head")
    x, y, z = e % 2, (e // 2) % 2, e // 4
    over_x, over_y = e + 1 - 2 * x, e + 2 - 4 * y
    near = over_x * (1 - h) + over_y * h
    far = over_y * (1 - h) + over_x * h
    along = [((z + k) % 4) * 4 + e % 4 for k in range(4)]
    return e, h, near, far, along


def greet(h, peers):
    barrier = pltpu.get_barrier_semaphore()
    for peer in peers:
        pl.semaphore_signal(barrier, inc=1, device_id=peer, device_id_type=MESH)
    pl.semaphore_wait(barrier, len(peers))


def selection(tables, k, own, other):
    slot = lax.broadcasted_iota(jnp.int32, (2 * SLOTS, 2 * FLAT), 0)
    lane = lax.broadcasted_iota(jnp.int32, (2 * SLOTS, 2 * FLAT), 1)
    wanted = (slot - jnp.where(lane >= FLAT, SLOTS, 0)).astype(jnp.float32)
    parts = []
    for chip in (own, other):
        for j in range(2):
            row = jnp.concatenate(
                [tables[k, a, pl.ds(2 * chip + j, 1), :] for a in range(2)], axis=1
            )
            parts.append(jnp.where(row == wanted, 1.0, 0.0))
    return jnp.concatenate(parts, axis=0)


def expert_rows_of(tables, k, own, other):
    parts = []
    for chip in (own, other):
        for j in range(2):
            row = jnp.concatenate(
                [tables[k, a, pl.ds(2 * chip + j, 1), :] for a in range(2)], axis=1
            )
            parts.append(jnp.broadcast_to(row, (2 * SLOTS, 2 * FLAT)))
    return jnp.concatenate(parts, axis=0)


def dispatch_kernel(
    branch,
    tokens,
    norm_two,
    w_router,
    table,
    member,
    out_rows,
    middle_out,
    xn_out,
    probs_out,
    tables,
    x_slots,
    g_slots,
    gates_own,
    gates_far,
    branch_in,
    x_all,
    g_all,
    gate_tables,
    x_send,
    g_send,
    gate_send,
    pick,
    sems_send,
    sems_recv,
):
    e, h, near, far, along = places()
    greet(h, [(e, 1 - h), (near, h), (far, h)] + [(along[k], h) for k in (1, 2, 3)])
    started = []

    def go(source, target, number, device):
        copy = remote(source, target, sems_send.at[number], sems_recv.at[number], device)
        copy.start()
        started.append(copy)
        return copy

    half = pl.multiple_of(h * FLAT, FLAT)
    other_half = pl.multiple_of((1 - h) * FLAT, FLAT)
    pair_copy = go(branch.at[pl.ds(other_half, FLAT)], branch_in, 0, (e, 1 - h))
    copies = {}

    def spread(name, own_block, gathered, base):
        for k in (1, 2, 3):
            copies[name, "z", k] = go(own_block, gathered.at[k, 0], base + k, (along[k], h))
        copies[name, "a", 0] = go(own_block, gathered.at[0, 1], base + 4, (near, h))

    def pass_on(name, gathered, base, k):
        copies[name, "z", k].wait_recv()
        copies[name, "a", k] = go(gathered.at[k, 0], gathered.at[k, 1], base + 4 + k, (near, h))

    spread("t", table, tables, 0)
    spread("g", out_rows, g_all, 8)
    tables[0, 0] = table[...]
    g_all[0, 0] = out_rows[...]
    pair_copy.wait_recv()
    middle = tokens[pl.ds(half, FLAT), :].astype(jnp.float32) + RESIDUAL_SCALE * (
        branch[pl.ds(half, FLAT), :] + branch_in[...]
    )
    middle_out[...] = middle
    xn = rms_scale(middle, norm_two[...]).astype(jnp.bfloat16)
    xn_out[...] = xn
    x_all[0, 0] = xn
    spread("x", xn_out, x_all, 24)
    logits = lax.dot_general(
        w_router[...], xn, (((0,), (1,)), ((), ())), preferred_element_type=jnp.float32
    )
    chosen = jnp.where(member[...] > 0, logits, MASKED_SCORE)
    weights = jnp.exp(chosen - jnp.max(chosen, axis=0, keepdims=True))
    probs = weights / jnp.sum(weights, axis=0, keepdims=True)
    probs_out[...] = probs
    gate_tables[0, 0] = probs.astype(jnp.bfloat16).astype(jnp.float32)
    spread("p", gate_tables.at[0, 0], gate_tables, 16)

    for k in (1, 2, 3):
        pass_on("t", tables, 0, k)
        pass_on("g", g_all, 8, k)
    for k in range(4):
        copies["t", "a", k].wait_recv()
        copies["g", "a", k].wait_recv()
        chosen_rows = selection(tables, k, e, far).astype(jnp.bfloat16)
        pick[k] = chosen_rows
        rows = jnp.dot(
            chosen_rows,
            g_all[k].reshape(2 * FLAT, -1),
            preferred_element_type=jnp.float32,
        ).astype(jnp.bfloat16)
        g_slots[k] = rows[: 4 * SLOTS].reshape(2, 2 * SLOTS, -1)
        g_send[k] = rows[4 * SLOTS :].reshape(2, 2 * SLOTS, -1)
        copies["g", "b", k] = go(g_send.at[k], g_slots.at[4 + k], 32 + k, (far, h))
    for k in (1, 2, 3):
        pass_on("x", x_all, 24, k)
        pass_on("p", gate_tables, 16, k)
    lane = lax.broadcasted_iota(jnp.int32, (4 * SLOTS, FLAT), 1)
    own_gates = jnp.zeros((4 * SLOTS, FLAT), jnp.float32)
    far_gates = jnp.zeros((4 * SLOTS, FLAT), jnp.float32)
    for k in range(4):
        copies["x", "a", k].wait_recv()
        rows = jnp.dot(
            pick[k], x_all[k].reshape(2 * FLAT, -1), preferred_element_type=jnp.float32
        ).astype(jnp.bfloat16)
        x_slots[k] = rows[: 4 * SLOTS].reshape(2, 2 * SLOTS, -1)
        x_send[k] = rows[4 * SLOTS :].reshape(2, 2 * SLOTS, -1)
        copies["x", "b", k] = go(x_send.at[k], x_slots.at[4 + k], 36 + k, (far, h))
        copies["p", "a", k].wait_recv()
        slot_gates = jnp.sum(
            pick[k].astype(jnp.float32) * expert_rows_of(gate_tables, k, e, far),
            axis=1,
            keepdims=True,
        )
        own_gates += jnp.where(lane == k, slot_gates[: 4 * SLOTS], 0.0)
        far_gates += jnp.where(lane == 4 + k, slot_gates[4 * SLOTS :], 0.0)
    gates_own[...] = own_gates
    gate_send[...] = far_gates
    copies["p", "b", 0] = go(gate_send, gates_far, 40, (far, h))
    for k in range(4):
        copies["g", "b", k].wait_recv()
        copies["x", "b", k].wait_recv()
    copies["p", "b", 0].wait_recv()
    for copy in started:
        copy.wait_send()


def dispatch(branch, tokens, norm_two, w_router, table, member, out_rows):
    width = tokens.shape[1]
    experts = w_router.shape[1]
    vmem = pl.BlockSpec(memory_space=pltpu.VMEM)
    block = (FLAT, width)
    slots = (8, 2, 2 * SLOTS, width)
    low, full = jnp.bfloat16, jnp.float32
    return pl.pallas_call(
        dispatch_kernel,
        out_shape=(
            jax.ShapeDtypeStruct(block, full),
            jax.ShapeDtypeStruct(block, low),
            jax.ShapeDtypeStruct((experts, FLAT), full),
            jax.ShapeDtypeStruct((4, 2, experts, FLAT), full),
            jax.ShapeDtypeStruct(slots, low),
            jax.ShapeDtypeStruct(slots, low),
            jax.ShapeDtypeStruct((4 * SLOTS, FLAT), full),
            jax.ShapeDtypeStruct((4 * SLOTS, FLAT), full),
        ),
        in_specs=[vmem] * 7,
        out_specs=(vmem,) * 8,
        scratch_shapes=[
            pltpu.VMEM(block, full),
            pltpu.VMEM((4, 2) + block, low),
            pltpu.VMEM((4, 2) + block, low),
            pltpu.VMEM((4, 2, experts, FLAT), full),
            pltpu.VMEM((4,) + slots[1:], low),
            pltpu.VMEM((4,) + slots[1:], low),
            pltpu.VMEM((4 * SLOTS, FLAT), full),
            pltpu.VMEM((4, 8 * SLOTS, 2 * FLAT), low),
            pltpu.SemaphoreType.DMA((41,)),
            pltpu.SemaphoreType.DMA((41,)),
        ],
        compiler_params=pltpu.CompilerParams(
            collective_id=0, has_side_effects=True, vmem_limit_bytes=50 << 20
        ),
        name="dispatch",
    )(branch, tokens, norm_two, w_router, table, member, out_rows)


def experts_kernel(
    x_slots,
    g_slots,
    gates_own,
    gates_far,
    w_gate,
    w_up,
    w_down,
    rows_out,
    weighted_out,
    parts_out,
    grad_gate,
    grad_up,
    grad_down,
    hidden_all,
    gate_all,
    up_all,
    result_all,
):
    j = pl.program_id(0)
    lane = lax.broadcasted_iota(jnp.int32, (2 * SLOTS, FLAT), 1)
    base = pl.multiple_of(j * 2 * SLOTS, 2 * SLOTS)
    gates = gates_own[pl.ds(base, 2 * SLOTS), :] + gates_far[pl.ds(base, 2 * SLOTS), :]
    parts = jnp.zeros((2 * SLOTS, FLAT), jnp.float32)
    pairs = 4
    span = pairs * 2 * SLOTS
    contract_last = (((1,), (1,)), ((), ()))
    contract_first = (((0,), (0,)), ((), ()))

    def mul(left, right, dims=(((1,), (0,)), ((), ()))):
        return lax.dot_general(left, right, dims, preferred_element_type=jnp.float32)

    for c in range(8 // pairs):
        which = slice(c * pairs, (c + 1) * pairs)
        rows = slice(c * span, (c + 1) * span)
        xs = x_slots[which, 0].reshape(span, -1)
        gs = g_slots[which, 0].reshape(span, -1)
        gate_col = jnp.concatenate(
            [gates[:, p : p + 1] for p in range(c * pairs, (c + 1) * pairs)], axis=0
        )
        gate_pre = mul(xs, w_gate[...])
        up_pre = mul(xs, w_up[...])
        sig = jax.nn.sigmoid(gate_pre)
        act = gate_pre * sig
        hidden = (act * up_pre).astype(jnp.bfloat16)
        hidden_all[rows] = hidden
        result = mul(hidden, w_down[...])
        weighted_out[which, 0] = (
            (gate_col * result).astype(jnp.bfloat16).reshape(pairs, 2 * SLOTS, -1)
        )
        gs_full = gs.astype(jnp.float32)
        part = jnp.sum(gs_full * result, axis=1, keepdims=True)
        part = part.astype(jnp.bfloat16).astype(jnp.float32)
        for p in range(pairs):
            parts += jnp.where(
                lane == c * pairs + p, part[p * 2 * SLOTS : (p + 1) * 2 * SLOTS], 0.0
            )
        result_grad = (gate_col * gs_full).astype(jnp.bfloat16)
        result_all[rows] = result_grad
        hidden_grad = mul(result_grad, w_down[...], contract_last)
        gate_pre_grad = (hidden_grad * up_pre * sig * (1.0 + gate_pre * (1.0 - sig))).astype(
            jnp.bfloat16
        )
        up_pre_grad = (hidden_grad * act).astype(jnp.bfloat16)
        gate_all[rows] = gate_pre_grad
        up_all[rows] = up_pre_grad
        rows_grad = mul(gate_pre_grad, w_gate[...], contract_last) + mul(
            up_pre_grad, w_up[...], contract_last
        )
        rows_out[which, 0] = rows_grad.astype(jnp.bfloat16).reshape(pairs, 2 * SLOTS, -1)
    parts_out[...] = parts
    xs = x_slots[:, 0].reshape(8 * 2 * SLOTS, -1)
    grad_gate[...] = mul(xs, gate_all[...], contract_first).astype(jnp.bfloat16)
    grad_up[...] = mul(xs, up_all[...], contract_first).astype(jnp.bfloat16)
    grad_down[...] = mul(hidden_all[...], result_all[...], contract_first).astype(jnp.bfloat16)


def run_experts(x_slots, g_slots, gates_own, gates_far, w_gate, w_up, w_down):
    width = w_gate.shape[0]
    low, full = jnp.bfloat16, jnp.float32
    slots = pl.BlockSpec((8, 1, 2 * SLOTS, width), lambda j: (0, j, 0, 0))
    whole = pl.BlockSpec((4 * SLOTS, FLAT), lambda j: (0, 0))
    cols = pl.BlockSpec((width, FF), lambda j: (0, j))
    rows = pl.BlockSpec((FF, width), lambda j: (j, 0))
    total = 8 * 2 * SLOTS
    return pl.pallas_call(
        experts_kernel,
        grid=(2,),
        out_shape=(
            jax.ShapeDtypeStruct(x_slots.shape, low),
            jax.ShapeDtypeStruct(x_slots.shape, low),
            jax.ShapeDtypeStruct((4 * SLOTS, FLAT), full),
            jax.ShapeDtypeStruct(w_gate.shape, low),
            jax.ShapeDtypeStruct(w_up.shape, low),
            jax.ShapeDtypeStruct(w_down.shape, low),
        ),
        in_specs=[slots, slots, whole, whole, cols, cols, rows],
        out_specs=(
            slots,
            slots,
            pl.BlockSpec((2 * SLOTS, FLAT), lambda j: (j, 0)),
            cols,
            cols,
            rows,
        ),
        scratch_shapes=[
            pltpu.VMEM((total, FF), low),
            pltpu.VMEM((total, FF), low),
            pltpu.VMEM((total, FF), low),
            pltpu.VMEM((total, width), low),
        ],
        compiler_params=pltpu.CompilerParams(vmem_limit_bytes=56 << 20),
        name="experts",
    )(x_slots, g_slots, gates_own, gates_far, w_gate, w_up, w_down)


def fold_rows(rows, rows_in, tables, near_in, along_in, kept, send, go, e, h, near, far, along, base):
    for k in (1, 2, 3, 0):
        go(rows.at[4 + k], rows_in.at[k], base + k, (far, h))


def combine_kernel(
    rows,
    parts,
    tables,
    probs,
    xn,
    w_router,
    middle,
    norm_two,
    cotangent,
    branch_grad,
    middle_grad,
    small,
    rows_in,
    parts_in,
    near_in,
    near_send,
    kept,
    along_in,
    along_send,
    gate_near_in,
    gate_near_send,
    gate_kept,
    gate_along_in,
    gate_along_send,
    sems_send,
    sems_recv,
):
    e, h, near, far, along = places()
    greet(h, [(e, 1 - h), (near, h), (far, h)] + [(along[k], h) for k in (1, 2, 3)])
    started = []

    def go(source, target, number, device):
        copy = remote(source, target, sems_send.at[number], sems_recv.at[number], device)
        copy.start()
        started.append(copy)
        return copy

    parts_copy = go(parts, parts_in, 0, (far, h))
    order = (2, 1, 3, 0)
    far_copies = {k: go(rows.at[4 + k], rows_in.at[k], 1 + k, (far, h)) for k in order}
    near_copies, gate_copies = {}, {}
    experts = probs.shape[0]
    index = lax.broadcasted_iota(jnp.int32, (experts, 2 * FLAT), 0)
    parts_copy.wait_recv()
    for k in order:
        far_copies[k].wait_recv()
        chosen = selection(tables, k, e, far)
        stacked = jnp.concatenate(
            [rows[k].reshape(4 * SLOTS, -1), rows_in[k].reshape(4 * SLOTS, -1)], axis=0
        )
        sums = lax.dot_general(
            chosen.astype(jnp.bfloat16),
            stacked,
            (((0,), (0,)), ((), ())),
            preferred_element_type=jnp.float32,
        )
        kept[k] = sums[:FLAT]
        near_send[k] = sums[FLAT:].astype(jnp.bfloat16)
        near_copies[k] = go(near_send.at[k], near_in.at[k], 5 + k, (near, h))
        column = jnp.concatenate(
            [parts[:, k : k + 1], parts_in[:, 4 + k : 5 + k]], axis=0
        )
        terms = chosen * column
        table = jnp.zeros((experts, 2 * FLAT), jnp.float32)
        for n, chip in enumerate((e, e, far, far)):
            total = jnp.sum(terms[n * 2 * SLOTS : (n + 1) * 2 * SLOTS], axis=0, keepdims=True)
            table += jnp.where(index == 2 * chip + n % 2, total, 0.0)
        gate_kept[k] = table[:, :FLAT]
        gate_near_send[k] = table[:, FLAT:]
        gate_copies[k] = go(gate_near_send.at[k], gate_near_in.at[k], 9 + k, (near, h))
    along_copies, gate_along_copies = {}, {}
    for k in order:
        near_copies[k].wait_recv()
        gate_copies[k].wait_recv()
        sums = kept[k] + near_in[k].astype(jnp.float32)
        gate_sums = gate_kept[k] + gate_near_in[k]
        if k == 0:
            kept[0] = sums
            gate_kept[0] = gate_sums
        else:
            device = (along[4 - k], h)
            along_send[k - 1] = sums.astype(jnp.bfloat16)
            gate_along_send[k - 1] = gate_sums
            along_copies[k] = go(along_send.at[k - 1], along_in.at[k - 1], 12 + k, device)
            gate_along_copies[k] = go(
                gate_along_send.at[k - 1], gate_along_in.at[k - 1], 15 + k, device
            )
    rows_grad, gate_grad = kept[0], gate_kept[0]
    for k in (1, 2, 3):
        along_copies[k].wait_recv()
        gate_along_copies[k].wait_recv()
        rows_grad = rows_grad + along_in[k - 1].astype(jnp.float32)
        gate_grad = gate_grad + gate_along_in[k - 1]
    gate_probs = probs[...]
    chosen_grad = gate_probs * (
        gate_grad - jnp.sum(gate_probs * gate_grad, axis=0, keepdims=True)
    )
    logit_grad = chosen_grad.astype(jnp.bfloat16)
    xn_grad = rows_grad + lax.dot_general(
        logit_grad, w_router[...], (((0,), (1,)), ((), ())), preferred_element_type=jnp.float32
    )
    mid = middle[...]
    scale = lax.rsqrt(jnp.mean(mid * mid, axis=-1, keepdims=True) + NORM_EPS)
    scaled = norm_two[...] * xn_grad
    pull = jnp.mean(scaled * mid, axis=-1, keepdims=True)
    grad = cotangent[...].astype(jnp.float32) + scale * scaled - mid * (scale * scale * scale * pull)
    middle_grad[...] = grad
    half = pl.multiple_of(h * FLAT, FLAT)
    branch_grad[pl.ds(half, FLAT), :] = (RESIDUAL_SCALE * grad).astype(jnp.bfloat16)
    mine = branch_grad.at[pl.ds(half, FLAT)]
    pair_copy = go(mine, mine, 19, (e, 1 - h))
    small[pl.ds(0, experts), :] = jnp.dot(
        logit_grad, xn[...], preferred_element_type=jnp.float32
    )
    small[pl.ds(experts, 8), :] = jnp.broadcast_to(
        jnp.sum(xn_grad * mid * scale, axis=0, keepdims=True), (8, mid.shape[1])
    )
    pair_copy.wait_recv()
    for copy in started:
        copy.wait_send()


def combine(rows, parts, tables, probs, xn, w_router, middle, norm_two, cotangent):
    width = xn.shape[1]
    experts = w_router.shape[1]
    vmem = pl.BlockSpec(memory_space=pltpu.VMEM)
    low, full = jnp.bfloat16, jnp.float32
    block = (FLAT, width)
    gate = (experts, FLAT)
    return pl.pallas_call(
        combine_kernel,
        out_shape=(
            jax.ShapeDtypeStruct((2 * FLAT, width), low),
            jax.ShapeDtypeStruct(block, full),
            jax.ShapeDtypeStruct((experts + 8, width), full),
        ),
        in_specs=[vmem] * 9,
        out_specs=(vmem,) * 3,
        scratch_shapes=[
            pltpu.VMEM((4,) + rows.shape[1:], low),
            pltpu.VMEM(parts.shape, full),
            pltpu.VMEM((4,) + block, low),
            pltpu.VMEM((4,) + block, low),
            pltpu.VMEM((4,) + block, full),
            pltpu.VMEM((3,) + block, low),
            pltpu.VMEM((3,) + block, low),
            pltpu.VMEM((4,) + gate, full),
            pltpu.VMEM((4,) + gate, full),
            pltpu.VMEM((4,) + gate, full),
            pltpu.VMEM((3,) + gate, full),
            pltpu.VMEM((3,) + gate, full),
            pltpu.SemaphoreType.DMA((20,)),
            pltpu.SemaphoreType.DMA((20,)),
        ],
        compiler_params=pltpu.CompilerParams(
            collective_id=1, has_side_effects=True, vmem_limit_bytes=50 << 20
        ),
        name="combine",
    )(rows, parts, tables, probs, xn, w_router, middle, norm_two, cotangent)


def finish_kernel(
    terms,
    tokens,
    norm_one,
    middle_grad,
    small,
    weighted,
    tables,
    middle,
    grads,
    gate_part,
    up_part,
    down_part,
    grad_tokens,
    small_out,
    layer_out,
    grads_out,
    gate_other,
    up_other,
    down_other,
    terms_in,
    rows_in,
    near_in,
    near_send,
    kept,
    along_in,
    along_send,
    far_sum_in,
    near_sum_in,
    near_sum_send,
    kept_sum,
    along_sum_in,
    along_sum_send,
    small_mine,
    small_in,
    small_all,
    sems_send,
    sems_recv,
):
    e, h, near, far, along = places()
    greet(h, [(e, 1 - h), (near, h), (far, h)] + [(along[k], h) for k in (1, 2, 3)])
    started = []
    count = [0]

    def go(source, target, device):
        number = count[0]
        count[0] += 1
        copy = remote(source, target, sems_send.at[number], sems_recv.at[number], device)
        copy.start()
        started.append(copy)
        return copy

    z = e // 4
    plane = [[e % 4, near % 4], [far % 4, 3 - e % 4]]

    def shard(b, a, k):
        return ((z + 4 - k) % 4) * 4 + plane[b][a]

    pair = (e, 1 - h)
    half = pl.multiple_of(h * FLAT, FLAT)
    other_half = pl.multiple_of((1 - h) * FLAT, FLAT)
    terms_copy = go(terms.at[pl.ds(other_half, FLAT)], terms_in, pair)
    order = (2, 1, 3, 0)
    far_sums = {}
    for a in (1, 0):
        for k in order:
            far_sums[a, k] = go(grads.at[shard(1, a, k)], far_sum_in.at[a, k], (far, h))
    far_rows = {k: go(weighted.at[4 + k], rows_in.at[k], (far, h)) for k in order}
    expert_copies = [
        go(mine, other, pair)
        for mine, other in ((gate_part, gate_other), (up_part, up_other), (down_part, down_other))
    ]

    terms_copy.wait_recv()
    xn_grad = (
        terms[pl.ds(half, FLAT), :].astype(jnp.float32) + terms_in[...].astype(jnp.float32)
    ).astype(jnp.bfloat16).astype(jnp.float32)
    x_half = tokens[pl.ds(half, FLAT), :].astype(jnp.float32)
    scale = lax.rsqrt(jnp.mean(x_half * x_half, axis=-1, keepdims=True) + NORM_EPS)
    scaled = norm_one[...] * xn_grad
    pull = jnp.mean(scaled * x_half, axis=-1, keepdims=True)
    grad_tokens[...] = (
        middle_grad[...] + scale * scaled - x_half * (scale * scale * scale * pull)
    )
    experts = small.shape[0] - 8
    small_mine[0, pl.ds(0, experts), :] = small[pl.ds(0, experts), :]
    row = lax.broadcasted_iota(jnp.int32, (8, x_half.shape[1]), 0)
    norm_rows = jnp.where(
        row == 0,
        small[pl.ds(experts, 8), :],
        jnp.sum(xn_grad * x_half * scale, axis=0, keepdims=True),
    )
    small_mine[0, pl.ds(experts, 8), :] = norm_rows
    small_copy = go(small_mine.at[0], small_in.at[0], pair)

    near_sums = {}
    for k in order:
        far_sums[1, k].wait_recv()
        near_sum_send[k] = (
            grads[shard(0, 1, k)].astype(jnp.float32) + far_sum_in[1, k].astype(jnp.float32)
        ).astype(jnp.bfloat16)
        near_sums[k] = go(near_sum_send.at[k], near_sum_in.at[k], (near, h))
    small_copy.wait_recv()
    small_mine[1] = small_mine[0] + small_in[0]
    small_copy = go(small_mine.at[1], small_in.at[1], (far, h))
    along_sums = {}
    for k in order:
        far_sums[0, k].wait_recv()
        near_sums[k].wait_recv()
        sums = (
            grads[shard(0, 0, k)].astype(jnp.float32)
            + far_sum_in[0, k].astype(jnp.float32)
            + near_sum_in[k].astype(jnp.float32)
        )
        if k == 0:
            kept_sum[...] = sums
        else:
            along_sum_send[k - 1] = sums.astype(jnp.bfloat16)
            along_sums[k] = go(
                along_sum_send.at[k - 1], along_sum_in.at[k - 1], (along[4 - k], h)
            )
    near_rows = {}
    for k in order:
        far_rows[k].wait_recv()
        chosen = selection(tables, k, e, far).astype(jnp.bfloat16)
        stacked = jnp.concatenate(
            [weighted[k].reshape(4 * SLOTS, -1), rows_in[k].reshape(4 * SLOTS, -1)], axis=0
        )
        sums = lax.dot_general(
            chosen, stacked, (((0,), (0,)), ((), ())), preferred_element_type=jnp.float32
        )
        kept[k] = sums[:FLAT]
        near_send[k] = sums[FLAT:].astype(jnp.bfloat16)
        near_rows[k] = go(near_send.at[k], near_in.at[k], (near, h))
    small_copy.wait_recv()
    small_mine[2] = small_mine[1] + small_in[1]
    small_copy = go(small_mine.at[2], small_in.at[2], (near, h))
    final = kept_sum[...]
    for k in (1, 2, 3):
        along_sums[k].wait_recv()
        final = final + along_sum_in[k - 1].astype(jnp.float32)
    grads_out[e] = final.astype(jnp.bfloat16)
    mine = grads_out.at[e]
    out_copies = {k: go(mine, mine, (along[k], h)) for k in (1, 2, 3)}
    near_out = {0: go(mine, mine, (near, h))}
    far_out = [go(mine, mine, (far, h))]
    along_rows = {}
    for k in order:
        near_rows[k].wait_recv()
        sums = kept[k] + near_in[k].astype(jnp.float32)
        if k == 0:
            kept[0] = sums
        else:
            along_send[k - 1] = sums.astype(jnp.bfloat16)
            along_rows[k] = go(along_send.at[k - 1], along_in.at[k - 1], (along[4 - k], h))
    small_copy.wait_recv()
    small_all[z] = small_mine[2] + small_in[2]
    small_copies = [go(small_all.at[z], small_all.at[z], (along[k], h)) for k in (1, 2, 3)]
    for k in (1, 2, 3):
        out_copies[k].wait_recv()
        block = grads_out.at[shard(0, 0, k)]
        near_out[k] = go(block, block, (near, h))
        far_out.append(go(block, block, (far, h)))
    for k in range(4):
        near_out[k].wait_recv()
        block = grads_out.at[shard(0, 1, k)]
        far_out.append(go(block, block, (far, h)))
    expert_sum = kept[0]
    for k in (1, 2, 3):
        along_rows[k].wait_recv()
        expert_sum = expert_sum + along_in[k - 1].astype(jnp.float32)
    layer_out[...] = (middle[...] + RESIDUAL_SCALE * expert_sum).astype(jnp.bfloat16)
    for copy in small_copies:
        copy.wait_recv()
    small_out[...] = ((small_all[0] + small_all[1]) + small_all[2]) + small_all[3]
    for copy in far_out:
        copy.wait_recv()
    for copy in expert_copies:
        copy.wait_recv()
    for copy in started:
        copy.wait_send()


def finish(
    terms, tokens, norm_one, middle_grad, small, weighted, tables, middle, grads, gate, up, down
):
    width = tokens.shape[1]
    vmem = pl.BlockSpec(memory_space=pltpu.VMEM)
    anywhere = pl.BlockSpec(memory_space=pl.ANY)
    low, full = jnp.bfloat16, jnp.float32
    block = (FLAT, width)
    shard = grads.shape[1:]
    return pl.pallas_call(
        finish_kernel,
        out_shape=(
            jax.ShapeDtypeStruct(block, full),
            jax.ShapeDtypeStruct(small.shape, full),
            jax.ShapeDtypeStruct(block, low),
            jax.ShapeDtypeStruct(grads.shape, low),
            jax.ShapeDtypeStruct(gate.shape, low),
            jax.ShapeDtypeStruct(up.shape, low),
            jax.ShapeDtypeStruct(down.shape, low),
        ),
        in_specs=[vmem] * 9 + [anywhere] * 3,
        out_specs=(vmem,) * 4 + (anywhere,) * 3,
        scratch_shapes=[
            pltpu.VMEM(block, low),
            pltpu.VMEM((4,) + weighted.shape[1:], low),
            pltpu.VMEM((4,) + block, low),
            pltpu.VMEM((4,) + block, low),
            pltpu.VMEM((4,) + block, full),
            pltpu.VMEM((3,) + block, low),
            pltpu.VMEM((3,) + block, low),
            pltpu.VMEM((2, 4) + shard, low),
            pltpu.VMEM((4,) + shard, low),
            pltpu.VMEM((4,) + shard, low),
            pltpu.VMEM(shard, full),
            pltpu.VMEM((3,) + shard, low),
            pltpu.VMEM((3,) + shard, low),
            pltpu.VMEM((3,) + small.shape, full),
            pltpu.VMEM((3,) + small.shape, full),
            pltpu.VMEM((4,) + small.shape, full),
            pltpu.SemaphoreType.DMA((60,)),
            pltpu.SemaphoreType.DMA((60,)),
        ],
        compiler_params=pltpu.CompilerParams(
            collective_id=2, has_side_effects=True, vmem_limit_bytes=56 << 20
        ),
        name="finish",
    )(terms, tokens, norm_one, middle_grad, small, weighted, tables, middle, grads, gate, up, down)


def quick_shards(
    tokens,
    norm_one,
    w_query,
    key_weight,
    value_weight,
    w_output,
    norm_two,
    w_router,
    w_gate,
    w_up,
    w_down,
    routes,
    priority,
    cotangent,
):
    tok_rows, model_width = tokens.shape
    head_rank = lax.axis_index("head")
    prompt_rows = tok_rows // 2
    cont_rows = tok_rows // 4
    kv_heads = key_weight.shape[1] // HEAD_DIMENSION
    query_groups = w_query.shape[1] // key_weight.shape[1]
    experts = w_router.shape[1]
    local_index = jnp.arange(tok_rows, dtype=jnp.int32)
    position = jnp.where(
        local_index < prompt_rows,
        local_index,
        prompt_rows + (local_index - prompt_rows) % cont_rows,
    )
    frequency = ROPE_BASE ** (
        -(2.0 * jnp.arange(HEAD_DIMENSION // 2, dtype=jnp.float32)) / HEAD_DIMENSION
    )
    angle_table = position.astype(jnp.float32)[:, None] * frequency[None, :]
    cosine_values = jnp.cos(angle_table)[:, None, :]
    sine_values = jnp.sin(angle_table)[:, None, :]
    x_full = tokens.astype(jnp.float32)
    normed = rms_scale(x_full, norm_one).astype(jnp.bfloat16)
    queries = apply_rotary(
        jnp.dot(normed, w_query, preferred_element_type=jnp.float32).reshape(
            tok_rows, -1, HEAD_DIMENSION
        ),
        cosine_values,
        sine_values,
    ).astype(jnp.bfloat16)
    keys_all = apply_rotary(
        jnp.dot(normed, key_weight, preferred_element_type=jnp.float32).reshape(
            tok_rows, -1, HEAD_DIMENSION
        ),
        cosine_values,
        sine_values,
    ).astype(jnp.bfloat16)
    values_all = (
        jnp.dot(normed, value_weight, preferred_element_type=jnp.float32)
        .astype(jnp.bfloat16)
        .reshape(tok_rows, kv_heads, HEAD_DIMENSION)
    )
    query_col = local_index[:, None]
    key_row = local_index[None, :]
    visible = (key_row < prompt_rows) & ((query_col >= prompt_rows) | (key_row <= query_col))
    visible |= (
        (key_row >= prompt_rows)
        & (query_col >= prompt_rows)
        & (key_row <= query_col)
        & ((key_row - prompt_rows) // cont_rows == (query_col - prompt_rows) // cont_rows)
    )
    query_block = queries.reshape(tok_rows, kv_heads, query_groups, HEAD_DIMENSION)
    raw_scores = (
        jnp.einsum("qhgd,khd->hgqk", query_block, keys_all, preferred_element_type=jnp.float32)
        * ATTENTION_SCALE
    )
    scores = jnp.where(visible[None, None], raw_scores, MASKED_SCORE)
    row_max = jnp.max(scores, axis=-1, keepdims=True)
    weights = jnp.exp(scores - row_max)
    probs = weights / jnp.sum(weights, axis=-1, keepdims=True)
    probs_low = probs.astype(jnp.bfloat16)
    mixed = jnp.einsum("hgqk,khd->qhgd", probs_low, values_all, preferred_element_type=jnp.float32)
    head_outputs = mixed.astype(jnp.bfloat16).reshape(tok_rows, -1)
    branch = jnp.dot(head_outputs, w_output, preferred_element_type=jnp.float32)

    my_routes = lax.dynamic_slice_in_dim(routes, head_rank * FLAT, FLAT, 0)
    names = jnp.arange(experts, dtype=jnp.int32)
    member = jnp.any(my_routes[None, :, :] == names[:, None, None], axis=-1)
    order_rank = priority[0]
    earlier = (order_rank[:, None] < order_rank[None, :]).astype(jnp.bfloat16)
    before = jnp.dot(member.astype(jnp.bfloat16), earlier, preferred_element_type=jnp.float32)
    table = jnp.where(member & (before < SLOTS), before, UNKEPT)
    out_rows = (RESIDUAL_SCALE * cotangent.astype(jnp.float32)).astype(jnp.bfloat16)

    norm_two_row = norm_two[None, :]
    middle, xn_two, gate_probs, tables, x_slots, g_slots, gates_own, gates_far = dispatch(
        branch,
        tokens,
        norm_two_row,
        w_router,
        table,
        member.astype(jnp.float32),
        out_rows,
    )
    row_grads, weighted, parts, grad_gate_w, grad_up_w, grad_down_w = run_experts(
        x_slots, g_slots, gates_own, gates_far, w_gate, w_up, w_down
    )
    branch_grad, middle_grad, small = combine(
        row_grads, parts, tables, gate_probs, xn_two, w_router, middle, norm_two_row, cotangent
    )
    heads_grad = jnp.einsum(
        "td,hd->th", branch_grad, w_output, preferred_element_type=jnp.float32
    ).astype(jnp.bfloat16)
    grad_output_w = jnp.einsum(
        "th,td->hd", head_outputs, branch_grad, preferred_element_type=jnp.float32
    ).astype(jnp.bfloat16)
    heads_block = heads_grad.reshape(tok_rows, kv_heads, query_groups, HEAD_DIMENSION)
    prob_grad = jnp.einsum(
        "qhgd,khd->hgqk", heads_block, values_all, preferred_element_type=jnp.float32
    )
    row_inner = jnp.sum(probs * prob_grad, axis=-1, keepdims=True)
    score_grad = (probs * (prob_grad - row_inner)).astype(jnp.bfloat16)
    query_grad = (
        jnp.einsum("hgqk,khd->qhgd", score_grad, keys_all, preferred_element_type=jnp.float32)
        * ATTENTION_SCALE
    )
    key_grad = (
        jnp.einsum("hgqk,qhgd->khd", score_grad, query_block, preferred_element_type=jnp.float32)
        * ATTENTION_SCALE
    )
    value_grad = jnp.einsum(
        "hgqk,qhgd->khd", probs_low, heads_block, preferred_element_type=jnp.float32
    )
    query_pre_grad = (
        rotate_back(query_grad.reshape(tok_rows, -1, HEAD_DIMENSION), cosine_values, sine_values)
        .reshape(tok_rows, -1)
        .astype(jnp.bfloat16)
    )
    key_pre_grad = (
        rotate_back(key_grad, cosine_values, sine_values).reshape(tok_rows, -1).astype(jnp.bfloat16)
    )
    value_low_grad = value_grad.reshape(tok_rows, -1).astype(jnp.bfloat16)
    head_grads = jnp.concatenate([query_pre_grad, key_pre_grad, value_low_grad], axis=1)
    grad_in = jnp.einsum(
        "td,th->dh", normed, head_grads, preferred_element_type=jnp.float32
    ).astype(jnp.bfloat16)
    xn_one_terms = (
        jnp.einsum("th,dh->td", query_pre_grad, w_query, preferred_element_type=jnp.float32)
        + jnp.einsum("th,dh->td", key_pre_grad, key_weight, preferred_element_type=jnp.float32)
        + jnp.einsum("th,dh->td", value_low_grad, value_weight, preferred_element_type=jnp.float32)
    ).astype(jnp.bfloat16)
    grads = jnp.concatenate([grad_in, grad_output_w], axis=0)
    flat_shape = grads.shape
    grads = grads.reshape(16, -1, model_width)
    grad_tokens, small, layer_out, grads, gate_other, up_other, down_other = finish(
        xn_one_terms,
        tokens,
        norm_one[None, :],
        middle_grad,
        small,
        weighted,
        tables,
        middle,
        grads,
        grad_gate_w,
        grad_up_w,
        grad_down_w,
    )
    grads = grads.reshape(flat_shape).astype(jnp.float32)
    q_cols, k_cols = w_query.shape[1], key_weight.shape[1]

    def both(mine, other):
        return mine.astype(jnp.float32) + other.astype(jnp.float32)

    return (
        layer_out,
        grad_tokens,
        small[experts + 1],
        grads[:model_width, :q_cols],
        grads[:model_width, q_cols : q_cols + k_cols],
        grads[:model_width, q_cols + k_cols :],
        grads[model_width:],
        small[experts],
        small[:experts].T,
        both(grad_gate_w, gate_other),
        both(grad_up_w, up_other),
        both(grad_down_w, down_other),
    )


def solution(mesh):
    body = quick_shards if dict(mesh.shape) == {"exp": 16, "head": 2} else shards
    return jax.shard_map(
        body,
        mesh=mesh,
        in_specs=(
            P("exp", None),
            P(),
            P(None, "head"),
            P(None, "head"),
            P(None, "head"),
            P("head", None),
            P(),
            P(),
            P(None, "exp"),
            P(None, "exp"),
            P("exp", None),
            P("exp", None),
            P(("exp", "head"), None),
            P(("exp", "head"), None),
        ),
        out_specs=(
            P(("exp", "head"), None),
            P(("exp", "head"), None),
            P(),
            P(None, "head"),
            P(None, "head"),
            P(None, "head"),
            P("head", None),
            P(),
            P(),
            P(None, "exp"),
            P(None, "exp"),
            P("exp", None),
        ),
        check_vma=False,
    )
```

```python
import functools
import types

import jax
import jax.numpy as jnp
from jax import lax
from jax.experimental import pallas as pl
from jax.experimental.pallas import tpu as pltpu
from jax.sharding import PartitionSpec as P

HEAD_DIMENSION = 64
FF = 512
TOPK = 8


RESIDUAL_SCALE = 0.22
ATTENTION_SCALE = 0.015625
ROPE_BASE = 10000.0
NORM_EPS = 1e-06
MASKED_SCORE = -1e30


def rms_scale(values, scale_row):
    return (
        values * lax.rsqrt(jnp.mean(values * values, axis=-1, keepdims=True) + NORM_EPS) * scale_row
    )


def apply_rotary(values, cosine_values, sine_values):
    half_width = values.shape[-1] // 2
    lower_part = values[..., :half_width]
    upper_part = values[..., half_width:]
    return jnp.concatenate(
        [
            lower_part * cosine_values - upper_part * sine_values,
            upper_part * cosine_values + lower_part * sine_values,
        ],
        axis=-1,
    )


def rotate_back(values, cosine_values, sine_values):
    half_width = values.shape[-1] // 2
    lower_part = values[..., :half_width]
    upper_part = values[..., half_width:]
    return jnp.concatenate(
        [
            lower_part * cosine_values + upper_part * sine_values,
            upper_part * cosine_values - lower_part * sine_values,
        ],
        axis=-1,
    )


def shards(
    tokens,
    norm_one,
    w_query,
    key_weight,
    value_weight,
    w_output,
    norm_two,
    w_router,
    w_gate,
    w_up,
    w_down,
    routes,
    priority,
    cotangent,
):
    tok_rows, model_width = tokens.shape
    heads_count = lax.axis_size("head")
    head_rank = lax.axis_index("head")
    exp_count = lax.axis_size("exp")
    half_rows = tok_rows // heads_count
    prompt_rows = tok_rows // 2
    cont_rows = tok_rows // 4
    kv_heads = key_weight.shape[1] // HEAD_DIMENSION
    query_groups = w_query.shape[1] // key_weight.shape[1]
    experts = w_router.shape[1]
    held_cols = w_gate.shape[1]
    held = max(1, held_cols // FF)
    split = max(1, FF // held_cols)
    block_width = held_cols // held
    capacity = max(2, (5 * half_rows * TOPK + 4 * experts - 1) // (4 * experts))
    rows_per_block = min(512, tok_rows)
    count_of_blocks = tok_rows // rows_per_block
    local_index = jnp.arange(tok_rows, dtype=jnp.int32)
    position = jnp.where(
        local_index < prompt_rows,
        local_index,
        prompt_rows + (local_index - prompt_rows) % cont_rows,
    )
    frequency = ROPE_BASE ** (
        -(2.0 * jnp.arange(HEAD_DIMENSION // 2, dtype=jnp.float32)) / HEAD_DIMENSION
    )
    angle_table = position.astype(jnp.float32)[:, None] * frequency[None, :]
    cosine_values = jnp.cos(angle_table)[:, None, :]
    sine_values = jnp.sin(angle_table)[:, None, :]
    x_full = tokens.astype(jnp.float32)
    normed_input_first = rms_scale(x_full, norm_one).astype(jnp.bfloat16)
    rotated_queries = apply_rotary(
        jnp.dot(normed_input_first, w_query, preferred_element_type=jnp.float32).reshape(
            tok_rows, -1, HEAD_DIMENSION
        ),
        cosine_values,
        sine_values,
    ).astype(jnp.bfloat16)
    keys_all = apply_rotary(
        jnp.dot(normed_input_first, key_weight, preferred_element_type=jnp.float32).reshape(
            tok_rows, -1, HEAD_DIMENSION
        ),
        cosine_values,
        sine_values,
    ).astype(jnp.bfloat16)
    values_all = (
        jnp.dot(normed_input_first, value_weight, preferred_element_type=jnp.float32)
        .astype(jnp.bfloat16)
        .reshape(tok_rows, kv_heads, HEAD_DIMENSION)
    )

    def visible_pairs(block_start):
        query_col = (block_start + jnp.arange(rows_per_block, dtype=jnp.int32))[:, None]
        key_row = jnp.arange(tok_rows, dtype=jnp.int32)[None, :]
        from_prompt = (key_row < prompt_rows) & (
            (query_col >= prompt_rows) | (key_row <= query_col)
        )
        same_cont = (
            (key_row >= prompt_rows)
            & (query_col >= prompt_rows)
            & (key_row <= query_col)
            & ((key_row - prompt_rows) // cont_rows == (query_col - prompt_rows) // cont_rows)
        )
        return from_prompt | same_cont

    def scores_of(query_block, block_start):
        raw_scores = (
            jnp.einsum("qhgd,khd->hgqk", query_block, keys_all, preferred_element_type=jnp.float32)
            * ATTENTION_SCALE
        )
        return jnp.where(visible_pairs(block_start)[None, None], raw_scores, MASKED_SCORE)

    def forward_block(parts):
        query_block, block_start = parts
        scores = scores_of(query_block, block_start)
        row_max = jnp.max(scores, axis=-1, keepdims=True)
        weights = jnp.exp(scores - row_max)
        row_total = jnp.sum(weights, axis=-1, keepdims=True)
        probs_low = (weights / row_total).astype(jnp.bfloat16)
        mixed = jnp.einsum(
            "hgqk,khd->qhgd", probs_low, values_all, preferred_element_type=jnp.float32
        )
        return (mixed.astype(jnp.bfloat16), row_max + jnp.log(row_total))

    query_blocks = rotated_queries.reshape(
        count_of_blocks, rows_per_block, kv_heads, query_groups, HEAD_DIMENSION
    )
    block_starts = jnp.arange(count_of_blocks, dtype=jnp.int32) * rows_per_block
    heads_blocks, log_total = lax.map(forward_block, (query_blocks, block_starts))
    head_outputs = heads_blocks.reshape(tok_rows, -1)
    head_terms = jnp.dot(head_outputs, w_output, preferred_element_type=jnp.float32)
    branch_half = lax.dynamic_slice_in_dim(
        lax.psum(head_terms, "head"), head_rank * half_rows, half_rows, 0
    )
    x_half = lax.dynamic_slice_in_dim(x_full, head_rank * half_rows, half_rows, 0)
    middle = x_half + RESIDUAL_SCALE * branch_half
    xn_two = rms_scale(middle, norm_two).astype(jnp.bfloat16)
    logits = jnp.dot(xn_two, w_router, preferred_element_type=jnp.float32)
    my_routes = lax.dynamic_slice_in_dim(routes, head_rank * half_rows, half_rows, 0)
    route_hot = my_routes[:, :, None] == jnp.arange(experts, dtype=jnp.int32)[None, None, :]
    chosen = jnp.sum(jnp.where(route_hot, logits[:, None, :], 0.0), axis=-1)
    chosen_max = jnp.max(chosen, axis=-1, keepdims=True)
    chosen_exp = jnp.exp(chosen - chosen_max)
    gate_probs = chosen_exp / jnp.sum(chosen_exp, axis=-1, keepdims=True)
    gate_low = gate_probs.astype(jnp.bfloat16)
    member = jnp.any(route_hot, axis=1).astype(jnp.bfloat16)
    order_rank = priority[0]
    earlier = (order_rank[None, :] < order_rank[:, None]).astype(jnp.bfloat16)
    before = jnp.dot(earlier, member, preferred_element_type=jnp.float32)
    slot_rank = jnp.sum(jnp.where(route_hot, before[:, None, :], 0.0), axis=-1).astype(jnp.int32)
    is_kept = slot_rank < capacity
    spare_slot = experts * capacity
    target = jnp.where(is_kept, my_routes * capacity + slot_rank, spare_slot)
    row_ids = jnp.broadcast_to(jnp.arange(half_rows, dtype=jnp.int32)[:, None], target.shape)
    assign_ids = jnp.arange(half_rows * TOPK, dtype=jnp.int32).reshape(target.shape)
    source_row = (
        jnp.zeros(spare_slot + 1, jnp.int32).at[target.ravel()].set(row_ids.ravel())[:spare_slot]
    )
    source_pick = (
        jnp.zeros(spare_slot + 1, jnp.int32).at[target.ravel()].set(assign_ids.ravel())[:spare_slot]
    )
    filled = jnp.zeros(spare_slot + 1, jnp.int32).at[target.ravel()].set(1)[:spare_slot] > 0
    slot_inputs = jnp.where(filled[:, None], xn_two[source_row], 0).reshape(
        experts, capacity, model_width
    )
    slot_gates = jnp.where(filled, gate_low.ravel()[source_pick], 0).reshape(experts, capacity)

    def to_owners(per_expert):
        shape_in = per_expert.shape
        spread = jnp.broadcast_to(per_expert[:, None], (shape_in[0], split) + shape_in[1:])
        return spread.reshape((exp_count, held) + shape_in[1:])

    def from_owners(per_owner):
        shape_in = per_owner.shape
        return jnp.sum(
            per_owner.reshape((experts, split) + shape_in[2:]).astype(jnp.float32), axis=1
        )

    gate_cols = w_gate.reshape(model_width, held, block_width)
    up_cols = w_up.reshape(model_width, held, block_width)
    down_rows = w_down.reshape(held, block_width, model_width)
    send_rows = to_owners(slot_inputs)
    send_gates = to_owners(slot_gates)
    slot_rows = lax.all_to_all(send_rows, "exp", split_axis=0, concat_axis=0, tiled=True)
    slot_gate = lax.all_to_all(send_gates, "exp", split_axis=0, concat_axis=0, tiled=True)
    gate_pre = jnp.einsum(
        "sjcd,djf->sjcf", slot_rows, gate_cols, preferred_element_type=jnp.float32
    )
    up_pre = jnp.einsum("sjcd,djf->sjcf", slot_rows, up_cols, preferred_element_type=jnp.float32)
    hidden = (gate_pre * jax.nn.sigmoid(gate_pre) * up_pre).astype(jnp.bfloat16)
    result = jnp.einsum("sjcf,jfd->sjcd", hidden, down_rows, preferred_element_type=jnp.float32)
    weighted = (slot_gate[..., None].astype(jnp.float32) * result).astype(jnp.bfloat16)
    returned = lax.all_to_all(weighted, "exp", split_axis=0, concat_axis=0, tiled=True)
    returned, held_rows, held_gates = (returned, slot_rows, slot_gate)
    back_flat = jnp.concatenate(
        [
            from_owners(returned).reshape(spare_slot, model_width),
            jnp.zeros((1, model_width), jnp.float32),
        ],
        axis=0,
    )
    expert_sum = jnp.sum(back_flat[target], axis=1)
    layer_out = (middle + RESIDUAL_SCALE * expert_sum).astype(jnp.bfloat16)
    out_grad = cotangent.astype(jnp.float32)
    weighted_rows = (RESIDUAL_SCALE * out_grad).astype(jnp.bfloat16)
    grad_slots = to_owners(
        jnp.where(filled[:, None], weighted_rows[source_row], 0).reshape(
            experts, capacity, model_width
        )
    )
    back_grads, back_rows, back_gates = (
        lax.all_to_all(grad_slots, "exp", split_axis=0, concat_axis=0, tiled=True),
        lax.all_to_all(send_rows, "exp", split_axis=0, concat_axis=0, tiled=True),
        lax.all_to_all(send_gates, "exp", split_axis=0, concat_axis=0, tiled=True),
    )
    owner_gates = back_gates[..., None].astype(jnp.float32)
    gate_pre = jnp.einsum(
        "sjcd,djf->sjcf", back_rows, gate_cols, preferred_element_type=jnp.float32
    )
    up_pre = jnp.einsum("sjcd,djf->sjcf", back_rows, up_cols, preferred_element_type=jnp.float32)
    gate_sigmoid = jax.nn.sigmoid(gate_pre)
    gate_act = gate_pre * gate_sigmoid
    hidden = (gate_act * up_pre).astype(jnp.bfloat16)
    result = jnp.einsum("sjcf,jfd->sjcd", hidden, down_rows, preferred_element_type=jnp.float32)
    gate_part = jnp.sum(back_grads.astype(jnp.float32) * result, axis=-1)
    result_grad = (owner_gates * back_grads).astype(jnp.bfloat16)
    grad_down_w = jnp.einsum(
        "sjcf,sjcd->jfd", hidden, result_grad, preferred_element_type=jnp.float32
    ).reshape(held_cols, model_width)
    hidden_grad = jnp.einsum(
        "sjcd,jfd->sjcf", result_grad, down_rows, preferred_element_type=jnp.float32
    )
    gate_pre_grad = (
        hidden_grad * up_pre * gate_sigmoid * (1.0 + gate_pre * (1.0 - gate_sigmoid))
    ).astype(jnp.bfloat16)
    up_pre_grad = (hidden_grad * gate_act).astype(jnp.bfloat16)
    grad_gate_w = jnp.einsum(
        "sjcd,sjcf->djf", back_rows, gate_pre_grad, preferred_element_type=jnp.float32
    ).reshape(model_width, held_cols)
    grad_up_w = jnp.einsum(
        "sjcd,sjcf->djf", back_rows, up_pre_grad, preferred_element_type=jnp.float32
    ).reshape(model_width, held_cols)
    rows_grad = (
        jnp.einsum("sjcf,djf->sjcd", gate_pre_grad, gate_cols, preferred_element_type=jnp.float32)
        + jnp.einsum("sjcf,djf->sjcd", up_pre_grad, up_cols, preferred_element_type=jnp.float32)
    ).astype(jnp.bfloat16)
    rows_back, gates_back = (
        lax.all_to_all(rows_grad, "exp", split_axis=0, concat_axis=0, tiled=True),
        lax.all_to_all(
            gate_part.astype(jnp.bfloat16), "exp", split_axis=0, concat_axis=0, tiled=True
        ),
    )
    rows_flat = jnp.concatenate(
        [
            from_owners(rows_back).reshape(spare_slot, model_width),
            jnp.zeros((1, model_width), jnp.float32),
        ],
        axis=0,
    )
    xn_two_grad = jnp.sum(rows_flat[target], axis=1)
    gate_total = from_owners(gates_back).astype(jnp.bfloat16).reshape(spare_slot)
    gates_flat = jnp.concatenate([gate_total, jnp.zeros((1,), jnp.bfloat16)], axis=0)
    gate_grad_tok = gates_flat[target].astype(jnp.float32)
    chosen_grad = gate_probs * (
        gate_grad_tok - jnp.sum(gate_probs * gate_grad_tok, axis=-1, keepdims=True)
    )
    logit_grad = jnp.sum(jnp.where(route_hot, chosen_grad[:, :, None], 0.0), axis=1).astype(
        jnp.bfloat16
    )
    grad_router = jnp.einsum("rd,re->de", xn_two, logit_grad, preferred_element_type=jnp.float32)
    xn_two_grad = xn_two_grad + jnp.einsum(
        "re,de->rd", logit_grad, w_router, preferred_element_type=jnp.float32
    )
    middle_norm_pull = jax.vjp(rms_scale, middle, norm_two)[1]
    middle_norm_grad, grad_norm_two = middle_norm_pull(xn_two_grad)
    middle_grad = out_grad + middle_norm_grad
    branch_rows = (RESIDUAL_SCALE * middle_grad).astype(jnp.bfloat16)
    branch_grad = lax.all_gather(branch_rows, "head", axis=0, tiled=True)
    heads_grad = jnp.einsum(
        "td,hd->th", branch_grad, w_output, preferred_element_type=jnp.float32
    ).astype(jnp.bfloat16)
    grad_output_w = jnp.einsum(
        "th,td->hd", head_outputs, branch_grad, preferred_element_type=jnp.float32
    )

    def backward_block(running, parts):
        key_grad, value_grad = running
        query_block, heads_block, block_total, block_start = parts
        scores = scores_of(query_block, block_start)
        probs = jnp.exp(scores - block_total)
        probs_low = probs.astype(jnp.bfloat16)
        prob_grad = jnp.einsum(
            "qhgd,khd->hgqk", heads_block, values_all, preferred_element_type=jnp.float32
        )
        row_inner = jnp.sum(probs * prob_grad, axis=-1, keepdims=True)
        score_grad = (probs * (prob_grad - row_inner)).astype(jnp.bfloat16)
        query_grad = (
            jnp.einsum("hgqk,khd->qhgd", score_grad, keys_all, preferred_element_type=jnp.float32)
            * ATTENTION_SCALE
        )
        key_grad = (
            key_grad
            + jnp.einsum(
                "hgqk,qhgd->khd", score_grad, query_block, preferred_element_type=jnp.float32
            )
            * ATTENTION_SCALE
        )
        value_grad = value_grad + jnp.einsum(
            "hgqk,qhgd->khd", probs_low, heads_block, preferred_element_type=jnp.float32
        )
        return ((key_grad, value_grad), query_grad)

    heads_grad_blocks = heads_grad.reshape(
        count_of_blocks, rows_per_block, kv_heads, query_groups, HEAD_DIMENSION
    )
    zero_keys = jnp.zeros((tok_rows, kv_heads, HEAD_DIMENSION), jnp.float32)
    (own_key, own_value), query_grad = lax.scan(
        backward_block,
        (zero_keys, zero_keys),
        (query_blocks, heads_grad_blocks, log_total, block_starts),
    )
    query_pre_grad = (
        rotate_back(query_grad.reshape(tok_rows, -1, HEAD_DIMENSION), cosine_values, sine_values)
        .reshape(tok_rows, -1)
        .astype(jnp.bfloat16)
    )
    key_pre_grad = (
        rotate_back(own_key, cosine_values, sine_values).reshape(tok_rows, -1).astype(jnp.bfloat16)
    )
    value_low_grad = own_value.reshape(tok_rows, -1).astype(jnp.bfloat16)
    grad_query_w = jnp.einsum(
        "td,th->dh", normed_input_first, query_pre_grad, preferred_element_type=jnp.float32
    )
    grad_key_w = jnp.einsum(
        "td,th->dh", normed_input_first, key_pre_grad, preferred_element_type=jnp.float32
    )
    grad_value_w = jnp.einsum(
        "td,th->dh", normed_input_first, value_low_grad, preferred_element_type=jnp.float32
    )
    xn_one_terms = (
        jnp.einsum("th,dh->td", query_pre_grad, w_query, preferred_element_type=jnp.float32)
        + jnp.einsum("th,dh->td", key_pre_grad, key_weight, preferred_element_type=jnp.float32)
        + jnp.einsum("th,dh->td", value_low_grad, value_weight, preferred_element_type=jnp.float32)
    )
    xn_one_grad = lax.psum_scatter(
        xn_one_terms.astype(jnp.bfloat16), "head", scatter_dimension=0, tiled=True
    ).astype(jnp.float32)
    input_norm_pull = jax.vjp(rms_scale, x_half, norm_one)[1]
    input_norm_grad, grad_norm_one = input_norm_pull(xn_one_grad)
    grad_tokens = middle_grad + input_norm_grad
    grad_gate_w, grad_up_w, grad_down_w, grad_router, grad_norm_one, grad_norm_two = (
        lax.psum(grad_gate_w.astype(jnp.bfloat16), "head").astype(jnp.float32),
        lax.psum(grad_up_w.astype(jnp.bfloat16), "head").astype(jnp.float32),
        lax.psum(grad_down_w.astype(jnp.bfloat16), "head").astype(jnp.float32),
        lax.psum(grad_router.astype(jnp.bfloat16), "head").astype(jnp.float32),
        lax.psum(grad_norm_one.astype(jnp.bfloat16), "head").astype(jnp.float32),
        lax.psum(grad_norm_two.astype(jnp.bfloat16), "head").astype(jnp.float32),
    )
    (
        grad_query_w,
        grad_key_w,
        grad_value_w,
        grad_output_w,
        grad_router,
        grad_norm_one,
        grad_norm_two,
    ) = lax.psum(
        (
            grad_query_w,
            grad_key_w,
            grad_value_w,
            grad_output_w,
            grad_router,
            grad_norm_one,
            grad_norm_two,
        ),
        "exp",
    )
    return (
        layer_out,
        grad_tokens,
        grad_norm_one,
        grad_query_w,
        grad_key_w,
        grad_value_w,
        grad_output_w,
        grad_norm_two,
        grad_router,
        grad_gate_w,
        grad_up_w,
        grad_down_w,
    )


MESH = pl.DeviceIdType.MESH
FLAT = 128
SLOTS = 40
PAIR = 2 * SLOTS
UNKEPT = -1000.0
LOW = jnp.bfloat16
FULL = jnp.float32
LAST = (((1,), (1,)), ((), ()))
FIRST = (((0,), (0,)), ((), ()))
USUAL = (((1,), (0,)), ((), ()))


def mul(left, right, dims=USUAL):
    return lax.dot_general(left, right, dims, preferred_element_type=FULL)


def remote(source, target, send_sem, recv_sem, device):
    return pltpu.make_async_remote_copy(
        src_ref=source,
        dst_ref=target,
        send_sem=send_sem,
        recv_sem=recv_sem,
        device_id=device,
        device_id_type=MESH,
    )


def part(ref, *index):
    return lambda: ref.at[index]


def whole(ref):
    return lambda: ref


class Places:
    def __init__(self):
        self.e = e = lax.axis_index("exp")
        self.h = h = lax.axis_index("head")
        x, y, self.z = e % 2, (e // 2) % 2, e // 4
        z = self.z
        over_x, over_y = e + 1 - 2 * x, e + 2 - 4 * y
        self.near_e = over_x * (1 - h) + over_y * h
        self.far_e = over_y * (1 - h) + over_x * h
        self.near = (self.near_e, h)
        self.far = (self.far_e, h)
        self.edge = (e + 4 - 8 * (z % 2), h)
        self.inner = ((3 - z) * 4 + e % 4, h)
        self.pair = (e, 1 - h)
        self.is_inner = (z == 1) | (z == 2)
        self.is_outer = (z == 0) | (z == 3)

    def greet(self):
        barrier = pltpu.get_barrier_semaphore()

        def signal(device):
            pl.semaphore_signal(barrier, inc=1, device_id=device, device_id_type=MESH)

        for device in (self.pair, self.near, self.far, self.edge):
            signal(device)

        @pl.when(self.is_inner)
        def _():
            signal(self.inner)
            pl.semaphore_wait(barrier, 5)

        @pl.when(self.is_outer)
        def _():
            pl.semaphore_wait(barrier, 4)


class Links:
    def __init__(self, places, send, recv):
        self.places, self.send, self.recv = places, send, recv
        self.sent, self.names = 0, {}
        self.pending = {"all": [], "inner": [], "outer": []}

    def number(self, name):
        return self.names.setdefault(name, len(self.names))

    def go(self, name, source, target, device, who="all"):
        number = self.sent
        remote(
            source(), target(), self.send.at[number], self.recv.at[self.number(name)], device
        ).start()
        self.sent += 1
        self.pending[who].append((number, source))

    def got(self, name, target):
        remote(
            target(), target(), self.send.at[0], self.recv.at[self.number(name)], self.places.near
        ).wait_recv()

    def sent_all(self, who):
        for number, source in self.pending[who]:
            remote(
                source(), source(), self.send.at[number], self.recv.at[0], self.places.near
            ).wait_send()

    def drain(self):
        self.sent_all("all")

        @pl.when(self.places.is_inner)
        def _():
            self.sent_all("inner")

        @pl.when(self.places.is_outer)
        def _():
            self.sent_all("outer")


class Spread:
    def __init__(self, links, name, gathered):
        self.links, self.name, self.gathered = links, name, gathered

    def start(self, block):
        links, places = self.links, self.links.places
        links.go((self.name, "z", 1), block, self.spot(1, 0), places.edge)
        links.go((self.name, "n", 0), block, self.spot(0, 1), places.near)

        @pl.when(places.is_inner)
        def _():
            links.go((self.name, "z", 2), block, self.spot(2, 0), places.inner, "inner")

    def pass_on(self, i):
        links, places = self.links, self.links.places
        block = self.spot(i, 0)
        links.got((self.name, "z", i), block)
        there = {1: 3, 2: 2, 3: 3}[i]
        device = places.inner if i == 1 else places.edge

        @pl.when(places.is_inner)
        def _():
            links.go((self.name, "z", there), block, self.spot(there, 0), device, "inner")

        links.go((self.name, "n", i), block, self.spot(i, 1), places.near)

    def wait(self, i):
        self.links.got((self.name, "n", i), self.spot(i, 1))

    def spot(self, i, a):
        return lambda: self.gathered.at[i, a]


class Gather:
    def __init__(self, links, name, send, recv):
        self.links, self.name, self.send, self.recv = links, name, send, recv

    def cast(self, value):
        return value.astype(self.send.dtype)

    def arrived(self, name, slot):
        self.links.got((self.name, name), part(self.recv, slot))
        return self.recv[slot].astype(FULL)

    def push(self, i, value):
        links, places, send, recv = self.links, self.links.places, self.send, self.recv
        if i == 1:

            @pl.when(places.is_outer)
            def _():
                send[1] = self.cast(value())
                links.go((self.name, "e1"), part(send, 1), part(recv, 1), places.edge, "outer")

            @pl.when(places.is_inner)
            def _():
                send[1] = self.cast(value() + self.arrived("i3", 4))
                links.go((self.name, "e1"), part(send, 1), part(recv, 1), places.edge, "inner")

        else:
            slot = {3: 4, 2: 0}[i]

            @pl.when(places.is_outer)
            def _():
                send[i] = self.cast(value())
                links.go((self.name, "e", i), part(send, i), part(recv, i), places.edge, "outer")

            @pl.when(places.is_inner)
            def _():
                self.links.got((self.name, "e", i), part(recv, i))
                send[i] = self.cast(value() + recv[i].astype(FULL))
                links.go((self.name, "i%d" % i), part(send, i), part(recv, slot), places.inner, "inner")

    def total(self, own, result):
        places = self.links.places
        result[...] = own + self.arrived("e1", 1)

        @pl.when(places.is_inner)
        def _():
            result[...] += self.arrived("i2", 0)


def table_rows(tables, i, places):
    rows = []
    for chip in (places.e, places.far_e):
        for j in range(2):
            rows.append(
                jnp.concatenate(
                    [tables[i, a, pl.ds(2 * chip + j, 1), :] for a in range(2)], axis=1
                )
            )
    return rows


def selection(tables, i, places):
    slot = lax.broadcasted_iota(jnp.int32, (PAIR, 2 * FLAT), 0)
    lane = lax.broadcasted_iota(jnp.int32, (PAIR, 2 * FLAT), 1)
    wanted = (slot - jnp.where(lane >= FLAT, SLOTS, 0)).astype(FULL)
    return jnp.concatenate(
        [jnp.where(row == wanted, 1.0, 0.0) for row in table_rows(tables, i, places)], axis=0
    )


def layer_kernel(names, *refs):
    r = types.SimpleNamespace(**dict(zip(names, refs, strict=True)))
    places = Places()
    h = places.h
    places.greet()
    links = Links(places, r.sems_send, r.sems_recv)
    experts = r.w_router.shape[1]
    width = r.tokens.shape[1]
    half = pl.multiple_of(h * FLAT, FLAT)
    other_half = pl.multiple_of((1 - h) * FLAT, FLAT)

    loads = [
        pltpu.make_async_copy(source, target, r.sems_local.at[n])
        for n, (source, target) in enumerate(
            ((r.w_gate, r.gate_w), (r.w_up, r.up_w), (r.w_down, r.down_w))
        )
    ]
    links.go("branch", part(r.branch, pl.ds(other_half, FLAT)), whole(r.branch_in), places.pair)
    t_spread = Spread(links, "t", r.tables)
    g_spread = Spread(links, "g", r.g_all)
    x_spread = Spread(links, "x", r.x_all)
    p_spread = Spread(links, "p", r.gate_tables)
    t_spread.start(whole(r.table))
    g_spread.start(whole(r.out_rows))
    for load in loads:
        load.start()
    r.tables[0, 0] = r.table[...]
    r.g_all[0, 0] = r.out_rows[...]

    links.got("branch", whole(r.branch_in))
    middle = r.tokens[pl.ds(half, FLAT), :].astype(FULL) + RESIDUAL_SCALE * (
        r.branch[pl.ds(half, FLAT), :] + r.branch_in[...]
    )
    r.middle[...] = middle
    xn = rms_scale(middle, r.norm_two[...]).astype(LOW)
    r.x_all[0, 0] = xn
    x_spread.start(part(r.x_all, 0, 0))
    logits = mul(r.w_router[...], xn, (((0,), (1,)), ((), ())))
    chosen = jnp.where(r.member[...] > 0, logits, MASKED_SCORE)
    weights = jnp.exp(chosen - jnp.max(chosen, axis=0, keepdims=True))
    probs = weights / jnp.sum(weights, axis=0, keepdims=True)
    r.probs[...] = probs
    r.gate_tables[0, 0] = probs.astype(LOW).astype(FULL)
    p_spread.start(part(r.gate_tables, 0, 0))

    def dispatch_out(i):
        t_spread.wait(i)
        g_spread.wait(i)
        picks = selection(r.tables, i, places).astype(LOW)
        r.pick[i] = picks
        rows = mul(picks, r.g_all[i].reshape(2 * FLAT, -1)).astype(LOW)
        r.g_slots[i] = rows[: 2 * PAIR].reshape(2, PAIR, -1)
        r.g_send[i] = rows[2 * PAIR :].reshape(2, PAIR, -1)
        links.go(("g", "f", i), part(r.g_send, i), part(r.g_slots, 4 + i), places.far)

    lane = lax.broadcasted_iota(jnp.int32, (2 * PAIR, FLAT), 1)
    r.gates[...] = jnp.zeros((2 * PAIR, FLAT), FULL)
    r.gate_send[...] = jnp.zeros((2 * PAIR, FLAT), FULL)

    def dispatch_in(i):
        x_spread.wait(i)
        picks = r.pick[i]
        rows = mul(picks, r.x_all[i].reshape(2 * FLAT, -1)).astype(LOW)
        r.x_slots[i] = rows[: 2 * PAIR].reshape(2, PAIR, -1)
        r.x_send[i] = rows[2 * PAIR :].reshape(2, PAIR, -1)
        links.go(("x", "f", i), part(r.x_send, i), part(r.x_slots, 4 + i), places.far)
        p_spread.wait(i)
        spread_gates = jnp.concatenate(
            [
                jnp.broadcast_to(row, (PAIR, 2 * FLAT))
                for row in table_rows(r.gate_tables, i, places)
            ],
            axis=0,
        )
        slot_gates = jnp.sum(picks.astype(FULL) * spread_gates, axis=1, keepdims=True)
        r.gates[...] += jnp.where(lane == i, slot_gates[: 2 * PAIR], 0.0)
        r.gate_send[...] += jnp.where(lane == 4 + i, slot_gates[2 * PAIR :], 0.0)

    def pass_out(i):
        t_spread.pass_on(i)
        g_spread.pass_on(i)

    def pass_in(i):
        x_spread.pass_on(i)
        p_spread.pass_on(i)

    dispatch_out(0)
    pass_out(1)
    dispatch_in(0)
    dispatch_out(1)
    pass_in(1)
    pass_out(2)
    pass_out(3)
    dispatch_in(1)
    dispatch_out(2)
    pass_in(2)
    dispatch_out(3)
    pass_in(3)
    dispatch_in(2)
    dispatch_in(3)
    links.go(("p", "f"), whole(r.gate_send), whole(r.gate_far), places.far)

    slot_lane = lax.broadcasted_iota(jnp.int32, (PAIR, FLAT), 1)
    r.parts[...] = jnp.zeros((2 * PAIR, FLAT), FULL)

    def run_experts(first, count):
        span = count * PAIR
        which = slice(first, first + count)
        place = slice(first * PAIR, (first + count) * PAIR)

        def one_expert(j, carry):
            base = pl.multiple_of(j * PAIR, PAIR)
            gates = r.gates[pl.ds(base, PAIR), :]
            gate_col = jnp.concatenate(
                [gates[:, p : p + 1] for p in range(first, first + count)], axis=0
            )
            columns = pl.ds(pl.multiple_of(j * FF, FF), FF)
            xs = r.x_slots[which, j].reshape(span, -1)
            gate_pre = mul(xs, r.gate_w[:, columns])
            up_pre = mul(xs, r.up_w[:, columns])
            sig = jax.nn.sigmoid(gate_pre)
            act = gate_pre * sig
            hidden = (act * up_pre).astype(LOW)
            r.hidden_all[j, place] = hidden
            result = mul(hidden, r.down_w[columns, :])
            gs = r.g_slots[which, j].reshape(span, -1).astype(FULL)
            r.g_slots[which, j] = (gate_col * result).astype(LOW).reshape(count, PAIR, -1)
            part = jnp.sum(gs * result, axis=1, keepdims=True).astype(LOW).astype(FULL)
            terms = jnp.zeros((PAIR, FLAT), FULL)
            for p in range(count):
                terms += jnp.where(
                    slot_lane == first + p, part[p * PAIR : (p + 1) * PAIR], 0.0
                )
            r.parts[pl.ds(base, PAIR), :] += terms
            result_grad = (gate_col * gs).astype(LOW)
            r.result_all[j, place] = result_grad
            hidden_grad = mul(result_grad, r.down_w[columns, :], LAST)
            gate_pre_grad = (
                hidden_grad * up_pre * sig * (1.0 + gate_pre * (1.0 - sig))
            ).astype(LOW)
            up_pre_grad = (hidden_grad * act).astype(LOW)
            r.gate_all[j, place] = gate_pre_grad
            r.up_all[j, place] = up_pre_grad
            rows_grad = mul(gate_pre_grad, r.gate_w[:, columns], LAST) + mul(
                up_pre_grad, r.up_w[:, columns], LAST
            )
            r.row_slots[which, j] = rows_grad.astype(LOW).reshape(count, PAIR, -1)
            return carry

        lax.fori_loop(0, 2, one_expert, 0)

    for load in loads:
        load.wait()
    run_experts(0, 4)
    links.got(("p", "f"), whole(r.gate_far))
    r.gates[...] += r.gate_far[...]
    for i in (2, 3):
        links.got(("g", "f", i), part(r.g_slots, 4 + i))
        links.got(("x", "f", i), part(r.x_slots, 4 + i))
    run_experts(6, 2)
    for i in (3, 2):
        links.go(("r", "f", i), part(r.row_slots, 4 + i), part(r.rows_in, i), places.far)
    for i in (0, 1):
        links.got(("g", "f", i), part(r.g_slots, 4 + i))
        links.got(("x", "f", i), part(r.x_slots, 4 + i))
    run_experts(4, 2)
    for i in (1, 0):
        links.go(("r", "f", i), part(r.row_slots, 4 + i), part(r.rows_in, i), places.far)
    links.go(("q", "f"), whole(r.parts), whole(r.parts_in), places.far)
    for i in (3, 2, 1, 0):
        links.go(("w", "f", i), part(r.g_slots, 4 + i), part(r.weighted_in, i), places.far)

    writes = []
    every = slice(None)

    def weight_grads(j):
        xs = r.x_slots[:, j].reshape(8 * PAIR, -1)
        r.grads[0, j] = mul(xs, r.gate_all[j], FIRST).astype(LOW)
        r.grads[1, j] = mul(xs, r.up_all[j], FIRST).astype(LOW)
        r.grads_down[j] = mul(r.hidden_all[j], r.result_all[j], FIRST).astype(LOW)
        columns = slice(j * FF, (j + 1) * FF)
        for n, (source, own, other) in enumerate(
            (
                (part(r.grads, 0, j), part(r.gate_own, every, columns), part(r.gate_other, every, columns)),
                (part(r.grads, 1, j), part(r.up_own, every, columns), part(r.up_other, every, columns)),
                (part(r.grads_down, j), part(r.down_own, columns), part(r.down_other, columns)),
            )
        ):
            copy = pltpu.make_async_copy(source(), own(), r.sems_local.at[3 + 3 * j + n])
            copy.start()
            writes.append(copy)
            links.go(("e", j, n), source, other, places.pair)

    weight_grads(0)

    index = lax.broadcasted_iota(jnp.int32, (experts, 2 * FLAT), 0)

    def fold(name, rows, rows_in, kept, near_send, near_in, i):
        links.got((name, "f", i), part(rows_in, i))
        stacked = jnp.concatenate(
            [rows[i].reshape(2 * PAIR, -1), rows_in[i].reshape(2 * PAIR, -1)], axis=0
        )
        sums = mul(r.pick[i], stacked, FIRST)
        kept[i] = sums[:FLAT]
        near_send[i] = sums[FLAT:].astype(LOW)
        links.go((name, "n", i), part(near_send, i), part(near_in, i), places.near)

    def fold_parts(i):
        column = jnp.concatenate(
            [r.parts[:, i : i + 1], r.parts_in[:, 4 + i : 5 + i]], axis=0
        )
        terms = r.pick[i].astype(FULL) * column
        table = jnp.zeros((experts, 2 * FLAT), FULL)
        chips = (places.e, places.e, places.far_e, places.far_e)
        for n, chip in enumerate(chips):
            total = jnp.sum(terms[n * PAIR : (n + 1) * PAIR], axis=0, keepdims=True)
            table += jnp.where(index == 2 * chip + n % 2, total, 0.0)
        r.part_kept[i] = table[:, :FLAT]
        r.part_send[i] = table[:, FLAT:]
        links.go(("q", "n", i), part(r.part_send, i), part(r.part_near, i), places.near)

    row_sums = Gather(links, "rz", r.row_z_send, r.row_z_in)
    part_sums = Gather(links, "qz", r.part_z_send, r.part_z_in)
    weighted_sums = Gather(links, "wz", r.weighted_z_send, r.weighted_z_in)

    def near_sum(name, kept, near_in, i):
        links.got((name, "n", i), part(near_in, i))
        return lambda: kept[i] + near_in[i].astype(FULL)

    def settle(i):
        row_sums.push(i, near_sum("r", r.row_kept, r.row_near, i))
        part_sums.push(i, near_sum("q", r.part_kept, r.part_near, i))

    fold("r", r.row_slots, r.rows_in, r.row_kept, r.row_near_send, r.row_near, 3)
    fold("r", r.row_slots, r.rows_in, r.row_kept, r.row_near_send, r.row_near, 2)
    links.got(("q", "f"), whole(r.parts_in))
    fold_parts(3)
    fold_parts(2)
    settle(3)
    fold("r", r.row_slots, r.rows_in, r.row_kept, r.row_near_send, r.row_near, 1)
    fold_parts(1)
    settle(2)
    fold("r", r.row_slots, r.rows_in, r.row_kept, r.row_near_send, r.row_near, 0)
    fold_parts(0)
    settle(1)
    weight_grads(1)
    row_sums.total(near_sum("r", r.row_kept, r.row_near, 0)(), r.row_total)
    part_sums.total(near_sum("q", r.part_kept, r.part_near, 0)(), r.part_total)

    gate_probs, gate_grad = r.probs[...], r.part_total[...]
    chosen_grad = gate_probs * (
        gate_grad - jnp.sum(gate_probs * gate_grad, axis=0, keepdims=True)
    )
    logit_grad = chosen_grad.astype(LOW)
    xn_grad = r.row_total[...] + mul(logit_grad, r.w_router[...], (((0,), (1,)), ((), ())))
    mid = r.middle[...]
    scale = lax.rsqrt(jnp.mean(mid * mid, axis=-1, keepdims=True) + NORM_EPS)
    scaled = r.norm_two[...] * xn_grad
    pull = jnp.mean(scaled * mid, axis=-1, keepdims=True)
    grad = r.cotangent[...].astype(FULL) + scale * scaled - mid * (scale * scale * scale * pull)
    r.middle_grad[...] = grad
    mine = part(r.branch_grad, pl.ds(half, FLAT))
    r.branch_grad[pl.ds(half, FLAT), :] = (RESIDUAL_SCALE * grad).astype(LOW)
    links.go("bg", mine, mine, places.pair)
    r.small[pl.ds(0, experts), :] = mul(logit_grad, r.x_all[0, 0])
    r.small[pl.ds(experts, 8), :] = jnp.broadcast_to(
        jnp.sum(xn_grad * mid * scale, axis=0, keepdims=True), (8, width)
    )

    def settle_weighted(i):
        weighted_sums.push(i, near_sum("w", r.weighted_kept, r.weighted_near, i))

    def fold_weighted(i):
        fold(
            "w",
            r.g_slots,
            r.weighted_in,
            r.weighted_kept,
            r.weighted_near_send,
            r.weighted_near,
            i,
        )

    fold_weighted(3)
    fold_weighted(2)
    settle_weighted(3)
    fold_weighted(1)
    settle_weighted(2)
    fold_weighted(0)
    settle_weighted(1)
    weighted_sums.total(
        near_sum("w", r.weighted_kept, r.weighted_near, 0)(), r.weighted_total
    )
    r.layer_out[...] = (mid + RESIDUAL_SCALE * r.weighted_total[...]).astype(LOW)
    links.got("bg", part(r.branch_grad, pl.ds(other_half, FLAT)))
    for j in range(2):
        columns = slice(j * FF, (j + 1) * FF)
        links.got(("e", j, 0), part(r.gate_other, every, columns))
        links.got(("e", j, 1), part(r.up_other, every, columns))
        links.got(("e", j, 2), part(r.down_other, columns))
    for copy in writes:
        copy.wait()
    links.drain()


def run_layer(**inputs):
    width = inputs["tokens"].shape[1]
    experts = inputs["w_router"].shape[1]
    vmem = pl.BlockSpec(memory_space=pltpu.VMEM)
    anywhere = pl.BlockSpec(memory_space=pl.ANY)
    block = (FLAT, width)
    gate = (experts, FLAT)
    slots = (2, PAIR, width)
    outputs = {
        "middle_grad": (block, FULL),
        "branch_grad": ((2 * FLAT, width), LOW),
        "small": ((experts + 8, width), FULL),
        "layer_out": (block, LOW),
    }
    held = {
        name + end: (inputs["w_" + name].shape, LOW)
        for end in ("_own", "_other")
        for name in ("gate", "up", "down")
    }
    scratch = {
        "branch_in": (block, FULL),
        "middle": (block, FULL),
        "probs": (gate, FULL),
        "tables": ((4, 2) + gate, FULL),
        "gate_tables": ((4, 2) + gate, FULL),
        "g_all": ((4, 2) + block, LOW),
        "x_all": ((4, 2) + block, LOW),
        "g_slots": ((8,) + slots, LOW),
        "x_slots": ((8,) + slots, LOW),
        "row_slots": ((8,) + slots, LOW),
        "g_send": ((4,) + slots, LOW),
        "x_send": ((4,) + slots, LOW),
        "gates": ((2 * PAIR, FLAT), FULL),
        "gate_send": ((2 * PAIR, FLAT), FULL),
        "gate_far": ((2 * PAIR, FLAT), FULL),
        "parts": ((2 * PAIR, FLAT), FULL),
        "parts_in": ((2 * PAIR, FLAT), FULL),
        "pick": ((4, 4 * PAIR, 2 * FLAT), LOW),
        "gate_w": (inputs["w_gate"].shape, LOW),
        "up_w": (inputs["w_up"].shape, LOW),
        "down_w": (inputs["w_down"].shape, LOW),
        "hidden_all": ((2, 8 * PAIR, FF), LOW),
        "gate_all": ((2, 8 * PAIR, FF), LOW),
        "up_all": ((2, 8 * PAIR, FF), LOW),
        "result_all": ((2, 8 * PAIR, width), LOW),
        "grads": ((2, 2, width, FF), LOW),
        "grads_down": ((2, FF, width), LOW),
        "rows_in": ((4,) + slots, LOW),
        "weighted_in": ((4,) + slots, LOW),
        "row_kept": ((4,) + block, FULL),
        "row_near": ((4,) + block, LOW),
        "row_near_send": ((4,) + block, LOW),
        "row_z_send": ((4,) + block, LOW),
        "row_z_in": ((5,) + block, LOW),
        "row_total": (block, FULL),
        "part_kept": ((4,) + gate, FULL),
        "part_near": ((4,) + gate, FULL),
        "part_send": ((4,) + gate, FULL),
        "part_z_send": ((4,) + gate, FULL),
        "part_z_in": ((5,) + gate, FULL),
        "part_total": (gate, FULL),
        "weighted_kept": ((4,) + block, FULL),
        "weighted_near": ((4,) + block, LOW),
        "weighted_near_send": ((4,) + block, LOW),
        "weighted_z_send": ((4,) + block, LOW),
        "weighted_z_in": ((5,) + block, LOW),
        "weighted_total": (block, FULL),
    }
    streamed = ("w_gate", "w_up", "w_down")
    names = [*inputs, *outputs, *held, *scratch, "sems_local", "sems_send", "sems_recv"]
    results = pl.pallas_call(
        functools.partial(layer_kernel, names),
        out_shape=[
            jax.ShapeDtypeStruct(shape, kind) for shape, kind in [*outputs.values(), *held.values()]
        ],
        in_specs=[anywhere if name in streamed else vmem for name in inputs],
        out_specs=[vmem] * len(outputs) + [anywhere] * len(held),
        scratch_shapes=[pltpu.VMEM(shape, kind) for shape, kind in scratch.values()]
        + [
            pltpu.SemaphoreType.DMA((9,)),
            pltpu.SemaphoreType.DMA((160,)),
            pltpu.SemaphoreType.DMA((120,)),
        ],
        compiler_params=pltpu.CompilerParams(
            collective_id=0, has_side_effects=True, vmem_limit_bytes=60 << 20
        ),
        name="layer",
    )(*inputs.values())
    return dict(zip([*outputs, *held], results))


def finish_kernel(names, *refs):
    r = types.SimpleNamespace(**dict(zip(names, refs, strict=True)))
    places = Places()
    h, e, z = places.h, places.e, places.z
    places.greet()
    links = Links(places, r.sems_send, r.sems_recv)
    ranks = [z, z + 1 - 2 * (z % 2), 2 - z // 2, 3 - 3 * (z // 2)]
    plane = [[e % 4, places.near_e % 4], [places.far_e % 4, 3 - e % 4]]

    def shard(b, a, i):
        return ranks[i] * 4 + plane[b][a]

    def along(name, spot):
        block = spot(0)
        links.go((name, "z", 1), block, block, places.edge)

        @pl.when(places.is_inner)
        def _():
            links.go((name, "z", 2), block, block, places.inner, "inner")

    def pass_along(name, spot, i):
        block = spot(i)
        links.got((name, "z", i), block)
        there = {1: 3, 2: 2, 3: 3}[i]
        device = places.inner if i == 1 else places.edge

        @pl.when(places.is_inner)
        def _():
            links.go((name, "z", there), block, block, device, "inner")

    half = pl.multiple_of(h * FLAT, FLAT)
    other_half = pl.multiple_of((1 - h) * FLAT, FLAT)
    links.go("terms", part(r.terms, pl.ds(other_half, FLAT)), whole(r.terms_in), places.pair)
    order = [(a, i) for i in (3, 2, 1, 0) for a in (1, 0)]

    def send_far(n):
        if n < len(order):
            a, i = order[n]
            links.go(("f", a, i), part(r.grads, shard(1, a, i)), part(r.far_in, a, i), places.far)

    for n in range(3):
        send_far(n)

    links.got("terms", whole(r.terms_in))
    xn_grad = (
        (r.terms[pl.ds(half, FLAT), :].astype(FULL) + r.terms_in[...].astype(FULL))
        .astype(LOW)
        .astype(FULL)
    )
    x_half = r.tokens[pl.ds(half, FLAT), :].astype(FULL)
    scale = lax.rsqrt(jnp.mean(x_half * x_half, axis=-1, keepdims=True) + NORM_EPS)
    scaled = r.norm_one[...] * xn_grad
    pull = jnp.mean(scaled * x_half, axis=-1, keepdims=True)
    r.grad_tokens[...] = (
        r.middle_grad[...] + scale * scaled - x_half * (scale * scale * scale * pull)
    )
    experts = r.small.shape[0] - 8
    r.small_mine[0, pl.ds(0, experts), :] = r.small[pl.ds(0, experts), :]
    row = lax.broadcasted_iota(jnp.int32, (8, x_half.shape[1]), 0)
    r.small_mine[0, pl.ds(experts, 8), :] = jnp.where(
        row == 0,
        r.small[pl.ds(experts, 8), :],
        jnp.sum(xn_grad * x_half * scale, axis=0, keepdims=True),
    )
    links.go(("s", 0), part(r.small_mine, 0), part(r.small_in, 0), places.pair)

    sums = Gather(links, "z", r.z_send, r.z_in)

    def settle(i):
        links.got(("n", i), part(r.near_in, i))
        return lambda: r.kept[i] + r.near_in[i].astype(FULL)

    for n, (a, i) in enumerate(order):
        links.got(("f", a, i), part(r.far_in, a, i))
        send_far(n + 3)
        total = r.grads[shard(0, a, i)].astype(FULL) + r.far_in[a, i].astype(FULL)
        if a:
            r.near_send[i] = total.astype(LOW)
            links.go(("n", i), part(r.near_send, i), part(r.near_in, i), places.near)
        else:
            r.kept[i] = total
            if i < 3:
                sums.push(i + 1, settle(i + 1))
        if n == 0:
            links.got(("s", 0), part(r.small_in, 0))
            r.small_mine[1] = r.small_mine[0] + r.small_in[0]
            links.go(("s", 1), part(r.small_mine, 1), part(r.small_in, 1), places.far)
        if n == 3:
            links.got(("s", 1), part(r.small_in, 1))
            r.small_mine[2] = r.small_mine[1] + r.small_in[1]
            links.go(("s", 2), part(r.small_mine, 2), part(r.small_in, 2), places.near)
        if n == 6:
            links.got(("s", 2), part(r.small_in, 2))
            r.small_all[z] = r.small_mine[2] + r.small_in[2]
            along("s", lambda i: part(r.small_all, ranks[i]))
    sums.total(settle(0)(), r.total)
    r.grads_out[e] = r.total[...].astype(LOW)

    def spot(b, a, i):
        return part(r.grads_out, shard(b, a, i))

    mine = spot(0, 0, 0)
    along("o", lambda i: spot(0, 0, i))
    links.go(("on", 0), mine, mine, places.near)
    links.go(("of", 0, 0), mine, mine, places.far)

    def pass_far(i):
        block = spot(0, 1, i)
        links.got(("on", i), block)
        links.go(("of", 1, i), block, block, places.far)

    pass_far(0)
    for i in (1, 2, 3):
        block = spot(0, 0, i)
        pass_along("o", lambda i: spot(0, 0, i), i)
        links.go(("on", i), block, block, places.near)
        links.go(("of", 0, i), block, block, places.far)
        pass_far(i)
    for i in (1, 2, 3):
        pass_along("s", lambda i: part(r.small_all, ranks[i]), i)
    r.small_out[...] = (
        (r.small_all[0] + r.small_all[1]) + r.small_all[2]
    ) + r.small_all[3]
    for i in range(4):
        for a in range(2):
            links.got(("of", a, i), spot(1, a, i))
    links.drain()


def finish(**inputs):
    width = inputs["tokens"].shape[1]
    vmem = pl.BlockSpec(memory_space=pltpu.VMEM)
    block = (FLAT, width)
    shard = inputs["grads"].shape[1:]
    small = inputs["small"].shape
    outputs = {
        "grad_tokens": (block, FULL),
        "small_out": (small, FULL),
        "grads_out": (inputs["grads"].shape, LOW),
    }
    scratch = {
        "terms_in": (block, LOW),
        "far_in": ((2, 4) + shard, LOW),
        "near_send": ((4,) + shard, LOW),
        "near_in": ((4,) + shard, LOW),
        "kept": ((4,) + shard, FULL),
        "z_send": ((4,) + shard, LOW),
        "z_in": ((5,) + shard, LOW),
        "total": (shard, FULL),
        "small_mine": ((3,) + small, FULL),
        "small_in": ((3,) + small, FULL),
        "small_all": ((4,) + small, FULL),
    }
    names = [*inputs, *outputs, *scratch, "sems_send", "sems_recv"]
    return pl.pallas_call(
        functools.partial(finish_kernel, names),
        out_shape=[jax.ShapeDtypeStruct(shape, kind) for shape, kind in outputs.values()],
        in_specs=[vmem] * len(inputs),
        out_specs=[vmem] * len(outputs),
        scratch_shapes=[pltpu.VMEM(shape, kind) for shape, kind in scratch.values()]
        + [pltpu.SemaphoreType.DMA((60,)), pltpu.SemaphoreType.DMA((60,))],
        compiler_params=pltpu.CompilerParams(
            collective_id=1, has_side_effects=True, vmem_limit_bytes=50 << 20
        ),
        name="finish",
    )(*inputs.values())


def quick_shards(
    tokens,
    norm_one,
    w_query,
    key_weight,
    value_weight,
    w_output,
    norm_two,
    w_router,
    w_gate,
    w_up,
    w_down,
    routes,
    priority,
    cotangent,
):
    tok_rows, model_width = tokens.shape
    head_rank = lax.axis_index("head")
    prompt_rows = tok_rows // 2
    cont_rows = tok_rows // 4
    kv_heads = key_weight.shape[1] // HEAD_DIMENSION
    query_groups = w_query.shape[1] // key_weight.shape[1]
    experts = w_router.shape[1]
    local_index = jnp.arange(tok_rows, dtype=jnp.int32)
    position = jnp.where(
        local_index < prompt_rows,
        local_index,
        prompt_rows + (local_index - prompt_rows) % cont_rows,
    )
    frequency = ROPE_BASE ** (
        -(2.0 * jnp.arange(HEAD_DIMENSION // 2, dtype=jnp.float32)) / HEAD_DIMENSION
    )
    angle_table = position.astype(jnp.float32)[:, None] * frequency[None, :]
    cosine_values = jnp.cos(angle_table)[:, None, :]
    sine_values = jnp.sin(angle_table)[:, None, :]
    x_full = tokens.astype(jnp.float32)
    normed = rms_scale(x_full, norm_one).astype(jnp.bfloat16)
    queries = apply_rotary(
        jnp.dot(normed, w_query, preferred_element_type=jnp.float32).reshape(
            tok_rows, -1, HEAD_DIMENSION
        ),
        cosine_values,
        sine_values,
    ).astype(jnp.bfloat16)
    keys_all = apply_rotary(
        jnp.dot(normed, key_weight, preferred_element_type=jnp.float32).reshape(
            tok_rows, -1, HEAD_DIMENSION
        ),
        cosine_values,
        sine_values,
    ).astype(jnp.bfloat16)
    values_all = (
        jnp.dot(normed, value_weight, preferred_element_type=jnp.float32)
        .astype(jnp.bfloat16)
        .reshape(tok_rows, kv_heads, HEAD_DIMENSION)
    )
    query_col = local_index[:, None]
    key_row = local_index[None, :]
    visible = (key_row < prompt_rows) & ((query_col >= prompt_rows) | (key_row <= query_col))
    visible |= (
        (key_row >= prompt_rows)
        & (query_col >= prompt_rows)
        & (key_row <= query_col)
        & ((key_row - prompt_rows) // cont_rows == (query_col - prompt_rows) // cont_rows)
    )
    query_block = queries.reshape(tok_rows, kv_heads, query_groups, HEAD_DIMENSION)
    raw_scores = (
        jnp.einsum("qhgd,khd->hgqk", query_block, keys_all, preferred_element_type=jnp.float32)
        * ATTENTION_SCALE
    )
    scores = jnp.where(visible[None, None], raw_scores, MASKED_SCORE)
    row_max = jnp.max(scores, axis=-1, keepdims=True)
    weights = jnp.exp(scores - row_max)
    probs = weights / jnp.sum(weights, axis=-1, keepdims=True)
    probs_low = probs.astype(jnp.bfloat16)
    mixed = jnp.einsum("hgqk,khd->qhgd", probs_low, values_all, preferred_element_type=jnp.float32)
    head_outputs = mixed.astype(jnp.bfloat16).reshape(tok_rows, -1)
    branch = jnp.dot(head_outputs, w_output, preferred_element_type=jnp.float32)

    my_routes = lax.dynamic_slice_in_dim(routes, head_rank * FLAT, FLAT, 0)
    names = jnp.arange(experts, dtype=jnp.int32)
    member = jnp.any(my_routes[None, :, :] == names[:, None, None], axis=-1)
    order_rank = priority[0]
    earlier = (order_rank[:, None] < order_rank[None, :]).astype(jnp.bfloat16)
    before = jnp.dot(member.astype(jnp.bfloat16), earlier, preferred_element_type=jnp.float32)
    table = jnp.where(member & (before < SLOTS), before, UNKEPT)
    out_rows = (RESIDUAL_SCALE * cotangent.astype(jnp.float32)).astype(jnp.bfloat16)

    done = run_layer(
        branch=branch,
        tokens=tokens,
        norm_two=norm_two[None, :],
        w_router=w_router,
        table=table,
        member=member.astype(jnp.float32),
        out_rows=out_rows,
        cotangent=cotangent,
        w_gate=w_gate,
        w_up=w_up,
        w_down=w_down,
    )
    branch_grad = done["branch_grad"]
    heads_grad = jnp.einsum(
        "td,hd->th", branch_grad, w_output, preferred_element_type=jnp.float32
    ).astype(jnp.bfloat16)
    grad_output_w = jnp.einsum(
        "th,td->hd", head_outputs, branch_grad, preferred_element_type=jnp.float32
    ).astype(jnp.bfloat16)
    heads_block = heads_grad.reshape(tok_rows, kv_heads, query_groups, HEAD_DIMENSION)
    prob_grad = jnp.einsum(
        "qhgd,khd->hgqk", heads_block, values_all, preferred_element_type=jnp.float32
    )
    row_inner = jnp.sum(probs * prob_grad, axis=-1, keepdims=True)
    score_grad = (probs * (prob_grad - row_inner)).astype(jnp.bfloat16)
    query_grad = (
        jnp.einsum("hgqk,khd->qhgd", score_grad, keys_all, preferred_element_type=jnp.float32)
        * ATTENTION_SCALE
    )
    key_grad = (
        jnp.einsum("hgqk,qhgd->khd", score_grad, query_block, preferred_element_type=jnp.float32)
        * ATTENTION_SCALE
    )
    value_grad = jnp.einsum(
        "hgqk,qhgd->khd", probs_low, heads_block, preferred_element_type=jnp.float32
    )
    query_pre_grad = (
        rotate_back(query_grad.reshape(tok_rows, -1, HEAD_DIMENSION), cosine_values, sine_values)
        .reshape(tok_rows, -1)
        .astype(jnp.bfloat16)
    )
    key_pre_grad = (
        rotate_back(key_grad, cosine_values, sine_values).reshape(tok_rows, -1).astype(jnp.bfloat16)
    )
    value_low_grad = value_grad.reshape(tok_rows, -1).astype(jnp.bfloat16)
    head_grads = jnp.concatenate([query_pre_grad, key_pre_grad, value_low_grad], axis=1)
    grad_in = jnp.einsum(
        "td,th->dh", normed, head_grads, preferred_element_type=jnp.float32
    ).astype(jnp.bfloat16)
    xn_one_terms = (
        jnp.einsum("th,dh->td", query_pre_grad, w_query, preferred_element_type=jnp.float32)
        + jnp.einsum("th,dh->td", key_pre_grad, key_weight, preferred_element_type=jnp.float32)
        + jnp.einsum("th,dh->td", value_low_grad, value_weight, preferred_element_type=jnp.float32)
    ).astype(jnp.bfloat16)
    grads = jnp.concatenate([grad_in, grad_output_w], axis=0)
    flat_shape = grads.shape
    grads = grads.reshape(16, -1, model_width)
    grad_tokens, small, grads = finish(
        terms=xn_one_terms,
        tokens=tokens,
        norm_one=norm_one[None, :],
        middle_grad=done["middle_grad"],
        small=done["small"],
        grads=grads,
    )
    grads = grads.reshape(flat_shape).astype(jnp.float32)
    q_cols, k_cols = w_query.shape[1], key_weight.shape[1]

    def both(mine, other):
        return mine.astype(jnp.float32) + other.astype(jnp.float32)

    return (
        done["layer_out"],
        grad_tokens,
        small[experts + 1],
        grads[:model_width, :q_cols],
        grads[:model_width, q_cols : q_cols + k_cols],
        grads[:model_width, q_cols + k_cols :],
        grads[model_width:],
        small[experts],
        small[:experts].T,
        both(done["gate_own"], done["gate_other"]),
        both(done["up_own"], done["up_other"]),
        both(done["down_own"], done["down_other"]),
    )


def solution(mesh):
    body = quick_shards if dict(mesh.shape) == {"exp": 16, "head": 2} else shards
    return jax.shard_map(
        body,
        mesh=mesh,
        in_specs=(
            P("exp", None),
            P(),
            P(None, "head"),
            P(None, "head"),
            P(None, "head"),
            P("head", None),
            P(),
            P(),
            P(None, "exp"),
            P(None, "exp"),
            P("exp", None),
            P("exp", None),
            P(("exp", "head"), None),
            P(("exp", "head"), None),
        ),
        out_specs=(
            P(("exp", "head"), None),
            P(("exp", "head"), None),
            P(),
            P(None, "head"),
            P(None, "head"),
            P(None, "head"),
            P("head", None),
            P(),
            P(),
            P(None, "exp"),
            P(None, "exp"),
            P("exp", None),
        ),
        check_vma=False,
    )
```

```python
import functools
import types

import jax
import jax.numpy as jnp
from jax import lax
from jax.experimental import pallas as pl
from jax.experimental.pallas import tpu as pltpu
from jax.sharding import PartitionSpec as P

HEAD_DIMENSION = 64
FF = 512
TOPK = 8


RESIDUAL_SCALE = 0.22
ATTENTION_SCALE = 0.015625
ROPE_BASE = 10000.0
NORM_EPS = 1e-06
MASKED_SCORE = -1e30


def rms_scale(values, scale_row):
    return (
        values * lax.rsqrt(jnp.mean(values * values, axis=-1, keepdims=True) + NORM_EPS) * scale_row
    )


def apply_rotary(values, cosine_values, sine_values):
    half_width = values.shape[-1] // 2
    lower_part = values[..., :half_width]
    upper_part = values[..., half_width:]
    return jnp.concatenate(
        [
            lower_part * cosine_values - upper_part * sine_values,
            upper_part * cosine_values + lower_part * sine_values,
        ],
        axis=-1,
    )


def rotate_back(values, cosine_values, sine_values):
    half_width = values.shape[-1] // 2
    lower_part = values[..., :half_width]
    upper_part = values[..., half_width:]
    return jnp.concatenate(
        [
            lower_part * cosine_values + upper_part * sine_values,
            upper_part * cosine_values - lower_part * sine_values,
        ],
        axis=-1,
    )


def shards(
    tokens,
    norm_one,
    w_query,
    key_weight,
    value_weight,
    w_output,
    norm_two,
    w_router,
    w_gate,
    w_up,
    w_down,
    routes,
    priority,
    cotangent,
):
    tok_rows, model_width = tokens.shape
    heads_count = lax.axis_size("head")
    head_rank = lax.axis_index("head")
    exp_count = lax.axis_size("exp")
    half_rows = tok_rows // heads_count
    prompt_rows = tok_rows // 2
    cont_rows = tok_rows // 4
    kv_heads = key_weight.shape[1] // HEAD_DIMENSION
    query_groups = w_query.shape[1] // key_weight.shape[1]
    experts = w_router.shape[1]
    held_cols = w_gate.shape[1]
    held = max(1, held_cols // FF)
    split = max(1, FF // held_cols)
    block_width = held_cols // held
    capacity = max(2, (5 * half_rows * TOPK + 4 * experts - 1) // (4 * experts))
    rows_per_block = min(512, tok_rows)
    count_of_blocks = tok_rows // rows_per_block
    local_index = jnp.arange(tok_rows, dtype=jnp.int32)
    position = jnp.where(
        local_index < prompt_rows,
        local_index,
        prompt_rows + (local_index - prompt_rows) % cont_rows,
    )
    frequency = ROPE_BASE ** (
        -(2.0 * jnp.arange(HEAD_DIMENSION // 2, dtype=jnp.float32)) / HEAD_DIMENSION
    )
    angle_table = position.astype(jnp.float32)[:, None] * frequency[None, :]
    cosine_values = jnp.cos(angle_table)[:, None, :]
    sine_values = jnp.sin(angle_table)[:, None, :]
    x_full = tokens.astype(jnp.float32)
    normed_input_first = rms_scale(x_full, norm_one).astype(jnp.bfloat16)
    rotated_queries = apply_rotary(
        jnp.dot(normed_input_first, w_query, preferred_element_type=jnp.float32).reshape(
            tok_rows, -1, HEAD_DIMENSION
        ),
        cosine_values,
        sine_values,
    ).astype(jnp.bfloat16)
    keys_all = apply_rotary(
        jnp.dot(normed_input_first, key_weight, preferred_element_type=jnp.float32).reshape(
            tok_rows, -1, HEAD_DIMENSION
        ),
        cosine_values,
        sine_values,
    ).astype(jnp.bfloat16)
    values_all = (
        jnp.dot(normed_input_first, value_weight, preferred_element_type=jnp.float32)
        .astype(jnp.bfloat16)
        .reshape(tok_rows, kv_heads, HEAD_DIMENSION)
    )

    def visible_pairs(block_start):
        query_col = (block_start + jnp.arange(rows_per_block, dtype=jnp.int32))[:, None]
        key_row = jnp.arange(tok_rows, dtype=jnp.int32)[None, :]
        from_prompt = (key_row < prompt_rows) & (
            (query_col >= prompt_rows) | (key_row <= query_col)
        )
        same_cont = (
            (key_row >= prompt_rows)
            & (query_col >= prompt_rows)
            & (key_row <= query_col)
            & ((key_row - prompt_rows) // cont_rows == (query_col - prompt_rows) // cont_rows)
        )
        return from_prompt | same_cont

    def scores_of(query_block, block_start):
        raw_scores = (
            jnp.einsum("qhgd,khd->hgqk", query_block, keys_all, preferred_element_type=jnp.float32)
            * ATTENTION_SCALE
        )
        return jnp.where(visible_pairs(block_start)[None, None], raw_scores, MASKED_SCORE)

    def forward_block(parts):
        query_block, block_start = parts
        scores = scores_of(query_block, block_start)
        row_max = jnp.max(scores, axis=-1, keepdims=True)
        weights = jnp.exp(scores - row_max)
        row_total = jnp.sum(weights, axis=-1, keepdims=True)
        probs_low = (weights / row_total).astype(jnp.bfloat16)
        mixed = jnp.einsum(
            "hgqk,khd->qhgd", probs_low, values_all, preferred_element_type=jnp.float32
        )
        return (mixed.astype(jnp.bfloat16), row_max + jnp.log(row_total))

    query_blocks = rotated_queries.reshape(
        count_of_blocks, rows_per_block, kv_heads, query_groups, HEAD_DIMENSION
    )
    block_starts = jnp.arange(count_of_blocks, dtype=jnp.int32) * rows_per_block
    heads_blocks, log_total = lax.map(forward_block, (query_blocks, block_starts))
    head_outputs = heads_blocks.reshape(tok_rows, -1)
    head_terms = jnp.dot(head_outputs, w_output, preferred_element_type=jnp.float32)
    branch_half = lax.dynamic_slice_in_dim(
        lax.psum(head_terms, "head"), head_rank * half_rows, half_rows, 0
    )
    x_half = lax.dynamic_slice_in_dim(x_full, head_rank * half_rows, half_rows, 0)
    middle = x_half + RESIDUAL_SCALE * branch_half
    xn_two = rms_scale(middle, norm_two).astype(jnp.bfloat16)
    logits = jnp.dot(xn_two, w_router, preferred_element_type=jnp.float32)
    my_routes = lax.dynamic_slice_in_dim(routes, head_rank * half_rows, half_rows, 0)
    route_hot = my_routes[:, :, None] == jnp.arange(experts, dtype=jnp.int32)[None, None, :]
    chosen = jnp.sum(jnp.where(route_hot, logits[:, None, :], 0.0), axis=-1)
    chosen_max = jnp.max(chosen, axis=-1, keepdims=True)
    chosen_exp = jnp.exp(chosen - chosen_max)
    gate_probs = chosen_exp / jnp.sum(chosen_exp, axis=-1, keepdims=True)
    gate_low = gate_probs.astype(jnp.bfloat16)
    member = jnp.any(route_hot, axis=1).astype(jnp.bfloat16)
    order_rank = priority[0]
    earlier = (order_rank[None, :] < order_rank[:, None]).astype(jnp.bfloat16)
    before = jnp.dot(earlier, member, preferred_element_type=jnp.float32)
    slot_rank = jnp.sum(jnp.where(route_hot, before[:, None, :], 0.0), axis=-1).astype(jnp.int32)
    is_kept = slot_rank < capacity
    spare_slot = experts * capacity
    target = jnp.where(is_kept, my_routes * capacity + slot_rank, spare_slot)
    row_ids = jnp.broadcast_to(jnp.arange(half_rows, dtype=jnp.int32)[:, None], target.shape)
    assign_ids = jnp.arange(half_rows * TOPK, dtype=jnp.int32).reshape(target.shape)
    source_row = (
        jnp.zeros(spare_slot + 1, jnp.int32).at[target.ravel()].set(row_ids.ravel())[:spare_slot]
    )
    source_pick = (
        jnp.zeros(spare_slot + 1, jnp.int32).at[target.ravel()].set(assign_ids.ravel())[:spare_slot]
    )
    filled = jnp.zeros(spare_slot + 1, jnp.int32).at[target.ravel()].set(1)[:spare_slot] > 0
    slot_inputs = jnp.where(filled[:, None], xn_two[source_row], 0).reshape(
        experts, capacity, model_width
    )
    slot_gates = jnp.where(filled, gate_low.ravel()[source_pick], 0).reshape(experts, capacity)

    def to_owners(per_expert):
        shape_in = per_expert.shape
        spread = jnp.broadcast_to(per_expert[:, None], (shape_in[0], split) + shape_in[1:])
        return spread.reshape((exp_count, held) + shape_in[1:])

    def from_owners(per_owner):
        shape_in = per_owner.shape
        return jnp.sum(
            per_owner.reshape((experts, split) + shape_in[2:]).astype(jnp.float32), axis=1
        )

    gate_cols = w_gate.reshape(model_width, held, block_width)
    up_cols = w_up.reshape(model_width, held, block_width)
    down_rows = w_down.reshape(held, block_width, model_width)
    send_rows = to_owners(slot_inputs)
    send_gates = to_owners(slot_gates)
    slot_rows = lax.all_to_all(send_rows, "exp", split_axis=0, concat_axis=0, tiled=True)
    slot_gate = lax.all_to_all(send_gates, "exp", split_axis=0, concat_axis=0, tiled=True)
    gate_pre = jnp.einsum(
        "sjcd,djf->sjcf", slot_rows, gate_cols, preferred_element_type=jnp.float32
    )
    up_pre = jnp.einsum("sjcd,djf->sjcf", slot_rows, up_cols, preferred_element_type=jnp.float32)
    hidden = (gate_pre * jax.nn.sigmoid(gate_pre) * up_pre).astype(jnp.bfloat16)
    result = jnp.einsum("sjcf,jfd->sjcd", hidden, down_rows, preferred_element_type=jnp.float32)
    weighted = (slot_gate[..., None].astype(jnp.float32) * result).astype(jnp.bfloat16)
    returned = lax.all_to_all(weighted, "exp", split_axis=0, concat_axis=0, tiled=True)
    returned, held_rows, held_gates = (returned, slot_rows, slot_gate)
    back_flat = jnp.concatenate(
        [
            from_owners(returned).reshape(spare_slot, model_width),
            jnp.zeros((1, model_width), jnp.float32),
        ],
        axis=0,
    )
    expert_sum = jnp.sum(back_flat[target], axis=1)
    layer_out = (middle + RESIDUAL_SCALE * expert_sum).astype(jnp.bfloat16)
    out_grad = cotangent.astype(jnp.float32)
    weighted_rows = (RESIDUAL_SCALE * out_grad).astype(jnp.bfloat16)
    grad_slots = to_owners(
        jnp.where(filled[:, None], weighted_rows[source_row], 0).reshape(
            experts, capacity, model_width
        )
    )
    back_grads, back_rows, back_gates = (
        lax.all_to_all(grad_slots, "exp", split_axis=0, concat_axis=0, tiled=True),
        lax.all_to_all(send_rows, "exp", split_axis=0, concat_axis=0, tiled=True),
        lax.all_to_all(send_gates, "exp", split_axis=0, concat_axis=0, tiled=True),
    )
    owner_gates = back_gates[..., None].astype(jnp.float32)
    gate_pre = jnp.einsum(
        "sjcd,djf->sjcf", back_rows, gate_cols, preferred_element_type=jnp.float32
    )
    up_pre = jnp.einsum("sjcd,djf->sjcf", back_rows, up_cols, preferred_element_type=jnp.float32)
    gate_sigmoid = jax.nn.sigmoid(gate_pre)
    gate_act = gate_pre * gate_sigmoid
    hidden = (gate_act * up_pre).astype(jnp.bfloat16)
    result = jnp.einsum("sjcf,jfd->sjcd", hidden, down_rows, preferred_element_type=jnp.float32)
    gate_part = jnp.sum(back_grads.astype(jnp.float32) * result, axis=-1)
    result_grad = (owner_gates * back_grads).astype(jnp.bfloat16)
    grad_down_w = jnp.einsum(
        "sjcf,sjcd->jfd", hidden, result_grad, preferred_element_type=jnp.float32
    ).reshape(held_cols, model_width)
    hidden_grad = jnp.einsum(
        "sjcd,jfd->sjcf", result_grad, down_rows, preferred_element_type=jnp.float32
    )
    gate_pre_grad = (
        hidden_grad * up_pre * gate_sigmoid * (1.0 + gate_pre * (1.0 - gate_sigmoid))
    ).astype(jnp.bfloat16)
    up_pre_grad = (hidden_grad * gate_act).astype(jnp.bfloat16)
    grad_gate_w = jnp.einsum(
        "sjcd,sjcf->djf", back_rows, gate_pre_grad, preferred_element_type=jnp.float32
    ).reshape(model_width, held_cols)
    grad_up_w = jnp.einsum(
        "sjcd,sjcf->djf", back_rows, up_pre_grad, preferred_element_type=jnp.float32
    ).reshape(model_width, held_cols)
    rows_grad = (
        jnp.einsum("sjcf,djf->sjcd", gate_pre_grad, gate_cols, preferred_element_type=jnp.float32)
        + jnp.einsum("sjcf,djf->sjcd", up_pre_grad, up_cols, preferred_element_type=jnp.float32)
    ).astype(jnp.bfloat16)
    rows_back, gates_back = (
        lax.all_to_all(rows_grad, "exp", split_axis=0, concat_axis=0, tiled=True),
        lax.all_to_all(
            gate_part.astype(jnp.bfloat16), "exp", split_axis=0, concat_axis=0, tiled=True
        ),
    )
    rows_flat = jnp.concatenate(
        [
            from_owners(rows_back).reshape(spare_slot, model_width),
            jnp.zeros((1, model_width), jnp.float32),
        ],
        axis=0,
    )
    xn_two_grad = jnp.sum(rows_flat[target], axis=1)
    gate_total = from_owners(gates_back).astype(jnp.bfloat16).reshape(spare_slot)
    gates_flat = jnp.concatenate([gate_total, jnp.zeros((1,), jnp.bfloat16)], axis=0)
    gate_grad_tok = gates_flat[target].astype(jnp.float32)
    chosen_grad = gate_probs * (
        gate_grad_tok - jnp.sum(gate_probs * gate_grad_tok, axis=-1, keepdims=True)
    )
    logit_grad = jnp.sum(jnp.where(route_hot, chosen_grad[:, :, None], 0.0), axis=1).astype(
        jnp.bfloat16
    )
    grad_router = jnp.einsum("rd,re->de", xn_two, logit_grad, preferred_element_type=jnp.float32)
    xn_two_grad = xn_two_grad + jnp.einsum(
        "re,de->rd", logit_grad, w_router, preferred_element_type=jnp.float32
    )
    middle_norm_pull = jax.vjp(rms_scale, middle, norm_two)[1]
    middle_norm_grad, grad_norm_two = middle_norm_pull(xn_two_grad)
    middle_grad = out_grad + middle_norm_grad
    branch_rows = (RESIDUAL_SCALE * middle_grad).astype(jnp.bfloat16)
    branch_grad = lax.all_gather(branch_rows, "head", axis=0, tiled=True)
    heads_grad = jnp.einsum(
        "td,hd->th", branch_grad, w_output, preferred_element_type=jnp.float32
    ).astype(jnp.bfloat16)
    grad_output_w = jnp.einsum(
        "th,td->hd", head_outputs, branch_grad, preferred_element_type=jnp.float32
    )

    def backward_block(running, parts):
        key_grad, value_grad = running
        query_block, heads_block, block_total, block_start = parts
        scores = scores_of(query_block, block_start)
        probs = jnp.exp(scores - block_total)
        probs_low = probs.astype(jnp.bfloat16)
        prob_grad = jnp.einsum(
            "qhgd,khd->hgqk", heads_block, values_all, preferred_element_type=jnp.float32
        )
        row_inner = jnp.sum(probs * prob_grad, axis=-1, keepdims=True)
        score_grad = (probs * (prob_grad - row_inner)).astype(jnp.bfloat16)
        query_grad = (
            jnp.einsum("hgqk,khd->qhgd", score_grad, keys_all, preferred_element_type=jnp.float32)
            * ATTENTION_SCALE
        )
        key_grad = (
            key_grad
            + jnp.einsum(
                "hgqk,qhgd->khd", score_grad, query_block, preferred_element_type=jnp.float32
            )
            * ATTENTION_SCALE
        )
        value_grad = value_grad + jnp.einsum(
            "hgqk,qhgd->khd", probs_low, heads_block, preferred_element_type=jnp.float32
        )
        return ((key_grad, value_grad), query_grad)

    heads_grad_blocks = heads_grad.reshape(
        count_of_blocks, rows_per_block, kv_heads, query_groups, HEAD_DIMENSION
    )
    zero_keys = jnp.zeros((tok_rows, kv_heads, HEAD_DIMENSION), jnp.float32)
    (own_key, own_value), query_grad = lax.scan(
        backward_block,
        (zero_keys, zero_keys),
        (query_blocks, heads_grad_blocks, log_total, block_starts),
    )
    query_pre_grad = (
        rotate_back(query_grad.reshape(tok_rows, -1, HEAD_DIMENSION), cosine_values, sine_values)
        .reshape(tok_rows, -1)
        .astype(jnp.bfloat16)
    )
    key_pre_grad = (
        rotate_back(own_key, cosine_values, sine_values).reshape(tok_rows, -1).astype(jnp.bfloat16)
    )
    value_low_grad = own_value.reshape(tok_rows, -1).astype(jnp.bfloat16)
    grad_query_w = jnp.einsum(
        "td,th->dh", normed_input_first, query_pre_grad, preferred_element_type=jnp.float32
    )
    grad_key_w = jnp.einsum(
        "td,th->dh", normed_input_first, key_pre_grad, preferred_element_type=jnp.float32
    )
    grad_value_w = jnp.einsum(
        "td,th->dh", normed_input_first, value_low_grad, preferred_element_type=jnp.float32
    )
    xn_one_terms = (
        jnp.einsum("th,dh->td", query_pre_grad, w_query, preferred_element_type=jnp.float32)
        + jnp.einsum("th,dh->td", key_pre_grad, key_weight, preferred_element_type=jnp.float32)
        + jnp.einsum("th,dh->td", value_low_grad, value_weight, preferred_element_type=jnp.float32)
    )
    xn_one_grad = lax.psum_scatter(
        xn_one_terms.astype(jnp.bfloat16), "head", scatter_dimension=0, tiled=True
    ).astype(jnp.float32)
    input_norm_pull = jax.vjp(rms_scale, x_half, norm_one)[1]
    input_norm_grad, grad_norm_one = input_norm_pull(xn_one_grad)
    grad_tokens = middle_grad + input_norm_grad
    grad_gate_w, grad_up_w, grad_down_w, grad_router, grad_norm_one, grad_norm_two = (
        lax.psum(grad_gate_w.astype(jnp.bfloat16), "head").astype(jnp.float32),
        lax.psum(grad_up_w.astype(jnp.bfloat16), "head").astype(jnp.float32),
        lax.psum(grad_down_w.astype(jnp.bfloat16), "head").astype(jnp.float32),
        lax.psum(grad_router.astype(jnp.bfloat16), "head").astype(jnp.float32),
        lax.psum(grad_norm_one.astype(jnp.bfloat16), "head").astype(jnp.float32),
        lax.psum(grad_norm_two.astype(jnp.bfloat16), "head").astype(jnp.float32),
    )
    (
        grad_query_w,
        grad_key_w,
        grad_value_w,
        grad_output_w,
        grad_router,
        grad_norm_one,
        grad_norm_two,
    ) = lax.psum(
        (
            grad_query_w,
            grad_key_w,
            grad_value_w,
            grad_output_w,
            grad_router,
            grad_norm_one,
            grad_norm_two,
        ),
        "exp",
    )
    return (
        layer_out,
        grad_tokens,
        grad_norm_one,
        grad_query_w,
        grad_key_w,
        grad_value_w,
        grad_output_w,
        grad_norm_two,
        grad_router,
        grad_gate_w,
        grad_up_w,
        grad_down_w,
    )


MESH = pl.DeviceIdType.MESH
FLAT = 128
SLOTS = 40
PAIR = 2 * SLOTS
UNKEPT = -1000.0
LOW = jnp.bfloat16
FULL = jnp.float32
LAST = (((1,), (1,)), ((), ()))
FIRST = (((0,), (0,)), ((), ()))
USUAL = (((1,), (0,)), ((), ()))


def mul(left, right, dims=USUAL):
    return lax.dot_general(left, right, dims, preferred_element_type=FULL)


def remote(source, target, send_sem, recv_sem, device):
    return pltpu.make_async_remote_copy(
        src_ref=source,
        dst_ref=target,
        send_sem=send_sem,
        recv_sem=recv_sem,
        device_id=device,
        device_id_type=MESH,
    )


def part(ref, *index):
    return lambda: ref.at[index]


def whole(ref):
    return lambda: ref


class Places:
    def __init__(self):
        self.e = e = lax.axis_index("exp")
        self.h = h = lax.axis_index("head")
        x, y, self.z = e % 2, (e // 2) % 2, e // 4
        z = self.z
        over_x, over_y = e + 1 - 2 * x, e + 2 - 4 * y
        self.near_e = over_x * (1 - h) + over_y * h
        self.far_e = over_y * (1 - h) + over_x * h
        self.near = (self.near_e, h)
        self.far = (self.far_e, h)
        self.edge = (e + 4 - 8 * (z % 2), h)
        self.inner = ((3 - z) * 4 + e % 4, h)
        self.pair = (e, 1 - h)
        self.is_inner = (z == 1) | (z == 2)
        self.is_outer = (z == 0) | (z == 3)

    def greet(self):
        barrier = pltpu.get_barrier_semaphore()

        def signal(device):
            pl.semaphore_signal(barrier, inc=1, device_id=device, device_id_type=MESH)

        for device in (self.pair, self.near, self.far, self.edge):
            signal(device)

        @pl.when(self.is_inner)
        def _():
            signal(self.inner)
            pl.semaphore_wait(barrier, 5)

        @pl.when(self.is_outer)
        def _():
            pl.semaphore_wait(barrier, 4)


class Links:
    def __init__(self, places, send, recv):
        self.places, self.send, self.recv = places, send, recv
        self.sent, self.names = 0, {}
        self.pending = {"all": [], "inner": [], "outer": []}

    def number(self, name):
        return self.names.setdefault(name, len(self.names))

    def go(self, name, source, target, device, who="all"):
        number = self.sent
        remote(
            source(), target(), self.send.at[number], self.recv.at[self.number(name)], device
        ).start()
        self.sent += 1
        self.pending[who].append((number, name, source))

    def got(self, name, target):
        remote(
            target(), target(), self.send.at[0], self.recv.at[self.number(name)], self.places.near
        ).wait_recv()

    def sent_all(self, who, of):
        for number, name, source in self.pending[who]:
            if of is None or name[0] == of:
                remote(
                    source(), source(), self.send.at[number], self.recv.at[0], self.places.near
                ).wait_send()

    def drain(self, of=None):
        self.sent_all("all", of)

        @pl.when(self.places.is_inner)
        def _():
            self.sent_all("inner", of)

        @pl.when(self.places.is_outer)
        def _():
            self.sent_all("outer", of)

        for who, sent in self.pending.items():
            self.pending[who] = [one for one in sent if of is not None and one[1][0] != of]


class Spread:
    def __init__(self, links, name, gathered):
        self.links, self.name, self.gathered = links, name, gathered

    def start(self, block):
        links, places = self.links, self.links.places
        links.go((self.name, "z", 1), block, self.spot(1, 0), places.edge)
        links.go((self.name, "n", 0), block, self.spot(0, 1), places.near)

        @pl.when(places.is_inner)
        def _():
            links.go((self.name, "z", 2), block, self.spot(2, 0), places.inner, "inner")

    def pass_on(self, i):
        links, places = self.links, self.links.places
        block = self.spot(i, 0)
        links.got((self.name, "z", i), block)
        there = {1: 3, 2: 2, 3: 3}[i]
        device = places.inner if i == 1 else places.edge

        @pl.when(places.is_inner)
        def _():
            links.go((self.name, "z", there), block, self.spot(there, 0), device, "inner")

        links.go((self.name, "n", i), block, self.spot(i, 1), places.near)

    def wait(self, i):
        self.links.got((self.name, "n", i), self.spot(i, 1))

    def spot(self, i, a):
        return lambda: self.gathered.at[i, a]


class Gather:
    def __init__(self, links, name, send, recv):
        self.links, self.name, self.send, self.recv = links, name, send, recv

    def cast(self, value):
        return value.astype(self.send.dtype)

    def arrived(self, name, slot):
        self.links.got((self.name, name), part(self.recv, slot))
        return self.recv[slot].astype(FULL)

    def push(self, i, value):
        links, places, send, recv = self.links, self.links.places, self.send, self.recv
        if i == 1:

            @pl.when(places.is_outer)
            def _():
                send[1] = self.cast(value())
                links.go((self.name, "e1"), part(send, 1), part(recv, 1), places.edge, "outer")

            @pl.when(places.is_inner)
            def _():
                send[1] = self.cast(value() + self.arrived("i3", 4))
                links.go((self.name, "e1"), part(send, 1), part(recv, 1), places.edge, "inner")

        else:
            slot = {3: 4, 2: 0}[i]

            @pl.when(places.is_outer)
            def _():
                send[i] = self.cast(value())
                links.go((self.name, "e", i), part(send, i), part(recv, i), places.edge, "outer")

            @pl.when(places.is_inner)
            def _():
                self.links.got((self.name, "e", i), part(recv, i))
                send[i] = self.cast(value() + recv[i].astype(FULL))
                links.go((self.name, "i%d" % i), part(send, i), part(recv, slot), places.inner, "inner")

    def total(self, own, result):
        places = self.links.places
        result[...] = own + self.arrived("e1", 1)

        @pl.when(places.is_inner)
        def _():
            result[...] += self.arrived("i2", 0)


def table_rows(tables, i, places):
    rows = []
    for chip in (places.e, places.far_e):
        for j in range(2):
            rows.append(
                jnp.concatenate(
                    [tables[i, a, pl.ds(2 * chip + j, 1), :] for a in range(2)], axis=1
                )
            )
    return rows


def selection(tables, i, places):
    slot = lax.broadcasted_iota(jnp.int32, (PAIR, 2 * FLAT), 0)
    lane = lax.broadcasted_iota(jnp.int32, (PAIR, 2 * FLAT), 1)
    wanted = (slot - jnp.where(lane >= FLAT, SLOTS, 0)).astype(FULL)
    return jnp.concatenate(
        [jnp.where(row == wanted, 1.0, 0.0) for row in table_rows(tables, i, places)], axis=0
    )


def turn(block, cosine, sine, sign):
    lane = lax.broadcasted_iota(jnp.int32, block.shape, 1) % HEAD_DIMENSION
    quarter = HEAD_DIMENSION // 2
    other = jnp.where(
        lane < quarter,
        -sign * pltpu.roll(block, FLAT - quarter, 1),
        sign * pltpu.roll(block, quarter, 1),
    )
    return block * cosine + other * sine


def layer_kernel(names, *refs):
    r = types.SimpleNamespace(**dict(zip(names, refs, strict=True)))
    places = Places()
    h, e, z = places.h, places.e, places.z
    places.greet()
    links = Links(places, r.sems_send, r.sems_recv)
    experts = r.w_router.shape[1]
    rows_here, width = r.tokens.shape
    q_cols, k_cols = r.w_query.shape[1], r.key_weight.shape[1]
    kv_heads = k_cols // HEAD_DIMENSION
    every = slice(None)
    half = pl.multiple_of(h * FLAT, FLAT)
    other_half = pl.multiple_of((1 - h) * FLAT, FLAT)
    locals_used = [0]

    def load(source, target):
        copy = pltpu.make_async_copy(source, target, r.sems_local.at[locals_used[0]])
        locals_used[0] += 1
        copy.start()
        return copy

    rank_row = r.priority[...]
    row_id = lax.broadcasted_iota(jnp.int32, (FLAT, FLAT), 0)
    col_id = lax.broadcasted_iota(jnp.int32, (FLAT, FLAT), 1)
    rank_col = jnp.sum(
        jnp.where(row_id == col_id, jnp.broadcast_to(rank_row, (FLAT, FLAT)), 0),
        axis=1,
        keepdims=True,
    )
    earlier = jnp.where(rank_row < rank_col, 1.0, 0.0).astype(LOW)
    same = jnp.where(row_id == col_id, 1.0, 0.0).astype(LOW)
    names_row = lax.broadcasted_iota(jnp.int32, (FLAT, experts), 1)
    my_routes = r.routes[pl.ds(half, FLAT), :]
    named = jnp.zeros((FLAT, experts), FULL)
    for k in range(TOPK):
        named += jnp.where(my_routes[:, k : k + 1] == names_row, 1.0, 0.0)
    named = named.astype(LOW)
    member = mul(named, same, (((0,), (1,)), ((), ())))
    before = mul(named, earlier, (((0,), (1,)), ((), ())))
    r.tables[0, 0] = jnp.where((member > 0.5) & (before < SLOTS), before, UNKEPT)
    r.g_all[0, 0] = (RESIDUAL_SCALE * r.cotangent[...].astype(FULL)).astype(LOW)
    t_spread = Spread(links, "t", r.tables)
    g_spread = Spread(links, "g", r.g_all)
    x_spread = Spread(links, "x", r.x_all)
    p_spread = Spread(links, "p", r.gate_tables)
    t_spread.start(part(r.tables, 0, 0))
    g_spread.start(part(r.g_all, 0, 0))

    in_loads = [
        load(r.w_query, r.w_in.at[:, :q_cols]),
        load(r.key_weight, r.w_in.at[:, q_cols : q_cols + k_cols]),
        load(r.value_weight, r.w_in.at[:, q_cols + k_cols :]),
    ]
    out_load = load(r.w_output, r.w_out)
    expert_loads = [load(r.w_gate, r.gate_w), load(r.w_up, r.up_w), load(r.w_down, r.down_w)]

    x_full = r.tokens[...].astype(FULL)
    r.normed[...] = rms_scale(x_full, r.norm_one[...]).astype(LOW)
    for copy in in_loads:
        copy.wait()
    projected = mul(r.normed[...], r.w_in[...])
    cosine, sine = r.cosine[...], r.sine[...]
    lane = lax.broadcasted_iota(jnp.int32, (rows_here, FLAT), 1)
    low_lanes = lane < HEAD_DIMENSION
    for g in range(kv_heads):
        r.q[g] = turn(projected[:, g * FLAT : (g + 1) * FLAT], cosine, sine, 1.0).astype(LOW)
    for m in range(kv_heads // 2):
        start = q_cols + m * FLAT
        keys = turn(projected[:, start : start + FLAT], cosine, sine, 1.0)
        start += k_cols
        values = projected[:, start : start + FLAT]
        for block, store in ((keys, r.keys), (values, r.values)):
            rolled = pltpu.roll(block, HEAD_DIMENSION, 1)
            store[2 * m, 0] = jnp.where(low_lanes, block, 0.0).astype(LOW)
            store[2 * m, 1] = jnp.where(low_lanes, 0.0, rolled).astype(LOW)
            store[2 * m + 1, 0] = jnp.where(low_lanes, rolled, 0.0).astype(LOW)
            store[2 * m + 1, 1] = jnp.where(low_lanes, 0.0, block).astype(LOW)
    prompt, cont = rows_here // 2, rows_here // 4
    query_id = lax.broadcasted_iota(jnp.int32, (rows_here, rows_here), 0)
    key_id = lax.broadcasted_iota(jnp.int32, (rows_here, rows_here), 1)
    query_cont = jnp.where(query_id < prompt, 0, 1 + (query_id - prompt) // cont)
    key_cont = jnp.where(key_id < prompt, 0, 1 + (key_id - prompt) // cont)
    visible = ((key_cont == 0) & (query_cont > 0)) | (
        (key_cont == query_cont) & (key_id <= query_id)
    )
    r.bias[...] = jnp.where(visible, 0.0, MASKED_SCORE)

    def attend(first, count):
        def one(g, carry):
            mixed = jnp.zeros((rows_here, FLAT), FULL)
            for s in range(2):
                raw = mul(r.q[g], r.keys[g, s], LAST) * ATTENTION_SCALE
                scores = jnp.where(r.bias[...] < 0.0, MASKED_SCORE, raw)
                weights = jnp.exp(scores - jnp.max(scores, axis=1, keepdims=True))
                probs = weights / jnp.sum(weights, axis=1, keepdims=True)
                r.att_probs[g, s] = probs
                mixed += mul(probs.astype(LOW), r.values[g, s])
            r.heads[:, pl.ds(pl.multiple_of(g * FLAT, FLAT), FLAT)] = mixed.astype(LOW)
            return carry

        lax.fori_loop(first, first + count, one, 0)

    def dispatch_out(i):
        t_spread.wait(i)
        g_spread.wait(i)
        picks = selection(r.tables, i, places).astype(LOW)
        r.pick[i] = picks
        rows = mul(picks, r.g_all[i].reshape(2 * FLAT, -1)).astype(LOW)
        r.g_slots[i] = rows[: 2 * PAIR].reshape(2, PAIR, -1)
        r.g_send[i] = rows[2 * PAIR :].reshape(2, PAIR, -1)
        links.go(("g", "f", i), part(r.g_send, i), part(r.g_slots, 4 + i), places.far)

    def pass_out(i):
        t_spread.pass_on(i)
        g_spread.pass_on(i)

    attend(0, 2)
    pass_out(1)
    attend(2, 2)
    out_load.wait()
    r.branch_send[...] = mul(r.heads[pl.ds(other_half, FLAT), :], r.w_out[...])
    links.go("branch", whole(r.branch_send), whole(r.branch_in), places.pair)
    own_branch = mul(r.heads[pl.ds(half, FLAT), :], r.w_out[...])
    dispatch_out(0)
    pass_out(2)
    links.got("branch", whole(r.branch_in))
    middle = r.tokens[pl.ds(half, FLAT), :].astype(FULL) + RESIDUAL_SCALE * (
        own_branch + r.branch_in[...]
    )
    r.middle[...] = middle
    xn = rms_scale(middle, r.norm_two[...]).astype(LOW)
    r.x_all[0, 0] = xn
    x_spread.start(part(r.x_all, 0, 0))
    logits = mul(r.w_router[...], xn, (((0,), (1,)), ((), ())))
    chosen = jnp.where(member > 0.5, logits, MASKED_SCORE)
    weights = jnp.exp(chosen - jnp.max(chosen, axis=0, keepdims=True))
    probs = weights / jnp.sum(weights, axis=0, keepdims=True)
    r.probs[...] = probs
    r.gate_tables[0, 0] = probs.astype(LOW).astype(FULL)
    p_spread.start(part(r.gate_tables, 0, 0))

    slots_lane = lax.broadcasted_iota(jnp.int32, (2 * PAIR, FLAT), 1)
    r.gates[...] = jnp.zeros((2 * PAIR, FLAT), FULL)
    r.gate_send[...] = jnp.zeros((2 * PAIR, FLAT), FULL)

    def dispatch_in(i):
        x_spread.wait(i)
        picks = r.pick[i]
        rows = mul(picks, r.x_all[i].reshape(2 * FLAT, -1)).astype(LOW)
        r.x_slots[i] = rows[: 2 * PAIR].reshape(2, PAIR, -1)
        r.x_send[i] = rows[2 * PAIR :].reshape(2, PAIR, -1)
        links.go(("x", "f", i), part(r.x_send, i), part(r.x_slots, 4 + i), places.far)
        p_spread.wait(i)
        spread_gates = jnp.concatenate(
            [
                jnp.broadcast_to(row, (PAIR, 2 * FLAT))
                for row in table_rows(r.gate_tables, i, places)
            ],
            axis=0,
        )
        slot_gates = jnp.sum(picks.astype(FULL) * spread_gates, axis=1, keepdims=True)
        r.gates[...] += jnp.where(slots_lane == i, slot_gates[: 2 * PAIR], 0.0)
        r.gate_send[...] += jnp.where(slots_lane == 4 + i, slot_gates[2 * PAIR :], 0.0)

    def pass_in(i):
        x_spread.pass_on(i)
        p_spread.pass_on(i)

    dispatch_out(1)
    pass_out(3)
    dispatch_in(0)
    dispatch_out(2)
    pass_in(1)
    dispatch_out(3)
    pass_in(2)
    dispatch_in(1)
    pass_in(3)
    dispatch_in(2)
    dispatch_in(3)
    links.go(("p", "f"), whole(r.gate_send), whole(r.gate_far), places.far)

    slot_lane = lax.broadcasted_iota(jnp.int32, (PAIR, FLAT), 1)
    r.parts[...] = jnp.zeros((2 * PAIR, FLAT), FULL)

    def run_experts(first, count):
        span = count * PAIR
        which = slice(first, first + count)
        place = slice(first * PAIR, (first + count) * PAIR)

        def one_expert(j, carry):
            base = pl.multiple_of(j * PAIR, PAIR)
            gates = r.gates[pl.ds(base, PAIR), :]
            gate_col = jnp.concatenate(
                [gates[:, p : p + 1] for p in range(first, first + count)], axis=0
            )
            columns = pl.ds(pl.multiple_of(j * FF, FF), FF)
            xs = r.x_slots[which, j].reshape(span, -1)
            gate_pre = mul(xs, r.gate_w[:, columns])
            up_pre = mul(xs, r.up_w[:, columns])
            sig = jax.nn.sigmoid(gate_pre)
            act = gate_pre * sig
            hidden = (act * up_pre).astype(LOW)
            r.hidden_all[j, place] = hidden
            result = mul(hidden, r.down_w[columns, :])
            gs = r.g_slots[which, j].reshape(span, -1).astype(FULL)
            r.g_slots[which, j] = (gate_col * result).astype(LOW).reshape(count, PAIR, -1)
            part = jnp.sum(gs * result, axis=1, keepdims=True).astype(LOW).astype(FULL)
            terms = jnp.zeros((PAIR, FLAT), FULL)
            for p in range(count):
                terms += jnp.where(
                    slot_lane == first + p, part[p * PAIR : (p + 1) * PAIR], 0.0
                )
            r.parts[pl.ds(base, PAIR), :] += terms
            result_grad = (gate_col * gs).astype(LOW)
            r.result_all[j, place] = result_grad
            hidden_grad = mul(result_grad, r.down_w[columns, :], LAST)
            gate_pre_grad = (
                hidden_grad * up_pre * sig * (1.0 + gate_pre * (1.0 - sig))
            ).astype(LOW)
            up_pre_grad = (hidden_grad * act).astype(LOW)
            r.gate_all[j, place] = gate_pre_grad
            r.up_all[j, place] = up_pre_grad
            rows_grad = mul(gate_pre_grad, r.gate_w[:, columns], LAST) + mul(
                up_pre_grad, r.up_w[:, columns], LAST
            )
            r.row_slots[which, j] = rows_grad.astype(LOW).reshape(count, PAIR, -1)
            return carry

        lax.fori_loop(0, 2, one_expert, 0)

    for copy in expert_loads:
        copy.wait()
    run_experts(0, 4)
    links.got(("p", "f"), whole(r.gate_far))
    r.gates[...] += r.gate_far[...]
    for i in (2, 3):
        links.got(("g", "f", i), part(r.g_slots, 4 + i))
        links.got(("x", "f", i), part(r.x_slots, 4 + i))
    run_experts(6, 2)
    for i in (3, 2):
        links.go(("r", "f", i), part(r.row_slots, 4 + i), part(r.rows_in, i), places.far)
    for i in (0, 1):
        links.got(("g", "f", i), part(r.g_slots, 4 + i))
        links.got(("x", "f", i), part(r.x_slots, 4 + i))
    run_experts(4, 2)
    links.drain()
    for i in (1, 0):
        links.go(("r", "f", i), part(r.row_slots, 4 + i), part(r.rows_in, i), places.far)
    links.go(("q", "f"), whole(r.parts), whole(r.parts_in), places.far)
    writes = []

    def weight_grads(j):
        xs = r.x_slots[:, j].reshape(8 * PAIR, -1)
        columns = slice(j * FF, (j + 1) * FF)
        r.gate_w[:, columns] = mul(xs, r.gate_all[j], FIRST).astype(LOW)
        r.up_w[:, columns] = mul(xs, r.up_all[j], FIRST).astype(LOW)
        r.down_w[columns, :] = mul(r.hidden_all[j], r.result_all[j], FIRST).astype(LOW)

    def send_grads(j):
        columns = slice(j * FF, (j + 1) * FF)
        for n, (source, own, other) in enumerate(
            (
                (
                    part(r.gate_w, every, columns),
                    part(r.gate_own, every, columns),
                    part(r.gate_other, every, columns),
                ),
                (
                    part(r.up_w, every, columns),
                    part(r.up_own, every, columns),
                    part(r.up_other, every, columns),
                ),
                (part(r.down_w, columns), part(r.down_own, columns), part(r.down_other, columns)),
            )
        ):
            writes.append(load(source(), own()))
            links.go(("e", j, n), source, other, places.pair)

    weight_grads(0)
    send_grads(0)

    index = lax.broadcasted_iota(jnp.int32, (experts, 2 * FLAT), 0)

    def fold(name, rows, rows_in, kept, near_send, near_in, i):
        links.got((name, "f", i), part(rows_in, i))
        send = near_send(i)
        stacked = jnp.concatenate(
            [rows[i].reshape(2 * PAIR, -1), rows_in[i].reshape(2 * PAIR, -1)], axis=0
        )
        sums = mul(r.pick[i], stacked, FIRST)
        kept[i] = sums[:FLAT]
        send()[...] = sums[FLAT:].astype(LOW)
        links.go((name, "n", i), send, part(near_in, i), places.near)

    def fold_parts(i):
        column = jnp.concatenate(
            [r.parts[:, i : i + 1], r.parts_in[:, 4 + i : 5 + i]], axis=0
        )
        terms = r.pick[i].astype(FULL) * column
        table = jnp.zeros((experts, 2 * FLAT), FULL)
        chips = (places.e, places.e, places.far_e, places.far_e)
        for n, chip in enumerate(chips):
            total = jnp.sum(terms[n * PAIR : (n + 1) * PAIR], axis=0, keepdims=True)
            table += jnp.where(index == 2 * chip + n % 2, total, 0.0)
        r.part_kept[i] = table[:, :FLAT]
        r.part_send[i] = table[:, FLAT:]
        links.go(("q", "n", i), part(r.part_send, i), part(r.part_near, i), places.near)

    row_sums = Gather(links, "rz", r.row_z_send, r.row_z_in)
    part_sums = Gather(links, "qz", r.part_z_send, r.part_z_in)
    weighted_sums = Gather(links, "wz", r.row_z_send, r.weighted_z_in)

    def near_sum(name, kept, near_in, i):
        links.got((name, "n", i), part(near_in, i))
        return lambda: kept[i] + near_in[i].astype(FULL)

    def settle(i):
        row_sums.push(i, near_sum("r", r.row_kept, r.row_near, i))
        part_sums.push(i, near_sum("q", r.part_kept, r.part_near, i))

    fold("r", r.row_slots, r.rows_in, r.row_kept, lambda i: part(r.row_near_send, i), r.row_near, 3)
    fold("r", r.row_slots, r.rows_in, r.row_kept, lambda i: part(r.row_near_send, i), r.row_near, 2)
    links.got(("q", "f"), whole(r.parts_in))
    fold_parts(3)
    fold_parts(2)
    settle(3)
    fold("r", r.row_slots, r.rows_in, r.row_kept, lambda i: part(r.row_near_send, i), r.row_near, 1)
    fold_parts(1)
    settle(2)
    fold("r", r.row_slots, r.rows_in, r.row_kept, lambda i: part(r.row_near_send, i), r.row_near, 0)
    fold_parts(0)
    for i in (3, 2, 1, 0):
        links.go(("w", "f", i), part(r.g_slots, 4 + i), part(r.g_send, i), places.far)
    settle(1)
    weight_grads(1)
    row_sums.total(near_sum("r", r.row_kept, r.row_near, 0)(), r.branch_in)
    part_sums.total(near_sum("q", r.part_kept, r.part_near, 0)(), r.part_total)

    gate_probs, gate_grad = r.probs[...], r.part_total[...]
    chosen_grad = gate_probs * (
        gate_grad - jnp.sum(gate_probs * gate_grad, axis=0, keepdims=True)
    )
    logit_grad = chosen_grad.astype(LOW)
    xn_grad = r.branch_in[...] + mul(logit_grad, r.w_router[...], (((0,), (1,)), ((), ())))
    mid = r.middle[...]
    scale = lax.rsqrt(jnp.mean(mid * mid, axis=-1, keepdims=True) + NORM_EPS)
    scaled = r.norm_two[...] * xn_grad
    pull = jnp.mean(scaled * mid, axis=-1, keepdims=True)
    grad = r.cotangent[...].astype(FULL) + scale * scaled - mid * (scale * scale * scale * pull)
    r.grad_tokens[...] = grad
    mine = part(r.branch_grad, pl.ds(half, FLAT))
    r.branch_grad[pl.ds(half, FLAT), :] = (RESIDUAL_SCALE * grad).astype(LOW)
    links.go("bg", mine, mine, places.pair)
    r.small[pl.ds(0, experts), :] = mul(logit_grad, r.x_all[0, 0])
    r.small[pl.ds(experts, 8), :] = jnp.broadcast_to(
        jnp.sum(xn_grad * mid * scale, axis=0, keepdims=True), (8, width)
    )

    links.drain("rz")

    def settle_weighted(i):
        weighted_sums.push(i, near_sum("w", r.row_kept, r.weighted_near, i))

    def fold_weighted(i):
        fold(
            "w",
            r.g_slots,
            r.g_send,
            r.row_kept,
            lambda i: part(r.x_all, i, 0),
            r.weighted_near,
            i,
        )

    links.got("bg", part(r.branch_grad, pl.ds(other_half, FLAT)))
    send_grads(1)
    r.heads_grad[...] = mul(r.branch_grad[...], r.w_out[...], LAST).astype(LOW)
    r.grads[pl.ds(width, q_cols), :] = mul(r.heads[...], r.branch_grad[...], FIRST).astype(LOW)
    fold_weighted(3)
    cosine, sine = r.cosine[...], r.sine[...]

    def attend_back(first, count):
        def one(g, carry):
            place = pl.ds(pl.multiple_of(g * FLAT, FLAT), FLAT)
            out_grad = r.heads_grad[:, place]
            query = r.q[g]
            query_grad = jnp.zeros((rows_here, FLAT), FULL)
            key_grads, value_grads = [], []
            for s in range(2):
                probs = r.att_probs[g, s]
                prob_grad = mul(out_grad, r.values[g, s], LAST)
                inner = jnp.sum(probs * prob_grad, axis=1, keepdims=True)
                score_grad = (probs * (prob_grad - inner)).astype(LOW)
                query_grad += mul(score_grad, r.keys[g, s])
                key_grads.append(mul(score_grad, query, FIRST))
                value_grads.append(mul(probs.astype(LOW), out_grad, FIRST))
            r.head_grads[:, place] = turn(
                query_grad * ATTENTION_SCALE, r.cosine[...], r.sine[...], -1.0
            ).astype(LOW)
            r.key_sums[g] = key_grads[0] + pltpu.roll(key_grads[1], HEAD_DIMENSION, 1)
            r.value_sums[g] = value_grads[0] + pltpu.roll(value_grads[1], HEAD_DIMENSION, 1)
            return carry

        lax.fori_loop(first, first + count, one, 0)

    attend_back(0, 1)
    fold_weighted(2)
    settle_weighted(3)
    attend_back(1, 1)
    fold_weighted(1)
    settle_weighted(2)
    attend_back(2, 1)
    fold_weighted(0)
    settle_weighted(1)
    attend_back(3, 1)
    for m in range(kv_heads // 2):
        start = q_cols + m * FLAT
        for sums, shift in ((r.key_sums, 0), (r.value_sums, k_cols)):
            block = jnp.where(
                low_lanes, sums[2 * m], pltpu.roll(sums[2 * m + 1], HEAD_DIMENSION, 1)
            )
            if shift == 0:
                block = turn(block * ATTENTION_SCALE, cosine, sine, -1.0)
            r.head_grads[:, start + shift : start + shift + FLAT] = block.astype(LOW)
    head_grads = r.head_grads
    r.result_all[1, 0:FLAT] = mul(head_grads[pl.ds(other_half, FLAT), :], r.w_in[...], LAST).astype(LOW)
    links.go("terms", part(r.result_all, 1, pl.ds(0, FLAT)), whole(r.terms_in), places.pair)
    own_terms = mul(head_grads[pl.ds(half, FLAT), :], r.w_in[...], LAST).astype(LOW)
    r.grads[pl.ds(0, width), :] = mul(r.normed[...], head_grads[...], FIRST).astype(LOW)

    ranks = [z, z + 1 - 2 * (z % 2), 2 - z // 2, 3 - 3 * (z // 2)]
    plane = [[e % 4, places.near_e % 4], [places.far_e % 4, 3 - e % 4]]
    depth = r.grads.shape[0] // 16

    def shard(b, a, i):
        return pl.ds(pl.multiple_of((ranks[i] * 4 + plane[b][a]) * depth, 16), depth)

    def along(name, spot):
        block = spot(0)
        links.go((name, "z", 1), block, block, places.edge)

        @pl.when(places.is_inner)
        def _():
            links.go((name, "z", 2), block, block, places.inner, "inner")

    def pass_along(name, spot, i):
        block = spot(i)
        links.got((name, "z", i), block)
        there = {1: 3, 2: 2, 3: 3}[i]
        device = places.inner if i == 1 else places.edge

        @pl.when(places.is_inner)
        def _():
            links.go((name, "z", there), block, block, device, "inner")

    order = [(a, i) for i in (3, 2, 1, 0) for a in (1, 0)]
    short = pl.ds(0, depth)

    def far_in(a, i):
        return part(r.g_all, i, a, short)

    def near_in(i):
        return part(r.x_all, i, 1, short)

    def near_send(i):
        return part(r.result_all, 0, pl.ds(i * depth, depth))

    def send_far(n):
        if n < len(order):
            a, i = order[n]
            links.go(("f", a, i), part(r.grads, shard(1, a, i)), far_in(a, i), places.far)

    for n in range(3):
        send_far(n)

    weighted_sums.total(near_sum("w", r.row_kept, r.weighted_near, 0)(), r.branch_in)
    r.layer_out[...] = (r.middle[...] + RESIDUAL_SCALE * r.branch_in[...]).astype(LOW)

    links.got("terms", whole(r.terms_in))
    xn_grad = (own_terms.astype(FULL) + r.terms_in[...].astype(FULL)).astype(LOW).astype(FULL)
    x_half = r.tokens[pl.ds(half, FLAT), :].astype(FULL)
    scale = lax.rsqrt(jnp.mean(x_half * x_half, axis=-1, keepdims=True) + NORM_EPS)
    scaled = r.norm_one[...] * xn_grad
    pull = jnp.mean(scaled * x_half, axis=-1, keepdims=True)
    r.grad_tokens[...] = (
        r.grad_tokens[...] + scale * scaled - x_half * (scale * scale * scale * pull)
    )
    r.small_mine[0, pl.ds(0, experts), :] = r.small[pl.ds(0, experts), :]
    row = lax.broadcasted_iota(jnp.int32, (8, width), 0)
    r.small_mine[0, pl.ds(experts, 8), :] = jnp.where(
        row == 0,
        r.small[pl.ds(experts, 8), :],
        jnp.sum(xn_grad * x_half * scale, axis=0, keepdims=True),
    )
    links.go(("s", 0), part(r.small_mine, 0), part(r.small_in, 0), places.pair)

    sums = Gather(links, "az", r.sum_z_send, r.sum_z_in)

    def settle_sum(i):
        links.got(("n", i), near_in(i))
        return lambda: r.row_kept[i, 0:depth] + r.x_all[i, 1, 0:depth].astype(FULL)

    for n, (a, i) in enumerate(order):
        links.got(("f", a, i), far_in(a, i))
        send_far(n + 3)
        total = r.grads[shard(0, a, i), :].astype(FULL) + r.g_all[i, a, 0:depth].astype(FULL)
        if a:
            r.result_all[0, i * depth : (i + 1) * depth] = total.astype(LOW)
            links.go(("n", i), near_send(i), near_in(i), places.near)
        else:
            r.row_kept[i, 0:depth] = total
            if i < 3:
                sums.push(i + 1, settle_sum(i + 1))
        if n == 0:
            links.got(("s", 0), part(r.small_in, 0))
            r.small_mine[1] = r.small_mine[0] + r.small_in[0]
            links.go(("s", 1), part(r.small_mine, 1), part(r.small_in, 1), places.far)
        if n == 3:
            links.got(("s", 1), part(r.small_in, 1))
            r.small_mine[2] = r.small_mine[1] + r.small_in[1]
            links.go(("s", 2), part(r.small_mine, 2), part(r.small_in, 2), places.near)
        if n == 6:
            links.got(("s", 2), part(r.small_in, 2))
            r.small_all[z] = r.small_mine[2] + r.small_in[2]
            along("s", lambda i: part(r.small_all, ranks[i]))
    sums.total(settle_sum(0)(), r.branch_in.at[pl.ds(0, depth)])
    r.result_all[1, FLAT : FLAT + depth] = r.branch_in[0:depth].astype(LOW)

    def spot(b, a, i):
        return part(r.grads_out, shard(b, a, i))

    mine, low = spot(0, 0, 0), part(r.result_all, 1, pl.ds(FLAT, depth))
    links.go(("o", "z", 1), low, mine, places.edge)
    links.go(("on", 0), low, mine, places.near)
    links.go(("of", 0, 0), low, mine, places.far)

    @pl.when(places.is_inner)
    def _():
        links.go(("o", "z", 2), low, mine, places.inner, "inner")

    writes.append(load(low(), mine()))

    def pass_far(i):
        block = spot(0, 1, i)
        links.got(("on", i), block)
        links.go(("of", 1, i), block, block, places.far)

    pass_far(0)
    for i in (1, 2, 3):
        block = spot(0, 0, i)
        pass_along("o", lambda i: spot(0, 0, i), i)
        links.go(("on", i), block, block, places.near)
        links.go(("of", 0, i), block, block, places.far)
        pass_far(i)
    for i in (1, 2, 3):
        pass_along("s", lambda i: part(r.small_all, ranks[i]), i)
    r.small_out[...] = ((r.small_all[0] + r.small_all[1]) + r.small_all[2]) + r.small_all[3]
    for i in range(4):
        for a in range(2):
            links.got(("of", a, i), spot(1, a, i))
    for j in range(2):
        columns = slice(j * FF, (j + 1) * FF)
        links.got(("e", j, 0), part(r.gate_other, every, columns))
        links.got(("e", j, 1), part(r.up_other, every, columns))
        links.got(("e", j, 2), part(r.down_other, columns))
    for copy in writes:
        copy.wait()
    links.drain()


def run_layer(**inputs):
    rows_here, width = inputs["tokens"].shape
    experts = inputs["w_router"].shape[1]
    q_cols, k_cols = inputs["w_query"].shape[1], inputs["key_weight"].shape[1]
    kv_heads = k_cols // HEAD_DIMENSION
    vmem = pl.BlockSpec(memory_space=pltpu.VMEM)
    anywhere = pl.BlockSpec(memory_space=pl.ANY)
    block = (FLAT, width)
    gate = (experts, FLAT)
    slots = (2, PAIR, width)
    small = (experts + 8, width)
    grads = (width + q_cols, width)
    depth = grads[0] // 16
    outputs = {
        "layer_out": (block, LOW),
        "grad_tokens": (block, FULL),
        "small_out": (small, FULL),
    }
    held = {"grads_out": (grads, LOW)} | {
        name + end: (inputs["w_" + name].shape, LOW)
        for end in ("_own", "_other")
        for name in ("gate", "up", "down")
    }
    heads = (kv_heads, 2, rows_here)
    scratch = {
        "w_in": ((width, q_cols + 2 * k_cols), LOW),
        "w_out": ((q_cols, width), LOW),
        "normed": ((rows_here, width), LOW),
        "q": ((kv_heads, rows_here, FLAT), LOW),
        "keys": (heads + (FLAT,), LOW),
        "values": (heads + (FLAT,), LOW),
        "bias": ((rows_here, rows_here), FULL),
        "att_probs": (heads + (rows_here,), FULL),
        "heads": ((rows_here, q_cols), LOW),
        "heads_grad": ((rows_here, q_cols), LOW),
        "head_grads": ((rows_here, q_cols + 2 * k_cols), LOW),
        "key_sums": ((kv_heads, rows_here, FLAT), FULL),
        "value_sums": ((kv_heads, rows_here, FLAT), FULL),
        "branch_send": (block, FULL),
        "branch_in": (block, FULL),
        "middle": (block, FULL),
        "branch_grad": ((rows_here, width), LOW),
        "small": (small, FULL),
        "terms_in": (block, LOW),
        "grads": (grads, LOW),
        "sum_z_send": ((4, depth, width), LOW),
        "sum_z_in": ((5, depth, width), LOW),
        "small_mine": ((3,) + small, FULL),
        "small_in": ((3,) + small, FULL),
        "small_all": ((4,) + small, FULL),
        "probs": (gate, FULL),
        "tables": ((4, 2) + gate, FULL),
        "gate_tables": ((4, 2) + gate, FULL),
        "g_all": ((4, 2) + block, LOW),
        "x_all": ((4, 2) + block, LOW),
        "g_slots": ((8,) + slots, LOW),
        "x_slots": ((8,) + slots, LOW),
        "row_slots": ((8,) + slots, LOW),
        "g_send": ((4,) + slots, LOW),
        "x_send": ((4,) + slots, LOW),
        "gates": ((2 * PAIR, FLAT), FULL),
        "gate_send": ((2 * PAIR, FLAT), FULL),
        "gate_far": ((2 * PAIR, FLAT), FULL),
        "parts": ((2 * PAIR, FLAT), FULL),
        "parts_in": ((2 * PAIR, FLAT), FULL),
        "pick": ((4, 4 * PAIR, 2 * FLAT), LOW),
        "gate_w": (inputs["w_gate"].shape, LOW),
        "up_w": (inputs["w_up"].shape, LOW),
        "down_w": (inputs["w_down"].shape, LOW),
        "hidden_all": ((2, 8 * PAIR, FF), LOW),
        "gate_all": ((2, 8 * PAIR, FF), LOW),
        "up_all": ((2, 8 * PAIR, FF), LOW),
        "result_all": ((2, 8 * PAIR, width), LOW),
        "rows_in": ((4,) + slots, LOW),
        "row_kept": ((4,) + block, FULL),
        "row_near": ((4,) + block, LOW),
        "row_near_send": ((4,) + block, LOW),
        "row_z_send": ((4,) + block, LOW),
        "row_z_in": ((5,) + block, LOW),
        "part_kept": ((4,) + gate, FULL),
        "part_near": ((4,) + gate, FULL),
        "part_send": ((4,) + gate, FULL),
        "part_z_send": ((4,) + gate, FULL),
        "part_z_in": ((5,) + gate, FULL),
        "part_total": (gate, FULL),
        "weighted_near": ((4,) + block, LOW),
        "weighted_z_in": ((5,) + block, LOW),
    }
    near_by = ("tokens", "norm_one", "norm_two", "w_router", "routes", "priority")
    near_by += ("cotangent", "cosine", "sine")
    names = [*inputs, *outputs, *held, *scratch, "sems_local", "sems_send", "sems_recv"]
    results = pl.pallas_call(
        functools.partial(layer_kernel, names),
        out_shape=[
            jax.ShapeDtypeStruct(shape, kind) for shape, kind in [*outputs.values(), *held.values()]
        ],
        in_specs=[vmem if name in near_by else anywhere for name in inputs],
        out_specs=[vmem] * len(outputs) + [anywhere] * len(held),
        scratch_shapes=[pltpu.VMEM(shape, kind) for shape, kind in scratch.values()]
        + [
            pltpu.SemaphoreType.DMA((20,)),
            pltpu.SemaphoreType.DMA((200,)),
            pltpu.SemaphoreType.DMA((160,)),
        ],
        compiler_params=pltpu.CompilerParams(
            collective_id=0, has_side_effects=True, vmem_limit_bytes=63 << 20
        ),
        name="layer",
    )(*inputs.values())
    return dict(zip([*outputs, *held], results))


def quick_shards(
    tokens,
    norm_one,
    w_query,
    key_weight,
    value_weight,
    w_output,
    norm_two,
    w_router,
    w_gate,
    w_up,
    w_down,
    routes,
    priority,
    cotangent,
):
    rows_here, width = tokens.shape
    experts = w_router.shape[1]
    q_cols, k_cols = w_query.shape[1], key_weight.shape[1]
    local_index = jnp.arange(rows_here, dtype=jnp.int32)
    prompt_rows, cont_rows = rows_here // 2, rows_here // 4
    position = jnp.where(
        local_index < prompt_rows,
        local_index,
        prompt_rows + (local_index - prompt_rows) % cont_rows,
    )
    frequency = ROPE_BASE ** (
        -(2.0 * jnp.arange(HEAD_DIMENSION // 2, dtype=jnp.float32)) / HEAD_DIMENSION
    )
    angle_table = position.astype(jnp.float32)[:, None] * jnp.tile(frequency, 4)[None, :]
    done = run_layer(
        tokens=tokens,
        norm_one=norm_one[None, :],
        norm_two=norm_two[None, :],
        w_router=w_router,
        routes=routes,
        priority=priority,
        cotangent=cotangent,
        cosine=jnp.cos(angle_table),
        sine=jnp.sin(angle_table),
        w_query=w_query,
        key_weight=key_weight,
        value_weight=value_weight,
        w_output=w_output,
        w_gate=w_gate,
        w_up=w_up,
        w_down=w_down,
    )
    grads = done["grads_out"].astype(jnp.float32)
    small = done["small_out"]

    def both(mine, other):
        return mine.astype(jnp.float32) + other.astype(jnp.float32)

    return (
        done["layer_out"],
        done["grad_tokens"],
        small[experts + 1],
        grads[:width, :q_cols],
        grads[:width, q_cols : q_cols + k_cols],
        grads[:width, q_cols + k_cols :],
        grads[width:],
        small[experts],
        small[:experts].T,
        both(done["gate_own"], done["gate_other"]),
        both(done["up_own"], done["up_other"]),
        both(done["down_own"], done["down_other"]),
    )


def solution(mesh):
    body = quick_shards if dict(mesh.shape) == {"exp": 16, "head": 2} else shards
    return jax.shard_map(
        body,
        mesh=mesh,
        in_specs=(
            P("exp", None),
            P(),
            P(None, "head"),
            P(None, "head"),
            P(None, "head"),
            P("head", None),
            P(),
            P(),
            P(None, "exp"),
            P(None, "exp"),
            P("exp", None),
            P("exp", None),
            P(("exp", "head"), None),
            P(("exp", "head"), None),
        ),
        out_specs=(
            P(("exp", "head"), None),
            P(("exp", "head"), None),
            P(),
            P(None, "head"),
            P(None, "head"),
            P(None, "head"),
            P("head", None),
            P(),
            P(),
            P(None, "exp"),
            P(None, "exp"),
            P("exp", None),
        ),
        check_vma=False,
    )
```

```python
import functools
import types

import jax
import jax.numpy as jnp
import numpy as np
from jax import lax
from jax.experimental import pallas as pl
from jax.experimental.pallas import tpu as pltpu
from jax.sharding import PartitionSpec as P

HEAD_DIMENSION = 64
FF = 512
TOPK = 8


RESIDUAL_SCALE = 0.22
ATTENTION_SCALE = 0.015625
ROPE_BASE = 10000.0
NORM_EPS = 1e-06
MASKED_SCORE = -1e30


def rms_scale(values, scale_row):
    return (
        values * lax.rsqrt(jnp.mean(values * values, axis=-1, keepdims=True) + NORM_EPS) * scale_row
    )


def apply_rotary(values, cosine_values, sine_values):
    half_width = values.shape[-1] // 2
    lower_part = values[..., :half_width]
    upper_part = values[..., half_width:]
    return jnp.concatenate(
        [
            lower_part * cosine_values - upper_part * sine_values,
            upper_part * cosine_values + lower_part * sine_values,
        ],
        axis=-1,
    )


def rotate_back(values, cosine_values, sine_values):
    half_width = values.shape[-1] // 2
    lower_part = values[..., :half_width]
    upper_part = values[..., half_width:]
    return jnp.concatenate(
        [
            lower_part * cosine_values + upper_part * sine_values,
            upper_part * cosine_values - lower_part * sine_values,
        ],
        axis=-1,
    )


def shards(
    tokens,
    norm_one,
    w_query,
    key_weight,
    value_weight,
    w_output,
    norm_two,
    w_router,
    w_gate,
    w_up,
    w_down,
    routes,
    priority,
    cotangent,
):
    tok_rows, model_width = tokens.shape
    heads_count = lax.axis_size("head")
    head_rank = lax.axis_index("head")
    exp_count = lax.axis_size("exp")
    half_rows = tok_rows // heads_count
    prompt_rows = tok_rows // 2
    cont_rows = tok_rows // 4
    kv_heads = key_weight.shape[1] // HEAD_DIMENSION
    query_groups = w_query.shape[1] // key_weight.shape[1]
    experts = w_router.shape[1]
    held_cols = w_gate.shape[1]
    held = max(1, held_cols // FF)
    split = max(1, FF // held_cols)
    block_width = held_cols // held
    capacity = max(2, (5 * half_rows * TOPK + 4 * experts - 1) // (4 * experts))
    rows_per_block = min(512, tok_rows)
    count_of_blocks = tok_rows // rows_per_block
    local_index = jnp.arange(tok_rows, dtype=jnp.int32)
    position = jnp.where(
        local_index < prompt_rows,
        local_index,
        prompt_rows + (local_index - prompt_rows) % cont_rows,
    )
    frequency = ROPE_BASE ** (
        -(2.0 * jnp.arange(HEAD_DIMENSION // 2, dtype=jnp.float32)) / HEAD_DIMENSION
    )
    angle_table = position.astype(jnp.float32)[:, None] * frequency[None, :]
    cosine_values = jnp.cos(angle_table)[:, None, :]
    sine_values = jnp.sin(angle_table)[:, None, :]
    x_full = tokens.astype(jnp.float32)
    normed_input_first = rms_scale(x_full, norm_one).astype(jnp.bfloat16)
    rotated_queries = apply_rotary(
        jnp.dot(normed_input_first, w_query, preferred_element_type=jnp.float32).reshape(
            tok_rows, -1, HEAD_DIMENSION
        ),
        cosine_values,
        sine_values,
    ).astype(jnp.bfloat16)
    keys_all = apply_rotary(
        jnp.dot(normed_input_first, key_weight, preferred_element_type=jnp.float32).reshape(
            tok_rows, -1, HEAD_DIMENSION
        ),
        cosine_values,
        sine_values,
    ).astype(jnp.bfloat16)
    values_all = (
        jnp.dot(normed_input_first, value_weight, preferred_element_type=jnp.float32)
        .astype(jnp.bfloat16)
        .reshape(tok_rows, kv_heads, HEAD_DIMENSION)
    )

    def visible_pairs(block_start):
        query_col = (block_start + jnp.arange(rows_per_block, dtype=jnp.int32))[:, None]
        key_row = jnp.arange(tok_rows, dtype=jnp.int32)[None, :]
        from_prompt = (key_row < prompt_rows) & (
            (query_col >= prompt_rows) | (key_row <= query_col)
        )
        same_cont = (
            (key_row >= prompt_rows)
            & (query_col >= prompt_rows)
            & (key_row <= query_col)
            & ((key_row - prompt_rows) // cont_rows == (query_col - prompt_rows) // cont_rows)
        )
        return from_prompt | same_cont

    def scores_of(query_block, block_start):
        raw_scores = (
            jnp.einsum("qhgd,khd->hgqk", query_block, keys_all, preferred_element_type=jnp.float32)
            * ATTENTION_SCALE
        )
        return jnp.where(visible_pairs(block_start)[None, None], raw_scores, MASKED_SCORE)

    def forward_block(parts):
        query_block, block_start = parts
        scores = scores_of(query_block, block_start)
        row_max = jnp.max(scores, axis=-1, keepdims=True)
        weights = jnp.exp(scores - row_max)
        row_total = jnp.sum(weights, axis=-1, keepdims=True)
        probs_low = (weights / row_total).astype(jnp.bfloat16)
        mixed = jnp.einsum(
            "hgqk,khd->qhgd", probs_low, values_all, preferred_element_type=jnp.float32
        )
        return (mixed.astype(jnp.bfloat16), row_max + jnp.log(row_total))

    query_blocks = rotated_queries.reshape(
        count_of_blocks, rows_per_block, kv_heads, query_groups, HEAD_DIMENSION
    )
    block_starts = jnp.arange(count_of_blocks, dtype=jnp.int32) * rows_per_block
    heads_blocks, log_total = lax.map(forward_block, (query_blocks, block_starts))
    head_outputs = heads_blocks.reshape(tok_rows, -1)
    head_terms = jnp.dot(head_outputs, w_output, preferred_element_type=jnp.float32)
    branch_half = lax.dynamic_slice_in_dim(
        lax.psum(head_terms, "head"), head_rank * half_rows, half_rows, 0
    )
    x_half = lax.dynamic_slice_in_dim(x_full, head_rank * half_rows, half_rows, 0)
    middle = x_half + RESIDUAL_SCALE * branch_half
    xn_two = rms_scale(middle, norm_two).astype(jnp.bfloat16)
    logits = jnp.dot(xn_two, w_router, preferred_element_type=jnp.float32)
    my_routes = lax.dynamic_slice_in_dim(routes, head_rank * half_rows, half_rows, 0)
    route_hot = my_routes[:, :, None] == jnp.arange(experts, dtype=jnp.int32)[None, None, :]
    chosen = jnp.sum(jnp.where(route_hot, logits[:, None, :], 0.0), axis=-1)
    chosen_max = jnp.max(chosen, axis=-1, keepdims=True)
    chosen_exp = jnp.exp(chosen - chosen_max)
    gate_probs = chosen_exp / jnp.sum(chosen_exp, axis=-1, keepdims=True)
    gate_low = gate_probs.astype(jnp.bfloat16)
    member = jnp.any(route_hot, axis=1).astype(jnp.bfloat16)
    order_rank = priority[0]
    earlier = (order_rank[None, :] < order_rank[:, None]).astype(jnp.bfloat16)
    before = jnp.dot(earlier, member, preferred_element_type=jnp.float32)
    slot_rank = jnp.sum(jnp.where(route_hot, before[:, None, :], 0.0), axis=-1).astype(jnp.int32)
    is_kept = slot_rank < capacity
    spare_slot = experts * capacity
    target = jnp.where(is_kept, my_routes * capacity + slot_rank, spare_slot)
    row_ids = jnp.broadcast_to(jnp.arange(half_rows, dtype=jnp.int32)[:, None], target.shape)
    assign_ids = jnp.arange(half_rows * TOPK, dtype=jnp.int32).reshape(target.shape)
    source_row = (
        jnp.zeros(spare_slot + 1, jnp.int32).at[target.ravel()].set(row_ids.ravel())[:spare_slot]
    )
    source_pick = (
        jnp.zeros(spare_slot + 1, jnp.int32).at[target.ravel()].set(assign_ids.ravel())[:spare_slot]
    )
    filled = jnp.zeros(spare_slot + 1, jnp.int32).at[target.ravel()].set(1)[:spare_slot] > 0
    slot_inputs = jnp.where(filled[:, None], xn_two[source_row], 0).reshape(
        experts, capacity, model_width
    )
    slot_gates = jnp.where(filled, gate_low.ravel()[source_pick], 0).reshape(experts, capacity)

    def to_owners(per_expert):
        shape_in = per_expert.shape
        spread = jnp.broadcast_to(per_expert[:, None], (shape_in[0], split) + shape_in[1:])
        return spread.reshape((exp_count, held) + shape_in[1:])

    def from_owners(per_owner):
        shape_in = per_owner.shape
        return jnp.sum(
            per_owner.reshape((experts, split) + shape_in[2:]).astype(jnp.float32), axis=1
        )

    gate_cols = w_gate.reshape(model_width, held, block_width)
    up_cols = w_up.reshape(model_width, held, block_width)
    down_rows = w_down.reshape(held, block_width, model_width)
    send_rows = to_owners(slot_inputs)
    send_gates = to_owners(slot_gates)
    slot_rows = lax.all_to_all(send_rows, "exp", split_axis=0, concat_axis=0, tiled=True)
    slot_gate = lax.all_to_all(send_gates, "exp", split_axis=0, concat_axis=0, tiled=True)
    gate_pre = jnp.einsum(
        "sjcd,djf->sjcf", slot_rows, gate_cols, preferred_element_type=jnp.float32
    )
    up_pre = jnp.einsum("sjcd,djf->sjcf", slot_rows, up_cols, preferred_element_type=jnp.float32)
    hidden = (gate_pre * jax.nn.sigmoid(gate_pre) * up_pre).astype(jnp.bfloat16)
    result = jnp.einsum("sjcf,jfd->sjcd", hidden, down_rows, preferred_element_type=jnp.float32)
    weighted = (slot_gate[..., None].astype(jnp.float32) * result).astype(jnp.bfloat16)
    returned = lax.all_to_all(weighted, "exp", split_axis=0, concat_axis=0, tiled=True)
    returned, held_rows, held_gates = (returned, slot_rows, slot_gate)
    back_flat = jnp.concatenate(
        [
            from_owners(returned).reshape(spare_slot, model_width),
            jnp.zeros((1, model_width), jnp.float32),
        ],
        axis=0,
    )
    expert_sum = jnp.sum(back_flat[target], axis=1)
    layer_out = (middle + RESIDUAL_SCALE * expert_sum).astype(jnp.bfloat16)
    out_grad = cotangent.astype(jnp.float32)
    weighted_rows = (RESIDUAL_SCALE * out_grad).astype(jnp.bfloat16)
    grad_slots = to_owners(
        jnp.where(filled[:, None], weighted_rows[source_row], 0).reshape(
            experts, capacity, model_width
        )
    )
    back_grads, back_rows, back_gates = (
        lax.all_to_all(grad_slots, "exp", split_axis=0, concat_axis=0, tiled=True),
        lax.all_to_all(send_rows, "exp", split_axis=0, concat_axis=0, tiled=True),
        lax.all_to_all(send_gates, "exp", split_axis=0, concat_axis=0, tiled=True),
    )
    owner_gates = back_gates[..., None].astype(jnp.float32)
    gate_pre = jnp.einsum(
        "sjcd,djf->sjcf", back_rows, gate_cols, preferred_element_type=jnp.float32
    )
    up_pre = jnp.einsum("sjcd,djf->sjcf", back_rows, up_cols, preferred_element_type=jnp.float32)
    gate_sigmoid = jax.nn.sigmoid(gate_pre)
    gate_act = gate_pre * gate_sigmoid
    hidden = (gate_act * up_pre).astype(jnp.bfloat16)
    result = jnp.einsum("sjcf,jfd->sjcd", hidden, down_rows, preferred_element_type=jnp.float32)
    gate_part = jnp.sum(back_grads.astype(jnp.float32) * result, axis=-1)
    result_grad = (owner_gates * back_grads).astype(jnp.bfloat16)
    grad_down_w = jnp.einsum(
        "sjcf,sjcd->jfd", hidden, result_grad, preferred_element_type=jnp.float32
    ).reshape(held_cols, model_width)
    hidden_grad = jnp.einsum(
        "sjcd,jfd->sjcf", result_grad, down_rows, preferred_element_type=jnp.float32
    )
    gate_pre_grad = (
        hidden_grad * up_pre * gate_sigmoid * (1.0 + gate_pre * (1.0 - gate_sigmoid))
    ).astype(jnp.bfloat16)
    up_pre_grad = (hidden_grad * gate_act).astype(jnp.bfloat16)
    grad_gate_w = jnp.einsum(
        "sjcd,sjcf->djf", back_rows, gate_pre_grad, preferred_element_type=jnp.float32
    ).reshape(model_width, held_cols)
    grad_up_w = jnp.einsum(
        "sjcd,sjcf->djf", back_rows, up_pre_grad, preferred_element_type=jnp.float32
    ).reshape(model_width, held_cols)
    rows_grad = (
        jnp.einsum("sjcf,djf->sjcd", gate_pre_grad, gate_cols, preferred_element_type=jnp.float32)
        + jnp.einsum("sjcf,djf->sjcd", up_pre_grad, up_cols, preferred_element_type=jnp.float32)
    ).astype(jnp.bfloat16)
    rows_back, gates_back = (
        lax.all_to_all(rows_grad, "exp", split_axis=0, concat_axis=0, tiled=True),
        lax.all_to_all(
            gate_part.astype(jnp.bfloat16), "exp", split_axis=0, concat_axis=0, tiled=True
        ),
    )
    rows_flat = jnp.concatenate(
        [
            from_owners(rows_back).reshape(spare_slot, model_width),
            jnp.zeros((1, model_width), jnp.float32),
        ],
        axis=0,
    )
    xn_two_grad = jnp.sum(rows_flat[target], axis=1)
    gate_total = from_owners(gates_back).astype(jnp.bfloat16).reshape(spare_slot)
    gates_flat = jnp.concatenate([gate_total, jnp.zeros((1,), jnp.bfloat16)], axis=0)
    gate_grad_tok = gates_flat[target].astype(jnp.float32)
    chosen_grad = gate_probs * (
        gate_grad_tok - jnp.sum(gate_probs * gate_grad_tok, axis=-1, keepdims=True)
    )
    logit_grad = jnp.sum(jnp.where(route_hot, chosen_grad[:, :, None], 0.0), axis=1).astype(
        jnp.bfloat16
    )
    grad_router = jnp.einsum("rd,re->de", xn_two, logit_grad, preferred_element_type=jnp.float32)
    xn_two_grad = xn_two_grad + jnp.einsum(
        "re,de->rd", logit_grad, w_router, preferred_element_type=jnp.float32
    )
    middle_norm_pull = jax.vjp(rms_scale, middle, norm_two)[1]
    middle_norm_grad, grad_norm_two = middle_norm_pull(xn_two_grad)
    middle_grad = out_grad + middle_norm_grad
    branch_rows = (RESIDUAL_SCALE * middle_grad).astype(jnp.bfloat16)
    branch_grad = lax.all_gather(branch_rows, "head", axis=0, tiled=True)
    heads_grad = jnp.einsum(
        "td,hd->th", branch_grad, w_output, preferred_element_type=jnp.float32
    ).astype(jnp.bfloat16)
    grad_output_w = jnp.einsum(
        "th,td->hd", head_outputs, branch_grad, preferred_element_type=jnp.float32
    )

    def backward_block(running, parts):
        key_grad, value_grad = running
        query_block, heads_block, block_total, block_start = parts
        scores = scores_of(query_block, block_start)
        probs = jnp.exp(scores - block_total)
        probs_low = probs.astype(jnp.bfloat16)
        prob_grad = jnp.einsum(
            "qhgd,khd->hgqk", heads_block, values_all, preferred_element_type=jnp.float32
        )
        row_inner = jnp.sum(probs * prob_grad, axis=-1, keepdims=True)
        score_grad = (probs * (prob_grad - row_inner)).astype(jnp.bfloat16)
        query_grad = (
            jnp.einsum("hgqk,khd->qhgd", score_grad, keys_all, preferred_element_type=jnp.float32)
            * ATTENTION_SCALE
        )
        key_grad = (
            key_grad
            + jnp.einsum(
                "hgqk,qhgd->khd", score_grad, query_block, preferred_element_type=jnp.float32
            )
            * ATTENTION_SCALE
        )
        value_grad = value_grad + jnp.einsum(
            "hgqk,qhgd->khd", probs_low, heads_block, preferred_element_type=jnp.float32
        )
        return ((key_grad, value_grad), query_grad)

    heads_grad_blocks = heads_grad.reshape(
        count_of_blocks, rows_per_block, kv_heads, query_groups, HEAD_DIMENSION
    )
    zero_keys = jnp.zeros((tok_rows, kv_heads, HEAD_DIMENSION), jnp.float32)
    (own_key, own_value), query_grad = lax.scan(
        backward_block,
        (zero_keys, zero_keys),
        (query_blocks, heads_grad_blocks, log_total, block_starts),
    )
    query_pre_grad = (
        rotate_back(query_grad.reshape(tok_rows, -1, HEAD_DIMENSION), cosine_values, sine_values)
        .reshape(tok_rows, -1)
        .astype(jnp.bfloat16)
    )
    key_pre_grad = (
        rotate_back(own_key, cosine_values, sine_values).reshape(tok_rows, -1).astype(jnp.bfloat16)
    )
    value_low_grad = own_value.reshape(tok_rows, -1).astype(jnp.bfloat16)
    grad_query_w = jnp.einsum(
        "td,th->dh", normed_input_first, query_pre_grad, preferred_element_type=jnp.float32
    )
    grad_key_w = jnp.einsum(
        "td,th->dh", normed_input_first, key_pre_grad, preferred_element_type=jnp.float32
    )
    grad_value_w = jnp.einsum(
        "td,th->dh", normed_input_first, value_low_grad, preferred_element_type=jnp.float32
    )
    xn_one_terms = (
        jnp.einsum("th,dh->td", query_pre_grad, w_query, preferred_element_type=jnp.float32)
        + jnp.einsum("th,dh->td", key_pre_grad, key_weight, preferred_element_type=jnp.float32)
        + jnp.einsum("th,dh->td", value_low_grad, value_weight, preferred_element_type=jnp.float32)
    )
    xn_one_grad = lax.psum_scatter(
        xn_one_terms.astype(jnp.bfloat16), "head", scatter_dimension=0, tiled=True
    ).astype(jnp.float32)
    input_norm_pull = jax.vjp(rms_scale, x_half, norm_one)[1]
    input_norm_grad, grad_norm_one = input_norm_pull(xn_one_grad)
    grad_tokens = middle_grad + input_norm_grad
    grad_gate_w, grad_up_w, grad_down_w, grad_router, grad_norm_one, grad_norm_two = (
        lax.psum(grad_gate_w.astype(jnp.bfloat16), "head").astype(jnp.float32),
        lax.psum(grad_up_w.astype(jnp.bfloat16), "head").astype(jnp.float32),
        lax.psum(grad_down_w.astype(jnp.bfloat16), "head").astype(jnp.float32),
        lax.psum(grad_router.astype(jnp.bfloat16), "head").astype(jnp.float32),
        lax.psum(grad_norm_one.astype(jnp.bfloat16), "head").astype(jnp.float32),
        lax.psum(grad_norm_two.astype(jnp.bfloat16), "head").astype(jnp.float32),
    )
    (
        grad_query_w,
        grad_key_w,
        grad_value_w,
        grad_output_w,
        grad_router,
        grad_norm_one,
        grad_norm_two,
    ) = lax.psum(
        (
            grad_query_w,
            grad_key_w,
            grad_value_w,
            grad_output_w,
            grad_router,
            grad_norm_one,
            grad_norm_two,
        ),
        "exp",
    )
    return (
        layer_out,
        grad_tokens,
        grad_norm_one,
        grad_query_w,
        grad_key_w,
        grad_value_w,
        grad_output_w,
        grad_norm_two,
        grad_router,
        grad_gate_w,
        grad_up_w,
        grad_down_w,
    )


MESH = pl.DeviceIdType.MESH
FLAT = 128
SLOTS = 40
PAIR = 2 * SLOTS
UNKEPT = -1000.0
LOW = jnp.bfloat16
FULL = jnp.float32
LAST = (((1,), (1,)), ((), ()))
FIRST = (((0,), (0,)), ((), ()))
USUAL = (((1,), (0,)), ((), ()))


def mul(left, right, dims=USUAL):
    return lax.dot_general(left, right, dims, preferred_element_type=FULL)


def remote(source, target, send_sem, recv_sem, device):
    return pltpu.make_async_remote_copy(
        src_ref=source,
        dst_ref=target,
        send_sem=send_sem,
        recv_sem=recv_sem,
        device_id=device,
        device_id_type=MESH,
    )


def part(ref, *index):
    return lambda: ref.at[index]


def whole(ref):
    return lambda: ref


class Places:
    def __init__(self):
        self.e = e = lax.axis_index("exp")
        self.h = h = lax.axis_index("head")
        x, y, self.z = e % 2, (e // 2) % 2, e // 4
        z = self.z
        over_x, over_y = e + 1 - 2 * x, e + 2 - 4 * y
        self.near_e = over_x * (1 - h) + over_y * h
        self.far_e = over_y * (1 - h) + over_x * h
        self.near = (self.near_e, h)
        self.far = (self.far_e, h)
        self.outer = (1 + z % 2 + z // 2) % 2
        self.ranks = [z, z + 1 - 2 * (z % 2), 2 - z // 2, 3 - 3 * (z // 2)]
        self.along = [(rank * 4 + e % 4, h) for rank in self.ranks]
        self.edge = self.along[1]
        self.inner = ((3 - z) * 4 + e % 4, h)
        self.pair = (e, 1 - h)
        self.is_inner = (z == 1) | (z == 2)

    def hello(self):
        barrier = pltpu.get_barrier_semaphore()
        for device in (self.pair, self.near, self.far, *self.along[1:]):
            pl.semaphore_signal(barrier, inc=1, device_id=device, device_id_type=MESH)

    def ready(self):
        pl.semaphore_wait(pltpu.get_barrier_semaphore(), 6)


class Links:
    def __init__(self, places, send, recv):
        self.places, self.send, self.recv = places, send, recv
        self.sent, self.names = 0, {}
        self.pending = {"all": [], "inner": []}

    def number(self, name):
        return self.names.setdefault(name, len(self.names))

    def go(self, name, source, target, device, who="all", number=None):
        arrival = self.number(name) if number is None else number
        number = self.sent
        remote(
            source(), target(), self.send.at[number], self.recv.at[arrival], device
        ).start()
        self.sent += 1
        self.pending[who].append((number, name, source))

    def got(self, name, target):
        remote(
            target(), target(), self.send.at[0], self.recv.at[self.number(name)], self.places.near
        ).wait_recv()

    def sent_all(self, who, of):
        for number, name, source in self.pending[who]:
            if of is None or name[0] == of:
                remote(
                    source(), source(), self.send.at[number], self.recv.at[0], self.places.near
                ).wait_send()

    def drain(self, of=None):
        self.sent_all("all", of)

        @pl.when(self.places.is_inner)
        def _():
            self.sent_all("inner", of)

        for who, sent in self.pending.items():
            self.pending[who] = [one for one in sent if of is not None and one[1][0] != of]


class Spread:
    def __init__(self, links, name, gathered, pieces=(slice(None),)):
        self.links, self.name, self.gathered, self.pieces = links, name, gathered, pieces

    def spot(self, i, a, n):
        return part(self.gathered, i, a, self.pieces[n])

    def start(self):
        links, places = self.links, self.links.places
        for n in range(len(self.pieces)):
            block = self.spot(0, 0, n)
            links.go((self.name, "z", 1, n), block, self.spot(1, 0, n), places.edge)
            links.go((self.name, "n", 0, n), block, self.spot(0, 1, n), places.near)

            @pl.when(places.is_inner)
            def _():
                links.go(
                    (self.name, "z", 2, n), block, self.spot(2, 0, n), places.inner, "inner"
                )

    def pass_on(self, i):
        links, places = self.links, self.links.places
        there = {1: 3, 2: 2, 3: 3}[i]
        device = places.inner if i == 1 else places.edge
        for n in range(len(self.pieces)):
            block = self.spot(i, 0, n)
            links.got((self.name, "z", i, n), block)

            @pl.when(places.is_inner)
            def _():
                links.go(
                    (self.name, "z", there, n), block, self.spot(there, 0, n), device, "inner"
                )

            links.go((self.name, "n", i, n), block, self.spot(i, 1, n), places.near)

    def wait(self, i):
        for n in range(len(self.pieces)):
            self.links.got((self.name, "n", i, n), self.spot(i, 1, n))


class Gather:
    def __init__(self, links, name, send, recv, pieces):
        self.links, self.name, self.send, self.recv, self.pieces = links, name, send, recv, pieces
        for n in range(len(pieces)):
            for slot in (1, 2, 3):
                links.number((name, n, slot))

    def push(self, i, value):
        links, places = self.links, self.links.places
        for n, piece in enumerate(self.pieces):
            spot = part(self.send, i, piece)
            spot()[...] = value(n).astype(self.send.dtype)
            slot = 1 if i == 1 else 2 + places.outer
            links.go(
                (self.name, n, 1),
                spot,
                part(self.recv, slot, piece),
                places.along[i],
                number=links.number((self.name, n, 1)) + slot - 1,
            )

    def total(self, own, result):
        for n, piece in enumerate(self.pieces):
            value = own(n)
            for slot in (1, 2, 3):
                spot = part(self.recv, slot, piece)
                self.links.got((self.name, n, slot), spot)
                value = value + spot()[...].astype(FULL)
            result(n)[...] = value


def table_rows(tables, i, places):
    rows = []
    for chip in (places.e, places.far_e):
        for j in range(2):
            rows.append(
                jnp.concatenate(
                    [tables[i, a, pl.ds(2 * chip + j, 1), :] for a in range(2)], axis=1
                )
            )
    return rows


def selection(tables, i, places):
    slot = lax.broadcasted_iota(jnp.int32, (PAIR, 2 * FLAT), 0)
    lane = lax.broadcasted_iota(jnp.int32, (PAIR, 2 * FLAT), 1)
    wanted = (slot - jnp.where(lane >= FLAT, SLOTS, 0)).astype(FULL)
    return jnp.concatenate(
        [jnp.where(row == wanted, 1.0, 0.0) for row in table_rows(tables, i, places)], axis=0
    )


def turn(block, cosine, sine, sign):
    lane = lax.broadcasted_iota(jnp.int32, block.shape, 1) % HEAD_DIMENSION
    quarter = HEAD_DIMENSION // 2
    other = jnp.where(
        lane < quarter,
        -sign * pltpu.roll(block, FLAT - quarter, 1),
        sign * pltpu.roll(block, quarter, 1),
    )
    return block * cosine + other * sine


def layer_kernel(names, *refs):
    r = types.SimpleNamespace(**dict(zip(names, refs, strict=True)))
    places = Places()
    h, e, z = places.h, places.e, places.z
    places.hello()
    links = Links(places, r.sems_send, r.sems_recv)
    experts = r.w_router.shape[0]
    rows_here, width = r.tokens.shape
    q_cols, k_cols = r.w_query.shape[1], r.key_weight.shape[1]
    kv_heads = k_cols // HEAD_DIMENSION
    every = slice(None)
    half = pl.multiple_of(h * FLAT, FLAT)
    other_half = pl.multiple_of((1 - h) * FLAT, FLAT)
    locals_used = [0]

    def load(source, target):
        copy = pltpu.make_async_copy(source, target, r.sems_local.at[locals_used[0]])
        locals_used[0] += 1
        copy.start()
        return copy

    in_loads = [
        load(r.w_query, r.w_in.at[:, :q_cols]),
        load(r.key_weight, r.w_in.at[:, q_cols : q_cols + k_cols]),
        load(r.value_weight, r.w_in.at[:, q_cols + k_cols :]),
    ]
    out_load = load(r.w_output, r.w_out)
    expert_loads = [load(r.w_gate, r.gate_w), load(r.w_up, r.up_w), load(r.w_down, r.down_w)]
    rank_row = r.priority[...]
    row_id = lax.broadcasted_iota(jnp.int32, (FLAT, FLAT), 0)
    col_id = lax.broadcasted_iota(jnp.int32, (FLAT, FLAT), 1)
    rank_col = jnp.sum(
        jnp.where(row_id == col_id, jnp.broadcast_to(rank_row, (FLAT, FLAT)), 0),
        axis=1,
        keepdims=True,
    )
    earlier = jnp.where(rank_row < rank_col, 1.0, 0.0).astype(LOW)
    expert_id = lax.broadcasted_iota(jnp.int32, (experts, FLAT), 0)
    my_routes = r.routes[:, pl.ds(half, FLAT)]
    member = jnp.zeros((experts, FLAT), FULL)
    for k in range(TOPK):
        member += jnp.where(my_routes[k : k + 1, :] == expert_id, 1.0, 0.0)
    before = mul(member.astype(LOW), earlier, LAST)
    r.tables[0, 0] = jnp.where((member > 0.5) & (before < SLOTS), before, UNKEPT)
    r.g_all[0, 0] = (RESIDUAL_SCALE * r.cotangent[...].astype(FULL)).astype(LOW)
    halves = [slice(0, FLAT // 2), slice(FLAT // 2, FLAT)]
    t_spread = Spread(links, "t", r.tables)
    g_spread = Spread(links, "g", r.g_all, halves)
    x_spread = Spread(links, "x", r.x_all, halves)
    p_spread = Spread(links, "p", r.gate_tables)
    x_full = r.tokens[...].astype(FULL)
    r.normed[...] = rms_scale(x_full, r.norm_one[...]).astype(LOW)
    places.ready()
    t_spread.start()
    g_spread.start()

    for copy in in_loads:
        copy.wait()
    projected = mul(r.normed[...], r.w_in[...])
    cosine, sine = r.cosine[...], r.sine[...]
    lane = lax.broadcasted_iota(jnp.int32, (rows_here, FLAT), 1)
    low_lanes = lane < HEAD_DIMENSION
    for g in range(kv_heads):
        r.q[g] = turn(projected[:, g * FLAT : (g + 1) * FLAT], cosine, sine, 1.0).astype(LOW)
    for m in range(kv_heads // 2):
        start = q_cols + m * FLAT
        keys = turn(projected[:, start : start + FLAT], cosine, sine, 1.0)
        start += k_cols
        values = projected[:, start : start + FLAT]
        for block, store in ((keys, r.keys), (values, r.values)):
            rolled = pltpu.roll(block, HEAD_DIMENSION, 1)
            store[2 * m, 0] = jnp.where(low_lanes, block, 0.0).astype(LOW)
            store[2 * m, 1] = jnp.where(low_lanes, 0.0, rolled).astype(LOW)
            store[2 * m + 1, 0] = jnp.where(low_lanes, rolled, 0.0).astype(LOW)
            store[2 * m + 1, 1] = jnp.where(low_lanes, 0.0, block).astype(LOW)
    prompt, cont = rows_here // 2, rows_here // 4
    query_id = lax.broadcasted_iota(jnp.int32, (rows_here, rows_here), 0)
    key_id = lax.broadcasted_iota(jnp.int32, (rows_here, rows_here), 1)
    query_cont = jnp.where(query_id < prompt, 0, 1 + (query_id - prompt) // cont)
    key_cont = jnp.where(key_id < prompt, 0, 1 + (key_id - prompt) // cont)
    visible = ((key_cont == 0) & (query_cont > 0)) | (
        (key_cont == query_cont) & (key_id <= query_id)
    )
    r.bias[...] = jnp.where(visible, 0.0, MASKED_SCORE)

    def attend(first, count):
        def one(g, carry):
            mixed = jnp.zeros((rows_here, FLAT), FULL)
            for s in range(2):
                raw = mul(r.q[g], r.keys[g, s], LAST) * ATTENTION_SCALE
                scores = jnp.where(r.bias[...] < 0.0, MASKED_SCORE, raw)
                weights = jnp.exp(scores - jnp.max(scores, axis=1, keepdims=True))
                probs = weights / jnp.sum(weights, axis=1, keepdims=True)
                r.att_probs[g, s] = probs
                mixed += mul(probs.astype(LOW), r.values[g, s])
            r.heads[:, pl.ds(pl.multiple_of(g * FLAT, FLAT), FLAT)] = mixed.astype(LOW)
            return carry

        lax.fori_loop(first, first + count, one, 0)

    def dispatch_out(i):
        t_spread.wait(i)
        g_spread.wait(i)
        picks = selection(r.tables, i, places).astype(LOW)
        r.pick[i] = picks
        rows = mul(picks, r.g_all[i].reshape(2 * FLAT, -1)).astype(LOW)
        r.g_slots[i] = rows[: 2 * PAIR].reshape(2, PAIR, -1)
        r.g_send[i] = rows[2 * PAIR :].reshape(2, PAIR, -1)
        links.go(("g", "f", i), part(r.g_send, i), part(r.g_slots, 4 + i), places.far)

    def pass_out(i):
        t_spread.pass_on(i)
        g_spread.pass_on(i)

    attend(0, 4)
    out_load.wait()
    r.branch_send[...] = mul(r.heads[pl.ds(other_half, FLAT), :], r.w_out[...])
    links.go("branch", whole(r.branch_send), whole(r.branch_in), places.pair)
    own_branch = mul(r.heads[pl.ds(half, FLAT), :], r.w_out[...])
    pass_out(1)
    dispatch_out(0)
    links.got("branch", whole(r.branch_in))
    middle = r.tokens[pl.ds(half, FLAT), :].astype(FULL) + RESIDUAL_SCALE * (
        own_branch + r.branch_in[...]
    )
    r.middle[...] = middle
    xn = rms_scale(middle, r.norm_two[...]).astype(LOW)
    r.x_all[0, 0] = xn
    x_spread.start()
    logits = mul(r.w_router[...], xn, LAST)
    chosen = jnp.where(member > 0.5, logits, MASKED_SCORE)
    weights = jnp.exp(chosen - jnp.max(chosen, axis=0, keepdims=True))
    probs = weights / jnp.sum(weights, axis=0, keepdims=True)
    r.probs[...] = probs
    r.gate_tables[0, 0] = probs.astype(LOW).astype(FULL)
    p_spread.start()

    slots_lane = lax.broadcasted_iota(jnp.int32, (2 * PAIR, FLAT), 1)
    r.gates[...] = jnp.zeros((2 * PAIR, FLAT), FULL)
    r.gate_send[...] = jnp.zeros((2 * PAIR, FLAT), FULL)

    def dispatch_in(i):
        x_spread.wait(i)
        picks = r.pick[i]
        rows = mul(picks, r.x_all[i].reshape(2 * FLAT, -1)).astype(LOW)
        r.x_slots[i] = rows[: 2 * PAIR].reshape(2, PAIR, -1)
        r.x_send[i] = rows[2 * PAIR :].reshape(2, PAIR, -1)
        links.go(("x", "f", i), part(r.x_send, i), part(r.x_slots, 4 + i), places.far)
        p_spread.wait(i)
        spread_gates = jnp.concatenate(
            [
                jnp.broadcast_to(row, (PAIR, 2 * FLAT))
                for row in table_rows(r.gate_tables, i, places)
            ],
            axis=0,
        )
        slot_gates = jnp.sum(picks.astype(FULL) * spread_gates, axis=1, keepdims=True)
        r.gates[...] += jnp.where(slots_lane == i, slot_gates[: 2 * PAIR], 0.0)
        r.gate_send[...] += jnp.where(slots_lane == 4 + i, slot_gates[2 * PAIR :], 0.0)

    def pass_in(i):
        x_spread.pass_on(i)
        p_spread.pass_on(i)

    pass_out(2)
    dispatch_out(1)
    pass_out(3)
    dispatch_in(0)
    dispatch_out(2)
    pass_in(1)
    pass_in(2)
    dispatch_out(3)
    dispatch_in(1)
    pass_in(3)
    dispatch_in(2)
    dispatch_in(3)
    links.go(("p", "f"), whole(r.gate_send), whole(r.gate_far), places.far)

    slot_lane = lax.broadcasted_iota(jnp.int32, (PAIR, FLAT), 1)
    r.parts[...] = jnp.zeros((2 * PAIR, FLAT), FULL)

    def run_experts(first, count):
        span = count * PAIR
        which = slice(first, first + count)
        place = slice(first * PAIR, (first + count) * PAIR)

        def one_expert(j, carry):
            base = pl.multiple_of(j * PAIR, PAIR)
            gates = r.gates[pl.ds(base, PAIR), :]
            gate_col = jnp.concatenate(
                [gates[:, p : p + 1] for p in range(first, first + count)], axis=0
            )
            columns = pl.ds(pl.multiple_of(j * FF, FF), FF)
            xs = r.x_slots[which, j].reshape(span, -1)
            gate_pre = mul(xs, r.gate_w[:, columns])
            up_pre = mul(xs, r.up_w[:, columns])
            sig = jax.nn.sigmoid(gate_pre)
            act = gate_pre * sig
            hidden = (act * up_pre).astype(LOW)
            r.hidden_all[j, place] = hidden
            result = mul(hidden, r.down_w[columns, :])
            gs = r.g_slots[which, j].reshape(span, -1).astype(FULL)
            r.g_slots[which, j] = (gate_col * result).astype(LOW).reshape(count, PAIR, -1)
            part = jnp.sum(gs * result, axis=1, keepdims=True).astype(LOW).astype(FULL)
            terms = jnp.zeros((PAIR, FLAT), FULL)
            for p in range(count):
                terms += jnp.where(
                    slot_lane == first + p, part[p * PAIR : (p + 1) * PAIR], 0.0
                )
            r.parts[pl.ds(base, PAIR), :] += terms
            result_grad = (gate_col * gs).astype(LOW)
            r.result_all[j, place] = result_grad
            hidden_grad = mul(result_grad, r.down_w[columns, :], LAST)
            gate_pre_grad = (
                hidden_grad * up_pre * sig * (1.0 + gate_pre * (1.0 - sig))
            ).astype(LOW)
            up_pre_grad = (hidden_grad * act).astype(LOW)
            r.gate_all[j, place] = gate_pre_grad
            r.up_all[j, place] = up_pre_grad
            rows_grad = mul(gate_pre_grad, r.gate_w[:, columns], LAST) + mul(
                up_pre_grad, r.up_w[:, columns], LAST
            )
            r.row_slots[which, j] = rows_grad.astype(LOW).reshape(count, PAIR, -1)
            return carry

        lax.fori_loop(0, 2, one_expert, 0)

    for copy in expert_loads:
        copy.wait()
    run_experts(0, 4)
    links.got(("p", "f"), whole(r.gate_far))
    r.gates[...] += r.gate_far[...]
    writes = []

    def weight_grads(j):
        xs = r.x_slots[:, j].reshape(8 * PAIR, -1)
        columns = slice(j * FF, (j + 1) * FF)
        r.gate_w[:, columns] = mul(xs, r.gate_all[j], FIRST).astype(LOW)
        r.up_w[:, columns] = mul(xs, r.up_all[j], FIRST).astype(LOW)
        r.down_w[columns, :] = mul(r.hidden_all[j], r.result_all[j], FIRST).astype(LOW)

    def send_grads(j):
        columns = slice(j * FF, (j + 1) * FF)
        for n, (source, own, other) in enumerate(
            (
                (
                    part(r.gate_w, every, columns),
                    part(r.gate_own, every, columns),
                    part(r.gate_other, every, columns),
                ),
                (
                    part(r.up_w, every, columns),
                    part(r.up_own, every, columns),
                    part(r.up_other, every, columns),
                ),
                (part(r.down_w, columns), part(r.down_own, columns), part(r.down_other, columns)),
            )
        ):
            writes.append(load(source(), own()))
            links.go(("e", j, n), source, other, places.pair)


    index = lax.broadcasted_iota(jnp.int32, (experts, 2 * FLAT), 0)

    def fold(name, rows, rows_in, kept, near_send, near_in, i):
        links.got((name, "f", i), part(rows_in, i))
        send = near_send(i)
        stacked = jnp.concatenate(
            [rows[i].reshape(2 * PAIR, -1), rows_in[i].reshape(2 * PAIR, -1)], axis=0
        )
        sums = mul(r.pick[i], stacked, FIRST)
        kept[i] = sums[:FLAT]
        send()[...] = sums[FLAT:].astype(LOW)
        links.go((name, "n", i), send, part(near_in, i), places.near)

    def fold_parts(i):
        column = jnp.concatenate(
            [r.parts[:, i : i + 1], r.parts_in[:, 4 + i : 5 + i]], axis=0
        )
        terms = r.pick[i].astype(FULL) * column
        table = jnp.zeros((experts, 2 * FLAT), FULL)
        chips = (places.e, places.e, places.far_e, places.far_e)
        for n, chip in enumerate(chips):
            total = jnp.sum(terms[n * PAIR : (n + 1) * PAIR], axis=0, keepdims=True)
            table += jnp.where(index == 2 * chip + n % 2, total, 0.0)
        r.part_kept[i] = table[:, :FLAT]
        r.part_send[i] = table[:, FLAT:]
        links.go(("q", "n", i), part(r.part_send, i), part(r.part_near, i), places.near)

    row_sums = Gather(links, "rz", r.row_z_send, r.row_z_in, halves)
    part_sums = Gather(links, "qz", r.part_z_send, r.part_z_in, [slice(0, experts)])
    weighted_sums = Gather(links, "wz", r.row_near_send, r.weighted_z_in, halves)

    def near_sum(name, kept, near_in, i, pieces):
        links.got((name, "n", i), part(near_in, i))
        return lambda n: kept[i, pieces[n]] + near_in[i, pieces[n]].astype(FULL)

    def settle_rows(i):
        row_sums.push(i, near_sum("r", r.row_kept, r.row_near, i, row_sums.pieces))

    def settle_parts(i):
        part_sums.push(i, near_sum("q", r.part_kept, r.part_near, i, part_sums.pieces))

    def settle_weighted(i):
        weighted_sums.push(i, near_sum("w", r.row_kept, r.weighted_near, i, halves))

    def fold_weighted(i):
        fold(
            "w",
            r.g_slots,
            r.g_send,
            r.row_kept,
            lambda i: part(r.x_all, i, 0),
            r.weighted_near,
            i,
        )

    def far_experts(i):
        links.got(("g", "f", i), part(r.g_slots, 4 + i))
        links.got(("x", "f", i), part(r.x_slots, 4 + i))
        run_experts(4 + i, 1)
        links.go(("r", "f", i), part(r.row_slots, 4 + i), part(r.rows_in, i), places.far)

    def fold_rows(i):
        fold(
            "r",
            r.row_slots,
            r.rows_in,
            r.row_kept,
            lambda i: part(r.row_near_send, i),
            r.row_near,
            i,
        )

    links.drain()
    far_experts(0)
    far_experts(3)
    far_experts(2)
    fold_rows(3)
    far_experts(1)
    links.go(("q", "f"), whole(r.parts), whole(r.parts_in), places.far)
    fold_rows(2)
    settle_rows(3)
    fold_rows(1)
    settle_rows(2)
    fold_rows(0)
    for i in (3, 2, 1, 0):
        links.go(("w", "f", i), part(r.g_slots, 4 + i), part(r.g_send, i), places.far)
    settle_rows(1)
    links.got(("q", "f"), whole(r.parts_in))
    for i in (3, 2, 1, 0):
        fold_parts(i)
    for i in (3, 2, 1):
        settle_parts(i)
    weight_grads(0)
    send_grads(0)
    fold_weighted(3)
    fold_weighted(2)
    weight_grads(1)
    fold_weighted(1)
    row_sums.total(
        near_sum("r", r.row_kept, r.row_near, 0, halves), lambda n: r.branch_in.at[halves[n]]
    )
    part_sums.total(
        near_sum("q", r.part_kept, r.part_near, 0, part_sums.pieces), lambda n: r.part_total
    )

    gate_probs, gate_grad = r.probs[...], r.part_total[...]
    chosen_grad = gate_probs * (
        gate_grad - jnp.sum(gate_probs * gate_grad, axis=0, keepdims=True)
    )
    logit_grad = chosen_grad.astype(LOW)
    xn_grad = r.branch_in[...] + mul(logit_grad, r.w_router[...], FIRST)
    mid = r.middle[...]
    scale = lax.rsqrt(jnp.mean(mid * mid, axis=-1, keepdims=True) + NORM_EPS)
    scaled = r.norm_two[...] * xn_grad
    pull = jnp.mean(scaled * mid, axis=-1, keepdims=True)
    grad = r.cotangent[...].astype(FULL) + scale * scaled - mid * (scale * scale * scale * pull)
    r.grad_tokens[...] = grad
    mine = part(r.branch_grad, pl.ds(half, FLAT))
    r.branch_grad[pl.ds(half, FLAT), :] = (RESIDUAL_SCALE * grad).astype(LOW)
    links.go("bg", mine, mine, places.pair)
    r.small[pl.ds(0, experts), :] = mul(logit_grad, r.x_all[0, 0])
    r.small[pl.ds(experts, 8), :] = jnp.broadcast_to(
        jnp.sum(xn_grad * mid * scale, axis=0, keepdims=True), (8, width)
    )

    links.drain("r")
    for i in (3, 2, 1):
        settle_weighted(i)
    fold_weighted(0)
    links.got("bg", part(r.branch_grad, pl.ds(other_half, FLAT)))
    r.heads_grad[...] = mul(r.branch_grad[...], r.w_out[...], LAST).astype(LOW)
    r.grads[pl.ds(width, q_cols), :] = mul(r.heads[...], r.branch_grad[...], FIRST).astype(LOW)
    cosine, sine = r.cosine[...], r.sine[...]

    def attend_back(first, count):
        def one(g, carry):
            place = pl.ds(pl.multiple_of(g * FLAT, FLAT), FLAT)
            out_grad = r.heads_grad[:, place]
            query = r.q[g]
            query_grad = jnp.zeros((rows_here, FLAT), FULL)
            key_grads, value_grads = [], []
            for s in range(2):
                probs = r.att_probs[g, s]
                prob_grad = mul(out_grad, r.values[g, s], LAST)
                inner = jnp.sum(probs * prob_grad, axis=1, keepdims=True)
                score_grad = (probs * (prob_grad - inner)).astype(LOW)
                query_grad += mul(score_grad, r.keys[g, s])
                key_grads.append(mul(score_grad, query, FIRST))
                value_grads.append(mul(probs.astype(LOW), out_grad, FIRST))
            r.head_grads[:, place] = turn(
                query_grad * ATTENTION_SCALE, r.cosine[...], r.sine[...], -1.0
            ).astype(LOW)
            r.key_sums[g] = key_grads[0] + pltpu.roll(key_grads[1], HEAD_DIMENSION, 1)
            r.value_sums[g] = value_grads[0] + pltpu.roll(value_grads[1], HEAD_DIMENSION, 1)
            return carry

        lax.fori_loop(first, first + count, one, 0)

    ranks = places.ranks
    plane = [[e % 4, places.near_e % 4], [places.far_e % 4, 3 - e % 4]]

    def along(name, spot):
        block = spot(0)
        links.go((name, "z", 1), block, block, places.edge)

        @pl.when(places.is_inner)
        def _():
            links.go((name, "z", 2), block, block, places.inner, "inner")

    def pass_along(name, spot, i):
        block = spot(i)
        links.got((name, "z", i), block)
        there = {1: 3, 2: 2, 3: 3}[i]
        device = places.inner if i == 1 else places.edge

        @pl.when(places.is_inner)
        def _():
            links.go((name, "z", there), block, block, device, "inner")

    class Reduce:
        order = [(a, i) for i in (3, 2, 1, 0) for a in (1, 0)]

        def __init__(self, name, first, count, room):
            self.name, self.first, self.depth, self.room = name, first, count // 16, room
            self.rows = slice(room, room + self.depth)
            self.issued = 0
            self.sums = Gather(links, name + "z", r.sum_z_send, r.sum_z_in, [self.rows])

        def shard(self, b, a, i):
            start = self.first + (ranks[i] * 4 + plane[b][a]) * self.depth
            return pl.ds(pl.multiple_of(start, 16), self.depth)

        def far_in(self, a, i):
            return part(r.g_all, i, a, self.rows)

        def near_in(self, i):
            return part(r.x_all, i, 1, self.rows)

        def near_send(self, i):
            return part(r.result_all, 0, pl.ds(4 * self.room + i * self.depth, self.depth))

        def send(self, count):
            for a, i in self.order[self.issued : self.issued + count]:
                source = part(r.grads, self.shard(1, a, i))
                links.go((self.name, "f", a, i), source, self.far_in(a, i), places.far)
            self.issued += count

        def fold(self, i):
            for a in (1, 0):
                links.got((self.name, "f", a, i), self.far_in(a, i))
                self.send(1)
                if a:
                    total = r.grads[self.shard(0, 1, i), :].astype(FULL) + r.g_all[
                        i, 1, self.rows
                    ].astype(FULL)
                    self.near_send(i)()[...] = total.astype(LOW)
                    links.go(
                        (self.name, "n", i), self.near_send(i), self.near_in(i), places.near
                    )

        def near_sum(self, i):
            links.got((self.name, "n", i), self.near_in(i))
            mine = self.shard(0, 0, i)
            return lambda n: (
                r.grads[mine, :].astype(FULL)
                + r.g_all[i, 0, self.rows].astype(FULL)
                + r.x_all[i, 1, self.rows].astype(FULL)
            )

        def settle(self, i):
            self.sums.push(i, self.near_sum(i))

        def spot(self, b, a, i):
            return part(r.grads_out, self.shard(b, a, i))

        def share(self):
            total = r.branch_send.at[self.rows]
            self.sums.total(self.near_sum(0), lambda n: total)
            low = part(r.result_all, 1, pl.ds(FLAT + self.room, self.depth))
            low()[...] = total[...].astype(LOW)
            mine = self.spot(0, 0, 0)
            links.go((self.name + "o", "z", 1), low, mine, places.edge)
            links.go((self.name, "on", 0), low, mine, places.near)

            @pl.when(places.is_inner)
            def _():
                links.go((self.name + "o", "z", 2), low, mine, places.inner, "inner")

            links.go((self.name, "of", 0, 0), low, mine, places.far)
            writes.append(load(low(), mine()))

        def pass_far(self, i):
            block = self.spot(0, 1, i)
            links.got((self.name, "on", i), block)
            links.go((self.name, "of", 1, i), block, block, places.far)

        def pass_on(self, i):
            block = self.spot(0, 0, i)
            pass_along(self.name + "o", lambda i: self.spot(0, 0, i), i)
            links.go((self.name, "on", i), block, block, places.near)
            links.go((self.name, "of", 0, i), block, block, places.far)

        def finish(self):
            for i in range(4):
                for a in range(2):
                    links.got((self.name, "of", a, i), self.spot(1, a, i))

    late = Reduce("b", width, q_cols, 0)
    early = Reduce("a", 0, width, q_cols // 16)
    late.send(8)
    attend_back(0, 4)
    for m in range(kv_heads // 2):
        start = q_cols + m * FLAT
        for sums, shift in ((r.key_sums, 0), (r.value_sums, k_cols)):
            block = jnp.where(
                low_lanes, sums[2 * m], pltpu.roll(sums[2 * m + 1], HEAD_DIMENSION, 1)
            )
            if shift == 0:
                block = turn(block * ATTENTION_SCALE, cosine, sine, -1.0)
            r.head_grads[:, start + shift : start + shift + FLAT] = block.astype(LOW)
    head_grads = r.head_grads
    r.grads[pl.ds(0, width), :] = mul(r.normed[...], head_grads[...], FIRST).astype(LOW)
    early.send(4)
    r.result_all[1, 0:FLAT] = mul(
        head_grads[pl.ds(other_half, FLAT), :], r.w_in[...], LAST
    ).astype(LOW)
    links.go("terms", part(r.result_all, 1, pl.ds(0, FLAT)), whole(r.terms_in), places.pair)
    own_terms = mul(head_grads[pl.ds(half, FLAT), :], r.w_in[...], LAST).astype(LOW)
    send_grads(1)
    late.fold(3)
    late.fold(2)
    late.fold(1)
    late.fold(0)
    early.fold(3)
    early.fold(2)
    late.settle(3)
    late.settle(2)
    late.settle(1)
    early.settle(3)
    early.fold(1)
    early.settle(2)
    early.fold(0)
    early.settle(1)
    late.share()
    links.got("terms", whole(r.terms_in))
    xn_grad = (own_terms.astype(FULL) + r.terms_in[...].astype(FULL)).astype(LOW).astype(FULL)
    x_half = r.tokens[pl.ds(half, FLAT), :].astype(FULL)
    scale = lax.rsqrt(jnp.mean(x_half * x_half, axis=-1, keepdims=True) + NORM_EPS)
    scaled = r.norm_one[...] * xn_grad
    pull = jnp.mean(scaled * x_half, axis=-1, keepdims=True)
    r.grad_tokens[...] = (
        r.grad_tokens[...] + scale * scaled - x_half * (scale * scale * scale * pull)
    )
    r.small_mine[0, pl.ds(0, experts), :] = r.small[pl.ds(0, experts), :]
    row = lax.broadcasted_iota(jnp.int32, (8, width), 0)
    r.small_mine[0, pl.ds(experts, 8), :] = jnp.where(
        row == 0,
        r.small[pl.ds(experts, 8), :],
        jnp.sum(xn_grad * x_half * scale, axis=0, keepdims=True),
    )
    links.go(("s", 0), part(r.small_mine, 0), part(r.small_in, 0), places.pair)
    late.pass_far(0)
    late.pass_on(1)
    early.share()
    links.got(("s", 0), part(r.small_in, 0))
    r.small_mine[1] = r.small_mine[0] + r.small_in[0]
    links.go(("s", 1), part(r.small_mine, 1), part(r.small_in, 1), places.far)
    late.pass_far(1)
    late.pass_on(2)
    early.pass_far(0)
    late.pass_far(2)
    late.pass_on(3)
    late.pass_far(3)
    links.got(("s", 1), part(r.small_in, 1))
    r.small_mine[2] = r.small_mine[1] + r.small_in[1]
    links.go(("s", 2), part(r.small_mine, 2), part(r.small_in, 2), places.near)
    early.pass_on(1)
    early.pass_far(1)
    early.pass_on(2)
    links.got(("s", 2), part(r.small_in, 2))
    r.small_all[z] = r.small_mine[2] + r.small_in[2]
    along("s", lambda i: part(r.small_all, ranks[i]))
    early.pass_far(2)
    early.pass_on(3)
    early.pass_far(3)
    weighted_sums.total(
        near_sum("w", r.row_kept, r.weighted_near, 0, halves),
        lambda n: r.branch_in.at[halves[n]],
    )
    r.layer_out[...] = (r.middle[...] + RESIDUAL_SCALE * r.branch_in[...]).astype(LOW)

    for i in (1, 2, 3):
        pass_along("s", lambda i: part(r.small_all, ranks[i]), i)
    r.small_out[...] = ((r.small_all[0] + r.small_all[1]) + r.small_all[2]) + r.small_all[3]
    late.finish()
    early.finish()
    for j in range(2):
        columns = slice(j * FF, (j + 1) * FF)
        links.got(("e", j, 0), part(r.gate_other, every, columns))
        links.got(("e", j, 1), part(r.up_other, every, columns))
        links.got(("e", j, 2), part(r.down_other, columns))
    for copy in writes:
        copy.wait()
    links.drain()


def run_layer(**inputs):
    rows_here, width = inputs["tokens"].shape
    experts = inputs["w_router"].shape[0]
    q_cols, k_cols = inputs["w_query"].shape[1], inputs["key_weight"].shape[1]
    kv_heads = k_cols // HEAD_DIMENSION
    vmem = pl.BlockSpec(memory_space=pltpu.VMEM)
    anywhere = pl.BlockSpec(memory_space=pl.ANY)
    block = (FLAT, width)
    gate = (experts, FLAT)
    slots = (2, PAIR, width)
    small = (experts + 8, width)
    grads = (width + q_cols, width)
    depth = grads[0] // 16
    outputs = {
        "layer_out": (block, LOW),
        "grad_tokens": (block, FULL),
        "small_out": (small, FULL),
    }
    held = {"grads_out": (grads, LOW)} | {
        name + end: (inputs["w_" + name].shape, LOW)
        for end in ("_own", "_other")
        for name in ("gate", "up", "down")
    }
    heads = (kv_heads, 2, rows_here)
    scratch = {
        "w_in": ((width, q_cols + 2 * k_cols), LOW),
        "w_out": ((q_cols, width), LOW),
        "normed": ((rows_here, width), LOW),
        "q": ((kv_heads, rows_here, FLAT), LOW),
        "keys": (heads + (FLAT,), LOW),
        "values": (heads + (FLAT,), LOW),
        "bias": ((rows_here, rows_here), FULL),
        "att_probs": (heads + (rows_here,), FULL),
        "heads": ((rows_here, q_cols), LOW),
        "heads_grad": ((rows_here, q_cols), LOW),
        "head_grads": ((rows_here, q_cols + 2 * k_cols), LOW),
        "key_sums": ((kv_heads, rows_here, FLAT), FULL),
        "value_sums": ((kv_heads, rows_here, FLAT), FULL),
        "branch_send": (block, FULL),
        "branch_in": (block, FULL),
        "middle": (block, FULL),
        "branch_grad": ((rows_here, width), LOW),
        "small": (small, FULL),
        "terms_in": (block, LOW),
        "grads": (grads, LOW),
        "sum_z_send": ((4, depth, width), LOW),
        "sum_z_in": ((4, depth, width), LOW),
        "small_mine": ((3,) + small, FULL),
        "small_in": ((3,) + small, FULL),
        "small_all": ((4,) + small, FULL),
        "probs": (gate, FULL),
        "tables": ((4, 2) + gate, FULL),
        "gate_tables": ((4, 2) + gate, FULL),
        "g_all": ((4, 2) + block, LOW),
        "x_all": ((4, 2) + block, LOW),
        "g_slots": ((8,) + slots, LOW),
        "x_slots": ((8,) + slots, LOW),
        "row_slots": ((8,) + slots, LOW),
        "g_send": ((4,) + slots, LOW),
        "x_send": ((4,) + slots, LOW),
        "gates": ((2 * PAIR, FLAT), FULL),
        "gate_send": ((2 * PAIR, FLAT), FULL),
        "gate_far": ((2 * PAIR, FLAT), FULL),
        "parts": ((2 * PAIR, FLAT), FULL),
        "parts_in": ((2 * PAIR, FLAT), FULL),
        "pick": ((4, 4 * PAIR, 2 * FLAT), LOW),
        "gate_w": (inputs["w_gate"].shape, LOW),
        "up_w": (inputs["w_up"].shape, LOW),
        "down_w": (inputs["w_down"].shape, LOW),
        "hidden_all": ((2, 8 * PAIR, FF), LOW),
        "gate_all": ((2, 8 * PAIR, FF), LOW),
        "up_all": ((2, 8 * PAIR, FF), LOW),
        "result_all": ((2, 8 * PAIR, width), LOW),
        "rows_in": ((4,) + slots, LOW),
        "row_kept": ((4,) + block, FULL),
        "row_near": ((4,) + block, LOW),
        "row_near_send": ((4,) + block, LOW),
        "row_z_send": ((4,) + block, LOW),
        "row_z_in": ((4,) + block, LOW),
        "part_kept": ((4,) + gate, FULL),
        "part_near": ((4,) + gate, FULL),
        "part_send": ((4,) + gate, FULL),
        "part_z_send": ((4,) + gate, FULL),
        "part_z_in": ((4,) + gate, FULL),
        "part_total": (gate, FULL),
        "weighted_near": ((4,) + block, LOW),
        "weighted_z_in": ((4,) + block, LOW),
    }
    near_by = ("tokens", "norm_one", "norm_two", "w_router", "routes", "priority")
    near_by += ("cotangent", "cosine", "sine")
    names = [*inputs, *outputs, *held, *scratch, "sems_local", "sems_send", "sems_recv"]
    results = pl.pallas_call(
        functools.partial(layer_kernel, names),
        out_shape=[
            jax.ShapeDtypeStruct(shape, kind) for shape, kind in [*outputs.values(), *held.values()]
        ],
        in_specs=[vmem if name in near_by else anywhere for name in inputs],
        out_specs=[vmem] * len(outputs) + [anywhere] * len(held),
        scratch_shapes=[pltpu.VMEM(shape, kind) for shape, kind in scratch.values()]
        + [
            pltpu.SemaphoreType.DMA((20,)),
            pltpu.SemaphoreType.DMA((260,)),
            pltpu.SemaphoreType.DMA((220,)),
        ],
        compiler_params=pltpu.CompilerParams(
            collective_id=0, has_side_effects=True, vmem_limit_bytes=63 << 20
        ),
        name="layer",
    )(*inputs.values())
    return dict(zip([*outputs, *held], results))


def cast_kernel(
    gate_own, gate_other, up_own, up_other, down_own, down_other, first, second, *outs
):
    gate, up, down, query, key, value, output = outs
    pairs = ((gate, gate_own, gate_other), (up, up_own, up_other), (down, down_own, down_other))
    for out, own, other in pairs:
        out[...] = own[...].astype(FULL) + other[...].astype(FULL)
    q_cols, k_cols = query.shape[1], key.shape[1]
    query[...] = first[:, :q_cols].astype(FULL)
    key[...] = first[:, q_cols : q_cols + k_cols].astype(FULL)
    value[...] = first[:, q_cols + k_cols :].astype(FULL)
    output[...] = second[...].astype(FULL)


def cast_grads(done, q_cols, k_cols, steps=4):
    shape = done["gate_own"].shape
    rows = shape[0] // steps
    width = done["grads_out"].shape[1]
    tall, short = width // steps, q_cols // steps
    held = pl.BlockSpec((rows, shape[1]), lambda i: (i, 0))
    outs = [(shape, rows)] * 3
    outs += [((width, cols), tall) for cols in (q_cols, k_cols, k_cols)]
    outs += [((q_cols, width), short)]
    parts = [done[name + end] for name in ("gate", "up", "down") for end in ("_own", "_other")]
    return pl.pallas_call(
        cast_kernel,
        grid=(steps,),
        out_shape=[jax.ShapeDtypeStruct(size, FULL) for size, _ in outs],
        in_specs=[held] * 6
        + [
            pl.BlockSpec((tall, width), lambda i: (i, 0)),
            pl.BlockSpec((short, width), lambda i: (width // short + i, 0)),
        ],
        out_specs=[pl.BlockSpec((block, size[1]), lambda i: (i, 0)) for size, block in outs],
        name="cast_grads",
    )(*parts, done["grads_out"], done["grads_out"])


def quick_shards(
    tokens,
    norm_one,
    w_query,
    key_weight,
    value_weight,
    w_output,
    norm_two,
    w_router,
    w_gate,
    w_up,
    w_down,
    routes,
    priority,
    cotangent,
):
    rows_here, width = tokens.shape
    experts = w_router.shape[1]
    q_cols, k_cols = w_query.shape[1], key_weight.shape[1]
    local_index = np.arange(rows_here, dtype=np.int32)
    prompt_rows, cont_rows = rows_here // 2, rows_here // 4
    position = np.where(
        local_index < prompt_rows,
        local_index,
        prompt_rows + (local_index - prompt_rows) % cont_rows,
    )
    frequency = ROPE_BASE ** (
        -(2.0 * np.arange(HEAD_DIMENSION // 2, dtype=np.float32)) / HEAD_DIMENSION
    )
    frequency = frequency.astype(np.float32)
    angle_table = position.astype(np.float32)[:, None] * np.tile(frequency, 4)[None, :]
    done = run_layer(
        tokens=tokens,
        norm_one=norm_one[None, :],
        norm_two=norm_two[None, :],
        w_router=w_router.T,
        routes=routes.T,
        priority=priority,
        cotangent=cotangent,
        cosine=jnp.asarray(np.cos(angle_table), FULL),
        sine=jnp.asarray(np.sin(angle_table), FULL),
        w_query=w_query,
        key_weight=key_weight,
        value_weight=value_weight,
        w_output=w_output,
        w_gate=w_gate,
        w_up=w_up,
        w_down=w_down,
    )
    small = done["small_out"]
    gate, up, down, query, key, value, output = cast_grads(done, q_cols, k_cols)
    return (
        done["layer_out"],
        done["grad_tokens"],
        small[experts + 1],
        query,
        key,
        value,
        output,
        small[experts],
        small[:experts].T,
        gate,
        up,
        down,
    )


def solution(mesh):
    body = quick_shards if dict(mesh.shape) == {"exp": 16, "head": 2} else shards
    return jax.shard_map(
        body,
        mesh=mesh,
        in_specs=(
            P("exp", None),
            P(),
            P(None, "head"),
            P(None, "head"),
            P(None, "head"),
            P("head", None),
            P(),
            P(),
            P(None, "exp"),
            P(None, "exp"),
            P("exp", None),
            P("exp", None),
            P(("exp", "head"), None),
            P(("exp", "head"), None),
        ),
        out_specs=(
            P(("exp", "head"), None),
            P(("exp", "head"), None),
            P(),
            P(None, "head"),
            P(None, "head"),
            P(None, "head"),
            P("head", None),
            P(),
            P(),
            P(None, "exp"),
            P(None, "exp"),
            P("exp", None),
        ),
        check_vma=False,
    )
```

```python
import functools
import types

import jax
import jax.numpy as jnp
import numpy as np
from jax import lax
from jax.experimental import pallas as pl
from jax.experimental.pallas import tpu as pltpu
from jax.sharding import PartitionSpec as P

HEAD_DIMENSION = 64
FF = 512
TOPK = 8


RESIDUAL_SCALE = 0.22
ATTENTION_SCALE = 0.015625
ROPE_BASE = 10000.0
NORM_EPS = 1e-06
MASKED_SCORE = -1e30


def rms_scale(values, scale_row):
    return (
        values * lax.rsqrt(jnp.mean(values * values, axis=-1, keepdims=True) + NORM_EPS) * scale_row
    )


def apply_rotary(values, cosine_values, sine_values):
    half_width = values.shape[-1] // 2
    lower_part = values[..., :half_width]
    upper_part = values[..., half_width:]
    return jnp.concatenate(
        [
            lower_part * cosine_values - upper_part * sine_values,
            upper_part * cosine_values + lower_part * sine_values,
        ],
        axis=-1,
    )


def rotate_back(values, cosine_values, sine_values):
    half_width = values.shape[-1] // 2
    lower_part = values[..., :half_width]
    upper_part = values[..., half_width:]
    return jnp.concatenate(
        [
            lower_part * cosine_values + upper_part * sine_values,
            upper_part * cosine_values - lower_part * sine_values,
        ],
        axis=-1,
    )


def shards(
    tokens,
    norm_one,
    w_query,
    key_weight,
    value_weight,
    w_output,
    norm_two,
    w_router,
    w_gate,
    w_up,
    w_down,
    routes,
    priority,
    cotangent,
):
    tok_rows, model_width = tokens.shape
    heads_count = lax.axis_size("head")
    head_rank = lax.axis_index("head")
    exp_count = lax.axis_size("exp")
    half_rows = tok_rows // heads_count
    prompt_rows = tok_rows // 2
    cont_rows = tok_rows // 4
    kv_heads = key_weight.shape[1] // HEAD_DIMENSION
    query_groups = w_query.shape[1] // key_weight.shape[1]
    experts = w_router.shape[1]
    held_cols = w_gate.shape[1]
    held = max(1, held_cols // FF)
    split = max(1, FF // held_cols)
    block_width = held_cols // held
    capacity = max(2, (5 * half_rows * TOPK + 4 * experts - 1) // (4 * experts))
    rows_per_block = min(512, tok_rows)
    count_of_blocks = tok_rows // rows_per_block
    local_index = jnp.arange(tok_rows, dtype=jnp.int32)
    position = jnp.where(
        local_index < prompt_rows,
        local_index,
        prompt_rows + (local_index - prompt_rows) % cont_rows,
    )
    frequency = ROPE_BASE ** (
        -(2.0 * jnp.arange(HEAD_DIMENSION // 2, dtype=jnp.float32)) / HEAD_DIMENSION
    )
    angle_table = position.astype(jnp.float32)[:, None] * frequency[None, :]
    cosine_values = jnp.cos(angle_table)[:, None, :]
    sine_values = jnp.sin(angle_table)[:, None, :]
    x_full = tokens.astype(jnp.float32)
    normed_input_first = rms_scale(x_full, norm_one).astype(jnp.bfloat16)
    rotated_queries = apply_rotary(
        jnp.dot(normed_input_first, w_query, preferred_element_type=jnp.float32).reshape(
            tok_rows, -1, HEAD_DIMENSION
        ),
        cosine_values,
        sine_values,
    ).astype(jnp.bfloat16)
    keys_all = apply_rotary(
        jnp.dot(normed_input_first, key_weight, preferred_element_type=jnp.float32).reshape(
            tok_rows, -1, HEAD_DIMENSION
        ),
        cosine_values,
        sine_values,
    ).astype(jnp.bfloat16)
    values_all = (
        jnp.dot(normed_input_first, value_weight, preferred_element_type=jnp.float32)
        .astype(jnp.bfloat16)
        .reshape(tok_rows, kv_heads, HEAD_DIMENSION)
    )

    def visible_pairs(block_start):
        query_col = (block_start + jnp.arange(rows_per_block, dtype=jnp.int32))[:, None]
        key_row = jnp.arange(tok_rows, dtype=jnp.int32)[None, :]
        from_prompt = (key_row < prompt_rows) & (
            (query_col >= prompt_rows) | (key_row <= query_col)
        )
        same_cont = (
            (key_row >= prompt_rows)
            & (query_col >= prompt_rows)
            & (key_row <= query_col)
            & ((key_row - prompt_rows) // cont_rows == (query_col - prompt_rows) // cont_rows)
        )
        return from_prompt | same_cont

    def scores_of(query_block, block_start):
        raw_scores = (
            jnp.einsum("qhgd,khd->hgqk", query_block, keys_all, preferred_element_type=jnp.float32)
            * ATTENTION_SCALE
        )
        return jnp.where(visible_pairs(block_start)[None, None], raw_scores, MASKED_SCORE)

    def forward_block(parts):
        query_block, block_start = parts
        scores = scores_of(query_block, block_start)
        row_max = jnp.max(scores, axis=-1, keepdims=True)
        weights = jnp.exp(scores - row_max)
        row_total = jnp.sum(weights, axis=-1, keepdims=True)
        probs_low = (weights / row_total).astype(jnp.bfloat16)
        mixed = jnp.einsum(
            "hgqk,khd->qhgd", probs_low, values_all, preferred_element_type=jnp.float32
        )
        return (mixed.astype(jnp.bfloat16), row_max + jnp.log(row_total))

    query_blocks = rotated_queries.reshape(
        count_of_blocks, rows_per_block, kv_heads, query_groups, HEAD_DIMENSION
    )
    block_starts = jnp.arange(count_of_blocks, dtype=jnp.int32) * rows_per_block
    heads_blocks, log_total = lax.map(forward_block, (query_blocks, block_starts))
    head_outputs = heads_blocks.reshape(tok_rows, -1)
    head_terms = jnp.dot(head_outputs, w_output, preferred_element_type=jnp.float32)
    branch_half = lax.dynamic_slice_in_dim(
        lax.psum(head_terms, "head"), head_rank * half_rows, half_rows, 0
    )
    x_half = lax.dynamic_slice_in_dim(x_full, head_rank * half_rows, half_rows, 0)
    middle = x_half + RESIDUAL_SCALE * branch_half
    xn_two = rms_scale(middle, norm_two).astype(jnp.bfloat16)
    logits = jnp.dot(xn_two, w_router, preferred_element_type=jnp.float32)
    my_routes = lax.dynamic_slice_in_dim(routes, head_rank * half_rows, half_rows, 0)
    route_hot = my_routes[:, :, None] == jnp.arange(experts, dtype=jnp.int32)[None, None, :]
    chosen = jnp.sum(jnp.where(route_hot, logits[:, None, :], 0.0), axis=-1)
    chosen_max = jnp.max(chosen, axis=-1, keepdims=True)
    chosen_exp = jnp.exp(chosen - chosen_max)
    gate_probs = chosen_exp / jnp.sum(chosen_exp, axis=-1, keepdims=True)
    gate_low = gate_probs.astype(jnp.bfloat16)
    member = jnp.any(route_hot, axis=1).astype(jnp.bfloat16)
    order_rank = priority[0]
    earlier = (order_rank[None, :] < order_rank[:, None]).astype(jnp.bfloat16)
    before = jnp.dot(earlier, member, preferred_element_type=jnp.float32)
    slot_rank = jnp.sum(jnp.where(route_hot, before[:, None, :], 0.0), axis=-1).astype(jnp.int32)
    is_kept = slot_rank < capacity
    spare_slot = experts * capacity
    target = jnp.where(is_kept, my_routes * capacity + slot_rank, spare_slot)
    row_ids = jnp.broadcast_to(jnp.arange(half_rows, dtype=jnp.int32)[:, None], target.shape)
    assign_ids = jnp.arange(half_rows * TOPK, dtype=jnp.int32).reshape(target.shape)
    source_row = (
        jnp.zeros(spare_slot + 1, jnp.int32).at[target.ravel()].set(row_ids.ravel())[:spare_slot]
    )
    source_pick = (
        jnp.zeros(spare_slot + 1, jnp.int32).at[target.ravel()].set(assign_ids.ravel())[:spare_slot]
    )
    filled = jnp.zeros(spare_slot + 1, jnp.int32).at[target.ravel()].set(1)[:spare_slot] > 0
    slot_inputs = jnp.where(filled[:, None], xn_two[source_row], 0).reshape(
        experts, capacity, model_width
    )
    slot_gates = jnp.where(filled, gate_low.ravel()[source_pick], 0).reshape(experts, capacity)

    def to_owners(per_expert):
        shape_in = per_expert.shape
        spread = jnp.broadcast_to(per_expert[:, None], (shape_in[0], split) + shape_in[1:])
        return spread.reshape((exp_count, held) + shape_in[1:])

    def from_owners(per_owner):
        shape_in = per_owner.shape
        return jnp.sum(
            per_owner.reshape((experts, split) + shape_in[2:]).astype(jnp.float32), axis=1
        )

    gate_cols = w_gate.reshape(model_width, held, block_width)
    up_cols = w_up.reshape(model_width, held, block_width)
    down_rows = w_down.reshape(held, block_width, model_width)
    send_rows = to_owners(slot_inputs)
    send_gates = to_owners(slot_gates)
    slot_rows = lax.all_to_all(send_rows, "exp", split_axis=0, concat_axis=0, tiled=True)
    slot_gate = lax.all_to_all(send_gates, "exp", split_axis=0, concat_axis=0, tiled=True)
    gate_pre = jnp.einsum(
        "sjcd,djf->sjcf", slot_rows, gate_cols, preferred_element_type=jnp.float32
    )
    up_pre = jnp.einsum("sjcd,djf->sjcf", slot_rows, up_cols, preferred_element_type=jnp.float32)
    hidden = (gate_pre * jax.nn.sigmoid(gate_pre) * up_pre).astype(jnp.bfloat16)
    result = jnp.einsum("sjcf,jfd->sjcd", hidden, down_rows, preferred_element_type=jnp.float32)
    weighted = (slot_gate[..., None].astype(jnp.float32) * result).astype(jnp.bfloat16)
    returned = lax.all_to_all(weighted, "exp", split_axis=0, concat_axis=0, tiled=True)
    returned, held_rows, held_gates = (returned, slot_rows, slot_gate)
    back_flat = jnp.concatenate(
        [
            from_owners(returned).reshape(spare_slot, model_width),
            jnp.zeros((1, model_width), jnp.float32),
        ],
        axis=0,
    )
    expert_sum = jnp.sum(back_flat[target], axis=1)
    layer_out = (middle + RESIDUAL_SCALE * expert_sum).astype(jnp.bfloat16)
    out_grad = cotangent.astype(jnp.float32)
    weighted_rows = (RESIDUAL_SCALE * out_grad).astype(jnp.bfloat16)
    grad_slots = to_owners(
        jnp.where(filled[:, None], weighted_rows[source_row], 0).reshape(
            experts, capacity, model_width
        )
    )
    back_grads, back_rows, back_gates = (
        lax.all_to_all(grad_slots, "exp", split_axis=0, concat_axis=0, tiled=True),
        lax.all_to_all(send_rows, "exp", split_axis=0, concat_axis=0, tiled=True),
        lax.all_to_all(send_gates, "exp", split_axis=0, concat_axis=0, tiled=True),
    )
    owner_gates = back_gates[..., None].astype(jnp.float32)
    gate_pre = jnp.einsum(
        "sjcd,djf->sjcf", back_rows, gate_cols, preferred_element_type=jnp.float32
    )
    up_pre = jnp.einsum("sjcd,djf->sjcf", back_rows, up_cols, preferred_element_type=jnp.float32)
    gate_sigmoid = jax.nn.sigmoid(gate_pre)
    gate_act = gate_pre * gate_sigmoid
    hidden = (gate_act * up_pre).astype(jnp.bfloat16)
    result = jnp.einsum("sjcf,jfd->sjcd", hidden, down_rows, preferred_element_type=jnp.float32)
    gate_part = jnp.sum(back_grads.astype(jnp.float32) * result, axis=-1)
    result_grad = (owner_gates * back_grads).astype(jnp.bfloat16)
    grad_down_w = jnp.einsum(
        "sjcf,sjcd->jfd", hidden, result_grad, preferred_element_type=jnp.float32
    ).reshape(held_cols, model_width)
    hidden_grad = jnp.einsum(
        "sjcd,jfd->sjcf", result_grad, down_rows, preferred_element_type=jnp.float32
    )
    gate_pre_grad = (
        hidden_grad * up_pre * gate_sigmoid * (1.0 + gate_pre * (1.0 - gate_sigmoid))
    ).astype(jnp.bfloat16)
    up_pre_grad = (hidden_grad * gate_act).astype(jnp.bfloat16)
    grad_gate_w = jnp.einsum(
        "sjcd,sjcf->djf", back_rows, gate_pre_grad, preferred_element_type=jnp.float32
    ).reshape(model_width, held_cols)
    grad_up_w = jnp.einsum(
        "sjcd,sjcf->djf", back_rows, up_pre_grad, preferred_element_type=jnp.float32
    ).reshape(model_width, held_cols)
    rows_grad = (
        jnp.einsum("sjcf,djf->sjcd", gate_pre_grad, gate_cols, preferred_element_type=jnp.float32)
        + jnp.einsum("sjcf,djf->sjcd", up_pre_grad, up_cols, preferred_element_type=jnp.float32)
    ).astype(jnp.bfloat16)
    rows_back, gates_back = (
        lax.all_to_all(rows_grad, "exp", split_axis=0, concat_axis=0, tiled=True),
        lax.all_to_all(
            gate_part.astype(jnp.bfloat16), "exp", split_axis=0, concat_axis=0, tiled=True
        ),
    )
    rows_flat = jnp.concatenate(
        [
            from_owners(rows_back).reshape(spare_slot, model_width),
            jnp.zeros((1, model_width), jnp.float32),
        ],
        axis=0,
    )
    xn_two_grad = jnp.sum(rows_flat[target], axis=1)
    gate_total = from_owners(gates_back).astype(jnp.bfloat16).reshape(spare_slot)
    gates_flat = jnp.concatenate([gate_total, jnp.zeros((1,), jnp.bfloat16)], axis=0)
    gate_grad_tok = gates_flat[target].astype(jnp.float32)
    chosen_grad = gate_probs * (
        gate_grad_tok - jnp.sum(gate_probs * gate_grad_tok, axis=-1, keepdims=True)
    )
    logit_grad = jnp.sum(jnp.where(route_hot, chosen_grad[:, :, None], 0.0), axis=1).astype(
        jnp.bfloat16
    )
    grad_router = jnp.einsum("rd,re->de", xn_two, logit_grad, preferred_element_type=jnp.float32)
    xn_two_grad = xn_two_grad + jnp.einsum(
        "re,de->rd", logit_grad, w_router, preferred_element_type=jnp.float32
    )
    middle_norm_pull = jax.vjp(rms_scale, middle, norm_two)[1]
    middle_norm_grad, grad_norm_two = middle_norm_pull(xn_two_grad)
    middle_grad = out_grad + middle_norm_grad
    branch_rows = (RESIDUAL_SCALE * middle_grad).astype(jnp.bfloat16)
    branch_grad = lax.all_gather(branch_rows, "head", axis=0, tiled=True)
    heads_grad = jnp.einsum(
        "td,hd->th", branch_grad, w_output, preferred_element_type=jnp.float32
    ).astype(jnp.bfloat16)
    grad_output_w = jnp.einsum(
        "th,td->hd", head_outputs, branch_grad, preferred_element_type=jnp.float32
    )

    def backward_block(running, parts):
        key_grad, value_grad = running
        query_block, heads_block, block_total, block_start = parts
        scores = scores_of(query_block, block_start)
        probs = jnp.exp(scores - block_total)
        probs_low = probs.astype(jnp.bfloat16)
        prob_grad = jnp.einsum(
            "qhgd,khd->hgqk", heads_block, values_all, preferred_element_type=jnp.float32
        )
        row_inner = jnp.sum(probs * prob_grad, axis=-1, keepdims=True)
        score_grad = (probs * (prob_grad - row_inner)).astype(jnp.bfloat16)
        query_grad = (
            jnp.einsum("hgqk,khd->qhgd", score_grad, keys_all, preferred_element_type=jnp.float32)
            * ATTENTION_SCALE
        )
        key_grad = (
            key_grad
            + jnp.einsum(
                "hgqk,qhgd->khd", score_grad, query_block, preferred_element_type=jnp.float32
            )
            * ATTENTION_SCALE
        )
        value_grad = value_grad + jnp.einsum(
            "hgqk,qhgd->khd", probs_low, heads_block, preferred_element_type=jnp.float32
        )
        return ((key_grad, value_grad), query_grad)

    heads_grad_blocks = heads_grad.reshape(
        count_of_blocks, rows_per_block, kv_heads, query_groups, HEAD_DIMENSION
    )
    zero_keys = jnp.zeros((tok_rows, kv_heads, HEAD_DIMENSION), jnp.float32)
    (own_key, own_value), query_grad = lax.scan(
        backward_block,
        (zero_keys, zero_keys),
        (query_blocks, heads_grad_blocks, log_total, block_starts),
    )
    query_pre_grad = (
        rotate_back(query_grad.reshape(tok_rows, -1, HEAD_DIMENSION), cosine_values, sine_values)
        .reshape(tok_rows, -1)
        .astype(jnp.bfloat16)
    )
    key_pre_grad = (
        rotate_back(own_key, cosine_values, sine_values).reshape(tok_rows, -1).astype(jnp.bfloat16)
    )
    value_low_grad = own_value.reshape(tok_rows, -1).astype(jnp.bfloat16)
    grad_query_w = jnp.einsum(
        "td,th->dh", normed_input_first, query_pre_grad, preferred_element_type=jnp.float32
    )
    grad_key_w = jnp.einsum(
        "td,th->dh", normed_input_first, key_pre_grad, preferred_element_type=jnp.float32
    )
    grad_value_w = jnp.einsum(
        "td,th->dh", normed_input_first, value_low_grad, preferred_element_type=jnp.float32
    )
    xn_one_terms = (
        jnp.einsum("th,dh->td", query_pre_grad, w_query, preferred_element_type=jnp.float32)
        + jnp.einsum("th,dh->td", key_pre_grad, key_weight, preferred_element_type=jnp.float32)
        + jnp.einsum("th,dh->td", value_low_grad, value_weight, preferred_element_type=jnp.float32)
    )
    xn_one_grad = lax.psum_scatter(
        xn_one_terms.astype(jnp.bfloat16), "head", scatter_dimension=0, tiled=True
    ).astype(jnp.float32)
    input_norm_pull = jax.vjp(rms_scale, x_half, norm_one)[1]
    input_norm_grad, grad_norm_one = input_norm_pull(xn_one_grad)
    grad_tokens = middle_grad + input_norm_grad
    grad_gate_w, grad_up_w, grad_down_w, grad_router, grad_norm_one, grad_norm_two = (
        lax.psum(grad_gate_w.astype(jnp.bfloat16), "head").astype(jnp.float32),
        lax.psum(grad_up_w.astype(jnp.bfloat16), "head").astype(jnp.float32),
        lax.psum(grad_down_w.astype(jnp.bfloat16), "head").astype(jnp.float32),
        lax.psum(grad_router.astype(jnp.bfloat16), "head").astype(jnp.float32),
        lax.psum(grad_norm_one.astype(jnp.bfloat16), "head").astype(jnp.float32),
        lax.psum(grad_norm_two.astype(jnp.bfloat16), "head").astype(jnp.float32),
    )
    (
        grad_query_w,
        grad_key_w,
        grad_value_w,
        grad_output_w,
        grad_router,
        grad_norm_one,
        grad_norm_two,
    ) = lax.psum(
        (
            grad_query_w,
            grad_key_w,
            grad_value_w,
            grad_output_w,
            grad_router,
            grad_norm_one,
            grad_norm_two,
        ),
        "exp",
    )
    return (
        layer_out,
        grad_tokens,
        grad_norm_one,
        grad_query_w,
        grad_key_w,
        grad_value_w,
        grad_output_w,
        grad_norm_two,
        grad_router,
        grad_gate_w,
        grad_up_w,
        grad_down_w,
    )


MESH = pl.DeviceIdType.MESH
FLAT = 128
SLOTS = 40
PAIR = 2 * SLOTS
UNKEPT = -1000.0
LOW = jnp.bfloat16
FULL = jnp.float32
LAST = (((1,), (1,)), ((), ()))
FIRST = (((0,), (0,)), ((), ()))
USUAL = (((1,), (0,)), ((), ()))


def mul(left, right, dims=USUAL):
    return lax.dot_general(left, right, dims, preferred_element_type=FULL)


def remote(source, target, send_sem, recv_sem, device):
    return pltpu.make_async_remote_copy(
        src_ref=source,
        dst_ref=target,
        send_sem=send_sem,
        recv_sem=recv_sem,
        device_id=device,
        device_id_type=MESH,
    )


def part(ref, *index):
    return lambda: ref.at[index]


def whole(ref):
    return lambda: ref


class Places:
    def __init__(self):
        self.e = e = lax.axis_index("exp")
        self.h = h = lax.axis_index("head")
        x, y, self.z = e % 2, (e // 2) % 2, e // 4
        z = self.z
        over_x, over_y = e + 1 - 2 * x, e + 2 - 4 * y
        self.near_e = over_x * (1 - h) + over_y * h
        self.far_e = over_y * (1 - h) + over_x * h
        self.near = (self.near_e, h)
        self.far = (self.far_e, h)
        self.outer = (1 + z % 2 + z // 2) % 2
        self.ranks = [z, z + 1 - 2 * (z % 2), 2 - z // 2, 3 - 3 * (z // 2)]
        self.along = [(rank * 4 + e % 4, h) for rank in self.ranks]
        self.edge = self.along[1]
        self.inner = ((3 - z) * 4 + e % 4, h)
        self.pair = (e, 1 - h)
        self.is_inner = (z == 1) | (z == 2)

    def hello(self):
        barrier = pltpu.get_barrier_semaphore()
        for device in (self.pair, self.near, self.far, *self.along[1:]):
            pl.semaphore_signal(barrier, inc=1, device_id=device, device_id_type=MESH)

    def ready(self):
        pl.semaphore_wait(pltpu.get_barrier_semaphore(), 6)


class Links:
    def __init__(self, places, send, recv):
        self.places, self.send, self.recv = places, send, recv
        self.sent, self.names = 0, {}
        self.pending = {"all": [], "inner": []}

    def number(self, name):
        return self.names.setdefault(name, len(self.names))

    def go(self, name, source, target, device, who="all", number=None):
        arrival = self.number(name) if number is None else number
        number = self.sent
        remote(
            source(), target(), self.send.at[number], self.recv.at[arrival], device
        ).start()
        self.sent += 1
        self.pending[who].append((number, name, source))

    def got(self, name, target):
        remote(
            target(), target(), self.send.at[0], self.recv.at[self.number(name)], self.places.near
        ).wait_recv()

    def sent_all(self, who, of):
        for number, name, source in self.pending[who]:
            if of is None or name[0] == of:
                remote(
                    source(), source(), self.send.at[number], self.recv.at[0], self.places.near
                ).wait_send()

    def drain(self, of=None):
        self.sent_all("all", of)

        @pl.when(self.places.is_inner)
        def _():
            self.sent_all("inner", of)

        for who, sent in self.pending.items():
            self.pending[who] = [one for one in sent if of is not None and one[1][0] != of]


class Spread:
    def __init__(self, links, name, gathered, pieces=(slice(None),)):
        self.links, self.name, self.gathered, self.pieces = links, name, gathered, pieces

    def spot(self, i, a, n):
        return part(self.gathered, i, a, self.pieces[n])

    def start(self):
        links, places = self.links, self.links.places
        for n in range(len(self.pieces)):
            block = self.spot(0, 0, n)
            links.go((self.name, "z", 1, n), block, self.spot(1, 0, n), places.edge)
            links.go((self.name, "n", 0, n), block, self.spot(0, 1, n), places.near)

            @pl.when(places.is_inner)
            def _():
                links.go(
                    (self.name, "z", 2, n), block, self.spot(2, 0, n), places.inner, "inner"
                )

    def pass_on(self, i):
        links, places = self.links, self.links.places
        there = {1: 3, 2: 2, 3: 3}[i]
        device = places.inner if i == 1 else places.edge
        for n in range(len(self.pieces)):
            block = self.spot(i, 0, n)
            links.got((self.name, "z", i, n), block)

            @pl.when(places.is_inner)
            def _():
                links.go(
                    (self.name, "z", there, n), block, self.spot(there, 0, n), device, "inner"
                )

            links.go((self.name, "n", i, n), block, self.spot(i, 1, n), places.near)

    def wait(self, i):
        for n in range(len(self.pieces)):
            self.links.got((self.name, "n", i, n), self.spot(i, 1, n))


class Gather:
    def __init__(self, links, name, send, recv, pieces):
        self.links, self.name, self.send, self.recv, self.pieces = links, name, send, recv, pieces
        for n in range(len(pieces)):
            for slot in (1, 2, 3):
                links.number((name, n, slot))

    def push(self, i, value):
        links, places = self.links, self.links.places
        for n, piece in enumerate(self.pieces):
            spot = part(self.send, i, piece)
            spot()[...] = value(n).astype(self.send.dtype)
            slot = 1 if i == 1 else 2 + places.outer
            links.go(
                (self.name, n, 1),
                spot,
                part(self.recv, slot, piece),
                places.along[i],
                number=links.number((self.name, n, 1)) + slot - 1,
            )

    def total(self, own, result):
        for n, piece in enumerate(self.pieces):
            value = own(n)
            for slot in (1, 2, 3):
                spot = part(self.recv, slot, piece)
                self.links.got((self.name, n, slot), spot)
                value = value + spot()[...].astype(FULL)
            result(n)[...] = value


def table_rows(tables, i, places):
    rows = []
    for chip in (places.e, places.far_e):
        for j in range(2):
            rows.append(
                jnp.concatenate(
                    [tables[i, a, pl.ds(2 * chip + j, 1), :] for a in range(2)], axis=1
                )
            )
    return rows


def selection(tables, i, places):
    slot = lax.broadcasted_iota(jnp.int32, (PAIR, 2 * FLAT), 0)
    lane = lax.broadcasted_iota(jnp.int32, (PAIR, 2 * FLAT), 1)
    wanted = (slot - jnp.where(lane >= FLAT, SLOTS, 0)).astype(FULL)
    return jnp.concatenate(
        [jnp.where(row == wanted, 1.0, 0.0) for row in table_rows(tables, i, places)], axis=0
    )


def turn(block, cosine, sine, sign):
    lane = lax.broadcasted_iota(jnp.int32, block.shape, 1) % HEAD_DIMENSION
    quarter = HEAD_DIMENSION // 2
    other = jnp.where(
        lane < quarter,
        -sign * pltpu.roll(block, FLAT - quarter, 1),
        sign * pltpu.roll(block, quarter, 1),
    )
    return block * cosine + other * sine


def layer_kernel(names, *refs):
    r = types.SimpleNamespace(**dict(zip(names, refs, strict=True)))
    places = Places()
    h, e, z = places.h, places.e, places.z
    places.hello()
    links = Links(places, r.sems_send, r.sems_recv)
    experts = r.w_router.shape[0]
    rows_here, width = r.tokens.shape
    q_cols, k_cols = r.w_query.shape[1], r.key_weight.shape[1]
    kv_heads = k_cols // HEAD_DIMENSION
    every = slice(None)
    half = pl.multiple_of(h * FLAT, FLAT)
    other_half = pl.multiple_of((1 - h) * FLAT, FLAT)
    locals_used = [0]

    def load(source, target):
        copy = pltpu.make_async_copy(source, target, r.sems_local.at[locals_used[0]])
        locals_used[0] += 1
        copy.start()
        return copy

    in_loads = [
        load(r.w_query, r.w_in.at[:, :q_cols]),
        load(r.key_weight, r.w_in.at[:, q_cols : q_cols + k_cols]),
        load(r.value_weight, r.w_in.at[:, q_cols + k_cols :]),
    ]
    out_load = load(r.w_output, r.w_out)
    expert_loads = [load(r.w_gate, r.gate_w), load(r.w_up, r.up_w), load(r.w_down, r.down_w)]
    rank_row = r.priority[...]
    row_id = lax.broadcasted_iota(jnp.int32, (FLAT, FLAT), 0)
    col_id = lax.broadcasted_iota(jnp.int32, (FLAT, FLAT), 1)
    rank_col = jnp.sum(
        jnp.where(row_id == col_id, jnp.broadcast_to(rank_row, (FLAT, FLAT)), 0),
        axis=1,
        keepdims=True,
    )
    earlier = jnp.where(rank_row < rank_col, 1.0, 0.0).astype(LOW)
    expert_id = lax.broadcasted_iota(jnp.int32, (experts, FLAT), 0)
    my_routes = r.routes[:, pl.ds(half, FLAT)]
    member = jnp.zeros((experts, FLAT), FULL)
    for k in range(TOPK):
        member += jnp.where(my_routes[k : k + 1, :] == expert_id, 1.0, 0.0)
    before = mul(member.astype(LOW), earlier, LAST)
    r.tables[0, 0] = jnp.where((member > 0.5) & (before < SLOTS), before, UNKEPT)
    r.g_all[0, 0] = (RESIDUAL_SCALE * r.cotangent[...].astype(FULL)).astype(LOW)
    halves = [slice(0, FLAT // 2), slice(FLAT // 2, FLAT)]
    t_spread = Spread(links, "t", r.tables)
    g_spread = Spread(links, "g", r.g_all, halves)
    x_spread = Spread(links, "x", r.x_all, halves)
    p_spread = Spread(links, "p", r.gate_tables)
    x_full = r.tokens[...].astype(FULL)
    r.normed[...] = rms_scale(x_full, r.norm_one[...]).astype(LOW)
    places.ready()
    t_spread.start()
    g_spread.start()

    for copy in in_loads:
        copy.wait()
    projected = mul(r.normed[...], r.w_in[...])
    cosine, sine = r.cosine[...], r.sine[...]
    lane = lax.broadcasted_iota(jnp.int32, (rows_here, FLAT), 1)
    low_lanes = lane < HEAD_DIMENSION
    for g in range(kv_heads):
        r.q[g] = turn(projected[:, g * FLAT : (g + 1) * FLAT], cosine, sine, 1.0).astype(LOW)
    for m in range(kv_heads // 2):
        start = q_cols + m * FLAT
        keys = turn(projected[:, start : start + FLAT], cosine, sine, 1.0)
        start += k_cols
        values = projected[:, start : start + FLAT]
        for block, store in ((keys, r.keys), (values, r.values)):
            rolled = pltpu.roll(block, HEAD_DIMENSION, 1)
            store[2 * m, 0] = jnp.where(low_lanes, block, 0.0).astype(LOW)
            store[2 * m, 1] = jnp.where(low_lanes, 0.0, rolled).astype(LOW)
            store[2 * m + 1, 0] = jnp.where(low_lanes, rolled, 0.0).astype(LOW)
            store[2 * m + 1, 1] = jnp.where(low_lanes, 0.0, block).astype(LOW)
    prompt, cont = rows_here // 2, rows_here // 4
    query_id = lax.broadcasted_iota(jnp.int32, (rows_here, rows_here), 0)
    key_id = lax.broadcasted_iota(jnp.int32, (rows_here, rows_here), 1)
    query_cont = jnp.where(query_id < prompt, 0, 1 + (query_id - prompt) // cont)
    key_cont = jnp.where(key_id < prompt, 0, 1 + (key_id - prompt) // cont)
    visible = ((key_cont == 0) & (query_cont > 0)) | (
        (key_cont == query_cont) & (key_id <= query_id)
    )
    r.bias[...] = jnp.where(visible, 0.0, MASKED_SCORE)

    def attend(first, count):
        def one(g, carry):
            mixed = jnp.zeros((rows_here, FLAT), FULL)
            for s in range(2):
                raw = mul(r.q[g], r.keys[g, s], LAST) * ATTENTION_SCALE
                scores = jnp.where(r.bias[...] < 0.0, MASKED_SCORE, raw)
                weights = jnp.exp(scores - jnp.max(scores, axis=1, keepdims=True))
                probs = weights / jnp.sum(weights, axis=1, keepdims=True)
                r.att_probs[g, s] = probs
                mixed += mul(probs.astype(LOW), r.values[g, s])
            r.heads[:, pl.ds(pl.multiple_of(g * FLAT, FLAT), FLAT)] = mixed.astype(LOW)
            return carry

        lax.fori_loop(first, first + count, one, 0)

    def dispatch_out(i):
        t_spread.wait(i)
        g_spread.wait(i)
        picks = selection(r.tables, i, places).astype(LOW)
        r.pick[i] = picks
        rows = mul(picks, r.g_all[i].reshape(2 * FLAT, -1)).astype(LOW)
        r.g_slots[i] = rows[: 2 * PAIR].reshape(2, PAIR, -1)
        r.g_send[i] = rows[2 * PAIR :].reshape(2, PAIR, -1)
        links.go(("g", "f", i), part(r.g_send, i), part(r.g_slots, 4 + i), places.far)

    def pass_out(i):
        t_spread.pass_on(i)
        g_spread.pass_on(i)

    attend(0, 4)
    out_load.wait()
    r.branch_send[...] = mul(r.heads[pl.ds(other_half, FLAT), :], r.w_out[...])
    links.go("branch", whole(r.branch_send), whole(r.branch_in), places.pair)
    own_branch = mul(r.heads[pl.ds(half, FLAT), :], r.w_out[...])
    links.got("branch", whole(r.branch_in))
    middle = r.tokens[pl.ds(half, FLAT), :].astype(FULL) + RESIDUAL_SCALE * (
        own_branch + r.branch_in[...]
    )
    r.middle[...] = middle
    xn = rms_scale(middle, r.norm_two[...]).astype(LOW)
    r.x_all[0, 0] = xn
    x_spread.start()
    logits = mul(r.w_router[...], xn, LAST)
    chosen = jnp.where(member > 0.5, logits, MASKED_SCORE)
    weights = jnp.exp(chosen - jnp.max(chosen, axis=0, keepdims=True))
    probs = weights / jnp.sum(weights, axis=0, keepdims=True)
    r.probs[...] = probs
    r.gate_tables[0, 0] = probs.astype(LOW).astype(FULL)
    p_spread.start()

    slots_lane = lax.broadcasted_iota(jnp.int32, (2 * PAIR, FLAT), 1)
    r.gates[...] = jnp.zeros((2 * PAIR, FLAT), FULL)
    r.gate_send[...] = jnp.zeros((2, 2 * PAIR, FLAT), LOW)

    def dispatch_in(i):
        x_spread.wait(i)
        picks = r.pick[i]
        rows = mul(picks, r.x_all[i].reshape(2 * FLAT, -1)).astype(LOW)
        r.x_slots[i] = rows[: 2 * PAIR].reshape(2, PAIR, -1)
        r.x_send[i] = rows[2 * PAIR :].reshape(2, PAIR, -1)
        links.go(("x", "f", i), part(r.x_send, i), part(r.x_slots, 4 + i), places.far)
        p_spread.wait(i)
        spread_gates = jnp.concatenate(
            [
                jnp.broadcast_to(row, (PAIR, 2 * FLAT))
                for row in table_rows(r.gate_tables, i, places)
            ],
            axis=0,
        )
        slot_gates = jnp.sum(picks.astype(FULL) * spread_gates, axis=1, keepdims=True)
        r.gates[...] += jnp.where(slots_lane == i, slot_gates[: 2 * PAIR], 0.0)
        far_gates = jnp.where(slots_lane == 4 + i, slot_gates[2 * PAIR :], 0.0)
        r.gate_send[i // 2] += far_gates.astype(LOW)

    def send_gates(n):
        links.go(("p", "f", n), part(r.gate_send, n), part(r.gate_far, n), places.far)

    def add_gates(n):
        links.got(("p", "f", n), part(r.gate_far, n))
        r.gates[...] += r.gate_far[n].astype(FULL)

    def pass_in(i):
        x_spread.pass_on(i)
        p_spread.pass_on(i)

    pass_out(1)
    dispatch_out(0)
    pass_out(2)
    dispatch_out(1)
    pass_out(3)
    dispatch_in(0)
    dispatch_out(2)
    pass_in(1)
    pass_in(2)
    dispatch_out(3)
    dispatch_in(1)
    send_gates(0)
    pass_in(3)
    dispatch_in(2)
    dispatch_in(3)
    send_gates(1)

    slot_lane = lax.broadcasted_iota(jnp.int32, (PAIR, FLAT), 1)
    r.parts[...] = jnp.zeros((2 * PAIR, FLAT), FULL)

    def run_experts(first, count):
        span = count * PAIR
        which = slice(first, first + count)
        place = slice(first * PAIR, (first + count) * PAIR)

        def one_expert(j, carry):
            base = pl.multiple_of(j * PAIR, PAIR)
            gates = r.gates[pl.ds(base, PAIR), :]
            gate_col = jnp.concatenate(
                [gates[:, p : p + 1] for p in range(first, first + count)], axis=0
            )
            columns = pl.ds(pl.multiple_of(j * FF, FF), FF)
            xs = r.x_slots[which, j].reshape(span, -1)
            gate_pre = mul(xs, r.gate_w[:, columns])
            up_pre = mul(xs, r.up_w[:, columns])
            sig = jax.nn.sigmoid(gate_pre)
            act = gate_pre * sig
            hidden = (act * up_pre).astype(LOW)
            r.hidden_all[j, place] = hidden
            result = mul(hidden, r.down_w[columns, :])
            gs = r.g_slots[which, j].reshape(span, -1).astype(FULL)
            r.g_slots[which, j] = (gate_col * result).astype(LOW).reshape(count, PAIR, -1)
            part = jnp.sum(gs * result, axis=1, keepdims=True).astype(LOW).astype(FULL)
            terms = jnp.zeros((PAIR, FLAT), FULL)
            for p in range(count):
                terms += jnp.where(
                    slot_lane == first + p, part[p * PAIR : (p + 1) * PAIR], 0.0
                )
            r.parts[pl.ds(base, PAIR), :] += terms
            result_grad = (gate_col * gs).astype(LOW)
            r.result_all[j, place] = result_grad
            hidden_grad = mul(result_grad, r.down_w[columns, :], LAST)
            gate_pre_grad = (
                hidden_grad * up_pre * sig * (1.0 + gate_pre * (1.0 - sig))
            ).astype(LOW)
            up_pre_grad = (hidden_grad * act).astype(LOW)
            r.gate_all[j, place] = gate_pre_grad
            r.up_all[j, place] = up_pre_grad
            rows_grad = mul(gate_pre_grad, r.gate_w[:, columns], LAST) + mul(
                up_pre_grad, r.up_w[:, columns], LAST
            )
            r.row_slots[which, j] = rows_grad.astype(LOW).reshape(count, PAIR, -1)
            return carry

        lax.fori_loop(0, 2, one_expert, 0)

    for copy in expert_loads:
        copy.wait()
    writes = []

    def weight_grads(j):
        xs = r.x_slots[:, j].reshape(8 * PAIR, -1)
        columns = slice(j * FF, (j + 1) * FF)
        r.gate_w[:, columns] = mul(xs, r.gate_all[j], FIRST).astype(LOW)
        r.up_w[:, columns] = mul(xs, r.up_all[j], FIRST).astype(LOW)
        r.down_w[columns, :] = mul(r.hidden_all[j], r.result_all[j], FIRST).astype(LOW)

    def send_grads(j):
        columns = slice(j * FF, (j + 1) * FF)
        for n, (source, own, other) in enumerate(
            (
                (
                    part(r.gate_w, every, columns),
                    part(r.gate_own, every, columns),
                    part(r.gate_other, every, columns),
                ),
                (
                    part(r.up_w, every, columns),
                    part(r.up_own, every, columns),
                    part(r.up_other, every, columns),
                ),
                (part(r.down_w, columns), part(r.down_own, columns), part(r.down_other, columns)),
            )
        ):
            writes.append(load(source(), own()))
            links.go(("e", j, n), source, other, places.pair)


    index = lax.broadcasted_iota(jnp.int32, (experts, 2 * FLAT), 0)

    def fold(name, rows, rows_in, kept, near_send, near_in, i):
        links.got((name, "f", i), part(rows_in, i))
        send = near_send(i)
        stacked = jnp.concatenate(
            [rows[i].reshape(2 * PAIR, -1), rows_in[i].reshape(2 * PAIR, -1)], axis=0
        )
        sums = mul(r.pick[i], stacked, FIRST)
        kept[i] = sums[:FLAT]
        send()[...] = sums[FLAT:].astype(LOW)
        links.go((name, "n", i), send, part(near_in, i), places.near)

    def fold_parts(i):
        column = jnp.concatenate(
            [r.parts[:, i : i + 1], r.parts_in[:, 4 + i : 5 + i]], axis=0
        )
        terms = r.pick[i].astype(FULL) * column
        table = jnp.zeros((experts, 2 * FLAT), FULL)
        chips = (places.e, places.e, places.far_e, places.far_e)
        for n, chip in enumerate(chips):
            total = jnp.sum(terms[n * PAIR : (n + 1) * PAIR], axis=0, keepdims=True)
            table += jnp.where(index == 2 * chip + n % 2, total, 0.0)
        r.part_kept[i] = table[:, :FLAT]
        r.part_send[i] = table[:, FLAT:]
        links.go(("q", "n", i), part(r.part_send, i), part(r.part_near, i), places.near)

    row_sums = Gather(links, "rz", r.row_z_send, r.row_z_in, halves)
    part_sums = Gather(links, "qz", r.part_z_send, r.part_z_in, [slice(0, experts)])
    weighted_sums = Gather(links, "wz", r.row_near_send, r.weighted_z_in, halves)

    def near_sum(name, kept, near_in, i, pieces):
        links.got((name, "n", i), part(near_in, i))
        return lambda n: kept[i, pieces[n]] + near_in[i, pieces[n]].astype(FULL)

    def settle_rows(i):
        row_sums.push(i, near_sum("r", r.row_kept, r.row_near, i, row_sums.pieces))

    def settle_parts(i):
        part_sums.push(i, near_sum("q", r.part_kept, r.part_near, i, part_sums.pieces))

    def settle_weighted(i):
        weighted_sums.push(i, near_sum("w", r.row_kept, r.weighted_near, i, halves))

    def fold_weighted(i):
        fold(
            "w",
            r.g_slots,
            r.g_send,
            r.row_kept,
            lambda i: part(r.x_all, i, 0),
            r.weighted_near,
            i,
        )

    def far_experts(i):
        links.got(("g", "f", i), part(r.g_slots, 4 + i))
        links.got(("x", "f", i), part(r.x_slots, 4 + i))
        run_experts(4 + i, 1)
        links.go(("r", "f", i), part(r.row_slots, 4 + i), part(r.rows_in, i), places.far)

    def fold_rows(i):
        fold(
            "r",
            r.row_slots,
            r.rows_in,
            r.row_kept,
            lambda i: part(r.row_near_send, i),
            r.row_near,
            i,
        )

    add_gates(0)
    far_experts(1)
    far_experts(0)
    run_experts(0, 4)
    links.drain()
    add_gates(1)
    fold_rows(1)
    far_experts(3)
    far_experts(2)
    links.go(("q", "f"), whole(r.parts), whole(r.parts_in), places.far)
    settle_rows(1)
    fold_rows(3)
    fold_rows(2)
    settle_rows(3)
    links.got(("q", "f"), whole(r.parts_in))
    for i in (3, 2, 1, 0):
        fold_parts(i)
    settle_rows(2)
    for i in (3, 2, 1):
        settle_parts(i)
    fold_rows(0)
    def send_weighted(i):
        links.go(("w", "f", i), part(r.g_slots, 4 + i), part(r.g_send, i), places.far)

    send_weighted(3)
    send_weighted(2)
    weight_grads(0)
    send_grads(0)
    weight_grads(1)
    fold_weighted(3)
    send_weighted(1)
    fold_weighted(2)
    send_weighted(0)
    fold_weighted(1)
    row_sums.total(
        near_sum("r", r.row_kept, r.row_near, 0, halves), lambda n: r.branch_in.at[halves[n]]
    )
    part_sums.total(
        near_sum("q", r.part_kept, r.part_near, 0, part_sums.pieces), lambda n: r.part_total
    )

    gate_probs, gate_grad = r.probs[...], r.part_total[...]
    chosen_grad = gate_probs * (
        gate_grad - jnp.sum(gate_probs * gate_grad, axis=0, keepdims=True)
    )
    logit_grad = chosen_grad.astype(LOW)
    xn_grad = r.branch_in[...] + mul(logit_grad, r.w_router[...], FIRST)
    mid = r.middle[...]
    scale = lax.rsqrt(jnp.mean(mid * mid, axis=-1, keepdims=True) + NORM_EPS)
    scaled = r.norm_two[...] * xn_grad
    pull = jnp.mean(scaled * mid, axis=-1, keepdims=True)
    grad = r.cotangent[...].astype(FULL) + scale * scaled - mid * (scale * scale * scale * pull)
    r.grad_tokens[...] = grad
    mine = part(r.branch_grad, pl.ds(half, FLAT))
    r.branch_grad[pl.ds(half, FLAT), :] = (RESIDUAL_SCALE * grad).astype(LOW)
    links.go("bg", mine, mine, places.pair)
    r.small[pl.ds(0, experts), :] = mul(logit_grad, r.x_all[0, 0])
    r.small[pl.ds(experts, 8), :] = jnp.broadcast_to(
        jnp.sum(xn_grad * mid * scale, axis=0, keepdims=True), (8, width)
    )

    links.drain("r")
    for i in (3, 2, 1):
        settle_weighted(i)
    fold_weighted(0)
    links.got("bg", part(r.branch_grad, pl.ds(other_half, FLAT)))
    r.heads_grad[...] = mul(r.branch_grad[...], r.w_out[...], LAST).astype(LOW)
    r.grads[pl.ds(width, q_cols), :] = mul(r.heads[...], r.branch_grad[...], FIRST).astype(LOW)
    cosine, sine = r.cosine[...], r.sine[...]

    def attend_back(first, count):
        def one(g, carry):
            place = pl.ds(pl.multiple_of(g * FLAT, FLAT), FLAT)
            out_grad = r.heads_grad[:, place]
            query = r.q[g]
            query_grad = jnp.zeros((rows_here, FLAT), FULL)
            key_grads, value_grads = [], []
            for s in range(2):
                probs = r.att_probs[g, s]
                prob_grad = mul(out_grad, r.values[g, s], LAST)
                inner = jnp.sum(probs * prob_grad, axis=1, keepdims=True)
                score_grad = (probs * (prob_grad - inner)).astype(LOW)
                query_grad += mul(score_grad, r.keys[g, s])
                key_grads.append(mul(score_grad, query, FIRST))
                value_grads.append(mul(probs.astype(LOW), out_grad, FIRST))
            r.head_grads[:, place] = turn(
                query_grad * ATTENTION_SCALE, r.cosine[...], r.sine[...], -1.0
            ).astype(LOW)
            r.key_sums[g] = key_grads[0] + pltpu.roll(key_grads[1], HEAD_DIMENSION, 1)
            r.value_sums[g] = value_grads[0] + pltpu.roll(value_grads[1], HEAD_DIMENSION, 1)
            return carry

        lax.fori_loop(first, first + count, one, 0)

    ranks = places.ranks
    plane = [[e % 4, places.near_e % 4], [places.far_e % 4, 3 - e % 4]]

    def along(name, spot):
        block = spot(0)
        links.go((name, "z", 1), block, block, places.edge)

        @pl.when(places.is_inner)
        def _():
            links.go((name, "z", 2), block, block, places.inner, "inner")

    def pass_along(name, spot, i):
        block = spot(i)
        links.got((name, "z", i), block)
        there = {1: 3, 2: 2, 3: 3}[i]
        device = places.inner if i == 1 else places.edge

        @pl.when(places.is_inner)
        def _():
            links.go((name, "z", there), block, block, device, "inner")

    class Reduce:
        order = [(a, i) for i in (3, 2, 1, 0) for a in (1, 0)]

        def __init__(self, name, first, count, room):
            self.name, self.first, self.depth, self.room = name, first, count // 16, room
            self.rows = slice(room, room + self.depth)
            self.issued = 0
            self.sums = Gather(links, name + "z", r.sum_z_send, r.sum_z_in, [self.rows])

        def shard(self, b, a, i):
            start = self.first + (ranks[i] * 4 + plane[b][a]) * self.depth
            return pl.ds(pl.multiple_of(start, 16), self.depth)

        def far_in(self, a, i):
            return part(r.g_all, i, a, self.rows)

        def near_in(self, i):
            return part(r.x_all, i, 1, self.rows)

        def near_send(self, i):
            return part(r.result_all, 0, pl.ds(4 * self.room + i * self.depth, self.depth))

        def send(self, count):
            for a, i in self.order[self.issued : self.issued + count]:
                source = part(r.grads, self.shard(1, a, i))
                links.go((self.name, "f", a, i), source, self.far_in(a, i), places.far)
            self.issued += count

        def fold(self, i):
            for a in (1, 0):
                links.got((self.name, "f", a, i), self.far_in(a, i))
                self.send(1)
                if a:
                    total = r.grads[self.shard(0, 1, i), :].astype(FULL) + r.g_all[
                        i, 1, self.rows
                    ].astype(FULL)
                    self.near_send(i)()[...] = total.astype(LOW)
                    links.go(
                        (self.name, "n", i), self.near_send(i), self.near_in(i), places.near
                    )

        def near_sum(self, i):
            links.got((self.name, "n", i), self.near_in(i))
            mine = self.shard(0, 0, i)
            return lambda n: (
                r.grads[mine, :].astype(FULL)
                + r.g_all[i, 0, self.rows].astype(FULL)
                + r.x_all[i, 1, self.rows].astype(FULL)
            )

        def settle(self, i):
            self.sums.push(i, self.near_sum(i))

        def spot(self, b, a, i):
            return part(r.grads_out, self.shard(b, a, i))

        def share(self):
            total = r.branch_send.at[self.rows]
            self.sums.total(self.near_sum(0), lambda n: total)
            low = part(r.result_all, 1, pl.ds(FLAT + self.room, self.depth))
            low()[...] = total[...].astype(LOW)
            mine = self.spot(0, 0, 0)
            links.go((self.name + "o", "z", 1), low, mine, places.edge)
            links.go((self.name, "on", 0), low, mine, places.near)

            @pl.when(places.is_inner)
            def _():
                links.go((self.name + "o", "z", 2), low, mine, places.inner, "inner")

            links.go((self.name, "of", 0, 0), low, mine, places.far)
            writes.append(load(low(), mine()))

        def pass_far(self, i):
            block = self.spot(0, 1, i)
            links.got((self.name, "on", i), block)
            links.go((self.name, "of", 1, i), block, block, places.far)

        def pass_on(self, i):
            block = self.spot(0, 0, i)
            pass_along(self.name + "o", lambda i: self.spot(0, 0, i), i)
            links.go((self.name, "on", i), block, block, places.near)
            links.go((self.name, "of", 0, i), block, block, places.far)

        def finish(self):
            for i in range(4):
                for a in range(2):
                    links.got((self.name, "of", a, i), self.spot(1, a, i))

    late = Reduce("b", width, q_cols, 0)
    early = Reduce("a", 0, width, q_cols // 16)
    late.send(8)
    attend_back(0, 4)
    for m in range(kv_heads // 2):
        start = q_cols + m * FLAT
        for sums, shift in ((r.key_sums, 0), (r.value_sums, k_cols)):
            block = jnp.where(
                low_lanes, sums[2 * m], pltpu.roll(sums[2 * m + 1], HEAD_DIMENSION, 1)
            )
            if shift == 0:
                block = turn(block * ATTENTION_SCALE, cosine, sine, -1.0)
            r.head_grads[:, start + shift : start + shift + FLAT] = block.astype(LOW)
    head_grads = r.head_grads
    r.grads[pl.ds(0, width), :] = mul(r.normed[...], head_grads[...], FIRST).astype(LOW)
    early.send(8)
    r.result_all[1, 0:FLAT] = mul(
        head_grads[pl.ds(other_half, FLAT), :], r.w_in[...], LAST
    ).astype(LOW)
    links.go("terms", part(r.result_all, 1, pl.ds(0, FLAT)), whole(r.terms_in), places.pair)
    own_terms = mul(head_grads[pl.ds(half, FLAT), :], r.w_in[...], LAST).astype(LOW)
    send_grads(1)
    late.fold(3)
    late.fold(2)
    late.fold(1)
    late.fold(0)
    late.settle(3)
    late.settle(2)
    late.settle(1)
    early.fold(3)
    early.fold(2)
    early.settle(3)
    early.fold(1)
    early.settle(2)
    early.fold(0)
    late.share()
    early.settle(1)
    links.got("terms", whole(r.terms_in))
    xn_grad = (own_terms.astype(FULL) + r.terms_in[...].astype(FULL)).astype(LOW).astype(FULL)
    x_half = r.tokens[pl.ds(half, FLAT), :].astype(FULL)
    scale = lax.rsqrt(jnp.mean(x_half * x_half, axis=-1, keepdims=True) + NORM_EPS)
    scaled = r.norm_one[...] * xn_grad
    pull = jnp.mean(scaled * x_half, axis=-1, keepdims=True)
    r.grad_tokens[...] = (
        r.grad_tokens[...] + scale * scaled - x_half * (scale * scale * scale * pull)
    )
    r.small_mine[0, pl.ds(0, experts), :] = r.small[pl.ds(0, experts), :]
    row = lax.broadcasted_iota(jnp.int32, (8, width), 0)
    r.small_mine[0, pl.ds(experts, 8), :] = jnp.where(
        row == 0,
        r.small[pl.ds(experts, 8), :],
        jnp.sum(xn_grad * x_half * scale, axis=0, keepdims=True),
    )
    links.go(("s", 0), part(r.small_mine, 0), part(r.small_in, 0), places.pair)
    late.pass_far(0)
    late.pass_on(1)
    early.share()
    links.got(("s", 0), part(r.small_in, 0))
    r.small_mine[1] = r.small_mine[0] + r.small_in[0]
    links.go(("s", 1), part(r.small_mine, 1), part(r.small_in, 1), places.far)
    late.pass_far(1)
    late.pass_on(2)
    early.pass_far(0)
    late.pass_far(2)
    late.pass_on(3)
    late.pass_far(3)
    links.got(("s", 1), part(r.small_in, 1))
    r.small_mine[2] = r.small_mine[1] + r.small_in[1]
    links.go(("s", 2), part(r.small_mine, 2), part(r.small_in, 2), places.near)
    early.pass_on(1)
    early.pass_far(1)
    early.pass_on(2)
    links.got(("s", 2), part(r.small_in, 2))
    r.small_all[z] = r.small_mine[2] + r.small_in[2]
    along("s", lambda i: part(r.small_all, ranks[i]))
    early.pass_far(2)
    early.pass_on(3)
    early.pass_far(3)
    weighted_sums.total(
        near_sum("w", r.row_kept, r.weighted_near, 0, halves),
        lambda n: r.branch_in.at[halves[n]],
    )
    r.layer_out[...] = (r.middle[...] + RESIDUAL_SCALE * r.branch_in[...]).astype(LOW)

    for i in (1, 2, 3):
        pass_along("s", lambda i: part(r.small_all, ranks[i]), i)
    small = ((r.small_all[0] + r.small_all[1]) + r.small_all[2]) + r.small_all[3]
    r.router_out[...] = small[:experts]
    r.norms_out[...] = small[experts:]
    late.finish()
    early.finish()
    for j in range(2):
        columns = slice(j * FF, (j + 1) * FF)
        links.got(("e", j, 0), part(r.gate_other, every, columns))
        links.got(("e", j, 1), part(r.up_other, every, columns))
        links.got(("e", j, 2), part(r.down_other, columns))
    for copy in writes:
        copy.wait()
    links.drain()


def run_layer(**inputs):
    rows_here, width = inputs["tokens"].shape
    experts = inputs["w_router"].shape[0]
    q_cols, k_cols = inputs["w_query"].shape[1], inputs["key_weight"].shape[1]
    kv_heads = k_cols // HEAD_DIMENSION
    vmem = pl.BlockSpec(memory_space=pltpu.VMEM)
    anywhere = pl.BlockSpec(memory_space=pl.ANY)
    block = (FLAT, width)
    gate = (experts, FLAT)
    slots = (2, PAIR, width)
    small = (experts + 8, width)
    grads = (width + q_cols, width)
    depth = grads[0] // 16
    outputs = {
        "layer_out": (block, LOW),
        "grad_tokens": (block, FULL),
        "router_out": (gate[:1] + (width,), FULL),
        "norms_out": ((8, width), FULL),
    }
    held = {"grads_out": (grads, LOW)} | {
        name + end: (inputs["w_" + name].shape, LOW)
        for end in ("_own", "_other")
        for name in ("gate", "up", "down")
    }
    heads = (kv_heads, 2, rows_here)
    scratch = {
        "w_in": ((width, q_cols + 2 * k_cols), LOW),
        "w_out": ((q_cols, width), LOW),
        "normed": ((rows_here, width), LOW),
        "q": ((kv_heads, rows_here, FLAT), LOW),
        "keys": (heads + (FLAT,), LOW),
        "values": (heads + (FLAT,), LOW),
        "bias": ((rows_here, rows_here), FULL),
        "att_probs": (heads + (rows_here,), FULL),
        "heads": ((rows_here, q_cols), LOW),
        "heads_grad": ((rows_here, q_cols), LOW),
        "head_grads": ((rows_here, q_cols + 2 * k_cols), LOW),
        "key_sums": ((kv_heads, rows_here, FLAT), FULL),
        "value_sums": ((kv_heads, rows_here, FLAT), FULL),
        "branch_send": (block, FULL),
        "branch_in": (block, FULL),
        "middle": (block, FULL),
        "branch_grad": ((rows_here, width), LOW),
        "small": (small, FULL),
        "terms_in": (block, LOW),
        "grads": (grads, LOW),
        "sum_z_send": ((4, depth, width), LOW),
        "sum_z_in": ((4, depth, width), LOW),
        "small_mine": ((3,) + small, FULL),
        "small_in": ((3,) + small, FULL),
        "small_all": ((4,) + small, FULL),
        "probs": (gate, FULL),
        "tables": ((4, 2) + gate, FULL),
        "gate_tables": ((4, 2) + gate, FULL),
        "g_all": ((4, 2) + block, LOW),
        "x_all": ((4, 2) + block, LOW),
        "g_slots": ((8,) + slots, LOW),
        "x_slots": ((8,) + slots, LOW),
        "row_slots": ((8,) + slots, LOW),
        "g_send": ((4,) + slots, LOW),
        "x_send": ((4,) + slots, LOW),
        "gates": ((2 * PAIR, FLAT), FULL),
        "gate_send": ((2, 2 * PAIR, FLAT), LOW),
        "gate_far": ((2, 2 * PAIR, FLAT), LOW),
        "parts": ((2 * PAIR, FLAT), FULL),
        "parts_in": ((2 * PAIR, FLAT), FULL),
        "pick": ((4, 4 * PAIR, 2 * FLAT), LOW),
        "gate_w": (inputs["w_gate"].shape, LOW),
        "up_w": (inputs["w_up"].shape, LOW),
        "down_w": (inputs["w_down"].shape, LOW),
        "hidden_all": ((2, 8 * PAIR, FF), LOW),
        "gate_all": ((2, 8 * PAIR, FF), LOW),
        "up_all": ((2, 8 * PAIR, FF), LOW),
        "result_all": ((2, 8 * PAIR, width), LOW),
        "rows_in": ((4,) + slots, LOW),
        "row_kept": ((4,) + block, FULL),
        "row_near": ((4,) + block, LOW),
        "row_near_send": ((4,) + block, LOW),
        "row_z_send": ((4,) + block, LOW),
        "row_z_in": ((4,) + block, LOW),
        "part_kept": ((4,) + gate, FULL),
        "part_near": ((4,) + gate, FULL),
        "part_send": ((4,) + gate, FULL),
        "part_z_send": ((4,) + gate, FULL),
        "part_z_in": ((4,) + gate, FULL),
        "part_total": (gate, FULL),
        "weighted_near": ((4,) + block, LOW),
        "weighted_z_in": ((4,) + block, LOW),
    }
    near_by = ("tokens", "norm_one", "norm_two", "w_router", "routes", "priority")
    near_by += ("cotangent", "cosine", "sine")
    names = [*inputs, *outputs, *held, *scratch, "sems_local", "sems_send", "sems_recv"]
    results = pl.pallas_call(
        functools.partial(layer_kernel, names),
        out_shape=[
            jax.ShapeDtypeStruct(shape, kind) for shape, kind in [*outputs.values(), *held.values()]
        ],
        in_specs=[vmem if name in near_by else anywhere for name in inputs],
        out_specs=[vmem] * len(outputs) + [anywhere] * len(held),
        scratch_shapes=[pltpu.VMEM(shape, kind) for shape, kind in scratch.values()]
        + [
            pltpu.SemaphoreType.DMA((20,)),
            pltpu.SemaphoreType.DMA((260,)),
            pltpu.SemaphoreType.DMA((220,)),
        ],
        compiler_params=pltpu.CompilerParams(
            collective_id=0, has_side_effects=True, vmem_limit_bytes=63 << 20
        ),
        name="layer",
    )(*inputs.values())
    return dict(zip([*outputs, *held], results))


def cast_kernel(*refs):
    parts, (first, second, layer, tokens, router, norms), outs = refs[:6], refs[6:12], refs[12:]
    q_cols, k_cols = outs[3].shape[1], outs[4].shape[1]
    for n in range(3):
        outs[n][...] = parts[2 * n][...].astype(FULL) + parts[2 * n + 1][...].astype(FULL)
    outs[3][...] = first[:, :q_cols].astype(FULL)
    outs[4][...] = first[:, q_cols : q_cols + k_cols].astype(FULL)
    outs[5][...] = first[:, q_cols + k_cols :].astype(FULL)
    outs[6][...] = second[...].astype(FULL)
    outs[7][...] = layer[...]
    outs[8][...] = tokens[...]
    outs[9][...] = router[...]
    outs[10][...] = norms[0:1, :]
    outs[11][...] = norms[1:2, :]


def cast_grads(done, q_cols, k_cols, steps=4):
    width = done["grads_out"].shape[1]
    parts = [done[name + end] for name in ("gate", "up", "down") for end in ("_own", "_other")]
    rest = [done[name] for name in ("layer_out", "grad_tokens", "router_out", "norms_out")]

    def rows(shape, offset=0):
        block = shape[0] // steps
        return pl.BlockSpec((block, shape[1]), lambda i: (offset // block + i, 0))

    shapes = [parts[0].shape] * 3 + [(width, cols) for cols in (q_cols, k_cols, k_cols)]
    shapes += [(q_cols, width)] + [one.shape for one in rest[:3]]
    row = pl.BlockSpec((1, width), lambda i: (0, 0))
    return pl.pallas_call(
        cast_kernel,
        grid=(steps,),
        out_shape=[
            jax.ShapeDtypeStruct(shape, LOW if n == 7 else FULL)
            for n, shape in enumerate(shapes + [(1, width)] * 2)
        ],
        in_specs=[rows(one.shape) for one in parts]
        + [rows((width, width)), rows((q_cols, width), width)]
        + [rows(one.shape) for one in rest[:3]]
        + [pl.BlockSpec(rest[3].shape, lambda i: (0, 0))],
        out_specs=[rows(shape) for shape in shapes] + [row, row],
        compiler_params=pltpu.CompilerParams(vmem_limit_bytes=62 << 20),
        name="cast_grads",
    )(*parts, done["grads_out"], done["grads_out"], *rest)


def quick_shards(
    tokens,
    norm_one,
    w_query,
    key_weight,
    value_weight,
    w_output,
    norm_two,
    w_router,
    w_gate,
    w_up,
    w_down,
    routes,
    priority,
    cotangent,
):
    rows_here, width = tokens.shape
    experts = w_router.shape[1]
    q_cols, k_cols = w_query.shape[1], key_weight.shape[1]
    local_index = np.arange(rows_here, dtype=np.int32)
    prompt_rows, cont_rows = rows_here // 2, rows_here // 4
    position = np.where(
        local_index < prompt_rows,
        local_index,
        prompt_rows + (local_index - prompt_rows) % cont_rows,
    )
    frequency = ROPE_BASE ** (
        -(2.0 * np.arange(HEAD_DIMENSION // 2, dtype=np.float32)) / HEAD_DIMENSION
    )
    frequency = frequency.astype(np.float32)
    angle_table = position.astype(np.float32)[:, None] * np.tile(frequency, 4)[None, :]
    done = run_layer(
        tokens=tokens,
        norm_one=norm_one[None, :],
        norm_two=norm_two[None, :],
        w_router=w_router.T,
        routes=routes.T,
        priority=priority,
        cotangent=cotangent,
        cosine=jnp.asarray(np.cos(angle_table), FULL),
        sine=jnp.asarray(np.sin(angle_table), FULL),
        w_query=w_query,
        key_weight=key_weight,
        value_weight=value_weight,
        w_output=w_output,
        w_gate=w_gate,
        w_up=w_up,
        w_down=w_down,
    )
    gate, up, down, query, key, value, output, layer, token, router, second, first = cast_grads(
        done, q_cols, k_cols
    )
    return (
        layer,
        token,
        first[0],
        query,
        key,
        value,
        output,
        second[0],
        router.T,
        gate,
        up,
        down,
    )


def solution(mesh):
    body = quick_shards if dict(mesh.shape) == {"exp": 16, "head": 2} else shards
    return jax.shard_map(
        body,
        mesh=mesh,
        in_specs=(
            P("exp", None),
            P(),
            P(None, "head"),
            P(None, "head"),
            P(None, "head"),
            P("head", None),
            P(),
            P(),
            P(None, "exp"),
            P(None, "exp"),
            P("exp", None),
            P("exp", None),
            P(("exp", "head"), None),
            P(("exp", "head"), None),
        ),
        out_specs=(
            P(("exp", "head"), None),
            P(("exp", "head"), None),
            P(),
            P(None, "head"),
            P(None, "head"),
            P(None, "head"),
            P("head", None),
            P(),
            P(),
            P(None, "exp"),
            P(None, "exp"),
            P("exp", None),
        ),
        check_vma=False,
    )
```

```python
import functools
import types

import jax
import jax.numpy as jnp
import numpy as np
from jax import lax
from jax.experimental import pallas as pl
from jax.experimental.pallas import tpu as pltpu
from jax.sharding import PartitionSpec as P

HEAD_DIMENSION = 64
FF = 512
TOPK = 8


RESIDUAL_SCALE = 0.22
ATTENTION_SCALE = 0.015625
ROPE_BASE = 10000.0
NORM_EPS = 1e-06
MASKED_SCORE = -1e30


def rms_scale(values, scale_row):
    return (
        values * lax.rsqrt(jnp.mean(values * values, axis=-1, keepdims=True) + NORM_EPS) * scale_row
    )


def apply_rotary(values, cosine_values, sine_values):
    half_width = values.shape[-1] // 2
    lower_part = values[..., :half_width]
    upper_part = values[..., half_width:]
    return jnp.concatenate(
        [
            lower_part * cosine_values - upper_part * sine_values,
            upper_part * cosine_values + lower_part * sine_values,
        ],
        axis=-1,
    )


def rotate_back(values, cosine_values, sine_values):
    half_width = values.shape[-1] // 2
    lower_part = values[..., :half_width]
    upper_part = values[..., half_width:]
    return jnp.concatenate(
        [
            lower_part * cosine_values + upper_part * sine_values,
            upper_part * cosine_values - lower_part * sine_values,
        ],
        axis=-1,
    )


def shards(
    tokens,
    norm_one,
    w_query,
    key_weight,
    value_weight,
    w_output,
    norm_two,
    w_router,
    w_gate,
    w_up,
    w_down,
    routes,
    priority,
    cotangent,
):
    tok_rows, model_width = tokens.shape
    heads_count = lax.axis_size("head")
    head_rank = lax.axis_index("head")
    exp_count = lax.axis_size("exp")
    half_rows = tok_rows // heads_count
    prompt_rows = tok_rows // 2
    cont_rows = tok_rows // 4
    kv_heads = key_weight.shape[1] // HEAD_DIMENSION
    query_groups = w_query.shape[1] // key_weight.shape[1]
    experts = w_router.shape[1]
    held_cols = w_gate.shape[1]
    held = max(1, held_cols // FF)
    split = max(1, FF // held_cols)
    block_width = held_cols // held
    capacity = max(2, (5 * half_rows * TOPK + 4 * experts - 1) // (4 * experts))
    rows_per_block = min(512, tok_rows)
    count_of_blocks = tok_rows // rows_per_block
    local_index = jnp.arange(tok_rows, dtype=jnp.int32)
    position = jnp.where(
        local_index < prompt_rows,
        local_index,
        prompt_rows + (local_index - prompt_rows) % cont_rows,
    )
    frequency = ROPE_BASE ** (
        -(2.0 * jnp.arange(HEAD_DIMENSION // 2, dtype=jnp.float32)) / HEAD_DIMENSION
    )
    angle_table = position.astype(jnp.float32)[:, None] * frequency[None, :]
    cosine_values = jnp.cos(angle_table)[:, None, :]
    sine_values = jnp.sin(angle_table)[:, None, :]
    x_full = tokens.astype(jnp.float32)
    normed_input_first = rms_scale(x_full, norm_one).astype(jnp.bfloat16)
    rotated_queries = apply_rotary(
        jnp.dot(normed_input_first, w_query, preferred_element_type=jnp.float32).reshape(
            tok_rows, -1, HEAD_DIMENSION
        ),
        cosine_values,
        sine_values,
    ).astype(jnp.bfloat16)
    keys_all = apply_rotary(
        jnp.dot(normed_input_first, key_weight, preferred_element_type=jnp.float32).reshape(
            tok_rows, -1, HEAD_DIMENSION
        ),
        cosine_values,
        sine_values,
    ).astype(jnp.bfloat16)
    values_all = (
        jnp.dot(normed_input_first, value_weight, preferred_element_type=jnp.float32)
        .astype(jnp.bfloat16)
        .reshape(tok_rows, kv_heads, HEAD_DIMENSION)
    )

    def visible_pairs(block_start):
        query_col = (block_start + jnp.arange(rows_per_block, dtype=jnp.int32))[:, None]
        key_row = jnp.arange(tok_rows, dtype=jnp.int32)[None, :]
        from_prompt = (key_row < prompt_rows) & (
            (query_col >= prompt_rows) | (key_row <= query_col)
        )
        same_cont = (
            (key_row >= prompt_rows)
            & (query_col >= prompt_rows)
            & (key_row <= query_col)
            & ((key_row - prompt_rows) // cont_rows == (query_col - prompt_rows) // cont_rows)
        )
        return from_prompt | same_cont

    def scores_of(query_block, block_start):
        raw_scores = (
            jnp.einsum("qhgd,khd->hgqk", query_block, keys_all, preferred_element_type=jnp.float32)
            * ATTENTION_SCALE
        )
        return jnp.where(visible_pairs(block_start)[None, None], raw_scores, MASKED_SCORE)

    def forward_block(parts):
        query_block, block_start = parts
        scores = scores_of(query_block, block_start)
        row_max = jnp.max(scores, axis=-1, keepdims=True)
        weights = jnp.exp(scores - row_max)
        row_total = jnp.sum(weights, axis=-1, keepdims=True)
        probs_low = (weights / row_total).astype(jnp.bfloat16)
        mixed = jnp.einsum(
            "hgqk,khd->qhgd", probs_low, values_all, preferred_element_type=jnp.float32
        )
        return (mixed.astype(jnp.bfloat16), row_max + jnp.log(row_total))

    query_blocks = rotated_queries.reshape(
        count_of_blocks, rows_per_block, kv_heads, query_groups, HEAD_DIMENSION
    )
    block_starts = jnp.arange(count_of_blocks, dtype=jnp.int32) * rows_per_block
    heads_blocks, log_total = lax.map(forward_block, (query_blocks, block_starts))
    head_outputs = heads_blocks.reshape(tok_rows, -1)
    head_terms = jnp.dot(head_outputs, w_output, preferred_element_type=jnp.float32)
    branch_half = lax.dynamic_slice_in_dim(
        lax.psum(head_terms, "head"), head_rank * half_rows, half_rows, 0
    )
    x_half = lax.dynamic_slice_in_dim(x_full, head_rank * half_rows, half_rows, 0)
    middle = x_half + RESIDUAL_SCALE * branch_half
    xn_two = rms_scale(middle, norm_two).astype(jnp.bfloat16)
    logits = jnp.dot(xn_two, w_router, preferred_element_type=jnp.float32)
    my_routes = lax.dynamic_slice_in_dim(routes, head_rank * half_rows, half_rows, 0)
    route_hot = my_routes[:, :, None] == jnp.arange(experts, dtype=jnp.int32)[None, None, :]
    chosen = jnp.sum(jnp.where(route_hot, logits[:, None, :], 0.0), axis=-1)
    chosen_max = jnp.max(chosen, axis=-1, keepdims=True)
    chosen_exp = jnp.exp(chosen - chosen_max)
    gate_probs = chosen_exp / jnp.sum(chosen_exp, axis=-1, keepdims=True)
    gate_low = gate_probs.astype(jnp.bfloat16)
    member = jnp.any(route_hot, axis=1).astype(jnp.bfloat16)
    order_rank = priority[0]
    earlier = (order_rank[None, :] < order_rank[:, None]).astype(jnp.bfloat16)
    before = jnp.dot(earlier, member, preferred_element_type=jnp.float32)
    slot_rank = jnp.sum(jnp.where(route_hot, before[:, None, :], 0.0), axis=-1).astype(jnp.int32)
    is_kept = slot_rank < capacity
    spare_slot = experts * capacity
    target = jnp.where(is_kept, my_routes * capacity + slot_rank, spare_slot)
    row_ids = jnp.broadcast_to(jnp.arange(half_rows, dtype=jnp.int32)[:, None], target.shape)
    assign_ids = jnp.arange(half_rows * TOPK, dtype=jnp.int32).reshape(target.shape)
    source_row = (
        jnp.zeros(spare_slot + 1, jnp.int32).at[target.ravel()].set(row_ids.ravel())[:spare_slot]
    )
    source_pick = (
        jnp.zeros(spare_slot + 1, jnp.int32).at[target.ravel()].set(assign_ids.ravel())[:spare_slot]
    )
    filled = jnp.zeros(spare_slot + 1, jnp.int32).at[target.ravel()].set(1)[:spare_slot] > 0
    slot_inputs = jnp.where(filled[:, None], xn_two[source_row], 0).reshape(
        experts, capacity, model_width
    )
    slot_gates = jnp.where(filled, gate_low.ravel()[source_pick], 0).reshape(experts, capacity)

    def to_owners(per_expert):
        shape_in = per_expert.shape
        spread = jnp.broadcast_to(per_expert[:, None], (shape_in[0], split) + shape_in[1:])
        return spread.reshape((exp_count, held) + shape_in[1:])

    def from_owners(per_owner):
        shape_in = per_owner.shape
        return jnp.sum(
            per_owner.reshape((experts, split) + shape_in[2:]).astype(jnp.float32), axis=1
        )

    gate_cols = w_gate.reshape(model_width, held, block_width)
    up_cols = w_up.reshape(model_width, held, block_width)
    down_rows = w_down.reshape(held, block_width, model_width)
    send_rows = to_owners(slot_inputs)
    send_gates = to_owners(slot_gates)
    slot_rows = lax.all_to_all(send_rows, "exp", split_axis=0, concat_axis=0, tiled=True)
    slot_gate = lax.all_to_all(send_gates, "exp", split_axis=0, concat_axis=0, tiled=True)
    gate_pre = jnp.einsum(
        "sjcd,djf->sjcf", slot_rows, gate_cols, preferred_element_type=jnp.float32
    )
    up_pre = jnp.einsum("sjcd,djf->sjcf", slot_rows, up_cols, preferred_element_type=jnp.float32)
    hidden = (gate_pre * jax.nn.sigmoid(gate_pre) * up_pre).astype(jnp.bfloat16)
    result = jnp.einsum("sjcf,jfd->sjcd", hidden, down_rows, preferred_element_type=jnp.float32)
    weighted = (slot_gate[..., None].astype(jnp.float32) * result).astype(jnp.bfloat16)
    returned = lax.all_to_all(weighted, "exp", split_axis=0, concat_axis=0, tiled=True)
    returned, held_rows, held_gates = (returned, slot_rows, slot_gate)
    back_flat = jnp.concatenate(
        [
            from_owners(returned).reshape(spare_slot, model_width),
            jnp.zeros((1, model_width), jnp.float32),
        ],
        axis=0,
    )
    expert_sum = jnp.sum(back_flat[target], axis=1)
    layer_out = (middle + RESIDUAL_SCALE * expert_sum).astype(jnp.bfloat16)
    out_grad = cotangent.astype(jnp.float32)
    weighted_rows = (RESIDUAL_SCALE * out_grad).astype(jnp.bfloat16)
    grad_slots = to_owners(
        jnp.where(filled[:, None], weighted_rows[source_row], 0).reshape(
            experts, capacity, model_width
        )
    )
    back_grads, back_rows, back_gates = (
        lax.all_to_all(grad_slots, "exp", split_axis=0, concat_axis=0, tiled=True),
        lax.all_to_all(send_rows, "exp", split_axis=0, concat_axis=0, tiled=True),
        lax.all_to_all(send_gates, "exp", split_axis=0, concat_axis=0, tiled=True),
    )
    owner_gates = back_gates[..., None].astype(jnp.float32)
    gate_pre = jnp.einsum(
        "sjcd,djf->sjcf", back_rows, gate_cols, preferred_element_type=jnp.float32
    )
    up_pre = jnp.einsum("sjcd,djf->sjcf", back_rows, up_cols, preferred_element_type=jnp.float32)
    gate_sigmoid = jax.nn.sigmoid(gate_pre)
    gate_act = gate_pre * gate_sigmoid
    hidden = (gate_act * up_pre).astype(jnp.bfloat16)
    result = jnp.einsum("sjcf,jfd->sjcd", hidden, down_rows, preferred_element_type=jnp.float32)
    gate_part = jnp.sum(back_grads.astype(jnp.float32) * result, axis=-1)
    result_grad = (owner_gates * back_grads).astype(jnp.bfloat16)
    grad_down_w = jnp.einsum(
        "sjcf,sjcd->jfd", hidden, result_grad, preferred_element_type=jnp.float32
    ).reshape(held_cols, model_width)
    hidden_grad = jnp.einsum(
        "sjcd,jfd->sjcf", result_grad, down_rows, preferred_element_type=jnp.float32
    )
    gate_pre_grad = (
        hidden_grad * up_pre * gate_sigmoid * (1.0 + gate_pre * (1.0 - gate_sigmoid))
    ).astype(jnp.bfloat16)
    up_pre_grad = (hidden_grad * gate_act).astype(jnp.bfloat16)
    grad_gate_w = jnp.einsum(
        "sjcd,sjcf->djf", back_rows, gate_pre_grad, preferred_element_type=jnp.float32
    ).reshape(model_width, held_cols)
    grad_up_w = jnp.einsum(
        "sjcd,sjcf->djf", back_rows, up_pre_grad, preferred_element_type=jnp.float32
    ).reshape(model_width, held_cols)
    rows_grad = (
        jnp.einsum("sjcf,djf->sjcd", gate_pre_grad, gate_cols, preferred_element_type=jnp.float32)
        + jnp.einsum("sjcf,djf->sjcd", up_pre_grad, up_cols, preferred_element_type=jnp.float32)
    ).astype(jnp.bfloat16)
    rows_back, gates_back = (
        lax.all_to_all(rows_grad, "exp", split_axis=0, concat_axis=0, tiled=True),
        lax.all_to_all(
            gate_part.astype(jnp.bfloat16), "exp", split_axis=0, concat_axis=0, tiled=True
        ),
    )
    rows_flat = jnp.concatenate(
        [
            from_owners(rows_back).reshape(spare_slot, model_width),
            jnp.zeros((1, model_width), jnp.float32),
        ],
        axis=0,
    )
    xn_two_grad = jnp.sum(rows_flat[target], axis=1)
    gate_total = from_owners(gates_back).astype(jnp.bfloat16).reshape(spare_slot)
    gates_flat = jnp.concatenate([gate_total, jnp.zeros((1,), jnp.bfloat16)], axis=0)
    gate_grad_tok = gates_flat[target].astype(jnp.float32)
    chosen_grad = gate_probs * (
        gate_grad_tok - jnp.sum(gate_probs * gate_grad_tok, axis=-1, keepdims=True)
    )
    logit_grad = jnp.sum(jnp.where(route_hot, chosen_grad[:, :, None], 0.0), axis=1).astype(
        jnp.bfloat16
    )
    grad_router = jnp.einsum("rd,re->de", xn_two, logit_grad, preferred_element_type=jnp.float32)
    xn_two_grad = xn_two_grad + jnp.einsum(
        "re,de->rd", logit_grad, w_router, preferred_element_type=jnp.float32
    )
    middle_norm_pull = jax.vjp(rms_scale, middle, norm_two)[1]
    middle_norm_grad, grad_norm_two = middle_norm_pull(xn_two_grad)
    middle_grad = out_grad + middle_norm_grad
    branch_rows = (RESIDUAL_SCALE * middle_grad).astype(jnp.bfloat16)
    branch_grad = lax.all_gather(branch_rows, "head", axis=0, tiled=True)
    heads_grad = jnp.einsum(
        "td,hd->th", branch_grad, w_output, preferred_element_type=jnp.float32
    ).astype(jnp.bfloat16)
    grad_output_w = jnp.einsum(
        "th,td->hd", head_outputs, branch_grad, preferred_element_type=jnp.float32
    )

    def backward_block(running, parts):
        key_grad, value_grad = running
        query_block, heads_block, block_total, block_start = parts
        scores = scores_of(query_block, block_start)
        probs = jnp.exp(scores - block_total)
        probs_low = probs.astype(jnp.bfloat16)
        prob_grad = jnp.einsum(
            "qhgd,khd->hgqk", heads_block, values_all, preferred_element_type=jnp.float32
        )
        row_inner = jnp.sum(probs * prob_grad, axis=-1, keepdims=True)
        score_grad = (probs * (prob_grad - row_inner)).astype(jnp.bfloat16)
        query_grad = (
            jnp.einsum("hgqk,khd->qhgd", score_grad, keys_all, preferred_element_type=jnp.float32)
            * ATTENTION_SCALE
        )
        key_grad = (
            key_grad
            + jnp.einsum(
                "hgqk,qhgd->khd", score_grad, query_block, preferred_element_type=jnp.float32
            )
            * ATTENTION_SCALE
        )
        value_grad = value_grad + jnp.einsum(
            "hgqk,qhgd->khd", probs_low, heads_block, preferred_element_type=jnp.float32
        )
        return ((key_grad, value_grad), query_grad)

    heads_grad_blocks = heads_grad.reshape(
        count_of_blocks, rows_per_block, kv_heads, query_groups, HEAD_DIMENSION
    )
    zero_keys = jnp.zeros((tok_rows, kv_heads, HEAD_DIMENSION), jnp.float32)
    (own_key, own_value), query_grad = lax.scan(
        backward_block,
        (zero_keys, zero_keys),
        (query_blocks, heads_grad_blocks, log_total, block_starts),
    )
    query_pre_grad = (
        rotate_back(query_grad.reshape(tok_rows, -1, HEAD_DIMENSION), cosine_values, sine_values)
        .reshape(tok_rows, -1)
        .astype(jnp.bfloat16)
    )
    key_pre_grad = (
        rotate_back(own_key, cosine_values, sine_values).reshape(tok_rows, -1).astype(jnp.bfloat16)
    )
    value_low_grad = own_value.reshape(tok_rows, -1).astype(jnp.bfloat16)
    grad_query_w = jnp.einsum(
        "td,th->dh", normed_input_first, query_pre_grad, preferred_element_type=jnp.float32
    )
    grad_key_w = jnp.einsum(
        "td,th->dh", normed_input_first, key_pre_grad, preferred_element_type=jnp.float32
    )
    grad_value_w = jnp.einsum(
        "td,th->dh", normed_input_first, value_low_grad, preferred_element_type=jnp.float32
    )
    xn_one_terms = (
        jnp.einsum("th,dh->td", query_pre_grad, w_query, preferred_element_type=jnp.float32)
        + jnp.einsum("th,dh->td", key_pre_grad, key_weight, preferred_element_type=jnp.float32)
        + jnp.einsum("th,dh->td", value_low_grad, value_weight, preferred_element_type=jnp.float32)
    )
    xn_one_grad = lax.psum_scatter(
        xn_one_terms.astype(jnp.bfloat16), "head", scatter_dimension=0, tiled=True
    ).astype(jnp.float32)
    input_norm_pull = jax.vjp(rms_scale, x_half, norm_one)[1]
    input_norm_grad, grad_norm_one = input_norm_pull(xn_one_grad)
    grad_tokens = middle_grad + input_norm_grad
    grad_gate_w, grad_up_w, grad_down_w, grad_router, grad_norm_one, grad_norm_two = (
        lax.psum(grad_gate_w.astype(jnp.bfloat16), "head").astype(jnp.float32),
        lax.psum(grad_up_w.astype(jnp.bfloat16), "head").astype(jnp.float32),
        lax.psum(grad_down_w.astype(jnp.bfloat16), "head").astype(jnp.float32),
        lax.psum(grad_router.astype(jnp.bfloat16), "head").astype(jnp.float32),
        lax.psum(grad_norm_one.astype(jnp.bfloat16), "head").astype(jnp.float32),
        lax.psum(grad_norm_two.astype(jnp.bfloat16), "head").astype(jnp.float32),
    )
    (
        grad_query_w,
        grad_key_w,
        grad_value_w,
        grad_output_w,
        grad_router,
        grad_norm_one,
        grad_norm_two,
    ) = lax.psum(
        (
            grad_query_w,
            grad_key_w,
            grad_value_w,
            grad_output_w,
            grad_router,
            grad_norm_one,
            grad_norm_two,
        ),
        "exp",
    )
    return (
        layer_out,
        grad_tokens,
        grad_norm_one,
        grad_query_w,
        grad_key_w,
        grad_value_w,
        grad_output_w,
        grad_norm_two,
        grad_router,
        grad_gate_w,
        grad_up_w,
        grad_down_w,
    )


MESH = pl.DeviceIdType.MESH
FLAT = 128
SLOTS = 40
PAIR = 2 * SLOTS
UNKEPT = -1000.0
LOW = jnp.bfloat16
FULL = jnp.float32
LAST = (((1,), (1,)), ((), ()))
FIRST = (((0,), (0,)), ((), ()))
USUAL = (((1,), (0,)), ((), ()))


def mul(left, right, dims=USUAL):
    return lax.dot_general(left, right, dims, preferred_element_type=FULL)


def remote(source, target, send_sem, recv_sem, device):
    return pltpu.make_async_remote_copy(
        src_ref=source,
        dst_ref=target,
        send_sem=send_sem,
        recv_sem=recv_sem,
        device_id=device,
        device_id_type=MESH,
    )


def part(ref, *index):
    return lambda: ref.at[index]


def whole(ref):
    return lambda: ref


class Places:
    def __init__(self):
        self.e = e = lax.axis_index("exp")
        self.h = h = lax.axis_index("head")
        x, y, self.z = e % 2, (e // 2) % 2, e // 4
        z = self.z
        over_x, over_y = e + 1 - 2 * x, e + 2 - 4 * y
        self.near_e = over_x * (1 - h) + over_y * h
        self.far_e = over_y * (1 - h) + over_x * h
        self.near = (self.near_e, h)
        self.far = (self.far_e, h)
        self.outer = (1 + z % 2 + z // 2) % 2
        self.ranks = [z, z + 1 - 2 * (z % 2), 2 - z // 2, 3 - 3 * (z // 2)]
        self.along = [(rank * 4 + e % 4, h) for rank in self.ranks]
        self.edge = self.along[1]
        self.inner = ((3 - z) * 4 + e % 4, h)
        self.pair = (e, 1 - h)
        self.is_inner = (z == 1) | (z == 2)

    def hello(self):
        barrier = pltpu.get_barrier_semaphore()
        for device in (self.pair, self.near, self.far, *self.along[1:]):
            pl.semaphore_signal(barrier, inc=1, device_id=device, device_id_type=MESH)

    def ready(self):
        pl.semaphore_wait(pltpu.get_barrier_semaphore(), 6)


class Links:
    def __init__(self, places, send, recv):
        self.places, self.send, self.recv = places, send, recv
        self.sent, self.names = 0, {}
        self.pending = {"all": [], "inner": []}

    def number(self, name):
        return self.names.setdefault(name, len(self.names))

    def go(self, name, source, target, device, who="all", number=None):
        arrival = self.number(name) if number is None else number
        number = self.sent
        remote(
            source(), target(), self.send.at[number], self.recv.at[arrival], device
        ).start()
        self.sent += 1
        self.pending[who].append((number, name, source))

    def got(self, name, target):
        remote(
            target(), target(), self.send.at[0], self.recv.at[self.number(name)], self.places.near
        ).wait_recv()

    def sent_all(self, who, of):
        for number, name, source in self.pending[who]:
            if of is None or name[0] == of:
                remote(
                    source(), source(), self.send.at[number], self.recv.at[0], self.places.near
                ).wait_send()

    def drain(self, of=None):
        self.sent_all("all", of)

        @pl.when(self.places.is_inner)
        def _():
            self.sent_all("inner", of)

        for who, sent in self.pending.items():
            self.pending[who] = [one for one in sent if of is not None and one[1][0] != of]


class Spread:
    def __init__(self, links, name, gathered, pieces=((),)):
        self.links, self.name, self.gathered, self.pieces = links, name, gathered, pieces

    def spot(self, i, a, n):
        return part(self.gathered, i, a, *self.pieces[n])

    def start(self):
        links, places = self.links, self.links.places
        for n in range(len(self.pieces)):
            block = self.spot(0, 0, n)
            links.go((self.name, "z", 1, n), block, self.spot(1, 0, n), places.edge)
            links.go((self.name, "n", 0, n), block, self.spot(0, 1, n), places.near)

            @pl.when(places.is_inner)
            def _():
                links.go(
                    (self.name, "z", 2, n), block, self.spot(2, 0, n), places.inner, "inner"
                )

    def pass_on(self, i):
        links, places = self.links, self.links.places
        there = {1: 3, 2: 2, 3: 3}[i]
        device = places.inner if i == 1 else places.edge
        for n in range(len(self.pieces)):
            block = self.spot(i, 0, n)
            links.got((self.name, "z", i, n), block)

            @pl.when(places.is_inner)
            def _():
                links.go(
                    (self.name, "z", there, n), block, self.spot(there, 0, n), device, "inner"
                )

            links.go((self.name, "n", i, n), block, self.spot(i, 1, n), places.near)

    def wait(self, i, n=0):
        self.links.got((self.name, "n", i, n), self.spot(i, 1, n))


class Gather:
    def __init__(self, links, name, send, recv, pieces):
        self.links, self.name, self.send, self.recv, self.pieces = links, name, send, recv, pieces
        for n in range(len(pieces)):
            for slot in (1, 2, 3):
                links.number((name, n, slot))

    def push(self, i, value):
        links, places = self.links, self.links.places
        for n, piece in enumerate(self.pieces):
            spot = part(self.send, i, *piece)
            spot()[...] = value(n).astype(self.send.dtype)
            slot = 1 if i == 1 else 2 + places.outer
            links.go(
                (self.name, n, 1),
                spot,
                part(self.recv, slot, *piece),
                places.along[i],
                number=links.number((self.name, n, 1)) + slot - 1,
            )

    def total(self, own, result):
        for n, piece in enumerate(self.pieces):
            value = own(n)
            for slot in (1, 2, 3):
                spot = part(self.recv, slot, *piece)
                self.links.got((self.name, n, slot), spot)
                value = value + spot()[...].astype(FULL)
            result(n)[...] = value


def table_rows(tables, i, places):
    rows = []
    for chip in (places.e, places.far_e):
        for j in range(2):
            rows.append(
                jnp.concatenate(
                    [tables[i, a, pl.ds(2 * chip + j, 1), :] for a in range(2)], axis=1
                )
            )
    return rows


def selection(tables, i, places):
    slot = lax.broadcasted_iota(jnp.int32, (PAIR, 2 * FLAT), 0)
    lane = lax.broadcasted_iota(jnp.int32, (PAIR, 2 * FLAT), 1)
    wanted = (slot - jnp.where(lane >= FLAT, SLOTS, 0)).astype(FULL)
    return jnp.concatenate(
        [jnp.where(row == wanted, 1.0, 0.0) for row in table_rows(tables, i, places)], axis=0
    )


def turn(block, cosine, sine, sign):
    lane = lax.broadcasted_iota(jnp.int32, block.shape, 1) % HEAD_DIMENSION
    quarter = HEAD_DIMENSION // 2
    other = jnp.where(
        lane < quarter,
        -sign * pltpu.roll(block, FLAT - quarter, 1),
        sign * pltpu.roll(block, quarter, 1),
    )
    return block * cosine + other * sine


def layer_kernel(names, *refs):
    r = types.SimpleNamespace(**dict(zip(names, refs, strict=True)))
    places = Places()
    h, e, z = places.h, places.e, places.z
    places.hello()
    links = Links(places, r.sems_send, r.sems_recv)
    experts = r.w_router.shape[0]
    rows_here, width = r.tokens.shape
    q_cols, k_cols = r.w_query.shape[1], r.key_weight.shape[1]
    kv_heads = k_cols // HEAD_DIMENSION
    every = slice(None)
    half = pl.multiple_of(h * FLAT, FLAT)
    other_half = pl.multiple_of((1 - h) * FLAT, FLAT)
    locals_used = [0]

    def load(source, target):
        copy = pltpu.make_async_copy(source, target, r.sems_local.at[locals_used[0]])
        locals_used[0] += 1
        copy.start()
        return copy

    in_loads = [
        load(r.w_query, r.w_in.at[:, :q_cols]),
        load(r.key_weight, r.w_in.at[:, q_cols : q_cols + k_cols]),
        load(r.value_weight, r.w_in.at[:, q_cols + k_cols :]),
    ]
    out_load = load(r.w_output, r.w_out)
    rank_row = r.priority[...]
    row_id = lax.broadcasted_iota(jnp.int32, (FLAT, FLAT), 0)
    col_id = lax.broadcasted_iota(jnp.int32, (FLAT, FLAT), 1)
    rank_col = jnp.sum(
        jnp.where(row_id == col_id, jnp.broadcast_to(rank_row, (FLAT, FLAT)), 0),
        axis=1,
        keepdims=True,
    )
    earlier = jnp.where(rank_row < rank_col, 1.0, 0.0).astype(LOW)
    expert_id = lax.broadcasted_iota(jnp.int32, (experts, FLAT), 0)
    my_routes = r.routes[:, pl.ds(half, FLAT)]
    member = jnp.zeros((experts, FLAT), FULL)
    for k in range(TOPK):
        member += jnp.where(my_routes[k : k + 1, :] == expert_id, 1.0, 0.0)
    before = mul(member.astype(LOW), earlier, LAST)
    r.tables[0, 0] = jnp.where((member > 0.5) & (before < SLOTS), before, UNKEPT)
    r.g_all[0, 0] = (RESIDUAL_SCALE * r.cotangent[...].astype(FULL)).astype(LOW)
    columns = [slice(0, width // 2), slice(width // 2, width)]
    halves = [(every, one) for one in columns]
    t_spread = Spread(links, "t", r.tables)
    g_spread = Spread(links, "g", r.g_all, halves)
    x_spread = Spread(links, "x", r.x_all, halves)
    p_spread = Spread(links, "p", r.gate_tables)
    x_full = r.tokens[...].astype(FULL)
    r.normed[...] = rms_scale(x_full, r.norm_one[...]).astype(LOW)
    places.ready()
    t_spread.start()
    g_spread.start()

    for copy in in_loads:
        copy.wait()
    expert_loads = [load(r.w_gate, r.gate_w), load(r.w_up, r.up_w), load(r.w_down, r.down_w)]
    projected = mul(r.normed[...], r.w_in[...])
    cosine, sine = r.cosine[...], r.sine[...]
    lane = lax.broadcasted_iota(jnp.int32, (rows_here, FLAT), 1)
    low_lanes = lane < HEAD_DIMENSION
    for g in range(kv_heads):
        r.q[g] = turn(projected[:, g * FLAT : (g + 1) * FLAT], cosine, sine, 1.0).astype(LOW)
    for m in range(kv_heads // 2):
        start = q_cols + m * FLAT
        keys = turn(projected[:, start : start + FLAT], cosine, sine, 1.0)
        start += k_cols
        values = projected[:, start : start + FLAT]
        for block, store in ((keys, r.keys), (values, r.values)):
            rolled = pltpu.roll(block, HEAD_DIMENSION, 1)
            store[2 * m, 0] = jnp.where(low_lanes, block, 0.0).astype(LOW)
            store[2 * m, 1] = jnp.where(low_lanes, 0.0, rolled).astype(LOW)
            store[2 * m + 1, 0] = jnp.where(low_lanes, rolled, 0.0).astype(LOW)
            store[2 * m + 1, 1] = jnp.where(low_lanes, 0.0, block).astype(LOW)
    prompt, cont = rows_here // 2, rows_here // 4
    query_id = lax.broadcasted_iota(jnp.int32, (rows_here, rows_here), 0)
    key_id = lax.broadcasted_iota(jnp.int32, (rows_here, rows_here), 1)
    query_cont = jnp.where(query_id < prompt, 0, 1 + (query_id - prompt) // cont)
    key_cont = jnp.where(key_id < prompt, 0, 1 + (key_id - prompt) // cont)
    visible = ((key_cont == 0) & (query_cont > 0)) | (
        (key_cont == query_cont) & (key_id <= query_id)
    )
    r.bias[...] = jnp.where(visible, 0.0, MASKED_SCORE)

    def attend(first, count):
        def one(g, carry):
            mixed = jnp.zeros((rows_here, FLAT), FULL)
            for s in range(2):
                raw = mul(r.q[g], r.keys[g, s], LAST) * ATTENTION_SCALE
                scores = jnp.where(r.bias[...] < 0.0, MASKED_SCORE, raw)
                weights = jnp.exp(scores - jnp.max(scores, axis=1, keepdims=True))
                probs = weights / jnp.sum(weights, axis=1, keepdims=True)
                r.att_probs[g, s] = probs
                mixed += mul(probs.astype(LOW), r.values[g, s])
            r.heads[:, pl.ds(pl.multiple_of(g * FLAT, FLAT), FLAT)] = mixed.astype(LOW)
            return carry

        lax.fori_loop(first, first + count, one, 0)

    def pick_rows(name, spread, picks, gathered, slots, send, i):
        for n, cols in enumerate(columns):
            spread.wait(i, n)
            rows = mul(picks, gathered[i, :, :, cols].reshape(2 * FLAT, -1)).astype(LOW)
            slots[i, :, :, cols] = rows[: 2 * PAIR].reshape(2, PAIR, -1)
            send[i, :, :, cols] = rows[2 * PAIR :].reshape(2, PAIR, -1)
            links.go(
                (name, "f", i, n),
                part(send, i, every, every, cols),
                part(slots, 4 + i, every, every, cols),
                places.far,
            )

    def dispatch_out(i):
        t_spread.wait(i)
        picks = selection(r.tables, i, places).astype(LOW)
        r.pick[i] = picks
        pick_rows("g", g_spread, picks, r.g_all, r.g_slots, r.g_send, i)

    def pass_out(i):
        t_spread.pass_on(i)
        g_spread.pass_on(i)

    attend(0, 4)
    out_load.wait()
    r.branch_send[...] = mul(r.heads[pl.ds(other_half, FLAT), :], r.w_out[...])
    links.go("branch", whole(r.branch_send), whole(r.branch_in), places.pair)
    own_branch = mul(r.heads[pl.ds(half, FLAT), :], r.w_out[...])
    links.got("branch", whole(r.branch_in))
    middle = r.tokens[pl.ds(half, FLAT), :].astype(FULL) + RESIDUAL_SCALE * (
        own_branch + r.branch_in[...]
    )
    r.middle[...] = middle
    xn = rms_scale(middle, r.norm_two[...]).astype(LOW)
    r.x_all[0, 0] = xn
    x_spread.start()
    logits = mul(r.w_router[...], xn, LAST)
    chosen = jnp.where(member > 0.5, logits, MASKED_SCORE)
    weights = jnp.exp(chosen - jnp.max(chosen, axis=0, keepdims=True))
    probs = weights / jnp.sum(weights, axis=0, keepdims=True)
    r.probs[...] = probs
    r.gate_tables[0, 0] = probs.astype(LOW).astype(FULL)
    p_spread.start()

    slots_lane = lax.broadcasted_iota(jnp.int32, (2 * PAIR, FLAT), 1)
    r.gates[...] = jnp.zeros((2 * PAIR, FLAT), FULL)
    r.gate_send[...] = jnp.zeros((2, 2 * PAIR, FLAT), LOW)

    def dispatch_in(i):
        picks = r.pick[i]
        pick_rows("x", x_spread, picks, r.x_all, r.x_slots, r.x_send, i)
        p_spread.wait(i)
        spread_gates = jnp.concatenate(
            [
                jnp.broadcast_to(row, (PAIR, 2 * FLAT))
                for row in table_rows(r.gate_tables, i, places)
            ],
            axis=0,
        )
        slot_gates = jnp.sum(picks.astype(FULL) * spread_gates, axis=1, keepdims=True)
        r.gates[...] += jnp.where(slots_lane == i, slot_gates[: 2 * PAIR], 0.0)
        far_gates = jnp.where(slots_lane == 4 + i, slot_gates[2 * PAIR :], 0.0)
        r.gate_send[i // 2] += far_gates.astype(LOW)

    def send_gates(n):
        links.go(("p", "f", n), part(r.gate_send, n), part(r.gate_far, n), places.far)

    def add_gates(n):
        links.got(("p", "f", n), part(r.gate_far, n))
        r.gates[...] += r.gate_far[n].astype(FULL)

    def pass_in(i):
        x_spread.pass_on(i)
        p_spread.pass_on(i)

    pass_out(1)
    dispatch_out(0)
    pass_out(2)
    dispatch_in(0)
    dispatch_out(1)
    pass_in(1)
    pass_out(3)
    dispatch_in(1)
    send_gates(0)
    pass_in(2)
    dispatch_out(2)
    pass_in(3)
    dispatch_out(3)
    dispatch_in(2)
    dispatch_in(3)
    send_gates(1)

    slot_lane = lax.broadcasted_iota(jnp.int32, (PAIR, FLAT), 1)
    r.parts[...] = jnp.zeros((2 * PAIR, FLAT), FULL)

    def run_experts(first, count):
        span = count * PAIR
        which = slice(first, first + count)
        place = slice(first * PAIR, (first + count) * PAIR)

        def one_expert(j, carry):
            base = pl.multiple_of(j * PAIR, PAIR)
            gates = r.gates[pl.ds(base, PAIR), :]
            gate_col = jnp.concatenate(
                [gates[:, p : p + 1] for p in range(first, first + count)], axis=0
            )
            columns = pl.ds(pl.multiple_of(j * FF, FF), FF)
            xs = r.x_slots[which, j].reshape(span, -1)
            gate_pre = mul(xs, r.gate_w[:, columns])
            up_pre = mul(xs, r.up_w[:, columns])
            sig = jax.nn.sigmoid(gate_pre)
            act = gate_pre * sig
            hidden = (act * up_pre).astype(LOW)
            r.hidden_all[j, place] = hidden
            result = mul(hidden, r.down_w[columns, :])
            gs = r.g_slots[which, j].reshape(span, -1).astype(FULL)
            r.g_slots[which, j] = (gate_col * result).astype(LOW).reshape(count, PAIR, -1)
            part = jnp.sum(gs * result, axis=1, keepdims=True).astype(LOW).astype(FULL)
            terms = jnp.zeros((PAIR, FLAT), FULL)
            for p in range(count):
                terms += jnp.where(
                    slot_lane == first + p, part[p * PAIR : (p + 1) * PAIR], 0.0
                )
            r.parts[pl.ds(base, PAIR), :] += terms
            result_grad = (gate_col * gs).astype(LOW)
            r.result_all[j, place] = result_grad
            hidden_grad = mul(result_grad, r.down_w[columns, :], LAST)
            gate_pre_grad = (
                hidden_grad * up_pre * sig * (1.0 + gate_pre * (1.0 - sig))
            ).astype(LOW)
            up_pre_grad = (hidden_grad * act).astype(LOW)
            r.gate_all[j, place] = gate_pre_grad
            r.up_all[j, place] = up_pre_grad
            rows_grad = mul(gate_pre_grad, r.gate_w[:, columns], LAST) + mul(
                up_pre_grad, r.up_w[:, columns], LAST
            )
            r.row_slots[which, j] = rows_grad.astype(LOW).reshape(count, PAIR, -1)
            return carry

        lax.fori_loop(0, 2, one_expert, 0)

    for copy in expert_loads:
        copy.wait()
    writes = []

    def weight_grads(j):
        xs = r.x_slots[:, j].reshape(8 * PAIR, -1)
        columns = slice(j * FF, (j + 1) * FF)
        r.gate_w[:, columns] = mul(xs, r.gate_all[j], FIRST).astype(LOW)
        r.up_w[:, columns] = mul(xs, r.up_all[j], FIRST).astype(LOW)
        r.down_w[columns, :] = mul(r.hidden_all[j], r.result_all[j], FIRST).astype(LOW)

    mine_at = pl.ds(pl.multiple_of(h * FF, FF), FF)
    theirs_at = pl.ds(pl.multiple_of((1 - h) * FF, FF), FF)
    top = r.hidden_all.shape[1]
    low_rows = width - top
    exchange = [
        (r.gate_w, (pl.ds(0, top), theirs_at), r.hidden_all, (0,)),
        (r.gate_w, (pl.ds(top, low_rows), theirs_at), r.hidden_all, (1, pl.ds(0, low_rows))),
        (r.up_w, (pl.ds(0, top), theirs_at), r.gate_all, (0,)),
        (r.up_w, (pl.ds(top, low_rows), theirs_at), r.gate_all, (1, pl.ds(0, low_rows))),
        (r.down_w, (theirs_at, pl.ds(0, FF)), r.up_all, (0, pl.ds(0, FF))),
        (r.down_w, (theirs_at, pl.ds(FF, FF)), r.up_all, (1, pl.ds(0, FF))),
    ]
    finals = [
        (r.gate_w, r.gate_out, (every, mine_at), (every, theirs_at)),
        (r.up_w, r.up_out, (every, mine_at), (every, theirs_at)),
        (r.down_w, r.down_out, (mine_at, every), (theirs_at, every)),
    ]

    def send_grads():
        for n, (source, spot, target, there) in enumerate(exchange):
            links.go(("e", n), part(source, *spot), part(target, *there), places.pair)

    def sum_grads():
        for n, (own, spot, other, there) in enumerate(exchange):
            links.got(("e", n), part(other, *there))
            spot = tuple(mine_at if one is theirs_at else one for one in spot)
            own[spot] = (own[spot].astype(FULL) + other[there].astype(FULL)).astype(LOW)
        for n, (source, out, spot, _) in enumerate(finals):
            writes.append(load(source.at[spot], out.at[spot]))
            links.go(("ef", n), part(source, *spot), part(out, *spot), places.pair)

    index = lax.broadcasted_iota(jnp.int32, (experts, 2 * FLAT), 0)

    def fold(name, rows, rows_in, kept, near_send, near_in, i):
        for n, cols in enumerate(columns):
            links.got((name, "f", i, n), part(rows_in, i, every, every, cols))
            stacked = jnp.concatenate(
                [
                    rows[i, :, :, cols].reshape(2 * PAIR, -1),
                    rows_in[i, :, :, cols].reshape(2 * PAIR, -1),
                ],
                axis=0,
            )
            sums = mul(r.pick[i], stacked, FIRST)
            kept[i, :, cols] = sums[:FLAT]
            send = near_send(i, cols)
            send()[...] = sums[FLAT:].astype(LOW)
            links.go((name, "n", i, n), send, part(near_in, i, every, cols), places.near)

    def send_far(name, rows, rows_in, i):
        for n, cols in enumerate(columns):
            links.go(
                (name, "f", i, n),
                part(rows, 4 + i, every, every, cols),
                part(rows_in, i, every, every, cols),
                places.far,
            )

    def fold_parts(i):
        column = jnp.concatenate(
            [r.parts[:, i : i + 1], r.parts_in[:, 4 + i : 5 + i]], axis=0
        )
        terms = r.pick[i].astype(FULL) * column
        table = jnp.zeros((experts, 2 * FLAT), FULL)
        chips = (places.e, places.e, places.far_e, places.far_e)
        for n, chip in enumerate(chips):
            total = jnp.sum(terms[n * PAIR : (n + 1) * PAIR], axis=0, keepdims=True)
            table += jnp.where(index == 2 * chip + n % 2, total, 0.0)
        r.part_kept[i] = table[:, :FLAT]
        r.part_send[i] = table[:, FLAT:]
        links.go(("q", "n", i, 0), part(r.part_send, i), part(r.part_near, i), places.near)

    row_sums = Gather(links, "rz", r.row_z_send, r.row_z_in, halves)
    part_sums = Gather(links, "qz", r.part_z_send, r.part_z_in, [()])
    weighted_sums = Gather(links, "wz", r.row_near_send, r.weighted_z_in, halves)

    def near_sum(name, kept, near_in, i, pieces):
        def value(n):
            spot = (i, *pieces[n])
            links.got((name, "n", i, n), part(near_in, *spot))
            return kept[spot] + near_in[spot].astype(FULL)

        return value

    def settle_rows(i):
        row_sums.push(i, near_sum("r", r.row_kept, r.row_near, i, row_sums.pieces))

    def settle_parts(i):
        part_sums.push(i, near_sum("q", r.part_kept, r.part_near, i, part_sums.pieces))

    def settle_weighted(i):
        weighted_sums.push(i, near_sum("w", r.row_kept, r.weighted_near, i, halves))

    def fold_weighted(i):
        fold(
            "w",
            r.g_slots,
            r.g_send,
            r.row_kept,
            lambda i, cols: part(r.x_all, i, 0, every, cols),
            r.weighted_near,
            i,
        )

    def far_experts(i):
        for n, cols in enumerate(columns):
            links.got(("g", "f", i, n), part(r.g_slots, 4 + i, every, every, cols))
            links.got(("x", "f", i, n), part(r.x_slots, 4 + i, every, every, cols))
        run_experts(4 + i, 1)
        send_far("r", r.row_slots, r.rows_in, i)

    def fold_rows(i):
        fold(
            "r",
            r.row_slots,
            r.rows_in,
            r.row_kept,
            lambda i, cols: part(r.row_near_send, i, every, cols),
            r.row_near,
            i,
        )

    add_gates(0)
    far_experts(1)
    far_experts(0)
    run_experts(0, 4)
    links.drain()
    add_gates(1)
    fold_rows(1)
    far_experts(3)
    far_experts(2)
    links.go(("q", "f"), whole(r.parts), whole(r.parts_in), places.far)
    settle_rows(1)
    fold_rows(3)
    fold_rows(2)
    settle_rows(3)
    links.got(("q", "f"), whole(r.parts_in))
    for i in (3, 2, 1, 0):
        fold_parts(i)
    settle_rows(2)
    for i in (3, 2, 1):
        settle_parts(i)
    fold_rows(0)
    def send_weighted(i):
        send_far("w", r.g_slots, r.g_send, i)

    send_weighted(3)
    send_weighted(2)
    weight_grads(0)
    weight_grads(1)
    fold_weighted(3)
    send_weighted(1)
    fold_weighted(2)
    send_weighted(0)
    fold_weighted(1)
    row_sums.total(
        near_sum("r", r.row_kept, r.row_near, 0, halves), lambda n: r.branch_in.at[halves[n]]
    )
    part_sums.total(
        near_sum("q", r.part_kept, r.part_near, 0, part_sums.pieces), lambda n: r.part_total
    )

    gate_probs, gate_grad = r.probs[...], r.part_total[...]
    chosen_grad = gate_probs * (
        gate_grad - jnp.sum(gate_probs * gate_grad, axis=0, keepdims=True)
    )
    logit_grad = chosen_grad.astype(LOW)
    xn_grad = r.branch_in[...] + mul(logit_grad, r.w_router[...], FIRST)
    mid = r.middle[...]
    scale = lax.rsqrt(jnp.mean(mid * mid, axis=-1, keepdims=True) + NORM_EPS)
    scaled = r.norm_two[...] * xn_grad
    pull = jnp.mean(scaled * mid, axis=-1, keepdims=True)
    grad = r.cotangent[...].astype(FULL) + scale * scaled - mid * (scale * scale * scale * pull)
    r.grad_tokens[...] = grad
    mine = part(r.branch_grad, pl.ds(half, FLAT))
    r.branch_grad[pl.ds(half, FLAT), :] = (RESIDUAL_SCALE * grad).astype(LOW)
    links.go("bg", mine, mine, places.pair)
    r.small[pl.ds(0, experts), :] = mul(logit_grad, r.x_all[0, 0])
    r.small[pl.ds(experts, 8), :] = jnp.broadcast_to(
        jnp.sum(xn_grad * mid * scale, axis=0, keepdims=True), (8, width)
    )

    links.drain("r")
    for i in (3, 2, 1):
        settle_weighted(i)
    fold_weighted(0)
    links.got("bg", part(r.branch_grad, pl.ds(other_half, FLAT)))
    r.heads_grad[...] = mul(r.branch_grad[...], r.w_out[...], LAST).astype(LOW)
    r.grads[pl.ds(width, q_cols), :] = mul(r.heads[...], r.branch_grad[...], FIRST).astype(LOW)
    cosine, sine = r.cosine[...], r.sine[...]

    def attend_back(first, count):
        def one(g, carry):
            place = pl.ds(pl.multiple_of(g * FLAT, FLAT), FLAT)
            out_grad = r.heads_grad[:, place]
            query = r.q[g]
            query_grad = jnp.zeros((rows_here, FLAT), FULL)
            key_grads, value_grads = [], []
            for s in range(2):
                probs = r.att_probs[g, s]
                prob_grad = mul(out_grad, r.values[g, s], LAST)
                inner = jnp.sum(probs * prob_grad, axis=1, keepdims=True)
                score_grad = (probs * (prob_grad - inner)).astype(LOW)
                query_grad += mul(score_grad, r.keys[g, s])
                key_grads.append(mul(score_grad, query, FIRST))
                value_grads.append(mul(probs.astype(LOW), out_grad, FIRST))
            r.head_grads[:, place] = turn(
                query_grad * ATTENTION_SCALE, r.cosine[...], r.sine[...], -1.0
            ).astype(LOW)
            r.key_sums[g] = key_grads[0] + pltpu.roll(key_grads[1], HEAD_DIMENSION, 1)
            r.value_sums[g] = value_grads[0] + pltpu.roll(value_grads[1], HEAD_DIMENSION, 1)
            return carry

        lax.fori_loop(first, first + count, one, 0)

    ranks = places.ranks
    plane = [[e % 4, places.near_e % 4], [places.far_e % 4, 3 - e % 4]]

    def along(name, spot):
        block = spot(0)
        links.go((name, "z", 1), block, block, places.edge)

        @pl.when(places.is_inner)
        def _():
            links.go((name, "z", 2), block, block, places.inner, "inner")

    def pass_along(name, spot, i):
        block = spot(i)
        links.got((name, "z", i), block)
        there = {1: 3, 2: 2, 3: 3}[i]
        device = places.inner if i == 1 else places.edge

        @pl.when(places.is_inner)
        def _():
            links.go((name, "z", there), block, block, device, "inner")

    class Reduce:
        order = [(a, i) for i in (3, 2, 1, 0) for a in (1, 0)]

        def __init__(self, name, first, count, room, near_first=False):
            self.name, self.first, self.depth, self.room = name, first, count // 16, room
            self.near_first = near_first
            self.rows = slice(room, room + self.depth)
            self.issued = 0
            self.sums = Gather(links, name + "z", r.sum_z_send, r.sum_z_in, [(self.rows,)])

        def shard(self, b, a, i):
            start = self.first + (ranks[i] * 4 + plane[b][a]) * self.depth
            return pl.ds(pl.multiple_of(start, 16), self.depth)

        def far_in(self, a, i):
            return part(r.g_all, i, a, self.rows)

        def near_in(self, i):
            return part(r.x_all, i, 1, self.rows)

        def near_send(self, i):
            return part(r.result_all, 0, pl.ds(4 * self.room + i * self.depth, self.depth))

        def send(self, count):
            for a, i in self.order[self.issued : self.issued + count]:
                source = part(r.grads, self.shard(1, a, i))
                links.go((self.name, "f", a, i), source, self.far_in(a, i), places.far)
            self.issued += count

        def fold(self, i):
            for a in (1, 0):
                links.got((self.name, "f", a, i), self.far_in(a, i))
                self.send(1)
                if a:
                    total = r.grads[self.shard(0, 1, i), :].astype(FULL) + r.g_all[
                        i, 1, self.rows
                    ].astype(FULL)
                    self.near_send(i)()[...] = total.astype(LOW)
                    links.go(
                        (self.name, "n", i), self.near_send(i), self.near_in(i), places.near
                    )

        def near_sum(self, i):
            links.got((self.name, "n", i), self.near_in(i))
            mine = self.shard(0, 0, i)
            return lambda n: (
                r.grads[mine, :].astype(FULL)
                + r.g_all[i, 0, self.rows].astype(FULL)
                + r.x_all[i, 1, self.rows].astype(FULL)
            )

        def settle(self, i):
            self.sums.push(i, self.near_sum(i))

        def spot(self, b, a, i):
            return part(r.grads_out, self.shard(b, a, i))

        def share(self):
            total = r.branch_send.at[self.rows]
            self.sums.total(self.near_sum(0), lambda n: total)
            low = part(r.result_all, 1, pl.ds(FLAT + self.room, self.depth))
            low()[...] = total[...].astype(LOW)
            mine = self.spot(0, 0, 0)
            links.go((self.name + "o", "z", 1), low, mine, places.edge)
            links.go((self.name, "on", 0), low, mine, places.near)

            @pl.when(places.is_inner)
            def _():
                links.go((self.name + "o", "z", 2), low, mine, places.inner, "inner")

            links.go((self.name, "of", 0, 0), low, mine, places.far)
            writes.append(load(low(), mine()))

        def pass_far(self, i):
            block = self.spot(0, 1, i)
            if i and self.near_first:
                pass_along(self.name + "p", lambda i: self.spot(0, 1, i), i)
            else:
                links.got((self.name, "on", i), block)
                if self.near_first:
                    along(self.name + "p", lambda i: self.spot(0, 1, i))
            links.go((self.name, "of", 1, i), block, block, places.far)

        def pass_on(self, i):
            block = self.spot(0, 0, i)
            pass_along(self.name + "o", lambda i: self.spot(0, 0, i), i)
            if not self.near_first:
                links.go((self.name, "on", i), block, block, places.near)
            links.go((self.name, "of", 0, i), block, block, places.far)

        def finish(self):
            for i in range(4):
                for a in range(2):
                    links.got((self.name, "of", a, i), self.spot(1, a, i))

    late = Reduce("b", width, q_cols, 0)
    early = Reduce("a", 0, width, q_cols // 16, near_first=True)
    late.send(8)
    attend_back(0, 4)
    for m in range(kv_heads // 2):
        start = q_cols + m * FLAT
        for sums, shift in ((r.key_sums, 0), (r.value_sums, k_cols)):
            block = jnp.where(
                low_lanes, sums[2 * m], pltpu.roll(sums[2 * m + 1], HEAD_DIMENSION, 1)
            )
            if shift == 0:
                block = turn(block * ATTENTION_SCALE, cosine, sine, -1.0)
            r.head_grads[:, start + shift : start + shift + FLAT] = block.astype(LOW)
    head_grads = r.head_grads
    r.grads[pl.ds(0, width), :] = mul(r.normed[...], head_grads[...], FIRST).astype(LOW)
    early.send(8)
    r.result_all[1, 0:FLAT] = mul(
        head_grads[pl.ds(other_half, FLAT), :], r.w_in[...], LAST
    ).astype(LOW)
    links.go("terms", part(r.result_all, 1, pl.ds(0, FLAT)), whole(r.terms_in), places.pair)
    own_terms = mul(head_grads[pl.ds(half, FLAT), :], r.w_in[...], LAST).astype(LOW)
    send_grads()
    late.fold(3)
    late.fold(2)
    late.fold(1)
    late.fold(0)
    late.settle(3)
    late.settle(2)
    late.settle(1)
    early.fold(3)
    early.fold(2)
    early.settle(3)
    early.fold(1)
    early.settle(2)
    early.fold(0)
    late.share()
    early.settle(1)
    links.got("terms", whole(r.terms_in))
    xn_grad = (own_terms.astype(FULL) + r.terms_in[...].astype(FULL)).astype(LOW).astype(FULL)
    x_half = r.tokens[pl.ds(half, FLAT), :].astype(FULL)
    scale = lax.rsqrt(jnp.mean(x_half * x_half, axis=-1, keepdims=True) + NORM_EPS)
    scaled = r.norm_one[...] * xn_grad
    pull = jnp.mean(scaled * x_half, axis=-1, keepdims=True)
    r.grad_tokens[...] = (
        r.grad_tokens[...] + scale * scaled - x_half * (scale * scale * scale * pull)
    )
    r.small_mine[0, pl.ds(0, experts), :] = r.small[pl.ds(0, experts), :]
    row = lax.broadcasted_iota(jnp.int32, (8, width), 0)
    r.small_mine[0, pl.ds(experts, 8), :] = jnp.where(
        row == 0,
        r.small[pl.ds(experts, 8), :],
        jnp.sum(xn_grad * x_half * scale, axis=0, keepdims=True),
    )
    links.go(("s", 0), part(r.small_mine, 0), part(r.small_in, 0), places.pair)
    late.pass_far(0)
    late.pass_on(1)
    early.share()
    sum_grads()
    links.got(("s", 0), part(r.small_in, 0))
    r.small_mine[1] = r.small_mine[0] + r.small_in[0]
    links.go(("s", 1), part(r.small_mine, 1), part(r.small_in, 1), places.far)
    late.pass_far(1)
    late.pass_on(2)
    early.pass_far(0)
    late.pass_far(2)
    late.pass_on(3)
    late.pass_far(3)
    links.got(("s", 1), part(r.small_in, 1))
    r.small_mine[2] = r.small_mine[1] + r.small_in[1]
    links.go(("s", 2), part(r.small_mine, 2), part(r.small_in, 2), places.near)
    early.pass_on(1)
    early.pass_far(1)
    early.pass_on(2)
    links.got(("s", 2), part(r.small_in, 2))
    r.small_all[z] = r.small_mine[2] + r.small_in[2]
    along("s", lambda i: part(r.small_all, ranks[i]))
    early.pass_far(2)
    early.pass_on(3)
    early.pass_far(3)
    weighted_sums.total(
        near_sum("w", r.row_kept, r.weighted_near, 0, halves),
        lambda n: r.branch_in.at[halves[n]],
    )
    r.layer_out[...] = (r.middle[...] + RESIDUAL_SCALE * r.branch_in[...]).astype(LOW)

    for i in (1, 2, 3):
        pass_along("s", lambda i: part(r.small_all, ranks[i]), i)
    small = ((r.small_all[0] + r.small_all[1]) + r.small_all[2]) + r.small_all[3]
    r.router_out[...] = small[:experts]
    r.norms_out[...] = small[experts:]
    late.finish()
    early.finish()
    for n, (_, out, _, spot) in enumerate(finals):
        links.got(("ef", n), part(out, *spot))
    for copy in writes:
        copy.wait()
    links.drain()


def run_layer(**inputs):
    rows_here, width = inputs["tokens"].shape
    experts = inputs["w_router"].shape[0]
    q_cols, k_cols = inputs["w_query"].shape[1], inputs["key_weight"].shape[1]
    kv_heads = k_cols // HEAD_DIMENSION
    vmem = pl.BlockSpec(memory_space=pltpu.VMEM)
    anywhere = pl.BlockSpec(memory_space=pl.ANY)
    block = (FLAT, width)
    gate = (experts, FLAT)
    slots = (2, PAIR, width)
    small = (experts + 8, width)
    grads = (width + q_cols, width)
    depth = grads[0] // 16
    outputs = {
        "layer_out": (block, LOW),
        "grad_tokens": (block, FULL),
        "router_out": (gate[:1] + (width,), FULL),
        "norms_out": ((8, width), FULL),
    }
    held = {"grads_out": (grads, LOW)} | {
        name + "_out": (inputs["w_" + name].shape, LOW) for name in ("gate", "up", "down")
    }
    heads = (kv_heads, 2, rows_here)
    scratch = {
        "w_in": ((width, q_cols + 2 * k_cols), LOW),
        "w_out": ((q_cols, width), LOW),
        "normed": ((rows_here, width), LOW),
        "q": ((kv_heads, rows_here, FLAT), LOW),
        "keys": (heads + (FLAT,), LOW),
        "values": (heads + (FLAT,), LOW),
        "bias": ((rows_here, rows_here), FULL),
        "att_probs": (heads + (rows_here,), FULL),
        "heads": ((rows_here, q_cols), LOW),
        "heads_grad": ((rows_here, q_cols), LOW),
        "head_grads": ((rows_here, q_cols + 2 * k_cols), LOW),
        "key_sums": ((kv_heads, rows_here, FLAT), FULL),
        "value_sums": ((kv_heads, rows_here, FLAT), FULL),
        "branch_send": (block, FULL),
        "branch_in": (block, FULL),
        "middle": (block, FULL),
        "branch_grad": ((rows_here, width), LOW),
        "small": (small, FULL),
        "terms_in": (block, LOW),
        "grads": (grads, LOW),
        "sum_z_send": ((4, depth, width), LOW),
        "sum_z_in": ((4, depth, width), LOW),
        "small_mine": ((3,) + small, FULL),
        "small_in": ((3,) + small, FULL),
        "small_all": ((4,) + small, FULL),
        "probs": (gate, FULL),
        "tables": ((4, 2) + gate, FULL),
        "gate_tables": ((4, 2) + gate, FULL),
        "g_all": ((4, 2) + block, LOW),
        "x_all": ((4, 2) + block, LOW),
        "g_slots": ((8,) + slots, LOW),
        "x_slots": ((8,) + slots, LOW),
        "row_slots": ((8,) + slots, LOW),
        "g_send": ((4,) + slots, LOW),
        "x_send": ((4,) + slots, LOW),
        "gates": ((2 * PAIR, FLAT), FULL),
        "gate_send": ((2, 2 * PAIR, FLAT), LOW),
        "gate_far": ((2, 2 * PAIR, FLAT), LOW),
        "parts": ((2 * PAIR, FLAT), FULL),
        "parts_in": ((2 * PAIR, FLAT), FULL),
        "pick": ((4, 4 * PAIR, 2 * FLAT), LOW),
        "gate_w": (inputs["w_gate"].shape, LOW),
        "up_w": (inputs["w_up"].shape, LOW),
        "down_w": (inputs["w_down"].shape, LOW),
        "hidden_all": ((2, 8 * PAIR, FF), LOW),
        "gate_all": ((2, 8 * PAIR, FF), LOW),
        "up_all": ((2, 8 * PAIR, FF), LOW),
        "result_all": ((2, 8 * PAIR, width), LOW),
        "rows_in": ((4,) + slots, LOW),
        "row_kept": ((4,) + block, FULL),
        "row_near": ((4,) + block, LOW),
        "row_near_send": ((4,) + block, LOW),
        "row_z_send": ((4,) + block, LOW),
        "row_z_in": ((4,) + block, LOW),
        "part_kept": ((4,) + gate, FULL),
        "part_near": ((4,) + gate, FULL),
        "part_send": ((4,) + gate, FULL),
        "part_z_send": ((4,) + gate, FULL),
        "part_z_in": ((4,) + gate, FULL),
        "part_total": (gate, FULL),
        "weighted_near": ((4,) + block, LOW),
        "weighted_z_in": ((4,) + block, LOW),
    }
    near_by = ("tokens", "norm_one", "norm_two", "w_router", "routes", "priority")
    near_by += ("cotangent", "cosine", "sine")
    names = [*inputs, *outputs, *held, *scratch, "sems_local", "sems_send", "sems_recv"]
    results = pl.pallas_call(
        functools.partial(layer_kernel, names),
        out_shape=[
            jax.ShapeDtypeStruct(shape, kind) for shape, kind in [*outputs.values(), *held.values()]
        ],
        in_specs=[vmem if name in near_by else anywhere for name in inputs],
        out_specs=[vmem] * len(outputs) + [anywhere] * len(held),
        scratch_shapes=[pltpu.VMEM(shape, kind) for shape, kind in scratch.values()]
        + [
            pltpu.SemaphoreType.DMA((20,)),
            pltpu.SemaphoreType.DMA((340,)),
            pltpu.SemaphoreType.DMA((320,)),
        ],
        compiler_params=pltpu.CompilerParams(
            collective_id=0, has_side_effects=True, vmem_limit_bytes=63 << 20
        ),
        name="layer",
    )(*inputs.values())
    return dict(zip([*outputs, *held], results))


def cast_kernel(*refs):
    parts, (first, second, layer, tokens, router, norms), outs = refs[:3], refs[3:9], refs[9:]
    q_cols, k_cols = outs[3].shape[1], outs[4].shape[1]
    for n in range(3):
        outs[n][...] = parts[n][...].astype(FULL)
    outs[3][...] = first[:, :q_cols].astype(FULL)
    outs[4][...] = first[:, q_cols : q_cols + k_cols].astype(FULL)
    outs[5][...] = first[:, q_cols + k_cols :].astype(FULL)
    outs[6][...] = second[...].astype(FULL)
    outs[7][...] = layer[...]
    outs[8][...] = tokens[...]
    outs[9][...] = router[...]
    outs[10][...] = norms[0:1, :]
    outs[11][...] = norms[1:2, :]


def cast_grads(done, q_cols, k_cols, steps=4):
    width = done["grads_out"].shape[1]
    parts = [done[name + "_out"] for name in ("gate", "up", "down")]
    rest = [done[name] for name in ("layer_out", "grad_tokens", "router_out", "norms_out")]

    def rows(shape, offset=0):
        block = shape[0] // steps
        return pl.BlockSpec((block, shape[1]), lambda i: (offset // block + i, 0))

    shapes = [parts[0].shape] * 3 + [(width, cols) for cols in (q_cols, k_cols, k_cols)]
    shapes += [(q_cols, width)] + [one.shape for one in rest[:3]]
    row = pl.BlockSpec((1, width), lambda i: (0, 0))
    return pl.pallas_call(
        cast_kernel,
        grid=(steps,),
        out_shape=[
            jax.ShapeDtypeStruct(shape, LOW if n == 7 else FULL)
            for n, shape in enumerate(shapes + [(1, width)] * 2)
        ],
        in_specs=[rows(one.shape) for one in parts]
        + [rows((width, width)), rows((q_cols, width), width)]
        + [rows(one.shape) for one in rest[:3]]
        + [pl.BlockSpec(rest[3].shape, lambda i: (0, 0))],
        out_specs=[rows(shape) for shape in shapes] + [row, row],
        compiler_params=pltpu.CompilerParams(vmem_limit_bytes=62 << 20),
        name="cast_grads",
    )(*parts, done["grads_out"], done["grads_out"], *rest)


def quick_shards(
    tokens,
    norm_one,
    w_query,
    key_weight,
    value_weight,
    w_output,
    norm_two,
    w_router,
    w_gate,
    w_up,
    w_down,
    routes,
    priority,
    cotangent,
):
    rows_here, width = tokens.shape
    experts = w_router.shape[1]
    q_cols, k_cols = w_query.shape[1], key_weight.shape[1]
    local_index = np.arange(rows_here, dtype=np.int32)
    prompt_rows, cont_rows = rows_here // 2, rows_here // 4
    position = np.where(
        local_index < prompt_rows,
        local_index,
        prompt_rows + (local_index - prompt_rows) % cont_rows,
    )
    frequency = ROPE_BASE ** (
        -(2.0 * np.arange(HEAD_DIMENSION // 2, dtype=np.float32)) / HEAD_DIMENSION
    )
    frequency = frequency.astype(np.float32)
    angle_table = position.astype(np.float32)[:, None] * np.tile(frequency, 4)[None, :]
    done = run_layer(
        tokens=tokens,
        norm_one=norm_one[None, :],
        norm_two=norm_two[None, :],
        w_router=w_router.T,
        routes=routes.T,
        priority=priority,
        cotangent=cotangent,
        cosine=jnp.asarray(np.cos(angle_table), FULL),
        sine=jnp.asarray(np.sin(angle_table), FULL),
        w_query=w_query,
        key_weight=key_weight,
        value_weight=value_weight,
        w_output=w_output,
        w_gate=w_gate,
        w_up=w_up,
        w_down=w_down,
    )
    gate, up, down, query, key, value, output, layer, token, router, second, first = cast_grads(
        done, q_cols, k_cols
    )
    return (
        layer,
        token,
        first[0],
        query,
        key,
        value,
        output,
        second[0],
        router.T,
        gate,
        up,
        down,
    )


def solution(mesh):
    body = quick_shards if dict(mesh.shape) == {"exp": 16, "head": 2} else shards
    return jax.shard_map(
        body,
        mesh=mesh,
        in_specs=(
            P("exp", None),
            P(),
            P(None, "head"),
            P(None, "head"),
            P(None, "head"),
            P("head", None),
            P(),
            P(),
            P(None, "exp"),
            P(None, "exp"),
            P("exp", None),
            P("exp", None),
            P(("exp", "head"), None),
            P(("exp", "head"), None),
        ),
        out_specs=(
            P(("exp", "head"), None),
            P(("exp", "head"), None),
            P(),
            P(None, "head"),
            P(None, "head"),
            P(None, "head"),
            P("head", None),
            P(),
            P(),
            P(None, "exp"),
            P(None, "exp"),
            P("exp", None),
        ),
        check_vma=False,
    )
```

```python
import functools
import types

import jax
import jax.numpy as jnp
import numpy as np
from jax import lax
from jax.experimental import pallas as pl
from jax.experimental.pallas import tpu as pltpu
from jax.sharding import PartitionSpec as P

HEAD_DIMENSION = 64
FF = 512
TOPK = 8


RESIDUAL_SCALE = 0.22
ATTENTION_SCALE = 0.015625
ROPE_BASE = 10000.0
NORM_EPS = 1e-06
MASKED_SCORE = -1e30


def rms_scale(values, scale_row):
    return (
        values * lax.rsqrt(jnp.mean(values * values, axis=-1, keepdims=True) + NORM_EPS) * scale_row
    )


def apply_rotary(values, cosine_values, sine_values):
    half_width = values.shape[-1] // 2
    lower_part = values[..., :half_width]
    upper_part = values[..., half_width:]
    return jnp.concatenate(
        [
            lower_part * cosine_values - upper_part * sine_values,
            upper_part * cosine_values + lower_part * sine_values,
        ],
        axis=-1,
    )


def rotate_back(values, cosine_values, sine_values):
    half_width = values.shape[-1] // 2
    lower_part = values[..., :half_width]
    upper_part = values[..., half_width:]
    return jnp.concatenate(
        [
            lower_part * cosine_values + upper_part * sine_values,
            upper_part * cosine_values - lower_part * sine_values,
        ],
        axis=-1,
    )


def shards(
    tokens,
    norm_one,
    w_query,
    key_weight,
    value_weight,
    w_output,
    norm_two,
    w_router,
    w_gate,
    w_up,
    w_down,
    routes,
    priority,
    cotangent,
):
    tok_rows, model_width = tokens.shape
    heads_count = lax.axis_size("head")
    head_rank = lax.axis_index("head")
    exp_count = lax.axis_size("exp")
    half_rows = tok_rows // heads_count
    prompt_rows = tok_rows // 2
    cont_rows = tok_rows // 4
    kv_heads = key_weight.shape[1] // HEAD_DIMENSION
    query_groups = w_query.shape[1] // key_weight.shape[1]
    experts = w_router.shape[1]
    held_cols = w_gate.shape[1]
    held = max(1, held_cols // FF)
    split = max(1, FF // held_cols)
    block_width = held_cols // held
    capacity = max(2, (5 * half_rows * TOPK + 4 * experts - 1) // (4 * experts))
    rows_per_block = min(512, tok_rows)
    count_of_blocks = tok_rows // rows_per_block
    local_index = jnp.arange(tok_rows, dtype=jnp.int32)
    position = jnp.where(
        local_index < prompt_rows,
        local_index,
        prompt_rows + (local_index - prompt_rows) % cont_rows,
    )
    frequency = ROPE_BASE ** (
        -(2.0 * jnp.arange(HEAD_DIMENSION // 2, dtype=jnp.float32)) / HEAD_DIMENSION
    )
    angle_table = position.astype(jnp.float32)[:, None] * frequency[None, :]
    cosine_values = jnp.cos(angle_table)[:, None, :]
    sine_values = jnp.sin(angle_table)[:, None, :]
    x_full = tokens.astype(jnp.float32)
    normed_input_first = rms_scale(x_full, norm_one).astype(jnp.bfloat16)
    rotated_queries = apply_rotary(
        jnp.dot(normed_input_first, w_query, preferred_element_type=jnp.float32).reshape(
            tok_rows, -1, HEAD_DIMENSION
        ),
        cosine_values,
        sine_values,
    ).astype(jnp.bfloat16)
    keys_all = apply_rotary(
        jnp.dot(normed_input_first, key_weight, preferred_element_type=jnp.float32).reshape(
            tok_rows, -1, HEAD_DIMENSION
        ),
        cosine_values,
        sine_values,
    ).astype(jnp.bfloat16)
    values_all = (
        jnp.dot(normed_input_first, value_weight, preferred_element_type=jnp.float32)
        .astype(jnp.bfloat16)
        .reshape(tok_rows, kv_heads, HEAD_DIMENSION)
    )

    def visible_pairs(block_start):
        query_col = (block_start + jnp.arange(rows_per_block, dtype=jnp.int32))[:, None]
        key_row = jnp.arange(tok_rows, dtype=jnp.int32)[None, :]
        from_prompt = (key_row < prompt_rows) & (
            (query_col >= prompt_rows) | (key_row <= query_col)
        )
        same_cont = (
            (key_row >= prompt_rows)
            & (query_col >= prompt_rows)
            & (key_row <= query_col)
            & ((key_row - prompt_rows) // cont_rows == (query_col - prompt_rows) // cont_rows)
        )
        return from_prompt | same_cont

    def scores_of(query_block, block_start):
        raw_scores = (
            jnp.einsum("qhgd,khd->hgqk", query_block, keys_all, preferred_element_type=jnp.float32)
            * ATTENTION_SCALE
        )
        return jnp.where(visible_pairs(block_start)[None, None], raw_scores, MASKED_SCORE)

    def forward_block(parts):
        query_block, block_start = parts
        scores = scores_of(query_block, block_start)
        row_max = jnp.max(scores, axis=-1, keepdims=True)
        weights = jnp.exp(scores - row_max)
        row_total = jnp.sum(weights, axis=-1, keepdims=True)
        probs_low = (weights / row_total).astype(jnp.bfloat16)
        mixed = jnp.einsum(
            "hgqk,khd->qhgd", probs_low, values_all, preferred_element_type=jnp.float32
        )
        return (mixed.astype(jnp.bfloat16), row_max + jnp.log(row_total))

    query_blocks = rotated_queries.reshape(
        count_of_blocks, rows_per_block, kv_heads, query_groups, HEAD_DIMENSION
    )
    block_starts = jnp.arange(count_of_blocks, dtype=jnp.int32) * rows_per_block
    heads_blocks, log_total = lax.map(forward_block, (query_blocks, block_starts))
    head_outputs = heads_blocks.reshape(tok_rows, -1)
    head_terms = jnp.dot(head_outputs, w_output, preferred_element_type=jnp.float32)
    branch_half = lax.dynamic_slice_in_dim(
        lax.psum(head_terms, "head"), head_rank * half_rows, half_rows, 0
    )
    x_half = lax.dynamic_slice_in_dim(x_full, head_rank * half_rows, half_rows, 0)
    middle = x_half + RESIDUAL_SCALE * branch_half
    xn_two = rms_scale(middle, norm_two).astype(jnp.bfloat16)
    logits = jnp.dot(xn_two, w_router, preferred_element_type=jnp.float32)
    my_routes = lax.dynamic_slice_in_dim(routes, head_rank * half_rows, half_rows, 0)
    route_hot = my_routes[:, :, None] == jnp.arange(experts, dtype=jnp.int32)[None, None, :]
    chosen = jnp.sum(jnp.where(route_hot, logits[:, None, :], 0.0), axis=-1)
    chosen_max = jnp.max(chosen, axis=-1, keepdims=True)
    chosen_exp = jnp.exp(chosen - chosen_max)
    gate_probs = chosen_exp / jnp.sum(chosen_exp, axis=-1, keepdims=True)
    gate_low = gate_probs.astype(jnp.bfloat16)
    member = jnp.any(route_hot, axis=1).astype(jnp.bfloat16)
    order_rank = priority[0]
    earlier = (order_rank[None, :] < order_rank[:, None]).astype(jnp.bfloat16)
    before = jnp.dot(earlier, member, preferred_element_type=jnp.float32)
    slot_rank = jnp.sum(jnp.where(route_hot, before[:, None, :], 0.0), axis=-1).astype(jnp.int32)
    is_kept = slot_rank < capacity
    spare_slot = experts * capacity
    target = jnp.where(is_kept, my_routes * capacity + slot_rank, spare_slot)
    row_ids = jnp.broadcast_to(jnp.arange(half_rows, dtype=jnp.int32)[:, None], target.shape)
    assign_ids = jnp.arange(half_rows * TOPK, dtype=jnp.int32).reshape(target.shape)
    source_row = (
        jnp.zeros(spare_slot + 1, jnp.int32).at[target.ravel()].set(row_ids.ravel())[:spare_slot]
    )
    source_pick = (
        jnp.zeros(spare_slot + 1, jnp.int32).at[target.ravel()].set(assign_ids.ravel())[:spare_slot]
    )
    filled = jnp.zeros(spare_slot + 1, jnp.int32).at[target.ravel()].set(1)[:spare_slot] > 0
    slot_inputs = jnp.where(filled[:, None], xn_two[source_row], 0).reshape(
        experts, capacity, model_width
    )
    slot_gates = jnp.where(filled, gate_low.ravel()[source_pick], 0).reshape(experts, capacity)

    def to_owners(per_expert):
        shape_in = per_expert.shape
        spread = jnp.broadcast_to(per_expert[:, None], (shape_in[0], split) + shape_in[1:])
        return spread.reshape((exp_count, held) + shape_in[1:])

    def from_owners(per_owner):
        shape_in = per_owner.shape
        return jnp.sum(
            per_owner.reshape((experts, split) + shape_in[2:]).astype(jnp.float32), axis=1
        )

    gate_cols = w_gate.reshape(model_width, held, block_width)
    up_cols = w_up.reshape(model_width, held, block_width)
    down_rows = w_down.reshape(held, block_width, model_width)
    send_rows = to_owners(slot_inputs)
    send_gates = to_owners(slot_gates)
    slot_rows = lax.all_to_all(send_rows, "exp", split_axis=0, concat_axis=0, tiled=True)
    slot_gate = lax.all_to_all(send_gates, "exp", split_axis=0, concat_axis=0, tiled=True)
    gate_pre = jnp.einsum(
        "sjcd,djf->sjcf", slot_rows, gate_cols, preferred_element_type=jnp.float32
    )
    up_pre = jnp.einsum("sjcd,djf->sjcf", slot_rows, up_cols, preferred_element_type=jnp.float32)
    hidden = (gate_pre * jax.nn.sigmoid(gate_pre) * up_pre).astype(jnp.bfloat16)
    result = jnp.einsum("sjcf,jfd->sjcd", hidden, down_rows, preferred_element_type=jnp.float32)
    weighted = (slot_gate[..., None].astype(jnp.float32) * result).astype(jnp.bfloat16)
    returned = lax.all_to_all(weighted, "exp", split_axis=0, concat_axis=0, tiled=True)
    returned, held_rows, held_gates = (returned, slot_rows, slot_gate)
    back_flat = jnp.concatenate(
        [
            from_owners(returned).reshape(spare_slot, model_width),
            jnp.zeros((1, model_width), jnp.float32),
        ],
        axis=0,
    )
    expert_sum = jnp.sum(back_flat[target], axis=1)
    layer_out = (middle + RESIDUAL_SCALE * expert_sum).astype(jnp.bfloat16)
    out_grad = cotangent.astype(jnp.float32)
    weighted_rows = (RESIDUAL_SCALE * out_grad).astype(jnp.bfloat16)
    grad_slots = to_owners(
        jnp.where(filled[:, None], weighted_rows[source_row], 0).reshape(
            experts, capacity, model_width
        )
    )
    back_grads, back_rows, back_gates = (
        lax.all_to_all(grad_slots, "exp", split_axis=0, concat_axis=0, tiled=True),
        lax.all_to_all(send_rows, "exp", split_axis=0, concat_axis=0, tiled=True),
        lax.all_to_all(send_gates, "exp", split_axis=0, concat_axis=0, tiled=True),
    )
    owner_gates = back_gates[..., None].astype(jnp.float32)
    gate_pre = jnp.einsum(
        "sjcd,djf->sjcf", back_rows, gate_cols, preferred_element_type=jnp.float32
    )
    up_pre = jnp.einsum("sjcd,djf->sjcf", back_rows, up_cols, preferred_element_type=jnp.float32)
    gate_sigmoid = jax.nn.sigmoid(gate_pre)
    gate_act = gate_pre * gate_sigmoid
    hidden = (gate_act * up_pre).astype(jnp.bfloat16)
    result = jnp.einsum("sjcf,jfd->sjcd", hidden, down_rows, preferred_element_type=jnp.float32)
    gate_part = jnp.sum(back_grads.astype(jnp.float32) * result, axis=-1)
    result_grad = (owner_gates * back_grads).astype(jnp.bfloat16)
    grad_down_w = jnp.einsum(
        "sjcf,sjcd->jfd", hidden, result_grad, preferred_element_type=jnp.float32
    ).reshape(held_cols, model_width)
    hidden_grad = jnp.einsum(
        "sjcd,jfd->sjcf", result_grad, down_rows, preferred_element_type=jnp.float32
    )
    gate_pre_grad = (
        hidden_grad * up_pre * gate_sigmoid * (1.0 + gate_pre * (1.0 - gate_sigmoid))
    ).astype(jnp.bfloat16)
    up_pre_grad = (hidden_grad * gate_act).astype(jnp.bfloat16)
    grad_gate_w = jnp.einsum(
        "sjcd,sjcf->djf", back_rows, gate_pre_grad, preferred_element_type=jnp.float32
    ).reshape(model_width, held_cols)
    grad_up_w = jnp.einsum(
        "sjcd,sjcf->djf", back_rows, up_pre_grad, preferred_element_type=jnp.float32
    ).reshape(model_width, held_cols)
    rows_grad = (
        jnp.einsum("sjcf,djf->sjcd", gate_pre_grad, gate_cols, preferred_element_type=jnp.float32)
        + jnp.einsum("sjcf,djf->sjcd", up_pre_grad, up_cols, preferred_element_type=jnp.float32)
    ).astype(jnp.bfloat16)
    rows_back, gates_back = (
        lax.all_to_all(rows_grad, "exp", split_axis=0, concat_axis=0, tiled=True),
        lax.all_to_all(
            gate_part.astype(jnp.bfloat16), "exp", split_axis=0, concat_axis=0, tiled=True
        ),
    )
    rows_flat = jnp.concatenate(
        [
            from_owners(rows_back).reshape(spare_slot, model_width),
            jnp.zeros((1, model_width), jnp.float32),
        ],
        axis=0,
    )
    xn_two_grad = jnp.sum(rows_flat[target], axis=1)
    gate_total = from_owners(gates_back).astype(jnp.bfloat16).reshape(spare_slot)
    gates_flat = jnp.concatenate([gate_total, jnp.zeros((1,), jnp.bfloat16)], axis=0)
    gate_grad_tok = gates_flat[target].astype(jnp.float32)
    chosen_grad = gate_probs * (
        gate_grad_tok - jnp.sum(gate_probs * gate_grad_tok, axis=-1, keepdims=True)
    )
    logit_grad = jnp.sum(jnp.where(route_hot, chosen_grad[:, :, None], 0.0), axis=1).astype(
        jnp.bfloat16
    )
    grad_router = jnp.einsum("rd,re->de", xn_two, logit_grad, preferred_element_type=jnp.float32)
    xn_two_grad = xn_two_grad + jnp.einsum(
        "re,de->rd", logit_grad, w_router, preferred_element_type=jnp.float32
    )
    middle_norm_pull = jax.vjp(rms_scale, middle, norm_two)[1]
    middle_norm_grad, grad_norm_two = middle_norm_pull(xn_two_grad)
    middle_grad = out_grad + middle_norm_grad
    branch_rows = (RESIDUAL_SCALE * middle_grad).astype(jnp.bfloat16)
    branch_grad = lax.all_gather(branch_rows, "head", axis=0, tiled=True)
    heads_grad = jnp.einsum(
        "td,hd->th", branch_grad, w_output, preferred_element_type=jnp.float32
    ).astype(jnp.bfloat16)
    grad_output_w = jnp.einsum(
        "th,td->hd", head_outputs, branch_grad, preferred_element_type=jnp.float32
    )

    def backward_block(running, parts):
        key_grad, value_grad = running
        query_block, heads_block, block_total, block_start = parts
        scores = scores_of(query_block, block_start)
        probs = jnp.exp(scores - block_total)
        probs_low = probs.astype(jnp.bfloat16)
        prob_grad = jnp.einsum(
            "qhgd,khd->hgqk", heads_block, values_all, preferred_element_type=jnp.float32
        )
        row_inner = jnp.sum(probs * prob_grad, axis=-1, keepdims=True)
        score_grad = (probs * (prob_grad - row_inner)).astype(jnp.bfloat16)
        query_grad = (
            jnp.einsum("hgqk,khd->qhgd", score_grad, keys_all, preferred_element_type=jnp.float32)
            * ATTENTION_SCALE
        )
        key_grad = (
            key_grad
            + jnp.einsum(
                "hgqk,qhgd->khd", score_grad, query_block, preferred_element_type=jnp.float32
            )
            * ATTENTION_SCALE
        )
        value_grad = value_grad + jnp.einsum(
            "hgqk,qhgd->khd", probs_low, heads_block, preferred_element_type=jnp.float32
        )
        return ((key_grad, value_grad), query_grad)

    heads_grad_blocks = heads_grad.reshape(
        count_of_blocks, rows_per_block, kv_heads, query_groups, HEAD_DIMENSION
    )
    zero_keys = jnp.zeros((tok_rows, kv_heads, HEAD_DIMENSION), jnp.float32)
    (own_key, own_value), query_grad = lax.scan(
        backward_block,
        (zero_keys, zero_keys),
        (query_blocks, heads_grad_blocks, log_total, block_starts),
    )
    query_pre_grad = (
        rotate_back(query_grad.reshape(tok_rows, -1, HEAD_DIMENSION), cosine_values, sine_values)
        .reshape(tok_rows, -1)
        .astype(jnp.bfloat16)
    )
    key_pre_grad = (
        rotate_back(own_key, cosine_values, sine_values).reshape(tok_rows, -1).astype(jnp.bfloat16)
    )
    value_low_grad = own_value.reshape(tok_rows, -1).astype(jnp.bfloat16)
    grad_query_w = jnp.einsum(
        "td,th->dh", normed_input_first, query_pre_grad, preferred_element_type=jnp.float32
    )
    grad_key_w = jnp.einsum(
        "td,th->dh", normed_input_first, key_pre_grad, preferred_element_type=jnp.float32
    )
    grad_value_w = jnp.einsum(
        "td,th->dh", normed_input_first, value_low_grad, preferred_element_type=jnp.float32
    )
    xn_one_terms = (
        jnp.einsum("th,dh->td", query_pre_grad, w_query, preferred_element_type=jnp.float32)
        + jnp.einsum("th,dh->td", key_pre_grad, key_weight, preferred_element_type=jnp.float32)
        + jnp.einsum("th,dh->td", value_low_grad, value_weight, preferred_element_type=jnp.float32)
    )
    xn_one_grad = lax.psum_scatter(
        xn_one_terms.astype(jnp.bfloat16), "head", scatter_dimension=0, tiled=True
    ).astype(jnp.float32)
    input_norm_pull = jax.vjp(rms_scale, x_half, norm_one)[1]
    input_norm_grad, grad_norm_one = input_norm_pull(xn_one_grad)
    grad_tokens = middle_grad + input_norm_grad
    grad_gate_w, grad_up_w, grad_down_w, grad_router, grad_norm_one, grad_norm_two = (
        lax.psum(grad_gate_w.astype(jnp.bfloat16), "head").astype(jnp.float32),
        lax.psum(grad_up_w.astype(jnp.bfloat16), "head").astype(jnp.float32),
        lax.psum(grad_down_w.astype(jnp.bfloat16), "head").astype(jnp.float32),
        lax.psum(grad_router.astype(jnp.bfloat16), "head").astype(jnp.float32),
        lax.psum(grad_norm_one.astype(jnp.bfloat16), "head").astype(jnp.float32),
        lax.psum(grad_norm_two.astype(jnp.bfloat16), "head").astype(jnp.float32),
    )
    (
        grad_query_w,
        grad_key_w,
        grad_value_w,
        grad_output_w,
        grad_router,
        grad_norm_one,
        grad_norm_two,
    ) = lax.psum(
        (
            grad_query_w,
            grad_key_w,
            grad_value_w,
            grad_output_w,
            grad_router,
            grad_norm_one,
            grad_norm_two,
        ),
        "exp",
    )
    return (
        layer_out,
        grad_tokens,
        grad_norm_one,
        grad_query_w,
        grad_key_w,
        grad_value_w,
        grad_output_w,
        grad_norm_two,
        grad_router,
        grad_gate_w,
        grad_up_w,
        grad_down_w,
    )


MESH = pl.DeviceIdType.MESH
FLAT = 128
SLOTS = 40
PAIR = 2 * SLOTS
UNKEPT = -1000.0
LOW = jnp.bfloat16
FULL = jnp.float32
LAST = (((1,), (1,)), ((), ()))
FIRST = (((0,), (0,)), ((), ()))
USUAL = (((1,), (0,)), ((), ()))


def mul(left, right, dims=USUAL):
    return lax.dot_general(left, right, dims, preferred_element_type=FULL)


def remote(source, target, send_sem, recv_sem, device):
    return pltpu.make_async_remote_copy(
        src_ref=source,
        dst_ref=target,
        send_sem=send_sem,
        recv_sem=recv_sem,
        device_id=device,
        device_id_type=MESH,
    )


def part(ref, *index):
    return lambda: ref.at[index]


def whole(ref):
    return lambda: ref


class Places:
    def __init__(self):
        self.e = e = lax.axis_index("exp")
        self.h = h = lax.axis_index("head")
        x, y, self.z = e % 2, (e // 2) % 2, e // 4
        z = self.z
        over_x, over_y = e + 1 - 2 * x, e + 2 - 4 * y
        self.near_e = over_x * (1 - h) + over_y * h
        self.far_e = over_y * (1 - h) + over_x * h
        self.near = (self.near_e, h)
        self.far = (self.far_e, h)
        self.outer = (1 + z % 2 + z // 2) % 2
        self.ranks = [z, z + 1 - 2 * (z % 2), 2 - z // 2, 3 - 3 * (z // 2)]
        self.along = [(rank * 4 + e % 4, h) for rank in self.ranks]
        self.edge = self.along[1]
        self.inner = ((3 - z) * 4 + e % 4, h)
        self.pair = (e, 1 - h)
        self.is_inner = (z == 1) | (z == 2)

    def hello(self):
        barrier = pltpu.get_barrier_semaphore()
        for device in (self.pair, self.near, self.far, *self.along[1:]):
            pl.semaphore_signal(barrier, inc=1, device_id=device, device_id_type=MESH)

    def ready(self):
        pl.semaphore_wait(pltpu.get_barrier_semaphore(), 6)


class Links:
    def __init__(self, places, send, recv):
        self.places, self.send, self.recv = places, send, recv
        self.sent, self.names = 0, {}
        self.pending = {"all": [], "inner": []}

    def number(self, name):
        return self.names.setdefault(name, len(self.names))

    def go(self, name, source, target, device, who="all", number=None):
        arrival = self.number(name) if number is None else number
        number = self.sent
        remote(
            source(), target(), self.send.at[number], self.recv.at[arrival], device
        ).start()
        self.sent += 1
        self.pending[who].append((number, name, source))

    def got(self, name, target):
        remote(
            target(), target(), self.send.at[0], self.recv.at[self.number(name)], self.places.near
        ).wait_recv()

    def sent_all(self, who, of):
        for number, name, source in self.pending[who]:
            if of is None or name[0] == of:
                remote(
                    source(), source(), self.send.at[number], self.recv.at[0], self.places.near
                ).wait_send()

    def drain(self, of=None):
        self.sent_all("all", of)

        @pl.when(self.places.is_inner)
        def _():
            self.sent_all("inner", of)

        for who, sent in self.pending.items():
            self.pending[who] = [one for one in sent if of is not None and one[1][0] != of]


class Spread:
    def __init__(self, links, name, gathered, pieces=((),), cross=()):
        self.links, self.name, self.gathered = links, name, gathered
        self.pieces, self.cross = pieces, cross

    def spot(self, i, a, n):
        return part(self.gathered, i, a, *self.pieces[n])

    def launch(self, a, n):
        links, places = self.links, self.links.places
        block = self.spot(0, a, n)
        links.go((self.name, a, 1, n), block, self.spot(1, a, n), places.edge)

        @pl.when(places.is_inner)
        def _():
            links.go((self.name, a, 2, n), block, self.spot(2, a, n), places.inner, "inner")

    def start(self):
        for n in range(len(self.pieces)):
            self.launch(0, n)
            self.links.go(
                (self.name, "n", 0, n),
                self.spot(0, 0, n),
                self.spot(0, 1, n),
                self.links.places.near,
            )

    def forward(self, i, a, n):
        links, places = self.links, self.links.places
        there = {1: 3, 2: 2, 3: 3}[i]
        device = places.inner if i == 1 else places.edge
        block = self.spot(i, a, n)
        links.got((self.name, a, i, n), block)

        @pl.when(places.is_inner)
        def _():
            links.go((self.name, a, there, n), block, self.spot(there, a, n), device, "inner")

    def pass_on(self, i):
        for n in range(len(self.pieces)):
            self.forward(i, 0, n)
            if n not in self.cross:
                self.links.go(
                    (self.name, "n", i, n),
                    self.spot(i, 0, n),
                    self.spot(i, 1, n),
                    self.links.places.near,
                )

    def wait(self, i, n=0):
        if i and n in self.cross:
            self.forward(i, 1, n)
        else:
            self.links.got((self.name, "n", i, n), self.spot(i, 1, n))
            if n in self.cross:
                self.launch(1, n)


class Gather:
    def __init__(self, links, name, send, recv, pieces):
        self.links, self.name, self.send, self.recv, self.pieces = links, name, send, recv, pieces
        for n in range(len(pieces)):
            for slot in (1, 2, 3):
                links.number((name, n, slot))

    def push(self, i, value):
        links, places = self.links, self.links.places
        for n, piece in enumerate(self.pieces):
            spot = part(self.send, i, *piece)
            spot()[...] = value(n).astype(self.send.dtype)
            slot = 1 if i == 1 else 2 + places.outer
            links.go(
                (self.name, n, 1),
                spot,
                part(self.recv, slot, *piece),
                places.along[i],
                number=links.number((self.name, n, 1)) + slot - 1,
            )

    def total(self, own, result):
        for n, piece in enumerate(self.pieces):
            value = own(n)
            for slot in (1, 2, 3):
                spot = part(self.recv, slot, *piece)
                self.links.got((self.name, n, slot), spot)
                value = value + spot()[...].astype(FULL)
            result(n)[...] = value


def table_rows(tables, i, places):
    rows = []
    for chip in (places.e, places.far_e):
        for j in range(2):
            rows.append(
                jnp.concatenate(
                    [tables[i, a, pl.ds(2 * chip + j, 1), :] for a in range(2)], axis=1
                )
            )
    return rows


def selection(tables, i, places):
    slot = lax.broadcasted_iota(jnp.int32, (PAIR, 2 * FLAT), 0)
    lane = lax.broadcasted_iota(jnp.int32, (PAIR, 2 * FLAT), 1)
    wanted = (slot - jnp.where(lane >= FLAT, SLOTS, 0)).astype(FULL)
    return jnp.concatenate(
        [jnp.where(row == wanted, 1.0, 0.0) for row in table_rows(tables, i, places)], axis=0
    )


def turn(block, cosine, sine, sign):
    lane = lax.broadcasted_iota(jnp.int32, block.shape, 1) % HEAD_DIMENSION
    quarter = HEAD_DIMENSION // 2
    other = jnp.where(
        lane < quarter,
        -sign * pltpu.roll(block, FLAT - quarter, 1),
        sign * pltpu.roll(block, quarter, 1),
    )
    return block * cosine + other * sine


def layer_kernel(names, *refs):
    r = types.SimpleNamespace(**dict(zip(names, refs, strict=True)))
    places = Places()
    h, e, z = places.h, places.e, places.z
    places.hello()
    links = Links(places, r.sems_send, r.sems_recv)
    experts = r.w_router.shape[0]
    rows_here, width = r.tokens.shape
    q_cols, k_cols = r.w_query.shape[1], r.key_weight.shape[1]
    kv_heads = k_cols // HEAD_DIMENSION
    every = slice(None)
    half = pl.multiple_of(h * FLAT, FLAT)
    other_half = pl.multiple_of((1 - h) * FLAT, FLAT)
    locals_used = [0]

    def load(source, target):
        copy = pltpu.make_async_copy(source, target, r.sems_local.at[locals_used[0]])
        locals_used[0] += 1
        copy.start()
        return copy

    in_loads = [
        load(r.w_query, r.w_in.at[:, :q_cols]),
        load(r.key_weight, r.w_in.at[:, q_cols : q_cols + k_cols]),
        load(r.value_weight, r.w_in.at[:, q_cols + k_cols :]),
    ]
    out_load = load(r.w_output, r.w_out)
    rank_row = r.priority[...]
    row_id = lax.broadcasted_iota(jnp.int32, (FLAT, FLAT), 0)
    col_id = lax.broadcasted_iota(jnp.int32, (FLAT, FLAT), 1)
    rank_col = jnp.sum(
        jnp.where(row_id == col_id, jnp.broadcast_to(rank_row, (FLAT, FLAT)), 0),
        axis=1,
        keepdims=True,
    )
    earlier = jnp.where(rank_row < rank_col, 1.0, 0.0).astype(LOW)
    expert_id = lax.broadcasted_iota(jnp.int32, (experts, FLAT), 0)
    my_routes = r.routes[:, pl.ds(half, FLAT)]
    member = jnp.zeros((experts, FLAT), FULL)
    for k in range(TOPK):
        member += jnp.where(my_routes[k : k + 1, :] == expert_id, 1.0, 0.0)
    before = mul(member.astype(LOW), earlier, LAST)
    r.tables[0, 0] = jnp.where((member > 0.5) & (before < SLOTS), before, UNKEPT)
    r.g_all[0, 0] = (RESIDUAL_SCALE * r.cotangent[...].astype(FULL)).astype(LOW)
    columns = [slice(0, width // 2), slice(width // 2, width)]
    halves = [(every, one) for one in columns]
    t_spread = Spread(links, "t", r.tables)
    g_spread = Spread(links, "g", r.g_all, halves)
    x_spread = Spread(links, "x", r.x_all, halves, cross=(1,))
    p_spread = Spread(links, "p", r.gate_tables)
    x_full = r.tokens[...].astype(FULL)
    r.normed[...] = rms_scale(x_full, r.norm_one[...]).astype(LOW)
    places.ready()
    t_spread.start()
    g_spread.start()

    for copy in in_loads:
        copy.wait()
    expert_loads = [load(r.w_gate, r.gate_w), load(r.w_up, r.up_w), load(r.w_down, r.down_w)]
    projected = mul(r.normed[...], r.w_in[...])
    cosine, sine = r.cosine[...], r.sine[...]
    lane = lax.broadcasted_iota(jnp.int32, (rows_here, FLAT), 1)
    low_lanes = lane < HEAD_DIMENSION
    for g in range(kv_heads):
        r.q[g] = turn(projected[:, g * FLAT : (g + 1) * FLAT], cosine, sine, 1.0).astype(LOW)
    for m in range(kv_heads // 2):
        start = q_cols + m * FLAT
        keys = turn(projected[:, start : start + FLAT], cosine, sine, 1.0)
        start += k_cols
        values = projected[:, start : start + FLAT]
        for block, store in ((keys, r.keys), (values, r.values)):
            rolled = pltpu.roll(block, HEAD_DIMENSION, 1)
            store[2 * m, 0] = jnp.where(low_lanes, block, 0.0).astype(LOW)
            store[2 * m, 1] = jnp.where(low_lanes, 0.0, rolled).astype(LOW)
            store[2 * m + 1, 0] = jnp.where(low_lanes, rolled, 0.0).astype(LOW)
            store[2 * m + 1, 1] = jnp.where(low_lanes, 0.0, block).astype(LOW)
    prompt, cont = rows_here // 2, rows_here // 4
    query_id = lax.broadcasted_iota(jnp.int32, (rows_here, rows_here), 0)
    key_id = lax.broadcasted_iota(jnp.int32, (rows_here, rows_here), 1)
    query_cont = jnp.where(query_id < prompt, 0, 1 + (query_id - prompt) // cont)
    key_cont = jnp.where(key_id < prompt, 0, 1 + (key_id - prompt) // cont)
    visible = ((key_cont == 0) & (query_cont > 0)) | (
        (key_cont == query_cont) & (key_id <= query_id)
    )
    r.bias[...] = jnp.where(visible, 0.0, MASKED_SCORE)

    def attend(first, count):
        def one(g, carry):
            mixed = jnp.zeros((rows_here, FLAT), FULL)
            for s in range(2):
                raw = mul(r.q[g], r.keys[g, s], LAST) * ATTENTION_SCALE
                scores = jnp.where(r.bias[...] < 0.0, MASKED_SCORE, raw)
                weights = jnp.exp(scores - jnp.max(scores, axis=1, keepdims=True))
                probs = weights / jnp.sum(weights, axis=1, keepdims=True)
                r.att_probs[g, s] = probs
                mixed += mul(probs.astype(LOW), r.values[g, s])
            r.heads[:, pl.ds(pl.multiple_of(g * FLAT, FLAT), FLAT)] = mixed.astype(LOW)
            return carry

        lax.fori_loop(first, first + count, one, 0)

    def pick_rows(name, spread, picks, gathered, slots, send, i):
        for n, cols in enumerate(columns):
            spread.wait(i, n)
            rows = mul(picks, gathered[i, :, :, cols].reshape(2 * FLAT, -1)).astype(LOW)
            slots[i, :, :, cols] = rows[: 2 * PAIR].reshape(2, PAIR, -1)
            send[i, :, :, cols] = rows[2 * PAIR :].reshape(2, PAIR, -1)
            links.go(
                (name, "f", i, n),
                part(send, i, every, every, cols),
                part(slots, 4 + i, every, every, cols),
                places.far,
            )

    def dispatch_out(i):
        t_spread.wait(i)
        picks = selection(r.tables, i, places).astype(LOW)
        r.pick[i] = picks
        pick_rows("g", g_spread, picks, r.g_all, r.g_slots, r.g_send, i)

    def pass_out(i):
        t_spread.pass_on(i)
        g_spread.pass_on(i)

    attend(0, 4)
    out_load.wait()
    r.branch_send[...] = mul(r.heads[pl.ds(other_half, FLAT), :], r.w_out[...])
    links.go("branch", whole(r.branch_send), whole(r.branch_in), places.pair)
    own_branch = mul(r.heads[pl.ds(half, FLAT), :], r.w_out[...])
    links.got("branch", whole(r.branch_in))
    middle = r.tokens[pl.ds(half, FLAT), :].astype(FULL) + RESIDUAL_SCALE * (
        own_branch + r.branch_in[...]
    )
    r.middle[...] = middle
    xn = rms_scale(middle, r.norm_two[...]).astype(LOW)
    r.x_all[0, 0] = xn
    x_spread.start()
    logits = mul(r.w_router[...], xn, LAST)
    chosen = jnp.where(member > 0.5, logits, MASKED_SCORE)
    weights = jnp.exp(chosen - jnp.max(chosen, axis=0, keepdims=True))
    probs = weights / jnp.sum(weights, axis=0, keepdims=True)
    r.probs[...] = probs
    r.gate_tables[0, 0] = probs.astype(LOW).astype(FULL)
    p_spread.start()

    slots_lane = lax.broadcasted_iota(jnp.int32, (2 * PAIR, FLAT), 1)
    r.gates[...] = jnp.zeros((2 * PAIR, FLAT), FULL)
    r.gate_send[...] = jnp.zeros((2, 2 * PAIR, FLAT), LOW)

    def dispatch_in(i):
        picks = r.pick[i]
        pick_rows("x", x_spread, picks, r.x_all, r.x_slots, r.x_send, i)
        p_spread.wait(i)
        spread_gates = jnp.concatenate(
            [
                jnp.broadcast_to(row, (PAIR, 2 * FLAT))
                for row in table_rows(r.gate_tables, i, places)
            ],
            axis=0,
        )
        slot_gates = jnp.sum(picks.astype(FULL) * spread_gates, axis=1, keepdims=True)
        r.gates[...] += jnp.where(slots_lane == i, slot_gates[: 2 * PAIR], 0.0)
        far_gates = jnp.where(slots_lane == 4 + i, slot_gates[2 * PAIR :], 0.0)
        r.gate_send[i // 2] += far_gates.astype(LOW)

    def send_gates(n):
        links.go(("p", "f", n), part(r.gate_send, n), part(r.gate_far, n), places.far)

    def add_gates(n):
        links.got(("p", "f", n), part(r.gate_far, n))
        r.gates[...] += r.gate_far[n].astype(FULL)

    def pass_in(i):
        x_spread.pass_on(i)
        p_spread.pass_on(i)

    dispatch_out(0)
    pass_out(1)
    pass_out(2)
    dispatch_in(0)
    pass_in(1)
    dispatch_out(1)
    pass_out(3)
    dispatch_in(1)
    send_gates(0)
    pass_in(2)
    dispatch_out(2)
    pass_in(3)
    dispatch_out(3)
    dispatch_in(2)
    dispatch_in(3)
    send_gates(1)

    slot_lane = lax.broadcasted_iota(jnp.int32, (PAIR, FLAT), 1)
    r.parts[...] = jnp.zeros((2 * PAIR, FLAT), FULL)

    def run_experts(first, count):
        span = count * PAIR
        which = slice(first, first + count)
        place = slice(first * PAIR, (first + count) * PAIR)

        def one_expert(j, carry):
            base = pl.multiple_of(j * PAIR, PAIR)
            gates = r.gates[pl.ds(base, PAIR), :]
            gate_col = jnp.concatenate(
                [gates[:, p : p + 1] for p in range(first, first + count)], axis=0
            )
            columns = pl.ds(pl.multiple_of(j * FF, FF), FF)
            xs = r.x_slots[which, j].reshape(span, -1)
            gate_pre = mul(xs, r.gate_w[:, columns])
            up_pre = mul(xs, r.up_w[:, columns])
            sig = jax.nn.sigmoid(gate_pre)
            act = gate_pre * sig
            hidden = (act * up_pre).astype(LOW)
            r.hidden_all[j, place] = hidden
            result = mul(hidden, r.down_w[columns, :])
            gs = r.g_slots[which, j].reshape(span, -1).astype(FULL)
            r.g_slots[which, j] = (gate_col * result).astype(LOW).reshape(count, PAIR, -1)
            part = jnp.sum(gs * result, axis=1, keepdims=True).astype(LOW).astype(FULL)
            terms = jnp.zeros((PAIR, FLAT), FULL)
            for p in range(count):
                terms += jnp.where(
                    slot_lane == first + p, part[p * PAIR : (p + 1) * PAIR], 0.0
                )
            r.parts[pl.ds(base, PAIR), :] += terms
            result_grad = (gate_col * gs).astype(LOW)
            r.result_all[j, place] = result_grad
            hidden_grad = mul(result_grad, r.down_w[columns, :], LAST)
            gate_pre_grad = (
                hidden_grad * up_pre * sig * (1.0 + gate_pre * (1.0 - sig))
            ).astype(LOW)
            up_pre_grad = (hidden_grad * act).astype(LOW)
            r.gate_all[j, place] = gate_pre_grad
            r.up_all[j, place] = up_pre_grad
            rows_grad = mul(gate_pre_grad, r.gate_w[:, columns], LAST) + mul(
                up_pre_grad, r.up_w[:, columns], LAST
            )
            r.row_slots[which, j] = rows_grad.astype(LOW).reshape(count, PAIR, -1)
            return carry

        lax.fori_loop(0, 2, one_expert, 0)

    for copy in expert_loads:
        copy.wait()
    writes = []

    def weight_grads(j):
        xs = r.x_slots[:, j].reshape(8 * PAIR, -1)
        columns = slice(j * FF, (j + 1) * FF)
        r.gate_w[:, columns] = mul(xs, r.gate_all[j], FIRST).astype(LOW)
        r.up_w[:, columns] = mul(xs, r.up_all[j], FIRST).astype(LOW)
        r.down_w[columns, :] = mul(r.hidden_all[j], r.result_all[j], FIRST).astype(LOW)

    mine_at = pl.ds(pl.multiple_of(h * FF, FF), FF)
    theirs_at = pl.ds(pl.multiple_of((1 - h) * FF, FF), FF)
    top = r.hidden_all.shape[1]
    low_rows = width - top
    exchange = [
        (r.gate_w, (pl.ds(0, top), theirs_at), r.hidden_all, (0,)),
        (r.gate_w, (pl.ds(top, low_rows), theirs_at), r.hidden_all, (1, pl.ds(0, low_rows))),
        (r.up_w, (pl.ds(0, top), theirs_at), r.gate_all, (0,)),
        (r.up_w, (pl.ds(top, low_rows), theirs_at), r.gate_all, (1, pl.ds(0, low_rows))),
        (r.down_w, (theirs_at, pl.ds(0, FF)), r.up_all, (0, pl.ds(0, FF))),
        (r.down_w, (theirs_at, pl.ds(FF, FF)), r.up_all, (1, pl.ds(0, FF))),
    ]
    finals = [
        (r.gate_w, r.gate_out, (every, mine_at), (every, theirs_at)),
        (r.up_w, r.up_out, (every, mine_at), (every, theirs_at)),
        (r.down_w, r.down_out, (mine_at, every), (theirs_at, every)),
    ]

    def send_grads():
        for n, (source, spot, target, there) in enumerate(exchange):
            links.go(("e", n), part(source, *spot), part(target, *there), places.pair)

    def sum_grads():
        for n, (own, spot, other, there) in enumerate(exchange):
            links.got(("e", n), part(other, *there))
            spot = tuple(mine_at if one is theirs_at else one for one in spot)
            own[spot] = (own[spot].astype(FULL) + other[there].astype(FULL)).astype(LOW)
        for n, (source, out, spot, _) in enumerate(finals):
            writes.append(load(source.at[spot], out.at[spot]))
            links.go(("ef", n), part(source, *spot), part(out, *spot), places.pair)

    index = lax.broadcasted_iota(jnp.int32, (experts, 2 * FLAT), 0)

    def fold(name, rows, rows_in, kept, near_send, near_in, i):
        for n, cols in enumerate(columns):
            links.got((name, "f", i, n), part(rows_in, i, every, every, cols))
            stacked = jnp.concatenate(
                [
                    rows[i, :, :, cols].reshape(2 * PAIR, -1),
                    rows_in[i, :, :, cols].reshape(2 * PAIR, -1),
                ],
                axis=0,
            )
            sums = mul(r.pick[i], stacked, FIRST)
            kept[i, :, cols] = sums[:FLAT]
            send = near_send(i, cols)
            send()[...] = sums[FLAT:].astype(LOW)
            links.go((name, "n", i, n), send, part(near_in, i, every, cols), places.near)

    def send_far(name, rows, rows_in, i):
        for n, cols in enumerate(columns):
            links.go(
                (name, "f", i, n),
                part(rows, 4 + i, every, every, cols),
                part(rows_in, i, every, every, cols),
                places.far,
            )

    def fold_parts(i):
        column = jnp.concatenate(
            [r.parts[:, i : i + 1], r.parts_in[:, 4 + i : 5 + i]], axis=0
        )
        terms = r.pick[i].astype(FULL) * column
        table = jnp.zeros((experts, 2 * FLAT), FULL)
        chips = (places.e, places.e, places.far_e, places.far_e)
        for n, chip in enumerate(chips):
            total = jnp.sum(terms[n * PAIR : (n + 1) * PAIR], axis=0, keepdims=True)
            table += jnp.where(index == 2 * chip + n % 2, total, 0.0)
        r.part_kept[i] = table[:, :FLAT]
        r.part_send[i] = table[:, FLAT:]
        links.go(("q", "n", i, 0), part(r.part_send, i), part(r.part_near, i), places.near)

    row_sums = Gather(links, "rz", r.row_z_send, r.row_z_in, halves)
    part_sums = Gather(links, "qz", r.part_z_send, r.part_z_in, [()])
    weighted_sums = Gather(links, "wz", r.row_near_send, r.weighted_z_in, halves)

    def near_sum(name, kept, near_in, i, pieces):
        def value(n):
            spot = (i, *pieces[n])
            links.got((name, "n", i, n), part(near_in, *spot))
            return kept[spot] + near_in[spot].astype(FULL)

        return value

    def settle_rows(i):
        row_sums.push(i, near_sum("r", r.row_kept, r.row_near, i, row_sums.pieces))

    def settle_parts(i):
        part_sums.push(i, near_sum("q", r.part_kept, r.part_near, i, part_sums.pieces))

    def settle_weighted(i):
        weighted_sums.push(i, near_sum("w", r.row_kept, r.weighted_near, i, halves))

    def fold_weighted(i):
        fold(
            "w",
            r.g_slots,
            r.g_send,
            r.row_kept,
            lambda i, cols: part(r.x_all, i, 0, every, cols),
            r.weighted_near,
            i,
        )

    def far_experts(i):
        for n, cols in enumerate(columns):
            links.got(("g", "f", i, n), part(r.g_slots, 4 + i, every, every, cols))
            links.got(("x", "f", i, n), part(r.x_slots, 4 + i, every, every, cols))
        run_experts(4 + i, 1)
        send_far("r", r.row_slots, r.rows_in, i)

    def fold_rows(i):
        fold(
            "r",
            r.row_slots,
            r.rows_in,
            r.row_kept,
            lambda i, cols: part(r.row_near_send, i, every, cols),
            r.row_near,
            i,
        )

    add_gates(0)
    far_experts(1)
    far_experts(0)
    run_experts(0, 4)
    links.drain()
    add_gates(1)
    fold_rows(1)
    far_experts(3)
    far_experts(2)
    links.go(("q", "f"), whole(r.parts), whole(r.parts_in), places.far)
    settle_rows(1)
    fold_rows(3)
    fold_rows(2)
    settle_rows(3)
    links.got(("q", "f"), whole(r.parts_in))
    for i in (3, 2, 1, 0):
        fold_parts(i)
    settle_rows(2)
    for i in (3, 2, 1):
        settle_parts(i)
    fold_rows(0)
    def send_weighted(i):
        send_far("w", r.g_slots, r.g_send, i)

    send_weighted(3)
    send_weighted(2)
    weight_grads(0)
    weight_grads(1)
    fold_weighted(3)
    send_weighted(1)
    fold_weighted(2)
    send_weighted(0)
    fold_weighted(1)
    row_sums.total(
        near_sum("r", r.row_kept, r.row_near, 0, halves), lambda n: r.branch_in.at[halves[n]]
    )
    part_sums.total(
        near_sum("q", r.part_kept, r.part_near, 0, part_sums.pieces), lambda n: r.part_total
    )

    gate_probs, gate_grad = r.probs[...], r.part_total[...]
    chosen_grad = gate_probs * (
        gate_grad - jnp.sum(gate_probs * gate_grad, axis=0, keepdims=True)
    )
    logit_grad = chosen_grad.astype(LOW)
    xn_grad = r.branch_in[...] + mul(logit_grad, r.w_router[...], FIRST)
    mid = r.middle[...]
    scale = lax.rsqrt(jnp.mean(mid * mid, axis=-1, keepdims=True) + NORM_EPS)
    scaled = r.norm_two[...] * xn_grad
    pull = jnp.mean(scaled * mid, axis=-1, keepdims=True)
    grad = r.cotangent[...].astype(FULL) + scale * scaled - mid * (scale * scale * scale * pull)
    r.grad_tokens[...] = grad
    mine = part(r.branch_grad, pl.ds(half, FLAT))
    r.branch_grad[pl.ds(half, FLAT), :] = (RESIDUAL_SCALE * grad).astype(LOW)
    links.go("bg", mine, mine, places.pair)
    r.small[pl.ds(0, experts), :] = mul(logit_grad, r.x_all[0, 0])
    r.small[pl.ds(experts, 8), :] = jnp.broadcast_to(
        jnp.sum(xn_grad * mid * scale, axis=0, keepdims=True), (8, width)
    )

    links.drain("r")
    for i in (3, 2, 1):
        settle_weighted(i)
    fold_weighted(0)
    links.got("bg", part(r.branch_grad, pl.ds(other_half, FLAT)))
    r.heads_grad[...] = mul(r.branch_grad[...], r.w_out[...], LAST).astype(LOW)
    r.grads[pl.ds(width, q_cols), :] = mul(r.heads[...], r.branch_grad[...], FIRST).astype(LOW)
    cosine, sine = r.cosine[...], r.sine[...]

    def attend_back(first, count):
        def one(g, carry):
            place = pl.ds(pl.multiple_of(g * FLAT, FLAT), FLAT)
            out_grad = r.heads_grad[:, place]
            query = r.q[g]
            query_grad = jnp.zeros((rows_here, FLAT), FULL)
            key_grads, value_grads = [], []
            for s in range(2):
                probs = r.att_probs[g, s]
                prob_grad = mul(out_grad, r.values[g, s], LAST)
                inner = jnp.sum(probs * prob_grad, axis=1, keepdims=True)
                score_grad = (probs * (prob_grad - inner)).astype(LOW)
                query_grad += mul(score_grad, r.keys[g, s])
                key_grads.append(mul(score_grad, query, FIRST))
                value_grads.append(mul(probs.astype(LOW), out_grad, FIRST))
            r.head_grads[:, place] = turn(
                query_grad * ATTENTION_SCALE, r.cosine[...], r.sine[...], -1.0
            ).astype(LOW)
            r.key_sums[g] = key_grads[0] + pltpu.roll(key_grads[1], HEAD_DIMENSION, 1)
            r.value_sums[g] = value_grads[0] + pltpu.roll(value_grads[1], HEAD_DIMENSION, 1)
            return carry

        lax.fori_loop(first, first + count, one, 0)

    ranks = places.ranks
    plane = [[e % 4, places.near_e % 4], [places.far_e % 4, 3 - e % 4]]

    def along(name, spot):
        block = spot(0)
        links.go((name, "z", 1), block, block, places.edge)

        @pl.when(places.is_inner)
        def _():
            links.go((name, "z", 2), block, block, places.inner, "inner")

    def pass_along(name, spot, i):
        block = spot(i)
        links.got((name, "z", i), block)
        there = {1: 3, 2: 2, 3: 3}[i]
        device = places.inner if i == 1 else places.edge

        @pl.when(places.is_inner)
        def _():
            links.go((name, "z", there), block, block, device, "inner")

    class Reduce:
        order = [(a, i) for i in (3, 2, 1, 0) for a in (1, 0)]

        def __init__(self, name, first, count, room, near_first=False):
            self.name, self.first, self.depth, self.room = name, first, count // 16, room
            self.near_first = near_first
            self.rows = slice(room, room + self.depth)
            self.issued = 0
            self.sums = Gather(links, name + "z", r.sum_z_send, r.sum_z_in, [(self.rows,)])

        def shard(self, b, a, i):
            start = self.first + (ranks[i] * 4 + plane[b][a]) * self.depth
            return pl.ds(pl.multiple_of(start, 16), self.depth)

        def far_in(self, a, i):
            return part(r.g_all, i, a, self.rows)

        def near_in(self, i):
            return part(r.x_all, i, 1, self.rows)

        def near_send(self, i):
            return part(r.result_all, 0, pl.ds(4 * self.room + i * self.depth, self.depth))

        def send(self, count):
            for a, i in self.order[self.issued : self.issued + count]:
                source = part(r.grads, self.shard(1, a, i))
                links.go((self.name, "f", a, i), source, self.far_in(a, i), places.far)
            self.issued += count

        def fold(self, i):
            for a in (1, 0):
                links.got((self.name, "f", a, i), self.far_in(a, i))
                self.send(1)
                if a:
                    total = r.grads[self.shard(0, 1, i), :].astype(FULL) + r.g_all[
                        i, 1, self.rows
                    ].astype(FULL)
                    self.near_send(i)()[...] = total.astype(LOW)
                    links.go(
                        (self.name, "n", i), self.near_send(i), self.near_in(i), places.near
                    )

        def near_sum(self, i):
            links.got((self.name, "n", i), self.near_in(i))
            mine = self.shard(0, 0, i)
            return lambda n: (
                r.grads[mine, :].astype(FULL)
                + r.g_all[i, 0, self.rows].astype(FULL)
                + r.x_all[i, 1, self.rows].astype(FULL)
            )

        def settle(self, i):
            self.sums.push(i, self.near_sum(i))

        def spot(self, b, a, i):
            return part(r.grads_out, self.shard(b, a, i))

        def share(self):
            total = r.branch_send.at[self.rows]
            self.sums.total(self.near_sum(0), lambda n: total)
            low = part(r.result_all, 1, pl.ds(FLAT + self.room, self.depth))
            low()[...] = total[...].astype(LOW)
            mine = self.spot(0, 0, 0)
            links.go((self.name + "o", "z", 1), low, mine, places.edge)
            links.go((self.name, "on", 0), low, mine, places.near)

            @pl.when(places.is_inner)
            def _():
                links.go((self.name + "o", "z", 2), low, mine, places.inner, "inner")

            links.go((self.name, "of", 0, 0), low, mine, places.far)
            writes.append(load(low(), mine()))

        def pass_far(self, i):
            block = self.spot(0, 1, i)
            if i and self.near_first:
                pass_along(self.name + "p", lambda i: self.spot(0, 1, i), i)
            else:
                links.got((self.name, "on", i), block)
                if self.near_first:
                    along(self.name + "p", lambda i: self.spot(0, 1, i))
            links.go((self.name, "of", 1, i), block, block, places.far)

        def pass_on(self, i):
            block = self.spot(0, 0, i)
            pass_along(self.name + "o", lambda i: self.spot(0, 0, i), i)
            if not self.near_first:
                links.go((self.name, "on", i), block, block, places.near)
            links.go((self.name, "of", 0, i), block, block, places.far)

        def finish(self):
            for i in range(4):
                for a in range(2):
                    links.got((self.name, "of", a, i), self.spot(1, a, i))

    late = Reduce("b", width, q_cols, 0)
    early = Reduce("a", 0, width, q_cols // 16, near_first=True)
    late.send(8)
    attend_back(0, 4)
    for m in range(kv_heads // 2):
        start = q_cols + m * FLAT
        for sums, shift in ((r.key_sums, 0), (r.value_sums, k_cols)):
            block = jnp.where(
                low_lanes, sums[2 * m], pltpu.roll(sums[2 * m + 1], HEAD_DIMENSION, 1)
            )
            if shift == 0:
                block = turn(block * ATTENTION_SCALE, cosine, sine, -1.0)
            r.head_grads[:, start + shift : start + shift + FLAT] = block.astype(LOW)
    head_grads = r.head_grads
    r.grads[pl.ds(0, width), :] = mul(r.normed[...], head_grads[...], FIRST).astype(LOW)
    early.send(8)
    r.result_all[1, 0:FLAT] = mul(
        head_grads[pl.ds(other_half, FLAT), :], r.w_in[...], LAST
    ).astype(LOW)
    links.go("terms", part(r.result_all, 1, pl.ds(0, FLAT)), whole(r.terms_in), places.pair)
    own_terms = mul(head_grads[pl.ds(half, FLAT), :], r.w_in[...], LAST).astype(LOW)
    send_grads()
    late.fold(3)
    late.fold(2)
    late.fold(1)
    late.fold(0)
    late.settle(3)
    late.settle(2)
    late.settle(1)
    early.fold(3)
    early.fold(2)
    early.settle(3)
    early.fold(1)
    early.settle(2)
    early.fold(0)
    late.share()
    early.settle(1)
    links.got("terms", whole(r.terms_in))
    xn_grad = (own_terms.astype(FULL) + r.terms_in[...].astype(FULL)).astype(LOW).astype(FULL)
    x_half = r.tokens[pl.ds(half, FLAT), :].astype(FULL)
    scale = lax.rsqrt(jnp.mean(x_half * x_half, axis=-1, keepdims=True) + NORM_EPS)
    scaled = r.norm_one[...] * xn_grad
    pull = jnp.mean(scaled * x_half, axis=-1, keepdims=True)
    r.grad_tokens[...] = (
        r.grad_tokens[...] + scale * scaled - x_half * (scale * scale * scale * pull)
    )
    r.small_mine[0, pl.ds(0, experts), :] = r.small[pl.ds(0, experts), :]
    row = lax.broadcasted_iota(jnp.int32, (8, width), 0)
    r.small_mine[0, pl.ds(experts, 8), :] = jnp.where(
        row == 0,
        r.small[pl.ds(experts, 8), :],
        jnp.sum(xn_grad * x_half * scale, axis=0, keepdims=True),
    )
    links.go(("s", 0), part(r.small_mine, 0), part(r.small_in, 0), places.pair)
    late.pass_far(0)
    late.pass_on(1)
    early.share()
    sum_grads()
    links.got(("s", 0), part(r.small_in, 0))
    r.small_mine[1] = r.small_mine[0] + r.small_in[0]
    links.go(("s", 1), part(r.small_mine, 1), part(r.small_in, 1), places.far)
    late.pass_far(1)
    late.pass_on(2)
    early.pass_far(0)
    late.pass_far(2)
    late.pass_on(3)
    late.pass_far(3)
    links.got(("s", 1), part(r.small_in, 1))
    r.small_mine[2] = r.small_mine[1] + r.small_in[1]
    links.go(("s", 2), part(r.small_mine, 2), part(r.small_in, 2), places.near)
    early.pass_on(1)
    early.pass_far(1)
    early.pass_on(2)
    links.got(("s", 2), part(r.small_in, 2))
    r.small_all[z] = r.small_mine[2] + r.small_in[2]
    along("s", lambda i: part(r.small_all, ranks[i]))
    early.pass_far(2)
    early.pass_on(3)
    early.pass_far(3)
    weighted_sums.total(
        near_sum("w", r.row_kept, r.weighted_near, 0, halves),
        lambda n: r.branch_in.at[halves[n]],
    )
    r.layer_out[...] = (r.middle[...] + RESIDUAL_SCALE * r.branch_in[...]).astype(LOW)

    for i in (1, 2, 3):
        pass_along("s", lambda i: part(r.small_all, ranks[i]), i)
    small = ((r.small_all[0] + r.small_all[1]) + r.small_all[2]) + r.small_all[3]
    r.router_out[...] = small[:experts]
    r.norms_out[...] = small[experts:]
    late.finish()
    early.finish()
    for n, (_, out, _, spot) in enumerate(finals):
        links.got(("ef", n), part(out, *spot))
    for copy in writes:
        copy.wait()
    links.drain()


def run_layer(**inputs):
    rows_here, width = inputs["tokens"].shape
    experts = inputs["w_router"].shape[0]
    q_cols, k_cols = inputs["w_query"].shape[1], inputs["key_weight"].shape[1]
    kv_heads = k_cols // HEAD_DIMENSION
    vmem = pl.BlockSpec(memory_space=pltpu.VMEM)
    anywhere = pl.BlockSpec(memory_space=pl.ANY)
    block = (FLAT, width)
    gate = (experts, FLAT)
    slots = (2, PAIR, width)
    small = (experts + 8, width)
    grads = (width + q_cols, width)
    depth = grads[0] // 16
    outputs = {
        "layer_out": (block, LOW),
        "grad_tokens": (block, FULL),
        "router_out": (gate[:1] + (width,), FULL),
        "norms_out": ((8, width), FULL),
    }
    held = {"grads_out": (grads, LOW)} | {
        name + "_out": (inputs["w_" + name].shape, LOW) for name in ("gate", "up", "down")
    }
    heads = (kv_heads, 2, rows_here)
    scratch = {
        "w_in": ((width, q_cols + 2 * k_cols), LOW),
        "w_out": ((q_cols, width), LOW),
        "normed": ((rows_here, width), LOW),
        "q": ((kv_heads, rows_here, FLAT), LOW),
        "keys": (heads + (FLAT,), LOW),
        "values": (heads + (FLAT,), LOW),
        "bias": ((rows_here, rows_here), FULL),
        "att_probs": (heads + (rows_here,), FULL),
        "heads": ((rows_here, q_cols), LOW),
        "heads_grad": ((rows_here, q_cols), LOW),
        "head_grads": ((rows_here, q_cols + 2 * k_cols), LOW),
        "key_sums": ((kv_heads, rows_here, FLAT), FULL),
        "value_sums": ((kv_heads, rows_here, FLAT), FULL),
        "branch_send": (block, FULL),
        "branch_in": (block, FULL),
        "middle": (block, FULL),
        "branch_grad": ((rows_here, width), LOW),
        "small": (small, FULL),
        "terms_in": (block, LOW),
        "grads": (grads, LOW),
        "sum_z_send": ((4, depth, width), LOW),
        "sum_z_in": ((4, depth, width), LOW),
        "small_mine": ((3,) + small, FULL),
        "small_in": ((3,) + small, FULL),
        "small_all": ((4,) + small, FULL),
        "probs": (gate, FULL),
        "tables": ((4, 2) + gate, FULL),
        "gate_tables": ((4, 2) + gate, FULL),
        "g_all": ((4, 2) + block, LOW),
        "x_all": ((4, 2) + block, LOW),
        "g_slots": ((8,) + slots, LOW),
        "x_slots": ((8,) + slots, LOW),
        "row_slots": ((8,) + slots, LOW),
        "g_send": ((4,) + slots, LOW),
        "x_send": ((4,) + slots, LOW),
        "gates": ((2 * PAIR, FLAT), FULL),
        "gate_send": ((2, 2 * PAIR, FLAT), LOW),
        "gate_far": ((2, 2 * PAIR, FLAT), LOW),
        "parts": ((2 * PAIR, FLAT), FULL),
        "parts_in": ((2 * PAIR, FLAT), FULL),
        "pick": ((4, 4 * PAIR, 2 * FLAT), LOW),
        "gate_w": (inputs["w_gate"].shape, LOW),
        "up_w": (inputs["w_up"].shape, LOW),
        "down_w": (inputs["w_down"].shape, LOW),
        "hidden_all": ((2, 8 * PAIR, FF), LOW),
        "gate_all": ((2, 8 * PAIR, FF), LOW),
        "up_all": ((2, 8 * PAIR, FF), LOW),
        "result_all": ((2, 8 * PAIR, width), LOW),
        "rows_in": ((4,) + slots, LOW),
        "row_kept": ((4,) + block, FULL),
        "row_near": ((4,) + block, LOW),
        "row_near_send": ((4,) + block, LOW),
        "row_z_send": ((4,) + block, LOW),
        "row_z_in": ((4,) + block, LOW),
        "part_kept": ((4,) + gate, FULL),
        "part_near": ((4,) + gate, FULL),
        "part_send": ((4,) + gate, FULL),
        "part_z_send": ((4,) + gate, FULL),
        "part_z_in": ((4,) + gate, FULL),
        "part_total": (gate, FULL),
        "weighted_near": ((4,) + block, LOW),
        "weighted_z_in": ((4,) + block, LOW),
    }
    near_by = ("tokens", "norm_one", "norm_two", "w_router", "routes", "priority")
    near_by += ("cotangent", "cosine", "sine")
    names = [*inputs, *outputs, *held, *scratch, "sems_local", "sems_send", "sems_recv"]
    results = pl.pallas_call(
        functools.partial(layer_kernel, names),
        out_shape=[
            jax.ShapeDtypeStruct(shape, kind) for shape, kind in [*outputs.values(), *held.values()]
        ],
        in_specs=[vmem if name in near_by else anywhere for name in inputs],
        out_specs=[vmem] * len(outputs) + [anywhere] * len(held),
        scratch_shapes=[pltpu.VMEM(shape, kind) for shape, kind in scratch.values()]
        + [
            pltpu.SemaphoreType.DMA((20,)),
            pltpu.SemaphoreType.DMA((400,)),
            pltpu.SemaphoreType.DMA((380,)),
        ],
        compiler_params=pltpu.CompilerParams(
            collective_id=0, has_side_effects=True, vmem_limit_bytes=63 << 20
        ),
        name="layer",
    )(*inputs.values())
    return dict(zip([*outputs, *held], results))


def cast_kernel(*refs):
    parts, (first, second, layer, tokens, router, norms), outs = refs[:3], refs[3:9], refs[9:]
    q_cols, k_cols = outs[3].shape[1], outs[4].shape[1]
    for n in range(3):
        outs[n][...] = parts[n][...].astype(FULL)
    outs[3][...] = first[:, :q_cols].astype(FULL)
    outs[4][...] = first[:, q_cols : q_cols + k_cols].astype(FULL)
    outs[5][...] = first[:, q_cols + k_cols :].astype(FULL)
    outs[6][...] = second[...].astype(FULL)
    outs[7][...] = layer[...]
    outs[8][...] = tokens[...]
    outs[9][...] = router[...]
    outs[10][...] = norms[0:1, :]
    outs[11][...] = norms[1:2, :]


def cast_grads(done, q_cols, k_cols, steps=4):
    width = done["grads_out"].shape[1]
    parts = [done[name + "_out"] for name in ("gate", "up", "down")]
    rest = [done[name] for name in ("layer_out", "grad_tokens", "router_out", "norms_out")]

    def rows(shape, offset=0):
        block = shape[0] // steps
        return pl.BlockSpec((block, shape[1]), lambda i: (offset // block + i, 0))

    shapes = [parts[0].shape] * 3 + [(width, cols) for cols in (q_cols, k_cols, k_cols)]
    shapes += [(q_cols, width)] + [one.shape for one in rest[:3]]
    row = pl.BlockSpec((1, width), lambda i: (0, 0))
    return pl.pallas_call(
        cast_kernel,
        grid=(steps,),
        out_shape=[
            jax.ShapeDtypeStruct(shape, LOW if n == 7 else FULL)
            for n, shape in enumerate(shapes + [(1, width)] * 2)
        ],
        in_specs=[rows(one.shape) for one in parts]
        + [rows((width, width)), rows((q_cols, width), width)]
        + [rows(one.shape) for one in rest[:3]]
        + [pl.BlockSpec(rest[3].shape, lambda i: (0, 0))],
        out_specs=[rows(shape) for shape in shapes] + [row, row],
        compiler_params=pltpu.CompilerParams(vmem_limit_bytes=62 << 20),
        name="cast_grads",
    )(*parts, done["grads_out"], done["grads_out"], *rest)


def quick_shards(
    tokens,
    norm_one,
    w_query,
    key_weight,
    value_weight,
    w_output,
    norm_two,
    w_router,
    w_gate,
    w_up,
    w_down,
    routes,
    priority,
    cotangent,
):
    rows_here, width = tokens.shape
    experts = w_router.shape[1]
    q_cols, k_cols = w_query.shape[1], key_weight.shape[1]
    local_index = np.arange(rows_here, dtype=np.int32)
    prompt_rows, cont_rows = rows_here // 2, rows_here // 4
    position = np.where(
        local_index < prompt_rows,
        local_index,
        prompt_rows + (local_index - prompt_rows) % cont_rows,
    )
    frequency = ROPE_BASE ** (
        -(2.0 * np.arange(HEAD_DIMENSION // 2, dtype=np.float32)) / HEAD_DIMENSION
    )
    frequency = frequency.astype(np.float32)
    angle_table = position.astype(np.float32)[:, None] * np.tile(frequency, 4)[None, :]
    done = run_layer(
        tokens=tokens,
        norm_one=norm_one[None, :],
        norm_two=norm_two[None, :],
        w_router=w_router.T,
        routes=routes.T,
        priority=priority,
        cotangent=cotangent,
        cosine=jnp.asarray(np.cos(angle_table), FULL),
        sine=jnp.asarray(np.sin(angle_table), FULL),
        w_query=w_query,
        key_weight=key_weight,
        value_weight=value_weight,
        w_output=w_output,
        w_gate=w_gate,
        w_up=w_up,
        w_down=w_down,
    )
    gate, up, down, query, key, value, output, layer, token, router, second, first = cast_grads(
        done, q_cols, k_cols
    )
    return (
        layer,
        token,
        first[0],
        query,
        key,
        value,
        output,
        second[0],
        router.T,
        gate,
        up,
        down,
    )


def solution(mesh):
    body = quick_shards if dict(mesh.shape) == {"exp": 16, "head": 2} else shards
    return jax.shard_map(
        body,
        mesh=mesh,
        in_specs=(
            P("exp", None),
            P(),
            P(None, "head"),
            P(None, "head"),
            P(None, "head"),
            P("head", None),
            P(),
            P(),
            P(None, "exp"),
            P(None, "exp"),
            P("exp", None),
            P("exp", None),
            P(("exp", "head"), None),
            P(("exp", "head"), None),
        ),
        out_specs=(
            P(("exp", "head"), None),
            P(("exp", "head"), None),
            P(),
            P(None, "head"),
            P(None, "head"),
            P(None, "head"),
            P("head", None),
            P(),
            P(),
            P(None, "exp"),
            P(None, "exp"),
            P("exp", None),
        ),
        check_vma=False,
    )
```

```python
import functools
import types

import jax
import jax.numpy as jnp
import numpy as np
from jax import lax
from jax.experimental import pallas as pl
from jax.experimental.pallas import tpu as pltpu
from jax.sharding import PartitionSpec as P

HEAD_DIMENSION = 64
FF = 512
TOPK = 8


RESIDUAL_SCALE = 0.22
ATTENTION_SCALE = 0.015625
ROPE_BASE = 10000.0
NORM_EPS = 1e-06
MASKED_SCORE = -1e30


def rms_scale(values, scale_row):
    return (
        values * lax.rsqrt(jnp.mean(values * values, axis=-1, keepdims=True) + NORM_EPS) * scale_row
    )


def apply_rotary(values, cosine_values, sine_values):
    half_width = values.shape[-1] // 2
    lower_part = values[..., :half_width]
    upper_part = values[..., half_width:]
    return jnp.concatenate(
        [
            lower_part * cosine_values - upper_part * sine_values,
            upper_part * cosine_values + lower_part * sine_values,
        ],
        axis=-1,
    )


def rotate_back(values, cosine_values, sine_values):
    half_width = values.shape[-1] // 2
    lower_part = values[..., :half_width]
    upper_part = values[..., half_width:]
    return jnp.concatenate(
        [
            lower_part * cosine_values + upper_part * sine_values,
            upper_part * cosine_values - lower_part * sine_values,
        ],
        axis=-1,
    )


def shards(
    tokens,
    norm_one,
    w_query,
    key_weight,
    value_weight,
    w_output,
    norm_two,
    w_router,
    w_gate,
    w_up,
    w_down,
    routes,
    priority,
    cotangent,
):
    tok_rows, model_width = tokens.shape
    heads_count = lax.axis_size("head")
    head_rank = lax.axis_index("head")
    exp_count = lax.axis_size("exp")
    half_rows = tok_rows // heads_count
    prompt_rows = tok_rows // 2
    cont_rows = tok_rows // 4
    kv_heads = key_weight.shape[1] // HEAD_DIMENSION
    query_groups = w_query.shape[1] // key_weight.shape[1]
    experts = w_router.shape[1]
    held_cols = w_gate.shape[1]
    held = max(1, held_cols // FF)
    split = max(1, FF // held_cols)
    block_width = held_cols // held
    capacity = max(2, (5 * half_rows * TOPK + 4 * experts - 1) // (4 * experts))
    rows_per_block = min(512, tok_rows)
    count_of_blocks = tok_rows // rows_per_block
    local_index = jnp.arange(tok_rows, dtype=jnp.int32)
    position = jnp.where(
        local_index < prompt_rows,
        local_index,
        prompt_rows + (local_index - prompt_rows) % cont_rows,
    )
    frequency = ROPE_BASE ** (
        -(2.0 * jnp.arange(HEAD_DIMENSION // 2, dtype=jnp.float32)) / HEAD_DIMENSION
    )
    angle_table = position.astype(jnp.float32)[:, None] * frequency[None, :]
    cosine_values = jnp.cos(angle_table)[:, None, :]
    sine_values = jnp.sin(angle_table)[:, None, :]
    x_full = tokens.astype(jnp.float32)
    normed_input_first = rms_scale(x_full, norm_one).astype(jnp.bfloat16)
    rotated_queries = apply_rotary(
        jnp.dot(normed_input_first, w_query, preferred_element_type=jnp.float32).reshape(
            tok_rows, -1, HEAD_DIMENSION
        ),
        cosine_values,
        sine_values,
    ).astype(jnp.bfloat16)
    keys_all = apply_rotary(
        jnp.dot(normed_input_first, key_weight, preferred_element_type=jnp.float32).reshape(
            tok_rows, -1, HEAD_DIMENSION
        ),
        cosine_values,
        sine_values,
    ).astype(jnp.bfloat16)
    values_all = (
        jnp.dot(normed_input_first, value_weight, preferred_element_type=jnp.float32)
        .astype(jnp.bfloat16)
        .reshape(tok_rows, kv_heads, HEAD_DIMENSION)
    )

    def visible_pairs(block_start):
        query_col = (block_start + jnp.arange(rows_per_block, dtype=jnp.int32))[:, None]
        key_row = jnp.arange(tok_rows, dtype=jnp.int32)[None, :]
        from_prompt = (key_row < prompt_rows) & (
            (query_col >= prompt_rows) | (key_row <= query_col)
        )
        same_cont = (
            (key_row >= prompt_rows)
            & (query_col >= prompt_rows)
            & (key_row <= query_col)
            & ((key_row - prompt_rows) // cont_rows == (query_col - prompt_rows) // cont_rows)
        )
        return from_prompt | same_cont

    def scores_of(query_block, block_start):
        raw_scores = (
            jnp.einsum("qhgd,khd->hgqk", query_block, keys_all, preferred_element_type=jnp.float32)
            * ATTENTION_SCALE
        )
        return jnp.where(visible_pairs(block_start)[None, None], raw_scores, MASKED_SCORE)

    def forward_block(parts):
        query_block, block_start = parts
        scores = scores_of(query_block, block_start)
        row_max = jnp.max(scores, axis=-1, keepdims=True)
        weights = jnp.exp(scores - row_max)
        row_total = jnp.sum(weights, axis=-1, keepdims=True)
        probs_low = (weights / row_total).astype(jnp.bfloat16)
        mixed = jnp.einsum(
            "hgqk,khd->qhgd", probs_low, values_all, preferred_element_type=jnp.float32
        )
        return (mixed.astype(jnp.bfloat16), row_max + jnp.log(row_total))

    query_blocks = rotated_queries.reshape(
        count_of_blocks, rows_per_block, kv_heads, query_groups, HEAD_DIMENSION
    )
    block_starts = jnp.arange(count_of_blocks, dtype=jnp.int32) * rows_per_block
    heads_blocks, log_total = lax.map(forward_block, (query_blocks, block_starts))
    head_outputs = heads_blocks.reshape(tok_rows, -1)
    head_terms = jnp.dot(head_outputs, w_output, preferred_element_type=jnp.float32)
    branch_half = lax.dynamic_slice_in_dim(
        lax.psum(head_terms, "head"), head_rank * half_rows, half_rows, 0
    )
    x_half = lax.dynamic_slice_in_dim(x_full, head_rank * half_rows, half_rows, 0)
    middle = x_half + RESIDUAL_SCALE * branch_half
    xn_two = rms_scale(middle, norm_two).astype(jnp.bfloat16)
    logits = jnp.dot(xn_two, w_router, preferred_element_type=jnp.float32)
    my_routes = lax.dynamic_slice_in_dim(routes, head_rank * half_rows, half_rows, 0)
    route_hot = my_routes[:, :, None] == jnp.arange(experts, dtype=jnp.int32)[None, None, :]
    chosen = jnp.sum(jnp.where(route_hot, logits[:, None, :], 0.0), axis=-1)
    chosen_max = jnp.max(chosen, axis=-1, keepdims=True)
    chosen_exp = jnp.exp(chosen - chosen_max)
    gate_probs = chosen_exp / jnp.sum(chosen_exp, axis=-1, keepdims=True)
    gate_low = gate_probs.astype(jnp.bfloat16)
    member = jnp.any(route_hot, axis=1).astype(jnp.bfloat16)
    order_rank = priority[0]
    earlier = (order_rank[None, :] < order_rank[:, None]).astype(jnp.bfloat16)
    before = jnp.dot(earlier, member, preferred_element_type=jnp.float32)
    slot_rank = jnp.sum(jnp.where(route_hot, before[:, None, :], 0.0), axis=-1).astype(jnp.int32)
    is_kept = slot_rank < capacity
    spare_slot = experts * capacity
    target = jnp.where(is_kept, my_routes * capacity + slot_rank, spare_slot)
    row_ids = jnp.broadcast_to(jnp.arange(half_rows, dtype=jnp.int32)[:, None], target.shape)
    assign_ids = jnp.arange(half_rows * TOPK, dtype=jnp.int32).reshape(target.shape)
    source_row = (
        jnp.zeros(spare_slot + 1, jnp.int32).at[target.ravel()].set(row_ids.ravel())[:spare_slot]
    )
    source_pick = (
        jnp.zeros(spare_slot + 1, jnp.int32).at[target.ravel()].set(assign_ids.ravel())[:spare_slot]
    )
    filled = jnp.zeros(spare_slot + 1, jnp.int32).at[target.ravel()].set(1)[:spare_slot] > 0
    slot_inputs = jnp.where(filled[:, None], xn_two[source_row], 0).reshape(
        experts, capacity, model_width
    )
    slot_gates = jnp.where(filled, gate_low.ravel()[source_pick], 0).reshape(experts, capacity)

    def to_owners(per_expert):
        shape_in = per_expert.shape
        spread = jnp.broadcast_to(per_expert[:, None], (shape_in[0], split) + shape_in[1:])
        return spread.reshape((exp_count, held) + shape_in[1:])

    def from_owners(per_owner):
        shape_in = per_owner.shape
        return jnp.sum(
            per_owner.reshape((experts, split) + shape_in[2:]).astype(jnp.float32), axis=1
        )

    gate_cols = w_gate.reshape(model_width, held, block_width)
    up_cols = w_up.reshape(model_width, held, block_width)
    down_rows = w_down.reshape(held, block_width, model_width)
    send_rows = to_owners(slot_inputs)
    send_gates = to_owners(slot_gates)
    slot_rows = lax.all_to_all(send_rows, "exp", split_axis=0, concat_axis=0, tiled=True)
    slot_gate = lax.all_to_all(send_gates, "exp", split_axis=0, concat_axis=0, tiled=True)
    gate_pre = jnp.einsum(
        "sjcd,djf->sjcf", slot_rows, gate_cols, preferred_element_type=jnp.float32
    )
    up_pre = jnp.einsum("sjcd,djf->sjcf", slot_rows, up_cols, preferred_element_type=jnp.float32)
    hidden = (gate_pre * jax.nn.sigmoid(gate_pre) * up_pre).astype(jnp.bfloat16)
    result = jnp.einsum("sjcf,jfd->sjcd", hidden, down_rows, preferred_element_type=jnp.float32)
    weighted = (slot_gate[..., None].astype(jnp.float32) * result).astype(jnp.bfloat16)
    returned = lax.all_to_all(weighted, "exp", split_axis=0, concat_axis=0, tiled=True)
    returned, held_rows, held_gates = (returned, slot_rows, slot_gate)
    back_flat = jnp.concatenate(
        [
            from_owners(returned).reshape(spare_slot, model_width),
            jnp.zeros((1, model_width), jnp.float32),
        ],
        axis=0,
    )
    expert_sum = jnp.sum(back_flat[target], axis=1)
    layer_out = (middle + RESIDUAL_SCALE * expert_sum).astype(jnp.bfloat16)
    out_grad = cotangent.astype(jnp.float32)
    weighted_rows = (RESIDUAL_SCALE * out_grad).astype(jnp.bfloat16)
    grad_slots = to_owners(
        jnp.where(filled[:, None], weighted_rows[source_row], 0).reshape(
            experts, capacity, model_width
        )
    )
    back_grads, back_rows, back_gates = (
        lax.all_to_all(grad_slots, "exp", split_axis=0, concat_axis=0, tiled=True),
        lax.all_to_all(send_rows, "exp", split_axis=0, concat_axis=0, tiled=True),
        lax.all_to_all(send_gates, "exp", split_axis=0, concat_axis=0, tiled=True),
    )
    owner_gates = back_gates[..., None].astype(jnp.float32)
    gate_pre = jnp.einsum(
        "sjcd,djf->sjcf", back_rows, gate_cols, preferred_element_type=jnp.float32
    )
    up_pre = jnp.einsum("sjcd,djf->sjcf", back_rows, up_cols, preferred_element_type=jnp.float32)
    gate_sigmoid = jax.nn.sigmoid(gate_pre)
    gate_act = gate_pre * gate_sigmoid
    hidden = (gate_act * up_pre).astype(jnp.bfloat16)
    result = jnp.einsum("sjcf,jfd->sjcd", hidden, down_rows, preferred_element_type=jnp.float32)
    gate_part = jnp.sum(back_grads.astype(jnp.float32) * result, axis=-1)
    result_grad = (owner_gates * back_grads).astype(jnp.bfloat16)
    grad_down_w = jnp.einsum(
        "sjcf,sjcd->jfd", hidden, result_grad, preferred_element_type=jnp.float32
    ).reshape(held_cols, model_width)
    hidden_grad = jnp.einsum(
        "sjcd,jfd->sjcf", result_grad, down_rows, preferred_element_type=jnp.float32
    )
    gate_pre_grad = (
        hidden_grad * up_pre * gate_sigmoid * (1.0 + gate_pre * (1.0 - gate_sigmoid))
    ).astype(jnp.bfloat16)
    up_pre_grad = (hidden_grad * gate_act).astype(jnp.bfloat16)
    grad_gate_w = jnp.einsum(
        "sjcd,sjcf->djf", back_rows, gate_pre_grad, preferred_element_type=jnp.float32
    ).reshape(model_width, held_cols)
    grad_up_w = jnp.einsum(
        "sjcd,sjcf->djf", back_rows, up_pre_grad, preferred_element_type=jnp.float32
    ).reshape(model_width, held_cols)
    rows_grad = (
        jnp.einsum("sjcf,djf->sjcd", gate_pre_grad, gate_cols, preferred_element_type=jnp.float32)
        + jnp.einsum("sjcf,djf->sjcd", up_pre_grad, up_cols, preferred_element_type=jnp.float32)
    ).astype(jnp.bfloat16)
    rows_back, gates_back = (
        lax.all_to_all(rows_grad, "exp", split_axis=0, concat_axis=0, tiled=True),
        lax.all_to_all(
            gate_part.astype(jnp.bfloat16), "exp", split_axis=0, concat_axis=0, tiled=True
        ),
    )
    rows_flat = jnp.concatenate(
        [
            from_owners(rows_back).reshape(spare_slot, model_width),
            jnp.zeros((1, model_width), jnp.float32),
        ],
        axis=0,
    )
    xn_two_grad = jnp.sum(rows_flat[target], axis=1)
    gate_total = from_owners(gates_back).astype(jnp.bfloat16).reshape(spare_slot)
    gates_flat = jnp.concatenate([gate_total, jnp.zeros((1,), jnp.bfloat16)], axis=0)
    gate_grad_tok = gates_flat[target].astype(jnp.float32)
    chosen_grad = gate_probs * (
        gate_grad_tok - jnp.sum(gate_probs * gate_grad_tok, axis=-1, keepdims=True)
    )
    logit_grad = jnp.sum(jnp.where(route_hot, chosen_grad[:, :, None], 0.0), axis=1).astype(
        jnp.bfloat16
    )
    grad_router = jnp.einsum("rd,re->de", xn_two, logit_grad, preferred_element_type=jnp.float32)
    xn_two_grad = xn_two_grad + jnp.einsum(
        "re,de->rd", logit_grad, w_router, preferred_element_type=jnp.float32
    )
    middle_norm_pull = jax.vjp(rms_scale, middle, norm_two)[1]
    middle_norm_grad, grad_norm_two = middle_norm_pull(xn_two_grad)
    middle_grad = out_grad + middle_norm_grad
    branch_rows = (RESIDUAL_SCALE * middle_grad).astype(jnp.bfloat16)
    branch_grad = lax.all_gather(branch_rows, "head", axis=0, tiled=True)
    heads_grad = jnp.einsum(
        "td,hd->th", branch_grad, w_output, preferred_element_type=jnp.float32
    ).astype(jnp.bfloat16)
    grad_output_w = jnp.einsum(
        "th,td->hd", head_outputs, branch_grad, preferred_element_type=jnp.float32
    )

    def backward_block(running, parts):
        key_grad, value_grad = running
        query_block, heads_block, block_total, block_start = parts
        scores = scores_of(query_block, block_start)
        probs = jnp.exp(scores - block_total)
        probs_low = probs.astype(jnp.bfloat16)
        prob_grad = jnp.einsum(
            "qhgd,khd->hgqk", heads_block, values_all, preferred_element_type=jnp.float32
        )
        row_inner = jnp.sum(probs * prob_grad, axis=-1, keepdims=True)
        score_grad = (probs * (prob_grad - row_inner)).astype(jnp.bfloat16)
        query_grad = (
            jnp.einsum("hgqk,khd->qhgd", score_grad, keys_all, preferred_element_type=jnp.float32)
            * ATTENTION_SCALE
        )
        key_grad = (
            key_grad
            + jnp.einsum(
                "hgqk,qhgd->khd", score_grad, query_block, preferred_element_type=jnp.float32
            )
            * ATTENTION_SCALE
        )
        value_grad = value_grad + jnp.einsum(
            "hgqk,qhgd->khd", probs_low, heads_block, preferred_element_type=jnp.float32
        )
        return ((key_grad, value_grad), query_grad)

    heads_grad_blocks = heads_grad.reshape(
        count_of_blocks, rows_per_block, kv_heads, query_groups, HEAD_DIMENSION
    )
    zero_keys = jnp.zeros((tok_rows, kv_heads, HEAD_DIMENSION), jnp.float32)
    (own_key, own_value), query_grad = lax.scan(
        backward_block,
        (zero_keys, zero_keys),
        (query_blocks, heads_grad_blocks, log_total, block_starts),
    )
    query_pre_grad = (
        rotate_back(query_grad.reshape(tok_rows, -1, HEAD_DIMENSION), cosine_values, sine_values)
        .reshape(tok_rows, -1)
        .astype(jnp.bfloat16)
    )
    key_pre_grad = (
        rotate_back(own_key, cosine_values, sine_values).reshape(tok_rows, -1).astype(jnp.bfloat16)
    )
    value_low_grad = own_value.reshape(tok_rows, -1).astype(jnp.bfloat16)
    grad_query_w = jnp.einsum(
        "td,th->dh", normed_input_first, query_pre_grad, preferred_element_type=jnp.float32
    )
    grad_key_w = jnp.einsum(
        "td,th->dh", normed_input_first, key_pre_grad, preferred_element_type=jnp.float32
    )
    grad_value_w = jnp.einsum(
        "td,th->dh", normed_input_first, value_low_grad, preferred_element_type=jnp.float32
    )
    xn_one_terms = (
        jnp.einsum("th,dh->td", query_pre_grad, w_query, preferred_element_type=jnp.float32)
        + jnp.einsum("th,dh->td", key_pre_grad, key_weight, preferred_element_type=jnp.float32)
        + jnp.einsum("th,dh->td", value_low_grad, value_weight, preferred_element_type=jnp.float32)
    )
    xn_one_grad = lax.psum_scatter(
        xn_one_terms.astype(jnp.bfloat16), "head", scatter_dimension=0, tiled=True
    ).astype(jnp.float32)
    input_norm_pull = jax.vjp(rms_scale, x_half, norm_one)[1]
    input_norm_grad, grad_norm_one = input_norm_pull(xn_one_grad)
    grad_tokens = middle_grad + input_norm_grad
    grad_gate_w, grad_up_w, grad_down_w, grad_router, grad_norm_one, grad_norm_two = (
        lax.psum(grad_gate_w.astype(jnp.bfloat16), "head").astype(jnp.float32),
        lax.psum(grad_up_w.astype(jnp.bfloat16), "head").astype(jnp.float32),
        lax.psum(grad_down_w.astype(jnp.bfloat16), "head").astype(jnp.float32),
        lax.psum(grad_router.astype(jnp.bfloat16), "head").astype(jnp.float32),
        lax.psum(grad_norm_one.astype(jnp.bfloat16), "head").astype(jnp.float32),
        lax.psum(grad_norm_two.astype(jnp.bfloat16), "head").astype(jnp.float32),
    )
    (
        grad_query_w,
        grad_key_w,
        grad_value_w,
        grad_output_w,
        grad_router,
        grad_norm_one,
        grad_norm_two,
    ) = lax.psum(
        (
            grad_query_w,
            grad_key_w,
            grad_value_w,
            grad_output_w,
            grad_router,
            grad_norm_one,
            grad_norm_two,
        ),
        "exp",
    )
    return (
        layer_out,
        grad_tokens,
        grad_norm_one,
        grad_query_w,
        grad_key_w,
        grad_value_w,
        grad_output_w,
        grad_norm_two,
        grad_router,
        grad_gate_w,
        grad_up_w,
        grad_down_w,
    )


MESH = pl.DeviceIdType.MESH
FLAT = 128
SLOTS = 40
PAIR = 2 * SLOTS
UNKEPT = -1000.0
LOW = jnp.bfloat16
FULL = jnp.float32
LAST = (((1,), (1,)), ((), ()))
FIRST = (((0,), (0,)), ((), ()))
USUAL = (((1,), (0,)), ((), ()))


def mul(left, right, dims=USUAL):
    return lax.dot_general(left, right, dims, preferred_element_type=FULL)


def remote(source, target, send_sem, recv_sem, device):
    return pltpu.make_async_remote_copy(
        src_ref=source,
        dst_ref=target,
        send_sem=send_sem,
        recv_sem=recv_sem,
        device_id=device,
        device_id_type=MESH,
    )


def part(ref, *index):
    return lambda: ref.at[index]


def whole(ref):
    return lambda: ref


class Places:
    def __init__(self):
        self.e = e = lax.axis_index("exp")
        self.h = h = lax.axis_index("head")
        x, y, self.z = e % 2, (e // 2) % 2, e // 4
        z = self.z
        over_x, over_y = e + 1 - 2 * x, e + 2 - 4 * y
        self.near_e = over_x * (1 - h) + over_y * h
        self.far_e = over_y * (1 - h) + over_x * h
        self.near = (self.near_e, h)
        self.far = (self.far_e, h)
        self.outer = (1 + z % 2 + z // 2) % 2
        self.ranks = [z, z + 1 - 2 * (z % 2), 2 - z // 2, 3 - 3 * (z // 2)]
        self.along = [(rank * 4 + e % 4, h) for rank in self.ranks]
        self.edge = self.along[1]
        self.inner = ((3 - z) * 4 + e % 4, h)
        self.pair = (e, 1 - h)
        self.is_inner = (z == 1) | (z == 2)

    def hello(self):
        barrier = pltpu.get_barrier_semaphore()
        for device in (self.pair, self.near, self.far, *self.along[1:]):
            pl.semaphore_signal(barrier, inc=1, device_id=device, device_id_type=MESH)

    def ready(self):
        pl.semaphore_wait(pltpu.get_barrier_semaphore(), 6)


class Links:
    def __init__(self, places, send, recv):
        self.places, self.send, self.recv = places, send, recv
        self.sent, self.names = 0, {}
        self.pending = {"all": [], "inner": []}

    def number(self, name):
        return self.names.setdefault(name, len(self.names))

    def go(self, name, source, target, device, who="all", number=None):
        arrival = self.number(name) if number is None else number
        number = self.sent
        remote(
            source(), target(), self.send.at[number], self.recv.at[arrival], device
        ).start()
        self.sent += 1
        self.pending[who].append((number, name, source))

    def got(self, name, target):
        remote(
            target(), target(), self.send.at[0], self.recv.at[self.number(name)], self.places.near
        ).wait_recv()

    def sent_all(self, who, of):
        for number, name, source in self.pending[who]:
            if of is None or name[0] == of:
                remote(
                    source(), source(), self.send.at[number], self.recv.at[0], self.places.near
                ).wait_send()

    def drain(self, of=None):
        self.sent_all("all", of)

        @pl.when(self.places.is_inner)
        def _():
            self.sent_all("inner", of)

        for who, sent in self.pending.items():
            self.pending[who] = [one for one in sent if of is not None and one[1][0] != of]


class Spread:
    def __init__(self, links, name, gathered, pieces=((),), cross=()):
        self.links, self.name, self.gathered = links, name, gathered
        self.pieces, self.cross = pieces, cross

    def spot(self, i, a, n):
        return part(self.gathered, i, a, *self.pieces[n])

    def launch(self, a, n):
        links, places = self.links, self.links.places
        block = self.spot(0, a, n)
        links.go((self.name, a, 1, n), block, self.spot(1, a, n), places.edge)

        @pl.when(places.is_inner)
        def _():
            links.go((self.name, a, 2, n), block, self.spot(2, a, n), places.inner, "inner")

    def start(self):
        for n in range(len(self.pieces)):
            self.launch(0, n)
            self.links.go(
                (self.name, "n", 0, n),
                self.spot(0, 0, n),
                self.spot(0, 1, n),
                self.links.places.near,
            )

    def forward(self, i, a, n):
        links, places = self.links, self.links.places
        there = {1: 3, 2: 2, 3: 3}[i]
        device = places.inner if i == 1 else places.edge
        block = self.spot(i, a, n)
        links.got((self.name, a, i, n), block)

        @pl.when(places.is_inner)
        def _():
            links.go((self.name, a, there, n), block, self.spot(there, a, n), device, "inner")

    def pass_on(self, i):
        for n in range(len(self.pieces)):
            self.forward(i, 0, n)
            if n not in self.cross:
                self.links.go(
                    (self.name, "n", i, n),
                    self.spot(i, 0, n),
                    self.spot(i, 1, n),
                    self.links.places.near,
                )

    def wait(self, i, n=0):
        if i and n in self.cross:
            self.forward(i, 1, n)
        else:
            self.links.got((self.name, "n", i, n), self.spot(i, 1, n))
            if n in self.cross:
                self.launch(1, n)


class Gather:
    def __init__(self, links, name, send, recv, pieces):
        self.links, self.name, self.send, self.recv, self.pieces = links, name, send, recv, pieces
        for n in range(len(pieces)):
            for slot in (1, 2, 3):
                links.number((name, n, slot))

    def push(self, i, value):
        links, places = self.links, self.links.places
        for n, piece in enumerate(self.pieces):
            spot = part(self.send, i, *piece)
            spot()[...] = value(n).astype(self.send.dtype)
            slot = 1 if i == 1 else 2 + places.outer
            links.go(
                (self.name, n, 1),
                spot,
                part(self.recv, slot, *piece),
                places.along[i],
                number=links.number((self.name, n, 1)) + slot - 1,
            )

    def total(self, own, result):
        for n, piece in enumerate(self.pieces):
            value = own(n)
            for slot in (1, 2, 3):
                spot = part(self.recv, slot, *piece)
                self.links.got((self.name, n, slot), spot)
                value = value + spot()[...].astype(FULL)
            result(n)[...] = value


def table_rows(tables, i, places):
    rows = []
    for chip in (places.e, places.far_e):
        for j in range(2):
            rows.append(
                jnp.concatenate(
                    [tables[i, a, pl.ds(2 * chip + j, 1), :] for a in range(2)], axis=1
                )
            )
    return rows


def selection(tables, i, places):
    slot = lax.broadcasted_iota(jnp.int32, (PAIR, 2 * FLAT), 0)
    lane = lax.broadcasted_iota(jnp.int32, (PAIR, 2 * FLAT), 1)
    wanted = (slot - jnp.where(lane >= FLAT, SLOTS, 0)).astype(FULL)
    return jnp.concatenate(
        [jnp.where(row == wanted, 1.0, 0.0) for row in table_rows(tables, i, places)], axis=0
    )


def turn(block, cosine, sine, sign):
    lane = lax.broadcasted_iota(jnp.int32, block.shape, 1) % HEAD_DIMENSION
    quarter = HEAD_DIMENSION // 2
    other = jnp.where(
        lane < quarter,
        -sign * pltpu.roll(block, FLAT - quarter, 1),
        sign * pltpu.roll(block, quarter, 1),
    )
    return block * cosine + other * sine


def layer_kernel(names, *refs):
    r = types.SimpleNamespace(**dict(zip(names, refs, strict=True)))
    places = Places()
    h, e, z = places.h, places.e, places.z
    places.hello()
    links = Links(places, r.sems_send, r.sems_recv)
    experts = r.w_router.shape[0]
    rows_here, width = r.tokens.shape
    q_cols, k_cols = r.w_query.shape[1], r.key_weight.shape[1]
    kv_heads = k_cols // HEAD_DIMENSION
    every = slice(None)
    half = pl.multiple_of(h * FLAT, FLAT)
    other_half = pl.multiple_of((1 - h) * FLAT, FLAT)
    locals_used = [0]

    def load(source, target):
        copy = pltpu.make_async_copy(source, target, r.sems_local.at[locals_used[0]])
        locals_used[0] += 1
        copy.start()
        return copy

    in_loads = [
        load(r.w_query, r.w_in.at[:, :q_cols]),
        load(r.key_weight, r.w_in.at[:, q_cols : q_cols + k_cols]),
        load(r.value_weight, r.w_in.at[:, q_cols + k_cols :]),
    ]
    out_load = load(r.w_output, r.w_out)
    rank_row = r.priority[...]
    row_id = lax.broadcasted_iota(jnp.int32, (FLAT, FLAT), 0)
    col_id = lax.broadcasted_iota(jnp.int32, (FLAT, FLAT), 1)
    rank_col = jnp.sum(
        jnp.where(row_id == col_id, jnp.broadcast_to(rank_row, (FLAT, FLAT)), 0),
        axis=1,
        keepdims=True,
    )
    earlier = jnp.where(rank_row < rank_col, 1.0, 0.0).astype(LOW)
    expert_id = lax.broadcasted_iota(jnp.int32, (experts, FLAT), 0)
    my_routes = r.routes[:, pl.ds(half, FLAT)]
    member = jnp.zeros((experts, FLAT), FULL)
    for k in range(TOPK):
        member += jnp.where(my_routes[k : k + 1, :] == expert_id, 1.0, 0.0)
    before = mul(member.astype(LOW), earlier, LAST)
    r.tables[0, 0] = jnp.where((member > 0.5) & (before < SLOTS), before, UNKEPT)
    r.g_all[0, 0] = (RESIDUAL_SCALE * r.cotangent[...].astype(FULL)).astype(LOW)
    columns = [slice(0, width // 2), slice(width // 2, width)]
    halves = [(every, one) for one in columns]
    t_spread = Spread(links, "t", r.tables)
    g_columns = [slice(0, 384), slice(384, 768), slice(768, width)]
    g_spread = Spread(links, "g", r.g_all, [(every, one) for one in g_columns], cross=(2,))
    x_spread = Spread(links, "x", r.x_all, halves, cross=(1,))
    p_spread = Spread(links, "p", r.gate_tables)
    x_full = r.tokens[...].astype(FULL)
    r.normed[...] = rms_scale(x_full, r.norm_one[...]).astype(LOW)
    places.ready()
    t_spread.start()
    g_spread.start()

    for copy in in_loads:
        copy.wait()
    expert_loads = [load(r.w_gate, r.gate_w), load(r.w_up, r.up_w), load(r.w_down, r.down_w)]
    projected = mul(r.normed[...], r.w_in[...])
    cosine, sine = r.cosine[...], r.sine[...]
    lane = lax.broadcasted_iota(jnp.int32, (rows_here, FLAT), 1)
    low_lanes = lane < HEAD_DIMENSION
    for g in range(kv_heads):
        r.q[g] = turn(projected[:, g * FLAT : (g + 1) * FLAT], cosine, sine, 1.0).astype(LOW)
    for m in range(kv_heads // 2):
        start = q_cols + m * FLAT
        keys = turn(projected[:, start : start + FLAT], cosine, sine, 1.0)
        start += k_cols
        values = projected[:, start : start + FLAT]
        for block, store in ((keys, r.keys), (values, r.values)):
            rolled = pltpu.roll(block, HEAD_DIMENSION, 1)
            store[2 * m, 0] = jnp.where(low_lanes, block, 0.0).astype(LOW)
            store[2 * m, 1] = jnp.where(low_lanes, 0.0, rolled).astype(LOW)
            store[2 * m + 1, 0] = jnp.where(low_lanes, rolled, 0.0).astype(LOW)
            store[2 * m + 1, 1] = jnp.where(low_lanes, 0.0, block).astype(LOW)
    prompt, cont = rows_here // 2, rows_here // 4
    query_id = lax.broadcasted_iota(jnp.int32, (rows_here, rows_here), 0)
    key_id = lax.broadcasted_iota(jnp.int32, (rows_here, rows_here), 1)
    query_cont = jnp.where(query_id < prompt, 0, 1 + (query_id - prompt) // cont)
    key_cont = jnp.where(key_id < prompt, 0, 1 + (key_id - prompt) // cont)
    visible = ((key_cont == 0) & (query_cont > 0)) | (
        (key_cont == query_cont) & (key_id <= query_id)
    )
    r.bias[...] = jnp.where(visible, 0.0, MASKED_SCORE)

    def attend(first, count):
        def one(g, carry):
            mixed = jnp.zeros((rows_here, FLAT), FULL)
            for s in range(2):
                raw = mul(r.q[g], r.keys[g, s], LAST) * ATTENTION_SCALE
                scores = jnp.where(r.bias[...] < 0.0, MASKED_SCORE, raw)
                weights = jnp.exp(scores - jnp.max(scores, axis=1, keepdims=True))
                probs = weights / jnp.sum(weights, axis=1, keepdims=True)
                r.att_probs[g, s] = probs
                mixed += mul(probs.astype(LOW), r.values[g, s])
            r.heads[:, pl.ds(pl.multiple_of(g * FLAT, FLAT), FLAT)] = mixed.astype(LOW)
            return carry

        lax.fori_loop(first, first + count, one, 0)

    def pick_rows(name, spread, picks, gathered, slots, send, i):
        for n, (_, cols) in enumerate(spread.pieces):
            spread.wait(i, n)
            rows = mul(picks, gathered[i, :, :, cols].reshape(2 * FLAT, -1)).astype(LOW)
            slots[i, :, :, cols] = rows[: 2 * PAIR].reshape(2, PAIR, -1)
            send[i, :, :, cols] = rows[2 * PAIR :].reshape(2, PAIR, -1)
            links.go(
                (name, "f", i, n),
                part(send, i, every, every, cols),
                part(slots, 4 + i, every, every, cols),
                places.far,
            )

    def dispatch_out(i):
        t_spread.wait(i)
        picks = selection(r.tables, i, places).astype(LOW)
        r.pick[i] = picks
        pick_rows("g", g_spread, picks, r.g_all, r.g_slots, r.g_send, i)

    def pass_out(i):
        t_spread.pass_on(i)
        g_spread.pass_on(i)

    attend(0, 4)
    out_load.wait()
    r.branch_send[...] = mul(r.heads[pl.ds(other_half, FLAT), :], r.w_out[...])
    links.go("branch", whole(r.branch_send), whole(r.branch_in), places.pair)
    own_branch = mul(r.heads[pl.ds(half, FLAT), :], r.w_out[...])
    links.got("branch", whole(r.branch_in))
    middle = r.tokens[pl.ds(half, FLAT), :].astype(FULL) + RESIDUAL_SCALE * (
        own_branch + r.branch_in[...]
    )
    r.middle[...] = middle
    xn = rms_scale(middle, r.norm_two[...]).astype(LOW)
    r.x_all[0, 0] = xn
    x_spread.start()
    logits = mul(r.w_router[...], xn, LAST)
    chosen = jnp.where(member > 0.5, logits, MASKED_SCORE)
    weights = jnp.exp(chosen - jnp.max(chosen, axis=0, keepdims=True))
    probs = weights / jnp.sum(weights, axis=0, keepdims=True)
    r.probs[...] = probs
    r.gate_tables[0, 0] = probs.astype(LOW).astype(FULL)
    p_spread.start()

    slots_lane = lax.broadcasted_iota(jnp.int32, (2 * PAIR, FLAT), 1)
    r.gates[...] = jnp.zeros((2 * PAIR, FLAT), FULL)
    r.gate_send[...] = jnp.zeros((2, 2 * PAIR, FLAT), LOW)

    def dispatch_in(i):
        picks = r.pick[i]
        pick_rows("x", x_spread, picks, r.x_all, r.x_slots, r.x_send, i)
        p_spread.wait(i)
        spread_gates = jnp.concatenate(
            [
                jnp.broadcast_to(row, (PAIR, 2 * FLAT))
                for row in table_rows(r.gate_tables, i, places)
            ],
            axis=0,
        )
        slot_gates = jnp.sum(picks.astype(FULL) * spread_gates, axis=1, keepdims=True)
        r.gates[...] += jnp.where(slots_lane == i, slot_gates[: 2 * PAIR], 0.0)
        far_gates = jnp.where(slots_lane == 4 + i, slot_gates[2 * PAIR :], 0.0)
        r.gate_send[i // 2] += far_gates.astype(LOW)

    def send_gates(n):
        links.go(("p", "f", n), part(r.gate_send, n), part(r.gate_far, n), places.far)

    def add_gates(n):
        links.got(("p", "f", n), part(r.gate_far, n))
        r.gates[...] += r.gate_far[n].astype(FULL)

    def pass_in(i):
        x_spread.pass_on(i)
        p_spread.pass_on(i)

    dispatch_out(0)
    pass_out(1)
    pass_out(2)
    dispatch_in(0)
    pass_in(1)
    dispatch_out(1)
    pass_out(3)
    dispatch_in(1)
    send_gates(0)
    pass_in(2)
    dispatch_out(2)
    pass_in(3)
    dispatch_out(3)
    dispatch_in(2)
    dispatch_in(3)
    send_gates(1)

    slot_lane = lax.broadcasted_iota(jnp.int32, (PAIR, FLAT), 1)
    r.parts[...] = jnp.zeros((2 * PAIR, FLAT), FULL)

    def run_experts(first, count):
        span = count * PAIR
        which = slice(first, first + count)
        place = slice(first * PAIR, (first + count) * PAIR)

        def one_expert(j, carry):
            base = pl.multiple_of(j * PAIR, PAIR)
            gates = r.gates[pl.ds(base, PAIR), :]
            gate_col = jnp.concatenate(
                [gates[:, p : p + 1] for p in range(first, first + count)], axis=0
            )
            columns = pl.ds(pl.multiple_of(j * FF, FF), FF)
            xs = r.x_slots[which, j].reshape(span, -1)
            gate_pre = mul(xs, r.gate_w[:, columns])
            up_pre = mul(xs, r.up_w[:, columns])
            sig = jax.nn.sigmoid(gate_pre)
            act = gate_pre * sig
            hidden = (act * up_pre).astype(LOW)
            r.hidden_all[j, place] = hidden
            result = mul(hidden, r.down_w[columns, :])
            gs = r.g_slots[which, j].reshape(span, -1).astype(FULL)
            r.g_slots[which, j] = (gate_col * result).astype(LOW).reshape(count, PAIR, -1)
            part = jnp.sum(gs * result, axis=1, keepdims=True).astype(LOW).astype(FULL)
            terms = jnp.zeros((PAIR, FLAT), FULL)
            for p in range(count):
                terms += jnp.where(
                    slot_lane == first + p, part[p * PAIR : (p + 1) * PAIR], 0.0
                )
            r.parts[pl.ds(base, PAIR), :] += terms
            result_grad = (gate_col * gs).astype(LOW)
            r.result_all[j, place] = result_grad
            hidden_grad = mul(result_grad, r.down_w[columns, :], LAST)
            gate_pre_grad = (
                hidden_grad * up_pre * sig * (1.0 + gate_pre * (1.0 - sig))
            ).astype(LOW)
            up_pre_grad = (hidden_grad * act).astype(LOW)
            r.gate_all[j, place] = gate_pre_grad
            r.up_all[j, place] = up_pre_grad
            rows_grad = mul(gate_pre_grad, r.gate_w[:, columns], LAST) + mul(
                up_pre_grad, r.up_w[:, columns], LAST
            )
            r.row_slots[which, j] = rows_grad.astype(LOW).reshape(count, PAIR, -1)
            return carry

        lax.fori_loop(0, 2, one_expert, 0)

    for copy in expert_loads:
        copy.wait()
    writes = []

    def weight_grads(j):
        xs = r.x_slots[:, j].reshape(8 * PAIR, -1)
        columns = slice(j * FF, (j + 1) * FF)
        r.gate_w[:, columns] = mul(xs, r.gate_all[j], FIRST).astype(LOW)
        r.up_w[:, columns] = mul(xs, r.up_all[j], FIRST).astype(LOW)
        r.down_w[columns, :] = mul(r.hidden_all[j], r.result_all[j], FIRST).astype(LOW)

    mine_at = pl.ds(pl.multiple_of(h * FF, FF), FF)
    theirs_at = pl.ds(pl.multiple_of((1 - h) * FF, FF), FF)
    top = r.hidden_all.shape[1]
    low_rows = width - top
    exchange = [
        (r.gate_w, (pl.ds(0, top), theirs_at), r.hidden_all, (0,)),
        (r.gate_w, (pl.ds(top, low_rows), theirs_at), r.hidden_all, (1, pl.ds(0, low_rows))),
        (r.up_w, (pl.ds(0, top), theirs_at), r.gate_all, (0,)),
        (r.up_w, (pl.ds(top, low_rows), theirs_at), r.gate_all, (1, pl.ds(0, low_rows))),
        (r.down_w, (theirs_at, pl.ds(0, FF)), r.up_all, (0, pl.ds(0, FF))),
        (r.down_w, (theirs_at, pl.ds(FF, FF)), r.up_all, (1, pl.ds(0, FF))),
    ]
    finals = [
        (r.gate_w, r.gate_out, (every, mine_at), (every, theirs_at)),
        (r.up_w, r.up_out, (every, mine_at), (every, theirs_at)),
        (r.down_w, r.down_out, (mine_at, every), (theirs_at, every)),
    ]

    def send_grads():
        for n, (source, spot, target, there) in enumerate(exchange):
            links.go(("e", n), part(source, *spot), part(target, *there), places.pair)

    def sum_grads():
        for n, (own, spot, other, there) in enumerate(exchange):
            links.got(("e", n), part(other, *there))
            spot = tuple(mine_at if one is theirs_at else one for one in spot)
            own[spot] = (own[spot].astype(FULL) + other[there].astype(FULL)).astype(LOW)
        for n, (source, out, spot, _) in enumerate(finals):
            writes.append(load(source.at[spot], out.at[spot]))
            links.go(("ef", n), part(source, *spot), part(out, *spot), places.pair)

    index = lax.broadcasted_iota(jnp.int32, (experts, 2 * FLAT), 0)

    def fold(name, rows, rows_in, kept, near_send, near_in, i):
        for n, cols in enumerate(columns):
            links.got((name, "f", i, n), part(rows_in, i, every, every, cols))
            stacked = jnp.concatenate(
                [
                    rows[i, :, :, cols].reshape(2 * PAIR, -1),
                    rows_in[i, :, :, cols].reshape(2 * PAIR, -1),
                ],
                axis=0,
            )
            sums = mul(r.pick[i], stacked, FIRST)
            kept[i, :, cols] = sums[:FLAT]
            send = near_send(i, cols)
            send()[...] = sums[FLAT:].astype(LOW)
            links.go((name, "n", i, n), send, part(near_in, i, every, cols), places.near)

    def send_far(name, rows, rows_in, i):
        for n, cols in enumerate(columns):
            links.go(
                (name, "f", i, n),
                part(rows, 4 + i, every, every, cols),
                part(rows_in, i, every, every, cols),
                places.far,
            )

    def fold_parts(i):
        column = jnp.concatenate(
            [r.parts[:, i : i + 1], r.parts_in[:, 4 + i : 5 + i]], axis=0
        )
        terms = r.pick[i].astype(FULL) * column
        table = jnp.zeros((experts, 2 * FLAT), FULL)
        chips = (places.e, places.e, places.far_e, places.far_e)
        for n, chip in enumerate(chips):
            total = jnp.sum(terms[n * PAIR : (n + 1) * PAIR], axis=0, keepdims=True)
            table += jnp.where(index == 2 * chip + n % 2, total, 0.0)
        r.part_kept[i] = table[:, :FLAT]
        r.part_send[i] = table[:, FLAT:]
        links.go(("q", "n", i, 0), part(r.part_send, i), part(r.part_near, i), places.near)

    row_sums = Gather(links, "rz", r.row_z_send, r.row_z_in, halves)
    part_sums = Gather(links, "qz", r.part_z_send, r.part_z_in, [()])
    weighted_sums = Gather(links, "wz", r.row_near_send, r.weighted_z_in, halves)

    def near_sum(name, kept, near_in, i, pieces):
        def value(n):
            spot = (i, *pieces[n])
            links.got((name, "n", i, n), part(near_in, *spot))
            return kept[spot] + near_in[spot].astype(FULL)

        return value

    def settle_rows(i):
        row_sums.push(i, near_sum("r", r.row_kept, r.row_near, i, row_sums.pieces))

    def settle_parts(i):
        part_sums.push(i, near_sum("q", r.part_kept, r.part_near, i, part_sums.pieces))

    def settle_weighted(i):
        weighted_sums.push(i, near_sum("w", r.row_kept, r.weighted_near, i, halves))

    def fold_weighted(i):
        fold(
            "w",
            r.g_slots,
            r.g_send,
            r.row_kept,
            lambda i, cols: part(r.x_all, i, 0, every, cols),
            r.weighted_near,
            i,
        )

    def far_experts(i):
        for n, cols in enumerate(g_columns):
            links.got(("g", "f", i, n), part(r.g_slots, 4 + i, every, every, cols))
        for n, cols in enumerate(columns):
            links.got(("x", "f", i, n), part(r.x_slots, 4 + i, every, every, cols))
        run_experts(4 + i, 1)
        send_far("r", r.row_slots, r.rows_in, i)

    def fold_rows(i):
        fold(
            "r",
            r.row_slots,
            r.rows_in,
            r.row_kept,
            lambda i, cols: part(r.row_near_send, i, every, cols),
            r.row_near,
            i,
        )

    add_gates(0)
    far_experts(1)
    far_experts(0)
    run_experts(0, 4)
    links.drain()
    add_gates(1)
    fold_rows(1)
    far_experts(3)
    far_experts(2)
    links.go(("q", "f"), whole(r.parts), whole(r.parts_in), places.far)
    settle_rows(1)
    fold_rows(3)
    fold_rows(2)
    settle_rows(3)
    links.got(("q", "f"), whole(r.parts_in))
    for i in (3, 2, 1, 0):
        fold_parts(i)
    settle_rows(2)
    for i in (3, 2, 1):
        settle_parts(i)
    fold_rows(0)
    def send_weighted(i):
        send_far("w", r.g_slots, r.g_send, i)

    send_weighted(3)
    send_weighted(2)
    weight_grads(0)
    weight_grads(1)
    fold_weighted(3)
    send_weighted(1)
    fold_weighted(2)
    send_weighted(0)
    fold_weighted(1)
    row_sums.total(
        near_sum("r", r.row_kept, r.row_near, 0, halves), lambda n: r.branch_in.at[halves[n]]
    )
    part_sums.total(
        near_sum("q", r.part_kept, r.part_near, 0, part_sums.pieces), lambda n: r.part_total
    )

    gate_probs, gate_grad = r.probs[...], r.part_total[...]
    chosen_grad = gate_probs * (
        gate_grad - jnp.sum(gate_probs * gate_grad, axis=0, keepdims=True)
    )
    logit_grad = chosen_grad.astype(LOW)
    xn_grad = r.branch_in[...] + mul(logit_grad, r.w_router[...], FIRST)
    mid = r.middle[...]
    scale = lax.rsqrt(jnp.mean(mid * mid, axis=-1, keepdims=True) + NORM_EPS)
    scaled = r.norm_two[...] * xn_grad
    pull = jnp.mean(scaled * mid, axis=-1, keepdims=True)
    grad = r.cotangent[...].astype(FULL) + scale * scaled - mid * (scale * scale * scale * pull)
    r.grad_tokens[...] = grad
    mine = part(r.branch_grad, pl.ds(half, FLAT))
    r.branch_grad[pl.ds(half, FLAT), :] = (RESIDUAL_SCALE * grad).astype(LOW)
    links.go("bg", mine, mine, places.pair)
    r.small[pl.ds(0, experts), :] = mul(logit_grad, r.x_all[0, 0])
    r.small[pl.ds(experts, 8), :] = jnp.broadcast_to(
        jnp.sum(xn_grad * mid * scale, axis=0, keepdims=True), (8, width)
    )

    links.drain("r")
    for i in (3, 2, 1):
        settle_weighted(i)
    fold_weighted(0)
    links.got("bg", part(r.branch_grad, pl.ds(other_half, FLAT)))
    r.heads_grad[...] = mul(r.branch_grad[...], r.w_out[...], LAST).astype(LOW)
    r.grads[pl.ds(width, q_cols), :] = mul(r.heads[...], r.branch_grad[...], FIRST).astype(LOW)
    cosine, sine = r.cosine[...], r.sine[...]

    def attend_back(first, count):
        def one(g, carry):
            place = pl.ds(pl.multiple_of(g * FLAT, FLAT), FLAT)
            out_grad = r.heads_grad[:, place]
            query = r.q[g]
            query_grad = jnp.zeros((rows_here, FLAT), FULL)
            key_grads, value_grads = [], []
            for s in range(2):
                probs = r.att_probs[g, s]
                prob_grad = mul(out_grad, r.values[g, s], LAST)
                inner = jnp.sum(probs * prob_grad, axis=1, keepdims=True)
                score_grad = (probs * (prob_grad - inner)).astype(LOW)
                query_grad += mul(score_grad, r.keys[g, s])
                key_grads.append(mul(score_grad, query, FIRST))
                value_grads.append(mul(probs.astype(LOW), out_grad, FIRST))
            r.head_grads[:, place] = turn(
                query_grad * ATTENTION_SCALE, r.cosine[...], r.sine[...], -1.0
            ).astype(LOW)
            r.key_sums[g] = key_grads[0] + pltpu.roll(key_grads[1], HEAD_DIMENSION, 1)
            r.value_sums[g] = value_grads[0] + pltpu.roll(value_grads[1], HEAD_DIMENSION, 1)
            return carry

        lax.fori_loop(first, first + count, one, 0)

    ranks = places.ranks
    plane = [[e % 4, places.near_e % 4], [places.far_e % 4, 3 - e % 4]]

    def along(name, spot):
        block = spot(0)
        links.go((name, "z", 1), block, block, places.edge)

        @pl.when(places.is_inner)
        def _():
            links.go((name, "z", 2), block, block, places.inner, "inner")

    def pass_along(name, spot, i):
        block = spot(i)
        links.got((name, "z", i), block)
        there = {1: 3, 2: 2, 3: 3}[i]
        device = places.inner if i == 1 else places.edge

        @pl.when(places.is_inner)
        def _():
            links.go((name, "z", there), block, block, device, "inner")

    class Reduce:
        order = [(a, i) for i in (3, 2, 1, 0) for a in (1, 0)]

        def __init__(self, name, first, count, room, near_first=False):
            self.name, self.first, self.depth, self.room = name, first, count // 16, room
            self.near_first = near_first
            self.rows = slice(room, room + self.depth)
            self.issued = 0
            self.sums = Gather(links, name + "z", r.sum_z_send, r.sum_z_in, [(self.rows,)])

        def shard(self, b, a, i):
            start = self.first + (ranks[i] * 4 + plane[b][a]) * self.depth
            return pl.ds(pl.multiple_of(start, 16), self.depth)

        def far_in(self, a, i):
            return part(r.g_all, i, a, self.rows)

        def near_in(self, i):
            return part(r.x_all, i, 1, self.rows)

        def near_send(self, i):
            return part(r.result_all, 0, pl.ds(4 * self.room + i * self.depth, self.depth))

        def send(self, count):
            for a, i in self.order[self.issued : self.issued + count]:
                source = part(r.grads, self.shard(1, a, i))
                links.go((self.name, "f", a, i), source, self.far_in(a, i), places.far)
            self.issued += count

        def fold(self, i):
            for a in (1, 0):
                links.got((self.name, "f", a, i), self.far_in(a, i))
                self.send(1)
                if a:
                    total = r.grads[self.shard(0, 1, i), :].astype(FULL) + r.g_all[
                        i, 1, self.rows
                    ].astype(FULL)
                    self.near_send(i)()[...] = total.astype(LOW)
                    links.go(
                        (self.name, "n", i), self.near_send(i), self.near_in(i), places.near
                    )

        def near_sum(self, i):
            links.got((self.name, "n", i), self.near_in(i))
            mine = self.shard(0, 0, i)
            return lambda n: (
                r.grads[mine, :].astype(FULL)
                + r.g_all[i, 0, self.rows].astype(FULL)
                + r.x_all[i, 1, self.rows].astype(FULL)
            )

        def settle(self, i):
            self.sums.push(i, self.near_sum(i))

        def spot(self, b, a, i):
            return part(r.grads_out, self.shard(b, a, i))

        def share(self):
            total = r.branch_send.at[self.rows]
            self.sums.total(self.near_sum(0), lambda n: total)
            low = part(r.result_all, 1, pl.ds(FLAT + self.room, self.depth))
            low()[...] = total[...].astype(LOW)
            mine = self.spot(0, 0, 0)
            links.go((self.name + "o", "z", 1), low, mine, places.edge)
            links.go((self.name, "on", 0), low, mine, places.near)

            @pl.when(places.is_inner)
            def _():
                links.go((self.name + "o", "z", 2), low, mine, places.inner, "inner")

            links.go((self.name, "of", 0, 0), low, mine, places.far)
            writes.append(load(low(), mine()))

        def pass_far(self, i):
            block = self.spot(0, 1, i)
            if i and self.near_first:
                pass_along(self.name + "p", lambda i: self.spot(0, 1, i), i)
            else:
                links.got((self.name, "on", i), block)
                if self.near_first:
                    along(self.name + "p", lambda i: self.spot(0, 1, i))
            links.go((self.name, "of", 1, i), block, block, places.far)

        def pass_on(self, i):
            block = self.spot(0, 0, i)
            pass_along(self.name + "o", lambda i: self.spot(0, 0, i), i)
            if not self.near_first:
                links.go((self.name, "on", i), block, block, places.near)
            links.go((self.name, "of", 0, i), block, block, places.far)

        def finish(self):
            for i in range(4):
                for a in range(2):
                    links.got((self.name, "of", a, i), self.spot(1, a, i))

    late = Reduce("b", width, q_cols, 0)
    early = Reduce("a", 0, width, q_cols // 16, near_first=True)
    late.send(8)
    attend_back(0, 4)
    for m in range(kv_heads // 2):
        start = q_cols + m * FLAT
        for sums, shift in ((r.key_sums, 0), (r.value_sums, k_cols)):
            block = jnp.where(
                low_lanes, sums[2 * m], pltpu.roll(sums[2 * m + 1], HEAD_DIMENSION, 1)
            )
            if shift == 0:
                block = turn(block * ATTENTION_SCALE, cosine, sine, -1.0)
            r.head_grads[:, start + shift : start + shift + FLAT] = block.astype(LOW)
    head_grads = r.head_grads
    r.grads[pl.ds(0, width), :] = mul(r.normed[...], head_grads[...], FIRST).astype(LOW)
    early.send(8)
    r.result_all[1, 0:FLAT] = mul(
        head_grads[pl.ds(other_half, FLAT), :], r.w_in[...], LAST
    ).astype(LOW)
    links.go("terms", part(r.result_all, 1, pl.ds(0, FLAT)), whole(r.terms_in), places.pair)
    own_terms = mul(head_grads[pl.ds(half, FLAT), :], r.w_in[...], LAST).astype(LOW)
    send_grads()
    late.fold(3)
    late.fold(2)
    late.fold(1)
    late.fold(0)
    late.settle(3)
    late.settle(2)
    late.settle(1)
    early.fold(3)
    early.fold(2)
    early.settle(3)
    early.fold(1)
    early.settle(2)
    early.fold(0)
    late.share()
    early.settle(1)
    links.got("terms", whole(r.terms_in))
    xn_grad = (own_terms.astype(FULL) + r.terms_in[...].astype(FULL)).astype(LOW).astype(FULL)
    x_half = r.tokens[pl.ds(half, FLAT), :].astype(FULL)
    scale = lax.rsqrt(jnp.mean(x_half * x_half, axis=-1, keepdims=True) + NORM_EPS)
    scaled = r.norm_one[...] * xn_grad
    pull = jnp.mean(scaled * x_half, axis=-1, keepdims=True)
    r.grad_tokens[...] = (
        r.grad_tokens[...] + scale * scaled - x_half * (scale * scale * scale * pull)
    )
    r.small_mine[0, pl.ds(0, experts), :] = r.small[pl.ds(0, experts), :]
    row = lax.broadcasted_iota(jnp.int32, (8, width), 0)
    r.small_mine[0, pl.ds(experts, 8), :] = jnp.where(
        row == 0,
        r.small[pl.ds(experts, 8), :],
        jnp.sum(xn_grad * x_half * scale, axis=0, keepdims=True),
    )
    links.go(("s", 0), part(r.small_mine, 0), part(r.small_in, 0), places.pair)
    late.pass_far(0)
    late.pass_on(1)
    early.share()
    sum_grads()
    links.got(("s", 0), part(r.small_in, 0))
    r.small_mine[1] = r.small_mine[0] + r.small_in[0]
    links.go(("s", 1), part(r.small_mine, 1), part(r.small_in, 1), places.far)
    late.pass_far(1)
    late.pass_on(2)
    early.pass_far(0)
    late.pass_far(2)
    late.pass_on(3)
    late.pass_far(3)
    links.got(("s", 1), part(r.small_in, 1))
    r.small_mine[2] = r.small_mine[1] + r.small_in[1]
    links.go(("s", 2), part(r.small_mine, 2), part(r.small_in, 2), places.near)
    early.pass_on(1)
    early.pass_far(1)
    early.pass_on(2)
    links.got(("s", 2), part(r.small_in, 2))
    r.small_all[z] = r.small_mine[2] + r.small_in[2]
    along("s", lambda i: part(r.small_all, ranks[i]))
    early.pass_far(2)
    early.pass_on(3)
    early.pass_far(3)
    weighted_sums.total(
        near_sum("w", r.row_kept, r.weighted_near, 0, halves),
        lambda n: r.branch_in.at[halves[n]],
    )
    r.layer_out[...] = (r.middle[...] + RESIDUAL_SCALE * r.branch_in[...]).astype(LOW)

    for i in (1, 2, 3):
        pass_along("s", lambda i: part(r.small_all, ranks[i]), i)
    small = ((r.small_all[0] + r.small_all[1]) + r.small_all[2]) + r.small_all[3]
    r.router_out[...] = small[:experts]
    r.norms_out[...] = small[experts:]
    late.finish()
    early.finish()
    for n, (_, out, _, spot) in enumerate(finals):
        links.got(("ef", n), part(out, *spot))
    for copy in writes:
        copy.wait()
    links.drain()


def run_layer(**inputs):
    rows_here, width = inputs["tokens"].shape
    experts = inputs["w_router"].shape[0]
    q_cols, k_cols = inputs["w_query"].shape[1], inputs["key_weight"].shape[1]
    kv_heads = k_cols // HEAD_DIMENSION
    vmem = pl.BlockSpec(memory_space=pltpu.VMEM)
    anywhere = pl.BlockSpec(memory_space=pl.ANY)
    block = (FLAT, width)
    gate = (experts, FLAT)
    slots = (2, PAIR, width)
    small = (experts + 8, width)
    grads = (width + q_cols, width)
    depth = grads[0] // 16
    outputs = {
        "layer_out": (block, LOW),
        "grad_tokens": (block, FULL),
        "router_out": (gate[:1] + (width,), FULL),
        "norms_out": ((8, width), FULL),
    }
    held = {"grads_out": (grads, LOW)} | {
        name + "_out": (inputs["w_" + name].shape, LOW) for name in ("gate", "up", "down")
    }
    heads = (kv_heads, 2, rows_here)
    scratch = {
        "w_in": ((width, q_cols + 2 * k_cols), LOW),
        "w_out": ((q_cols, width), LOW),
        "normed": ((rows_here, width), LOW),
        "q": ((kv_heads, rows_here, FLAT), LOW),
        "keys": (heads + (FLAT,), LOW),
        "values": (heads + (FLAT,), LOW),
        "bias": ((rows_here, rows_here), FULL),
        "att_probs": (heads + (rows_here,), FULL),
        "heads": ((rows_here, q_cols), LOW),
        "heads_grad": ((rows_here, q_cols), LOW),
        "head_grads": ((rows_here, q_cols + 2 * k_cols), LOW),
        "key_sums": ((kv_heads, rows_here, FLAT), FULL),
        "value_sums": ((kv_heads, rows_here, FLAT), FULL),
        "branch_send": (block, FULL),
        "branch_in": (block, FULL),
        "middle": (block, FULL),
        "branch_grad": ((rows_here, width), LOW),
        "small": (small, FULL),
        "terms_in": (block, LOW),
        "grads": (grads, LOW),
        "sum_z_send": ((4, depth, width), LOW),
        "sum_z_in": ((4, depth, width), LOW),
        "small_mine": ((3,) + small, FULL),
        "small_in": ((3,) + small, FULL),
        "small_all": ((4,) + small, FULL),
        "probs": (gate, FULL),
        "tables": ((4, 2) + gate, FULL),
        "gate_tables": ((4, 2) + gate, FULL),
        "g_all": ((4, 2) + block, LOW),
        "x_all": ((4, 2) + block, LOW),
        "g_slots": ((8,) + slots, LOW),
        "x_slots": ((8,) + slots, LOW),
        "row_slots": ((8,) + slots, LOW),
        "g_send": ((4,) + slots, LOW),
        "x_send": ((4,) + slots, LOW),
        "gates": ((2 * PAIR, FLAT), FULL),
        "gate_send": ((2, 2 * PAIR, FLAT), LOW),
        "gate_far": ((2, 2 * PAIR, FLAT), LOW),
        "parts": ((2 * PAIR, FLAT), FULL),
        "parts_in": ((2 * PAIR, FLAT), FULL),
        "pick": ((4, 4 * PAIR, 2 * FLAT), LOW),
        "gate_w": (inputs["w_gate"].shape, LOW),
        "up_w": (inputs["w_up"].shape, LOW),
        "down_w": (inputs["w_down"].shape, LOW),
        "hidden_all": ((2, 8 * PAIR, FF), LOW),
        "gate_all": ((2, 8 * PAIR, FF), LOW),
        "up_all": ((2, 8 * PAIR, FF), LOW),
        "result_all": ((2, 8 * PAIR, width), LOW),
        "rows_in": ((4,) + slots, LOW),
        "row_kept": ((4,) + block, FULL),
        "row_near": ((4,) + block, LOW),
        "row_near_send": ((4,) + block, LOW),
        "row_z_send": ((4,) + block, LOW),
        "row_z_in": ((4,) + block, LOW),
        "part_kept": ((4,) + gate, FULL),
        "part_near": ((4,) + gate, FULL),
        "part_send": ((4,) + gate, FULL),
        "part_z_send": ((4,) + gate, FULL),
        "part_z_in": ((4,) + gate, FULL),
        "part_total": (gate, FULL),
        "weighted_near": ((4,) + block, LOW),
        "weighted_z_in": ((4,) + block, LOW),
    }
    near_by = ("tokens", "norm_one", "norm_two", "w_router", "routes", "priority")
    near_by += ("cotangent", "cosine", "sine")
    names = [*inputs, *outputs, *held, *scratch, "sems_local", "sems_send", "sems_recv"]
    results = pl.pallas_call(
        functools.partial(layer_kernel, names),
        out_shape=[
            jax.ShapeDtypeStruct(shape, kind) for shape, kind in [*outputs.values(), *held.values()]
        ],
        in_specs=[vmem if name in near_by else anywhere for name in inputs],
        out_specs=[vmem] * len(outputs) + [anywhere] * len(held),
        scratch_shapes=[pltpu.VMEM(shape, kind) for shape, kind in scratch.values()]
        + [
            pltpu.SemaphoreType.DMA((20,)),
            pltpu.SemaphoreType.DMA((400,)),
            pltpu.SemaphoreType.DMA((380,)),
        ],
        compiler_params=pltpu.CompilerParams(
            collective_id=0, has_side_effects=True, vmem_limit_bytes=63 << 20
        ),
        name="layer",
    )(*inputs.values())
    return dict(zip([*outputs, *held], results))


def cast_kernel(*refs):
    parts, (first, second, layer, tokens, router, norms), outs = refs[:3], refs[3:9], refs[9:]
    q_cols, k_cols = outs[3].shape[1], outs[4].shape[1]
    for n in range(3):
        outs[n][...] = parts[n][...].astype(FULL)
    outs[3][...] = first[:, :q_cols].astype(FULL)
    outs[4][...] = first[:, q_cols : q_cols + k_cols].astype(FULL)
    outs[5][...] = first[:, q_cols + k_cols :].astype(FULL)
    outs[6][...] = second[...].astype(FULL)
    outs[7][...] = layer[...]
    outs[8][...] = tokens[...]
    outs[9][...] = router[...]
    outs[10][...] = norms[0:1, :]
    outs[11][...] = norms[1:2, :]


def cast_grads(done, q_cols, k_cols, steps=4):
    width = done["grads_out"].shape[1]
    parts = [done[name + "_out"] for name in ("gate", "up", "down")]
    rest = [done[name] for name in ("layer_out", "grad_tokens", "router_out", "norms_out")]

    def rows(shape, offset=0):
        block = shape[0] // steps
        return pl.BlockSpec((block, shape[1]), lambda i: (offset // block + i, 0))

    shapes = [parts[0].shape] * 3 + [(width, cols) for cols in (q_cols, k_cols, k_cols)]
    shapes += [(q_cols, width)] + [one.shape for one in rest[:3]]
    row = pl.BlockSpec((1, width), lambda i: (0, 0))
    return pl.pallas_call(
        cast_kernel,
        grid=(steps,),
        out_shape=[
            jax.ShapeDtypeStruct(shape, LOW if n == 7 else FULL)
            for n, shape in enumerate(shapes + [(1, width)] * 2)
        ],
        in_specs=[rows(one.shape) for one in parts]
        + [rows((width, width)), rows((q_cols, width), width)]
        + [rows(one.shape) for one in rest[:3]]
        + [pl.BlockSpec(rest[3].shape, lambda i: (0, 0))],
        out_specs=[rows(shape) for shape in shapes] + [row, row],
        compiler_params=pltpu.CompilerParams(vmem_limit_bytes=62 << 20),
        name="cast_grads",
    )(*parts, done["grads_out"], done["grads_out"], *rest)


def quick_shards(
    tokens,
    norm_one,
    w_query,
    key_weight,
    value_weight,
    w_output,
    norm_two,
    w_router,
    w_gate,
    w_up,
    w_down,
    routes,
    priority,
    cotangent,
):
    rows_here, width = tokens.shape
    experts = w_router.shape[1]
    q_cols, k_cols = w_query.shape[1], key_weight.shape[1]
    local_index = np.arange(rows_here, dtype=np.int32)
    prompt_rows, cont_rows = rows_here // 2, rows_here // 4
    position = np.where(
        local_index < prompt_rows,
        local_index,
        prompt_rows + (local_index - prompt_rows) % cont_rows,
    )
    frequency = ROPE_BASE ** (
        -(2.0 * np.arange(HEAD_DIMENSION // 2, dtype=np.float32)) / HEAD_DIMENSION
    )
    frequency = frequency.astype(np.float32)
    angle_table = position.astype(np.float32)[:, None] * np.tile(frequency, 4)[None, :]
    done = run_layer(
        tokens=tokens,
        norm_one=norm_one[None, :],
        norm_two=norm_two[None, :],
        w_router=w_router.T,
        routes=routes.T,
        priority=priority,
        cotangent=cotangent,
        cosine=jnp.asarray(np.cos(angle_table), FULL),
        sine=jnp.asarray(np.sin(angle_table), FULL),
        w_query=w_query,
        key_weight=key_weight,
        value_weight=value_weight,
        w_output=w_output,
        w_gate=w_gate,
        w_up=w_up,
        w_down=w_down,
    )
    gate, up, down, query, key, value, output, layer, token, router, second, first = cast_grads(
        done, q_cols, k_cols
    )
    return (
        layer,
        token,
        first[0],
        query,
        key,
        value,
        output,
        second[0],
        router.T,
        gate,
        up,
        down,
    )


def solution(mesh):
    body = quick_shards if dict(mesh.shape) == {"exp": 16, "head": 2} else shards
    return jax.shard_map(
        body,
        mesh=mesh,
        in_specs=(
            P("exp", None),
            P(),
            P(None, "head"),
            P(None, "head"),
            P(None, "head"),
            P("head", None),
            P(),
            P(),
            P(None, "exp"),
            P(None, "exp"),
            P("exp", None),
            P("exp", None),
            P(("exp", "head"), None),
            P(("exp", "head"), None),
        ),
        out_specs=(
            P(("exp", "head"), None),
            P(("exp", "head"), None),
            P(),
            P(None, "head"),
            P(None, "head"),
            P(None, "head"),
            P("head", None),
            P(),
            P(),
            P(None, "exp"),
            P(None, "exp"),
            P("exp", None),
        ),
        check_vma=False,
    )
```
